32 devices in a mesh: dp: 8 (over z, x), mp: 4 (over y, core).
Axes of the slice: x: 2, y: 2, z: 4, core: 2. Of those that a mesh axis runs over, the one named last changes fastest.
Arguments:
- image_in: bfloat16 [32, 1024, 512], P('dp', None, 'mp'), may hold values from -6 to 6
- out_cotangent: bfloat16 [32, 1024, 512], P('dp', None, 'mp'), may hold values from -6 to 6
- timesteps: int32 [32], P('dp'), may hold values from 0 to 999
- clip_embed: bfloat16 [32, 2048], P('dp'), may hold values from -6 to 6
- context_tokens: bfloat16 [32, 4, 2048], P('dp'), may hold values from -6 to 6
- image_count: int32 [8], P('dp'), may hold values from 1 to 4, as said below
- norm1_gain: float32 [512], P('mp'), may hold values from 0.5 to 1.5
- norm1_bias: float32 [512], P('mp'), may hold values from -3 to 3
- conv1_weight: bfloat16 [3, 3, 512, 512], P(None, None, None, 'mp'), may hold values from -0.09375 to 0.09375
- embed_weight: bfloat16 [2048, 2, 512], P(None, None, 'mp'), may hold values from -0.125 to 0.125
- norm2_gain: float32 [512], P('mp'), may hold values from 0.5 to 1.5
- norm2_bias: float32 [512], P('mp'), may hold values from -3 to 3
- conv2_weight: bfloat16 [3, 3, 512, 512], P(None, None, None, 'mp'), may hold values from -0.09375 to 0.09375
- conv2_bias: float32 [512], P('mp'), may hold values from -3 to 3
- norm3_gain: float32 [512], P('mp'), may hold values from 0.5 to 1.5
- norm3_bias: float32 [512], P('mp'), may hold values from -3 to 3
- qkv_weight: bfloat16 [512, 3, 512], P(None, None, 'mp'), may hold values from -0.375 to 0.375
- context_weight: bfloat16 [2048, 2, 512], P(None, None, 'mp'), may hold values from -0.1875 to 0.1875
- proj_weight: bfloat16 [512, 512], P('mp'), may hold values from -1 to 1
Outputs:
- block_out: bfloat16 [32, 1024, 512], P('dp', None, 'mp')
- image_grad: bfloat16 [32, 1024, 512], P('dp', None, 'mp')
- norm1_gain_grad: float32 [512], P('mp')
- norm1_bias_grad: float32 [512], P('mp')
- conv1_grad: float32 [3, 3, 512, 512], P(None, None, None, 'mp')
- embed_grad: float32 [2048, 2, 512], P(None, None, 'mp')
- norm2_gain_grad: float32 [512], P('mp')
- norm2_bias_grad: float32 [512], P('mp')
- conv2_grad: float32 [3, 3, 512, 512], P(None, None, None, 'mp')
- conv2_bias_grad: float32 [512], P('mp')
- norm3_gain_grad: float32 [512], P('mp')
- norm3_bias_grad: float32 [512], P('mp')
- qkv_grad: float32 [512, 3, 512], P(None, None, 'mp')
- context_grad: float32 [2048, 2, 512], P(None, None, 'mp')
- proj_grad: float32 [512, 512], P('mp')
The draws below stay inside these ranges and needn't reach their ends.
Inputs may be any that keep to these rules, and one draw needn't show every extreme that they name: `image_count`: the live images of a group fill its first slots; counts rise along the groups with a jitter of one, and the last group holds exactly 4.
All inputs are finite; a program needn't handle non-finite values.
Results may differ from the reference program's by a relative error of at most 0.039.
Values may be sent and summed in bfloat16 or wider, within the bound.
No kernel may reach another device: no remote copies, remote signals or barrier semaphores. Data moves between devices by JAX's collectives and lax.ppermute only.
A program may use at most 128 MiB of HBM per device.

```python
import math
import jax
import jax.numpy as jnp
from jax import lax

C = 512
GROUPS = 32
HEADS = 8
HEAD = 64
EMB = 2048
CTXW = 2048
CTX = 4
SIDE = 32
QBLOCK = 512
CAP = 4
PIX = 1024
BUCKETS = 8
IMAGES = 32


def draw_image_count(key, part):
    group_total = BUCKETS
    positions = jnp.arange(group_total, dtype=jnp.int32)
    baseline = 1 + (CAP - 1) * positions // max(group_total - 1, 1)
    jitter = jax.random.randint(key, (group_total,), -1, 2, dtype=jnp.int32)
    counts = jnp.clip(baseline + jitter, 1, CAP)
    return counts.at[group_total - 1].set(CAP)


def with_ends(drawn, own_key, smallest, high):
    longest = drawn.shape.index(max(drawn.shape))
    spots = []
    for shift in (0, 1):
        where = [jax.random.randint(jax.random.fold_in(own_key, axis), (), 0, length) for axis, length in enumerate(drawn.shape)]
        where[longest] = (where[longest] + shift) % drawn.shape[longest]
        spots.append(tuple(where))
    return drawn.at[spots[0]].set(smallest).at[spots[1]].set(high)


def steps_of(own_key, extent, pieces, low, top_value):
    def one(position, blocks):
        draws = jax.random.uniform(jax.random.fold_in(jax.random.fold_in(own_key, 6), position), (blocks,), jnp.float32, low / len(pieces), top_value / len(pieces))
        return jnp.repeat(jnp.exp(draws), extent[position] // blocks).reshape((-1,) + (1,) * (len(extent) - position - 1))

    factor_of = one(*pieces[0])
    for cut in pieces[1:]:
        factor_of = factor_of * one(*cut)
    return factor_of


def bell_draw(key, dims, scale, reach, pieces=(), kind=jnp.bfloat16):
    array = scale * jax.random.normal(key, dims, jnp.float32)
    if pieces:
        array = array * steps_of(key, dims, pieces, -0.22, 0.18)
    return jnp.clip(array, -reach, reach).astype(kind)


def setup_inputs(seed: int = 0) -> dict:
    seeds = jax.random.split(jax.random.key(seed), 20)
    image_in = bell_draw(seeds[0], (IMAGES, PIX, C), 1.0, 6.0, ((0, 8), (2, 4)))
    out_cotangent = bell_draw(seeds[1], (IMAGES, PIX, C), 1.0, 6.0, ((0, 8), (2, 4)))
    timesteps = with_ends(jax.random.randint(seeds[2], (IMAGES,), 0, 1000), jax.random.fold_in(seeds[2], 1), 0, 999).astype(jnp.int32)
    clip_embed = bell_draw(seeds[3], (IMAGES, EMB), 1.0, 6.0, ((0, 8),))
    context_tokens = bell_draw(seeds[4], (IMAGES, CTX, CTXW), 1.0, 6.0, ((0, 8),))
    image_count = draw_image_count(jax.random.fold_in(seeds[19], 71), 0)
    norm1_gain = jnp.clip(1.0 + 0.1 * jax.random.normal(seeds[6], (C,), jnp.float32), 0.5, 1.5)
    norm1_bias = bell_draw(seeds[7], (C,), 0.5, 3.0, ((0, 4),), jnp.float32)
    conv1_weight = bell_draw(seeds[8], (3, 3, C, C), (9 * C) ** -0.5, 0.09375, ((3, 4),))
    embed_weight = bell_draw(seeds[9], (EMB, 2, C), EMB ** -0.5, 0.125, ((2, 4),))
    norm2_gain = jnp.clip(1.0 + 0.1 * jax.random.normal(seeds[10], (C,), jnp.float32), 0.5, 1.5)
    norm2_bias = bell_draw(seeds[11], (C,), 0.5, 3.0, ((0, 4),), jnp.float32)
    conv2_weight = bell_draw(seeds[12], (3, 3, C, C), (9 * C) ** -0.5, 0.09375, ((3, 4),))
    conv2_bias = bell_draw(seeds[13], (C,), 0.5, 3.0, ((0, 4),), jnp.float32)
    norm3_gain = jnp.clip(1.0 + 0.1 * jax.random.normal(seeds[14], (C,), jnp.float32), 0.5, 1.5)
    norm3_bias = bell_draw(seeds[15], (C,), 0.5, 3.0, ((0, 4),), jnp.float32)
    qkv_weight = bell_draw(seeds[16], (C, 3, C), (C // 2) ** -0.5, 0.375, ((2, 4),))
    context_weight = bell_draw(seeds[17], (CTXW, 2, C), (CTXW // 2) ** -0.5, 0.1875, ((2, 4),))
    proj_weight = bell_draw(seeds[18], (C, C), (C // 16) ** -0.5, 1.0, ((0, 4),))
    return {"image_in": image_in, "out_cotangent": out_cotangent, "timesteps": timesteps, "clip_embed": clip_embed, "context_tokens": context_tokens, "image_count": image_count, "norm1_gain": norm1_gain, "norm1_bias": norm1_bias, "conv1_weight": conv1_weight, "embed_weight": embed_weight, "norm2_gain": norm2_gain, "norm2_bias": norm2_bias, "conv2_weight": conv2_weight, "conv2_bias": conv2_bias, "norm3_gain": norm3_gain, "norm3_bias": norm3_bias, "qkv_weight": qkv_weight, "context_weight": context_weight, "proj_weight": proj_weight}


@jax.custom_vjp
def low(v):
    return lax.optimization_barrier(v.astype(jnp.bfloat16)).astype(jnp.float32)

@jax.custom_vjp
def low_back(v):
    return v

def low_keep(v):
    return (low(v), None)

def low_pass(kept, grad):
    return (grad,)

def back_keep(v):
    return (v, None)

def back_low(kept, grad):
    return (low(grad),)
low.defvjp(low_keep, low_pass)
low_back.defvjp(back_keep, back_low)
EPSILON = 1e-05
HIGHEST = lax.Precision.HIGHEST

def group_norm(values, gain, offset_bias):
    row_count = values.shape[0]
    grouped = values.reshape(row_count, GROUPS, -1)
    center = lax.optimization_barrier(jnp.mean(grouped, axis=(0, 2), keepdims=True))
    spread = lax.optimization_barrier(jnp.mean(jnp.square(grouped - center), axis=(0, 2), keepdims=True))
    normed = ((grouped - center) * lax.rsqrt(spread + EPSILON)).reshape(row_count, -1)
    return normed * gain + offset_bias

def conv_three(field, weight):
    grid = field.reshape(SIDE, SIDE, -1)
    padded = jnp.pad(grid, ((1, 1), (1, 1), (0, 0)))
    total_sum = jnp.zeros((SIDE * SIDE, weight.shape[3]), jnp.float32)
    for tap_row in range(3):
        for tap_col in range(3):
            window = padded[tap_row:tap_row + SIDE, tap_col:tap_col + SIDE].reshape(SIDE * SIDE, -1)
            total_sum = total_sum + jnp.dot(window, weight[tap_row, tap_col], precision=HIGHEST, preferred_element_type=jnp.float32)
    return total_sum

def attend(queries, keys, values):
    head_scale = 1.0 / math.sqrt(HEAD)
    heads_k = keys.reshape(-1, HEADS, HEAD)
    heads_v = values.reshape(-1, HEADS, HEAD)

    def one_block(query_block):
        heads_q = query_block.reshape(-1, HEADS, HEAD)
        raw_scores = low_back(jnp.einsum('qhd,khd->hqk', heads_q, heads_k, precision=HIGHEST))
        weights = low(jax.nn.softmax(raw_scores * head_scale, axis=-1))
        mixed = jnp.einsum('hqk,khd->qhd', weights, heads_v, precision=HIGHEST)
        return mixed.reshape(-1, C)
    blocks = queries.reshape(PIX // QBLOCK, QBLOCK, C)
    return lax.map(jax.checkpoint(one_block), blocks).reshape(PIX, C)

def forward(params, image, context, cond_row):
    norm1_gain, norm1_bias, conv1_weight, embed_weight, norm2_gain, norm2_bias, conv2_weight, conv2_bias, norm3_gain, norm3_bias, qkv_weight, context_weight, proj_weight = params
    first = low(jax.nn.silu(group_norm(image, norm1_gain, norm1_bias)))
    inner = low_back(conv_three(first, conv1_weight))
    scale_shift = jnp.dot(cond_row, embed_weight.reshape(EMB, 2 * C), precision=HIGHEST, preferred_element_type=jnp.float32)
    modulated = group_norm(inner, norm2_gain, norm2_bias) * (1.0 + scale_shift[:C]) + scale_shift[C:]
    second = low(jax.nn.silu(modulated))
    branch = low_back(conv_three(second, conv2_weight) + conv2_bias)
    middle = image + branch
    attn_in = low(group_norm(middle, norm3_gain, norm3_bias))
    qkv_all = low(low_back(jnp.dot(attn_in, qkv_weight.reshape(C, 3 * C), precision=HIGHEST, preferred_element_type=jnp.float32)))
    ctx_kv = low(low_back(jnp.dot(context, context_weight.reshape(CTXW, 2 * C), precision=HIGHEST, preferred_element_type=jnp.float32)))
    keys = jnp.concatenate([ctx_kv[:, :C], qkv_all[:, C:2 * C]], axis=0)
    values = jnp.concatenate([ctx_kv[:, C:], qkv_all[:, 2 * C:]], axis=0)
    mixed = low(low_back(attend(qkv_all[:, :C], keys, values)))
    return middle + jnp.dot(mixed, proj_weight, precision=HIGHEST, preferred_element_type=jnp.float32)

def condition(step_value, clip_row):
    half_width = EMB // 2
    frequency = jnp.exp(-math.log(10000.0) * jnp.arange(half_width, dtype=jnp.float32) / half_width)
    angles = step_value.astype(jnp.float32) * frequency
    return low(jax.nn.silu(jnp.concatenate([jnp.cos(angles), jnp.sin(angles)]) + clip_row))

def add_up(total_sum, fresh):
    return total_sum + fresh

def reference(image_in, out_cotangent, timesteps, clip_embed, context_tokens, image_count, norm1_gain, norm1_bias, conv1_weight, embed_weight, norm2_gain, norm2_bias, conv2_weight, conv2_bias, norm3_gain, norm3_bias, qkv_weight, context_weight, proj_weight):
    params = (norm1_gain.astype(jnp.float32), norm1_bias.astype(jnp.float32), conv1_weight.astype(jnp.float32), embed_weight.astype(jnp.float32), norm2_gain.astype(jnp.float32), norm2_bias.astype(jnp.float32), conv2_weight.astype(jnp.float32), conv2_bias.astype(jnp.float32), norm3_gain.astype(jnp.float32), norm3_bias.astype(jnp.float32), qkv_weight.astype(jnp.float32), context_weight.astype(jnp.float32), proj_weight.astype(jnp.float32))
    slot_index = jnp.arange(IMAGES, dtype=jnp.int32) % CAP
    live = (slot_index < jnp.repeat(image_count, CAP)).astype(jnp.float32)
    image_total = jnp.sum(image_count).astype(jnp.float32)
    zero_sums = jax.tree.map(jnp.zeros_like, params)

    def per_image(grad_sums, inputs):
        image, cotangent, step_value, clip_row, context, alive = inputs
        cond_row = condition(step_value, clip_row)

        def local_forward(weights, image_value):
            return forward(weights, image_value, context, cond_row)
        result, pullback = jax.vjp(local_forward, params, image)
        weight_grads, input_grad = pullback(cotangent * alive)
        grad_sums = jax.tree.map(add_up, grad_sums, weight_grads)
        return (grad_sums, ((result * alive).astype(jnp.bfloat16), input_grad.astype(jnp.bfloat16)))
    grad_sums, (block_out, image_grad) = lax.scan(per_image, zero_sums, (image_in.astype(jnp.float32), out_cotangent.astype(jnp.float32), timesteps, clip_embed.astype(jnp.float32), context_tokens.astype(jnp.float32), live))
    finals = tuple((member / image_total for member in grad_sums))
    return (block_out, image_grad, finals[0], finals[1], finals[2], finals[3], finals[4], finals[5], finals[6], finals[7], finals[8], finals[9], finals[10], finals[11], finals[12])
```

```python
import functools
import math

import jax
import jax.numpy as jnp
from jax import lax
from jax.experimental import pallas as pl
from jax.experimental.pallas import tpu as pltpu
from jax.sharding import PartitionSpec as P

C = 512
GROUPS = 32
HEAD = 64
EMB = 2048
CTX = 4
SIDE = 32
LANES = 128
PAD = SIDE
EPSILON = 1e-05
F32 = jnp.float32
BF16 = jnp.bfloat16
NEG = -1e30

E_SCALE, E_SHIFT, E_G1, E_B1, E_G2, E_B2, E_CB2, E_G3, E_B3 = range(9)
E_KEY, E_VALUE, E_ROWS = 16, 24, 32
S_G3, S_B3, S_CB2, S_G2, S_B2, S_SCALE, S_SHIFT, S_LIVE = range(8)
S_KEY, S_VALUE, S_ROWS = 8, 12, 16
VMEM_LIMIT = 56 << 20


def vmem():
    return pl.BlockSpec(memory_space=pltpu.VMEM)


def anywhere():
    return pl.BlockSpec(memory_space=pl.ANY)


def smem():
    return pl.BlockSpec(memory_space=pltpu.SMEM)


def struct(shape, dtype):
    return jax.ShapeDtypeStruct(shape, dtype)


def call(body, name, out_shape, in_specs, scratch, flops=0, moved=0):
    many = isinstance(out_shape, (list, tuple))
    return pl.pallas_call(
        body,
        name=name,
        out_shape=out_shape,
        in_specs=in_specs,
        out_specs=[vmem() for _ in out_shape] if many else vmem(),
        scratch_shapes=scratch,
        compiler_params=pltpu.CompilerParams(vmem_limit_bytes=VMEM_LIMIT),
        cost_estimate=pl.CostEstimate(flops=flops, transcendentals=0, bytes_accessed=moved),
    )


def fetch(sources, target, me, sems, first):
    copies = []
    for offset, source in enumerate(sources):
        copy = pltpu.make_async_copy(
            source, target.at[jnp.bitwise_xor(me, offset)], sems.at[first + offset]
        )
        copy.start()
        copies.append(copy)
    return copies


def wait_all(copies):
    for copy in copies:
        copy.wait()


def fold(values):
    rows = values.shape[0]
    return jnp.sum(values.reshape(rows // 8, 8, values.shape[1]), axis=0)


def group_sum(rows8):
    lane = lax.broadcasted_iota(jnp.int32, rows8.shape, 1)
    total = jnp.broadcast_to(jnp.sum(rows8, axis=0, keepdims=True), rows8.shape)
    for step in (1, 2, 4, 8):
        up = pltpu.roll(total, step, axis=1)
        down = pltpu.roll(total, LANES - step, axis=1)
        total = total + jnp.where((lane & step) != 0, up, down)
    return total[0:1]


def column_sum(rows8):
    return jnp.sum(rows8, axis=0, keepdims=True)


def accumulate(rows, strip, functions):
    def body(index, carry):
        start = pl.multiple_of(index * strip, strip)
        found = functions(start)
        return tuple(old + fold(new) for old, new in zip(carry, found))

    count = len(jax.eval_shape(lambda: functions(0))) if False else None
    del count
    return body


def sum_strips(pixels, strip, width, function):
    zero = tuple(jnp.zeros((8, LANES), F32) for _ in range(width))

    def body(index, carry):
        start = pl.multiple_of(index * strip, strip)
        return tuple(old + fold(new) for old, new in zip(carry, function(start)))

    return lax.fori_loop(0, pixels // strip, body, zero)


def norm_rows(pixels, strip, read):
    count = pixels * (C // GROUPS)
    sums = sum_strips(pixels, strip, 4, lambda start: [read(b, start) for b in range(4)])
    means = [group_sum(s) * (1.0 / count) for s in sums]
    squares = sum_strips(
        pixels,
        strip,
        4,
        lambda start: [jnp.square(read(b, start) - means[b]) for b in range(4)],
    )
    inverses = [lax.rsqrt(group_sum(s) * (1.0 / count) + EPSILON) for s in squares]
    return means, inverses


def shifted(values):
    rows = values.shape[0]
    column = lax.broadcasted_iota(jnp.int32, values.shape, 0) & (SIDE - 1)
    left = jnp.where(column == 0, 0.0, pltpu.roll(values, 1, axis=0))
    right = jnp.where(column == SIDE - 1, 0.0, pltpu.roll(values, rows - 1, axis=0))
    return left, values, right


def store_shifted(target, block, start, values):
    rows = values.shape[0]
    for position, part in enumerate(shifted(values)):
        target[position, block, pl.ds(pl.multiple_of(PAD + start, 32), rows), :] = part.astype(BF16)


def clear_padding(target, pixels):
    zero = jnp.zeros((PAD, LANES), BF16)
    for position in range(3):
        for block in range(4):
            target[position, block, 0:PAD, :] = zero
            target[position, block, PAD + pixels : PAD + pixels + PAD, :] = zero


def conv_tiles(field, weight, pixels, tile, write):
    def body(index, carry):
        start = pl.multiple_of(index * tile, tile)
        left = jnp.concatenate(
            [
                field[b, block, pl.ds(pl.multiple_of(start + a * SIDE, 32), tile), :]
                for a in range(3)
                for b in range(3)
                for block in range(4)
            ],
            axis=1,
        )
        right = jnp.concatenate([weight[s].reshape(9 * C, LANES) for s in range(4)], axis=1)
        write(start, jnp.dot(left, right, preferred_element_type=F32))
        return carry

    lax.fori_loop(0, pixels // tile, body, 0)


def conv_back_tiles(field, weight, pixels, tile, write):
    def body(index, carry):
        start = pl.multiple_of((index // 2) * tile, tile)
        half = index % 2
        left = jnp.concatenate(
            [
                field[2 - b, block, pl.ds(pl.multiple_of(start + (2 - a) * SIDE, 32), tile), :]
                for a in range(3)
                for b in range(3)
                for block in range(4)
            ],
            axis=1,
        )
        right = jnp.concatenate(
            [
                weight[block, 3 * a + b, pl.ds(pl.multiple_of(half * 256, 256), 256), :]
                for a in range(3)
                for b in range(3)
                for block in range(4)
            ],
            axis=1,
        )
        write(
            start,
            half,
            lax.dot_general(left, right, (((1,), (1,)), ((), ())), preferred_element_type=F32),
        )
        return carry

    lax.fori_loop(0, 2 * (pixels // tile), body, 0)


def silu_slope(before, grad_out):
    gate = jax.nn.sigmoid(before)
    return grad_out * gate * (1.0 + before * (1.0 - gate))


def kernel_first(
    meta, i0, i1, i2, i3, w0, w1, w2, w3, e0, e1, e2, e3,
    image, pack, first_t, inner, second, second_t, field, weight, sems,
):
    pixels = image.shape[1]
    me = meta[0]
    image_copies = fetch((i0, i1, i2, i3), image, me, sems, 0)
    pack_copies = fetch((e0, e1, e2, e3), pack, me, sems, 4)
    weight_copies = fetch((w0, w1, w2, w3), weight, me, sems, 8)
    clear_padding(field, pixels)
    wait_all(image_copies)
    wait_all(pack_copies)
    strip = 128

    def read(block, start):
        return image[block, pl.ds(start, strip), :].astype(F32)

    means, inverses = norm_rows(pixels, strip, read)

    def normalise(index, carry):
        start = pl.multiple_of(index * strip, strip)
        for b in range(4):
            gain = pack[b, E_G1 : E_G1 + 1, :]
            bias = pack[b, E_B1 : E_B1 + 1, :]
            before = (read(b, start) - means[b]) * inverses[b] * gain + bias
            after = before * jax.nn.sigmoid(before)
            store_shifted(field, b, start, after)
            first_t[b, :, pl.ds(start, strip)] = after.T.astype(BF16)
        return carry

    lax.fori_loop(0, pixels // strip, normalise, 0)
    wait_all(weight_copies)

    def write(start, tile):
        for b in range(4):
            inner[b, pl.ds(start, tile.shape[0]), :] = tile[:, b * LANES : (b + 1) * LANES]

    conv_tiles(field, weight, pixels, 512, write)
    means2, inverses2 = norm_rows(pixels, strip, lambda b, start: inner[b, pl.ds(start, strip), :])

    def modulate(index, carry):
        start = pl.multiple_of(index * strip, strip)
        for b in range(4):
            gain = pack[b, E_G2 : E_G2 + 1, :]
            bias = pack[b, E_B2 : E_B2 + 1, :]
            scale = pack[b, E_SCALE : E_SCALE + 1, :]
            shift = pack[b, E_SHIFT : E_SHIFT + 1, :]
            normed = (inner[b, pl.ds(start, strip), :] - means2[b]) * inverses2[b]
            modulated = (normed * gain + bias) * (1.0 + scale) + shift
            after = modulated * jax.nn.sigmoid(modulated)
            second[b, pl.ds(start, strip), :] = after.astype(BF16)
            second_t[b, :, pl.ds(start, strip)] = after.T.astype(BF16)
        return carry

    lax.fori_loop(0, pixels // strip, modulate, 0)


def kernel_second(
    meta, second, image, pack, w0, w1, w2, w3, p0, p1, p2, p3,
    middle, attn_t, qkv, field, weight, qkv_weight, attn, sems,
):
    pixels = image.shape[1]
    me = meta[0]
    weight_copies = fetch((w0, w1, w2, w3), weight, me, sems, 0)
    qkv_copies = fetch((p0, p1, p2, p3), qkv_weight, me, sems, 4)
    clear_padding(field, pixels)
    strip = 128

    def spread(index, carry):
        start = pl.multiple_of(index * strip, strip)
        for b in range(4):
            store_shifted(field, b, start, second[b, pl.ds(start, strip), :].astype(F32))
        return carry

    lax.fori_loop(0, pixels // strip, spread, 0)
    wait_all(weight_copies)

    def write(start, tile):
        rows = tile.shape[0]
        for b in range(4):
            branch = tile[:, b * LANES : (b + 1) * LANES] + pack[b, E_CB2 : E_CB2 + 1, :]
            middle[b, pl.ds(start, rows), :] = image[b, pl.ds(start, rows), :].astype(F32) + branch

    conv_tiles(field, weight, pixels, 512, write)
    means, inverses = norm_rows(pixels, strip, lambda b, start: middle[b, pl.ds(start, strip), :])

    def normalise(index, carry):
        start = pl.multiple_of(index * strip, strip)
        for b in range(4):
            normed = (middle[b, pl.ds(start, strip), :] - means[b]) * inverses[b]
            value = normed * pack[b, E_G3 : E_G3 + 1, :] + pack[b, E_B3 : E_B3 + 1, :]
            attn[b, pl.ds(start, strip), :] = value.astype(BF16)
            attn_t[b, :, pl.ds(start, strip)] = value.T.astype(BF16)
        return carry

    lax.fori_loop(0, pixels // strip, normalise, 0)
    wait_all(qkv_copies)

    def project(index, carry):
        s = index // 2
        start = pl.multiple_of((index % 2) * 512, 512)
        left = jnp.concatenate([attn[b, pl.ds(start, 512), :] for b in range(4)], axis=1)
        right = jnp.concatenate([qkv_weight[s, kind] for kind in range(3)], axis=1)
        qkv[s, pl.ds(start, 512), :] = jnp.dot(left, right, preferred_element_type=F32).astype(BF16)
        return carry

    lax.fori_loop(0, 4 * (pixels // 512), project, 0)


def kernel_attention(
    meta, qkv, pack, middle, c0, c1, c2, c3, w0, w1, w2, w3,
    o0, o1, o2, o3, cot, mixed, dqkv, dctx,
    weight, grad_mixed, score_ctx, grad_ctx_prob, prob_ctx, dscore_ctx, out_pix, dquery, dkey_t, dvalue_t, sems,
):
    pixels = qkv.shape[1]
    me = meta[0]
    alive = meta[1].astype(F32)
    cot_copies = fetch((c0, c1, c2, c3), cot, me, sems, 0)
    weight_copies = fetch((w0, w1, w2, w3), weight, me, sems, 4)
    scale = 1.0 / math.sqrt(HEAD)
    block = 256

    row32 = lax.broadcasted_iota(jnp.int32, (32, LANES), 0)
    lane32 = lax.broadcasted_iota(jnp.int32, (32, LANES), 1)

    def diagonal(kind):
        found = []
        for s in range(4):
            rows8 = pack[s, kind : kind + 8, :]
            tiled = jnp.concatenate([rows8] * 4, axis=0)
            own = (row32 // 4) == (2 * s + lane32 // HEAD)
            kept = jnp.where(own, tiled, 0.0)
            found.append(jnp.concatenate([kept, jnp.zeros((96, LANES), F32)], axis=0).astype(BF16))
        return jnp.concatenate(found, axis=1)

    keys_ctx = diagonal(E_KEY)
    values_ctx = diagonal(E_VALUE)
    wait_all(cot_copies)
    wait_all(weight_copies)

    def prepare(index, carry):
        start = pl.multiple_of(index * block, block)
        rows = pl.ds(start, block)
        for s in range(4):
            cot[s, rows, :] = (cot[s, rows, :].astype(F32) * alive).astype(BF16)
        all_cot = jnp.concatenate([cot[s, rows, :] for s in range(4)], axis=1)
        all_weight = weight[...].reshape(C, C)
        grad = lax.dot_general(
            all_cot, all_weight, (((1,), (1,)), ((), ())), preferred_element_type=F32
        ).astype(BF16)
        for s in range(4):
            grad_mixed[s, rows, :] = grad[:, s * LANES : (s + 1) * LANES]
        query = jnp.concatenate([qkv[s, rows, 0:LANES] for s in range(4)], axis=1)
        score_ctx[rows, :] = lax.dot_general(
            query, keys_ctx, (((1,), (1,)), ((), ())), preferred_element_type=F32
        )
        grad_ctx_prob[rows, :] = lax.dot_general(
            grad, values_ctx, (((1,), (1,)), ((), ())), preferred_element_type=F32
        )
        prob_ctx[rows, :] = jnp.zeros((block, LANES), F32)
        dscore_ctx[rows, :] = jnp.zeros((block, LANES), F32)
        return carry

    lax.fori_loop(0, pixels // block, prepare, 0)
    lane = lax.broadcasted_iota(jnp.int32, (block, LANES), 1)
    low = lane < HEAD
    ones = jnp.ones((pixels, LANES), BF16)
    blocks = pixels // block

    def attend(index, carry):
        s = index // blocks
        part = index % blocks
        rows = pl.ds(pl.multiple_of(part * block, block), block)

        @pl.when(part == 0)
        def _():
            dkey_t[...] = jnp.zeros((LANES, pixels), F32)
            dvalue_t[...] = jnp.zeros((LANES, pixels), F32)

        query = qkv[s, rows, 0:LANES]
        key = qkv[s, :, LANES : 2 * LANES]
        value = qkv[s, :, 2 * LANES : 3 * LANES]
        value_ones = jnp.concatenate([value, ones], axis=1)
        grad = grad_mixed[s, rows, :]
        ctx_scores = score_ctx[rows, :]
        ctx_grads = grad_ctx_prob[rows, :]
        exps, outs, inverses, ctx_exps, owns = [], [], [], [], []
        for h in range(2):
            mine = low if h == 0 else jnp.logical_not(low)
            own = lane // CTX == 2 * s + h
            score = lax.dot_general(
                jnp.where(mine, query, jnp.zeros_like(query)),
                key,
                (((1,), (1,)), ((), ())),
                preferred_element_type=F32,
            )
            top = jnp.maximum(
                jnp.max(score, axis=1, keepdims=True),
                jnp.max(jnp.where(own, ctx_scores, NEG), axis=1, keepdims=True),
            )
            exp = jnp.exp((score - top) * scale).astype(BF16)
            ctx_exp = jnp.where(own, jnp.exp((ctx_scores - top) * scale), 0.0)
            out = jnp.dot(exp, value_ones, preferred_element_type=F32)
            total = out[:, LANES:] + jnp.sum(ctx_exp, axis=1, keepdims=True)
            inverse = 1.0 / total
            exps.append(exp)
            outs.append(out[:, :LANES] * inverse)
            inverses.append(inverse)
            ctx_exps.append(ctx_exp)
            owns.append(own)
        out_pair = jnp.where(low, outs[0], outs[1])
        out_pix[s, rows, :] = out_pair
        inverse_pair = jnp.where(low, inverses[0], inverses[1])
        scaled = (grad.astype(F32) * (inverse_pair * scale)).astype(BF16)
        product = out_pair * scaled.astype(F32)
        query_t = query.astype(F32).T.astype(BF16)
        scaled_t = scaled.astype(F32).T.astype(BF16)
        prob_keep = prob_ctx[rows, :]
        dscore_keep = dscore_ctx[rows, :]
        dqs = []
        for h in range(2):
            mine = low if h == 0 else jnp.logical_not(low)
            own = owns[h]
            ctx_prob = ctx_exps[h] * inverses[h]
            ctx_grad = ctx_grads * (inverses[h] * scale)
            dot = jnp.sum(
                jnp.where(mine, product, 0.0) + ctx_prob * jnp.where(own, ctx_grad, 0.0),
                axis=1,
                keepdims=True,
            )
            weight_grad = lax.dot_general(
                jnp.where(mine, scaled, jnp.zeros_like(scaled)),
                value,
                (((1,), (1,)), ((), ())),
                preferred_element_type=F32,
            )
            dscore = (exps[h].astype(F32) * (weight_grad - dot)).astype(BF16)
            prob_keep = jnp.where(own, ctx_prob, prob_keep)
            dscore_keep = jnp.where(own, ctx_exps[h] * (ctx_grad - dot), dscore_keep)
            dqs.append(jnp.dot(dscore, key, preferred_element_type=F32))
            half = slice(h * HEAD, (h + 1) * HEAD)
            dkey_t[half, :] += jnp.dot(query_t[half], dscore, preferred_element_type=F32)
            dvalue_t[half, :] += jnp.dot(scaled_t[half], exps[h], preferred_element_type=F32)
        prob_ctx[rows, :] = prob_keep
        dscore_ctx[rows, :] = dscore_keep
        dquery[s, rows, :] = jnp.where(low, dqs[0], dqs[1])

        @pl.when(part == blocks - 1)
        def _():
            for piece in range(pixels // LANES):
                cut = slice(piece * LANES, (piece + 1) * LANES)
                dqkv[s, cut, LANES : 2 * LANES] = dkey_t[:, cut].T.astype(BF16)
                dqkv[s, cut, 2 * LANES : 3 * LANES] = (dvalue_t[:, cut] * (1.0 / scale)).T.astype(BF16)

        return carry

    lax.fori_loop(0, 4 * blocks, attend, 0)

    def finish(index, carry):
        dkeys, dvalues = carry
        start = pl.multiple_of(index * block, block)
        rows = pl.ds(start, block)
        prob = prob_ctx[rows, :].astype(BF16)
        dscore = dscore_ctx[rows, :].astype(BF16)
        out_ctx = jnp.dot(prob, values_ctx, preferred_element_type=F32)
        dquery_ctx = jnp.dot(dscore, keys_ctx, preferred_element_type=F32)
        parts = []
        for s in range(4):
            cut = slice(s * LANES, (s + 1) * LANES)
            both = (out_pix[s, rows, :] + out_ctx[:, cut]).astype(BF16)
            mixed[s, rows, :] = both
            parts.append(both)
            dqkv[s, rows, 0:LANES] = (dquery[s, rows, :] + dquery_ctx[:, cut]).astype(BF16)
        result = jnp.dot(
            jnp.concatenate(parts, axis=1), weight[...].reshape(C, C), preferred_element_type=F32
        )
        for offset, target in enumerate((o0, o1, o2, o3)):
            other = jnp.bitwise_xor(me, offset)
            value = jnp.zeros((block, LANES), F32)
            for s in range(4):
                value = jnp.where(other == s, result[:, s * LANES : (s + 1) * LANES], value)
            target[rows, :] = ((middle[other, rows, :] + value) * alive).astype(BF16)
        query = jnp.concatenate([qkv[s, rows, 0:LANES] for s in range(4)], axis=1)
        grad = jnp.concatenate([grad_mixed[s, rows, :] for s in range(4)], axis=1)
        dkeys = dkeys + jnp.dot(dscore_ctx[rows, :].T[0:32].astype(BF16), query, preferred_element_type=F32)
        dvalues = dvalues + jnp.dot(prob_ctx[rows, :].T[0:32].astype(BF16), grad, preferred_element_type=F32)
        return dkeys, dvalues

    zero = jnp.zeros((32, C), F32)
    dkeys, dvalues = lax.fori_loop(0, pixels // block, finish, (zero, zero))
    for s in range(4):
        own = (row32 // 4) == (2 * s + lane32 // HEAD)
        for position, source in enumerate((dkeys, dvalues)):
            kept = jnp.where(own, source[:, s * LANES : (s + 1) * LANES], 0.0)
            eight = jnp.sum(kept.reshape(4, 8, LANES), axis=0)
            folded = eight + pltpu.roll(eight, 4, axis=0)
            dctx[s, position * CTX : (position + 1) * CTX, :] = folded[0:CTX]


def norm_back_strips(pixels, strip, read_normed, read_grad, gains, inverses, write):
    count = pixels * (C // GROUPS)

    def terms(start):
        found = []
        for b in range(4):
            grad = read_grad(b, start)
            found += [grad, grad * read_normed(b, start)]
        return found

    sums = sum_strips(pixels, strip, 8, terms)
    bias_sums = [column_sum(sums[2 * b]) for b in range(4)]
    gain_sums = [column_sum(sums[2 * b + 1]) for b in range(4)]
    firsts = [
        group_sum(jnp.broadcast_to(bias_sums[b] * gains[b], (8, LANES)) * (1.0 / 8)) * (1.0 / count)
        for b in range(4)
    ]
    seconds = [
        group_sum(jnp.broadcast_to(gain_sums[b] * gains[b], (8, LANES)) * (1.0 / 8)) * (1.0 / count)
        for b in range(4)
    ]

    def body(index, carry):
        start = pl.multiple_of(index * strip, strip)
        for b in range(4):
            normed = read_normed(b, start)
            grad = read_grad(b, start) * gains[b]
            write(b, start, inverses[b] * (grad - firsts[b] - normed * seconds[b]))
        return carry

    lax.fori_loop(0, pixels // strip, body, 0)
    return gain_sums, bias_sums


def kernel_back_attention(
    meta, dqkv, mixed, attn_t, cot, middle, pack, dctx, p0, p1, p2, p3,
    keep, send, dmiddle, field, sums, qkv_weight, cot_t, dattn, sems,
):
    pixels = cot.shape[1]
    me = meta[0]
    alive = meta[1].astype(F32)
    qkv_copies = fetch((p0, p1, p2, p3), qkv_weight, me, sems, 0)
    strip = 128
    clear_padding(field, pixels)

    def turn(index, carry):
        start = pl.multiple_of(index * strip, strip)
        for b in range(4):
            cot_t[b, :, pl.ds(start, strip)] = cot[b, pl.ds(start, strip), :].astype(F32).T.astype(BF16)
        return carry

    lax.fori_loop(0, pixels // strip, turn, 0)
    wait_all(qkv_copies)

    def back(index, carry):
        start = pl.multiple_of(index * 256, 256)
        left = jnp.concatenate([dqkv[s, pl.ds(start, 256), :] for s in range(4)], axis=1)
        right = jnp.concatenate([qkv_weight[s, kind] for s in range(4) for kind in range(3)], axis=1)
        tile = lax.dot_general(left, right, (((1,), (1,)), ((), ())), preferred_element_type=F32)
        for b in range(4):
            dattn[b, pl.ds(start, 256), :] = tile[:, b * LANES : (b + 1) * LANES]
        return carry

    lax.fori_loop(0, pixels // 256, back, 0)

    def weights(offset, carry):
        s = jnp.bitwise_xor(me, offset)
        place = offset // 2
        attn_all = attn_t[...].reshape(C, pixels)
        cot_all = cot_t[...].reshape(C, pixels)
        grad = jnp.dot(attn_all, dqkv[s], preferred_element_type=F32).astype(BF16)
        other = jnp.dot(cot_all, mixed[s], preferred_element_type=F32).astype(BF16)

        def put(target):
            for kind in range(3):
                target[place, kind] = grad[:, kind * LANES : (kind + 1) * LANES]
            target[place, 3] = other

        @pl.when(offset % 2 == 0)
        def _():
            put(keep)

        @pl.when(offset % 2 == 1)
        def _():
            put(send)

        return carry

    lax.fori_loop(0, 4, weights, 0)
    means, inverses = norm_rows(pixels, strip, lambda b, start: middle[b, pl.ds(start, strip), :])
    gains = [pack[b, E_G3 : E_G3 + 1, :] for b in range(4)]

    def read_normed(b, start):
        return (middle[b, pl.ds(start, strip), :] - means[b]) * inverses[b]

    def write(b, start, value):
        total = cot[b, pl.ds(start, strip), :].astype(F32) + value
        dmiddle[b, pl.ds(start, strip), :] = total
        store_shifted(field, b, start, total.astype(BF16).astype(F32))

    gain_sums, bias_sums = norm_back_strips(
        pixels, strip, read_normed, lambda b, start: dattn[b, pl.ds(start, strip), :], gains, inverses, write
    )
    branch = sum_strips(
        pixels,
        strip,
        4,
        lambda start: [
            field[1, b, pl.ds(pl.multiple_of(PAD + start, 32), strip), :].astype(F32) for b in range(4)
        ],
    )
    for b in range(4):
        sums[b] = jnp.zeros((S_ROWS, LANES), F32)
        sums[b, S_G3 : S_G3 + 1, :] = gain_sums[b]
        sums[b, S_B3 : S_B3 + 1, :] = bias_sums[b]
        sums[b, S_CB2 : S_CB2 + 1, :] = column_sum(branch[b])
        sums[b, S_LIVE : S_LIVE + 1, :] = jnp.full((1, LANES), 1.0, F32) * alive
        sums[b, S_KEY : S_KEY + 8, :] = dctx[b]


def kernel_weight_grad(meta, source_t, field, keep, send):
    pixels = source_t.shape[2]
    me = meta[0]
    left = source_t[...].reshape(C, pixels)

    def body(index, carry):
        tap = index // 2
        side = index % 2
        a = tap // 3
        b = tap % 3
        start = pl.multiple_of((2 - a) * SIDE, 32)
        first = jnp.bitwise_xor(me, side)
        right = jnp.concatenate(
            [
                field[2 - b, first, pl.ds(start, pixels), :],
                field[2 - b, jnp.bitwise_xor(first, 2), pl.ds(start, pixels), :],
            ],
            axis=1,
        )
        grad = jnp.dot(left, right, preferred_element_type=F32).astype(BF16)

        @pl.when(side == 0)
        def _():
            keep[0, tap] = grad[:, :LANES]
            keep[1, tap] = grad[:, LANES:]

        @pl.when(side == 1)
        def _():
            send[0, tap] = grad[:, :LANES]
            send[1, tap] = grad[:, LANES:]

        return carry

    lax.fori_loop(0, 18, body, 0)


def kernel_back_second(
    meta, grad_field, inner, pack, sums_in, w0, w1, w2, w3,
    field, s0, s1, s2, s3, weight, grad, sems,
):
    pixels = inner.shape[1]
    me = meta[0]
    strip = 128
    weight_copies = fetch((w0, w1, w2, w3), weight, me, sems, 0)
    clear_padding(field, pixels)
    means, inverses = norm_rows(pixels, strip, lambda b, start: inner[b, pl.ds(start, strip), :])
    wait_all(weight_copies)

    def write_grad(start, half, tile):
        for b in range(2):
            grad[2 * half + b, pl.ds(start, tile.shape[0]), :] = tile[:, b * LANES : (b + 1) * LANES]

    conv_back_tiles(grad_field, weight, pixels, 512, write_grad)
    gains = [pack[b, E_G2 : E_G2 + 1, :] for b in range(4)]

    def read_normed(b, start):
        return (inner[b, pl.ds(start, strip), :] - means[b]) * inverses[b]

    def slope(index, carry):
        start = pl.multiple_of(index * strip, strip)
        found = []
        for b in range(4):
            bias = pack[b, E_B2 : E_B2 + 1, :]
            scale = pack[b, E_SCALE : E_SCALE + 1, :]
            shift = pack[b, E_SHIFT : E_SHIFT + 1, :]
            shaped = read_normed(b, start) * gains[b] + bias
            modulated = shaped * (1.0 + scale) + shift
            dmod = silu_slope(modulated, grad[b, pl.ds(start, strip), :])
            grad[b, pl.ds(start, strip), :] = dmod * (1.0 + scale)
            found += [dmod * shaped, dmod]
        return tuple(old + fold(new) for old, new in zip(carry, found))

    zero = tuple(jnp.zeros((8, LANES), F32) for _ in range(8))
    modulation = lax.fori_loop(0, pixels // strip, slope, zero)

    def write(b, start, value):
        store_shifted(field, b, start, value)

    gain_sums, bias_sums = norm_back_strips(
        pixels, strip, read_normed, lambda b, start: grad[b, pl.ds(start, strip), :], gains, inverses, write
    )
    for offset, target in enumerate((s0, s1, s2, s3)):
        other = jnp.bitwise_xor(me, offset)
        target[...] = sums_in[other]
        for b in range(4):

            @pl.when(other == b)
            def _():
                target[S_G2 : S_G2 + 1, :] = gain_sums[b]
                target[S_B2 : S_B2 + 1, :] = bias_sums[b]
                target[S_SCALE : S_SCALE + 1, :] = column_sum(modulation[2 * b])
                target[S_SHIFT : S_SHIFT + 1, :] = column_sum(modulation[2 * b + 1])


def kernel_back_first(
    meta, grad_field, image, pack, dmiddle, w0, w1, w2, w3,
    g0, g1, g2, g3, s0, s1, s2, s3, weight, grad, sems,
):
    pixels = image.shape[1]
    me = meta[0]
    strip = 128
    weight_copies = fetch((w0, w1, w2, w3), weight, me, sems, 0)

    def read(b, start):
        return image[b, pl.ds(start, strip), :].astype(F32)

    means, inverses = norm_rows(pixels, strip, read)
    wait_all(weight_copies)

    def write_grad(start, half, tile):
        for b in range(2):
            grad[2 * half + b, pl.ds(start, tile.shape[0]), :] = tile[:, b * LANES : (b + 1) * LANES]

    conv_back_tiles(grad_field, weight, pixels, 512, write_grad)
    gains = [pack[b, E_G1 : E_G1 + 1, :] for b in range(4)]

    def read_normed(b, start):
        return (read(b, start) - means[b]) * inverses[b]

    def slope(index, carry):
        start = pl.multiple_of(index * strip, strip)
        for b in range(4):
            before = read_normed(b, start) * gains[b] + pack[b, E_B1 : E_B1 + 1, :]
            grad[b, pl.ds(start, strip), :] = silu_slope(before, grad[b, pl.ds(start, strip), :])
        return carry

    lax.fori_loop(0, pixels // strip, slope, 0)

    def write(b, start, value):
        grad[b, pl.ds(start, strip), :] = dmiddle[b, pl.ds(start, strip), :] + value

    gain_sums, bias_sums = norm_back_strips(
        pixels, strip, read_normed, lambda b, start: grad[b, pl.ds(start, strip), :], gains, inverses, write
    )
    for offset, (target, small) in enumerate(zip((g0, g1, g2, g3), (s0, s1, s2, s3))):
        other = jnp.bitwise_xor(me, offset)
        target[...] = grad[other].astype(BF16)
        small[...] = jnp.zeros((8, LANES), F32)
        for b in range(4):

            @pl.when(other == b)
            def _():
                small[0:1, :] = gain_sums[b]
                small[1:2, :] = bias_sums[b]


def swap(value, axis, offset):
    size = lax.axis_size(axis)
    return lax.ppermute(value, axis, [(i, i ^ offset) for i in range(size)])


def share(shard):
    near = swap(shard, "mp", 1)
    far = swap(shard, "mp", 2)
    return shard, near, far, swap(far, "mp", 1)


def exchange(pieces):
    return (pieces[0],) + tuple(swap(pieces[k], "mp", k) for k in range(1, 4))


def pick(stack, me):
    return [lax.dynamic_index_in_dim(stack, me ^ k, 0, keepdims=False) for k in range(4)]


def dp_levels(size):
    levels = []
    low = 1
    while low < size:
        width = 2 if low == 1 or size // low < 4 else 4
        levels.append((low, width))
        low *= width
    return levels


def gather_dp(value):
    stacked = value[None]
    for low, width in dp_levels(lax.axis_size("dp")):
        stacked = jnp.concatenate(
            [stacked] + [swap(stacked, "dp", low * k) for k in range(1, width)], axis=0
        )
    return stacked


def reduce_grads(keep, send):
    got = swap(send, "mp", 1)
    far = keep[1].astype(F32) + got[1].astype(F32)
    own = keep[0].astype(F32) + got[0].astype(F32)
    value = (own + swap(far.astype(BF16), "mp", 2).astype(F32)).astype(BF16)
    blocks = value.shape[0]
    place = lax.axis_index("dp")
    path = []
    for low, width in dp_levels(lax.axis_size("dp")):
        rows = value.shape[1] // width
        digit = (place // low) % width
        cut = value.reshape(blocks, width, rows, LANES)
        parts = [
            lax.dynamic_index_in_dim(cut, digit ^ k, 1, keepdims=False) for k in range(width)
        ]
        total = parts[0].astype(F32)
        for k in range(1, width):
            total = total + swap(parts[k], "dp", low * k).astype(F32)
        value = total.astype(BF16)
        path.append((low, width, digit))
    for low, width, digit in reversed(path):
        rows = value.shape[1]
        whole = jnp.zeros((blocks, width, rows, LANES), BF16)
        for k in range(width):
            part = value if k == 0 else swap(value, "dp", low * k)
            whole = lax.dynamic_update_index_in_dim(whole, part, digit ^ k, 1)
        value = whole.reshape(blocks, width * rows, LANES)
    return value


def local(
    image_in,
    out_cotangent,
    timesteps,
    clip_embed,
    context_tokens,
    image_count,
    norm1_gain,
    norm1_bias,
    conv1_weight,
    embed_weight,
    norm2_gain,
    norm2_bias,
    conv2_weight,
    conv2_bias,
    norm3_gain,
    norm3_bias,
    qkv_weight,
    context_weight,
    proj_weight,
):
    slots, pixels, width = image_in.shape
    me = lax.axis_index("mp")
    meta = jnp.stack([me, (me < image_count[0]).astype(jnp.int32)]).astype(jnp.int32)

    images = exchange(pick(image_in, me))
    conv1 = share(conv1_weight.reshape(9, C, LANES))

    half = EMB // 2
    frequency = jnp.exp(-math.log(10000.0) * jnp.arange(half, dtype=F32) / half)
    angles = timesteps.astype(F32)[:, None] * frequency[None, :]
    condition = jax.nn.silu(
        jnp.concatenate([jnp.cos(angles), jnp.sin(angles)], axis=1) + clip_embed.astype(F32)
    ).astype(BF16)
    scale_shift = jnp.dot(
        condition, embed_weight.reshape(EMB, 2 * LANES), preferred_element_type=F32
    ).reshape(slots, 2, LANES)
    doubled = jnp.concatenate([context_tokens, context_tokens], axis=1)
    context = jnp.dot(
        doubled.reshape(slots * 2 * CTX, EMB),
        context_weight.reshape(EMB, 2 * LANES),
        preferred_element_type=F32,
    ).astype(BF16).astype(F32).reshape(slots, 2 * CTX, 2, LANES)
    vectors = jnp.stack(
        [norm1_gain, norm1_bias, norm2_gain, norm2_bias, conv2_bias, norm3_gain, norm3_bias]
    )
    early = jnp.concatenate(
        [
            scale_shift,
            jnp.broadcast_to(vectors[None], (slots, 7, LANES)),
            jnp.zeros((slots, 7, LANES), F32),
            context[:, :, 0],
            context[:, :, 1],
        ],
        axis=1,
    )
    packs = exchange(pick(early, me))
    conv2 = share(conv2_weight.reshape(9, C, LANES))
    qkv_w = share(jnp.transpose(qkv_weight, (1, 0, 2)))
    proj_w = share(proj_weight)
    cots = exchange(pick(out_cotangent, me))

    factors = gather_dp(jnp.concatenate([condition, context_tokens.reshape(slots * CTX, EMB)], axis=0))

    block = struct((4, pixels, LANES), BF16)
    block32 = struct((4, pixels, LANES), F32)
    turned = struct((4, LANES, pixels), BF16)
    fields = struct((3, 4, pixels + 2 * PAD, LANES), BF16)
    field_scratch = pltpu.VMEM((3, 4, pixels + 2 * PAD, LANES), BF16)
    conv_scratch = pltpu.VMEM((4, 9, C, LANES), BF16)
    qkv_scratch = pltpu.VMEM((4, 3, C, LANES), BF16)
    grad_scratch = pltpu.VMEM((4, pixels, LANES), F32)
    conv_flops = 2 * pixels * 9 * C * C

    image, pack, first_t, inner, second, second_t = call(
        kernel_first,
        "first",
        [block, struct((4, E_ROWS, LANES), F32), turned, block32, block, turned],
        [smem()] + [anywhere()] * 12,
        [field_scratch, conv_scratch, pltpu.SemaphoreType.DMA((12,))],
        conv_flops,
    )(meta, *images, *conv1, *packs)
    middle, attn_t, qkv = call(
        kernel_second,
        "second",
        [block32, turned, struct((4, pixels, 3 * LANES), BF16)],
        [smem()] + [vmem()] * 3 + [anywhere()] * 8,
        [
            field_scratch,
            conv_scratch,
            qkv_scratch,
            pltpu.VMEM((4, pixels, LANES), BF16),
            pltpu.SemaphoreType.DMA((8,)),
        ],
        conv_flops + 6 * pixels * C * C,
    )(meta, second, image, pack, *conv2, *qkv_w)
    ctx_scratch = pltpu.VMEM((pixels, LANES), F32)
    turned_scratch = pltpu.VMEM((LANES, pixels), F32)
    *outs, cot, mixed, dqkv, dctx = call(
        kernel_attention,
        "attention",
        [struct((pixels, LANES), BF16)] * 4
        + [block, block, struct((4, pixels, 3 * LANES), BF16), struct((4, 2 * CTX, LANES), F32)],
        [smem()] + [vmem()] * 3 + [anywhere()] * 8,
        [
            pltpu.VMEM((4, LANES, C), BF16),
            pltpu.VMEM((4, pixels, LANES), BF16),
            ctx_scratch,
            ctx_scratch,
            ctx_scratch,
            ctx_scratch,
            grad_scratch,
            grad_scratch,
            turned_scratch,
            turned_scratch,
            pltpu.SemaphoreType.DMA((8,)),
        ],
        4 * 12 * pixels * pixels * C,
    )(meta, qkv, pack, middle, *cots, *proj_w)
    att_keep, att_send, dmiddle, field2, sums = call(
        kernel_back_attention,
        "back_attention",
        [struct((2, 4, C, LANES), BF16)] * 2 + [block32, fields, struct((4, S_ROWS, LANES), F32)],
        [smem()] + [vmem()] * 7 + [anywhere()] * 4,
        [
            qkv_scratch,
            pltpu.VMEM((4, LANES, pixels), BF16),
            grad_scratch,
            pltpu.SemaphoreType.DMA((4,)),
        ],
        14 * pixels * C * C,
    )(meta, dqkv, mixed, attn_t, cot, middle, pack, dctx, *qkv_w)
    weight_grad = call(
        kernel_weight_grad,
        "weight_grad",
        [struct((2, 9, C, LANES), BF16)] * 2,
        [smem()] + [vmem()] * 2,
        [],
        conv_flops,
    )
    conv2_keep, conv2_send = weight_grad(meta, second_t, field2)
    field1, *terms = call(
        kernel_back_second,
        "back_second",
        [fields] + [struct((S_ROWS, LANES), F32)] * 4,
        [smem()] + [vmem()] * 4 + [anywhere()] * 4,
        [conv_scratch, grad_scratch, pltpu.SemaphoreType.DMA((4,))],
        conv_flops,
    )(meta, field2, inner, pack, sums, *conv2)
    conv1_keep, conv1_send = weight_grad(meta, first_t, field1)
    back = call(
        kernel_back_first,
        "back_first",
        [struct((pixels, LANES), BF16)] * 4 + [struct((8, LANES), F32)] * 4,
        [smem()] + [vmem()] * 4 + [anywhere()] * 4,
        [conv_scratch, grad_scratch, pltpu.SemaphoreType.DMA((4,))],
        conv_flops,
    )(meta, field1, image, pack, dmiddle, *conv1)
    image_grads, last_terms = back[:4], back[4:]

    order = me ^ jnp.arange(4)

    def in_slots(parts):
        whole = jnp.zeros((4,) + parts[0].shape, parts[0].dtype)
        for k in range(4):
            whole = lax.dynamic_update_index_in_dim(whole, parts[k], me ^ k, 0)
        return whole

    del order
    block_out = in_slots(exchange(outs))
    image_grad = in_slots(exchange(image_grads))
    small = gather_dp(in_slots(exchange(terms)))
    last = gather_dp(sum(exchange(last_terms)))
    groups = small.shape[0]
    small = small.reshape(groups * slots, S_ROWS, LANES)
    inverse_total = 1.0 / jnp.sum(small[:, S_LIVE, 0])
    vector_sums = jnp.sum(small[:, :S_SCALE], axis=0) * inverse_total
    last_sums = jnp.sum(last, axis=0) * inverse_total
    all_condition = factors[:, :slots].reshape(groups * slots, EMB)
    all_tokens = factors[:, slots:].reshape(groups * slots * CTX, EMB)
    dscale_shift = small[:, S_SCALE : S_SHIFT + 1].reshape(groups * slots, 2 * LANES)
    dcontext = jnp.concatenate(
        [small[:, S_KEY : S_KEY + CTX], small[:, S_VALUE : S_VALUE + CTX]], axis=2
    ).reshape(groups * slots * CTX, 2 * LANES)
    over_rows = (((0,), (0,)), ((), ()))
    embed_grad = (
        lax.dot_general(
            all_condition.astype(F32),
            dscale_shift,
            over_rows,
            precision=lax.Precision.HIGHEST,
            preferred_element_type=F32,
        )
        * inverse_total
    ).reshape(EMB, 2, LANES)
    context_grad = (
        lax.dot_general(all_tokens, dcontext.astype(BF16), over_rows, preferred_element_type=F32)
        * inverse_total
    ).reshape(EMB, 2, LANES)
    att = reduce_grads(att_keep, att_send).astype(F32) * inverse_total
    conv2_grad = reduce_grads(conv2_keep, conv2_send).astype(F32) * inverse_total
    conv1_grad = reduce_grads(conv1_keep, conv1_send).astype(F32) * inverse_total
    return (
        block_out,
        image_grad,
        last_sums[0],
        last_sums[1],
        conv1_grad.reshape(3, 3, C, LANES),
        embed_grad,
        vector_sums[S_G2],
        vector_sums[S_B2],
        conv2_grad.reshape(3, 3, C, LANES),
        vector_sums[S_CB2],
        vector_sums[S_G3],
        vector_sums[S_B3],
        jnp.transpose(att[:3], (1, 0, 2)),
        context_grad,
        att[3].T,
    )


def solution(mesh):
    return jax.shard_map(
        local,
        mesh=mesh,
        in_specs=(
            P("dp", None, "mp"),
            P("dp", None, "mp"),
            P("dp"),
            P("dp", None),
            P("dp", None, None),
            P("dp"),
            P("mp"),
            P("mp"),
            P(None, None, None, "mp"),
            P(None, None, "mp"),
            P("mp"),
            P("mp"),
            P(None, None, None, "mp"),
            P("mp"),
            P("mp"),
            P("mp"),
            P(None, None, "mp"),
            P(None, None, "mp"),
            P("mp", None),
        ),
        out_specs=(
            P("dp", None, "mp"),
            P("dp", None, "mp"),
            P("mp"),
            P("mp"),
            P(None, None, None, "mp"),
            P(None, None, "mp"),
            P("mp"),
            P("mp"),
            P(None, None, None, "mp"),
            P("mp"),
            P("mp"),
            P("mp"),
            P(None, None, "mp"),
            P(None, None, "mp"),
            P("mp", None),
        ),
        check_vma=False,
    )
```

```python
import functools
import math

import jax
import jax.numpy as jnp
from jax import lax
from jax.experimental import pallas as pl
from jax.experimental.pallas import tpu as pltpu
from jax.sharding import PartitionSpec as P

C = 512
GROUPS = 32
HEAD = 64
EMB = 2048
CTX = 4
SIDE = 32
LANES = 128
PAD = SIDE
EPSILON = 1e-05
F32 = jnp.float32
BF16 = jnp.bfloat16
NEG = -1e30

E_SCALE, E_SHIFT, E_G1, E_B1, E_G2, E_B2, E_CB2, E_G3, E_B3 = range(9)
E_KEY, E_VALUE, E_ROWS = 16, 24, 32
S_G3, S_B3, S_CB2, S_G2, S_B2, S_SCALE, S_SHIFT, S_LIVE = range(8)
S_KEY, S_VALUE, S_G1, S_B1, S_ROWS = 8, 12, 16, 17, 24
VMEM_LIMIT = 30 << 20


def vmem():
    return pl.BlockSpec(memory_space=pltpu.VMEM)


def anywhere():
    return pl.BlockSpec(memory_space=pltpu.HBM)


def smem():
    return pl.BlockSpec(memory_space=pltpu.SMEM)


def struct(shape, dtype):
    return jax.ShapeDtypeStruct(shape, dtype)


def call(body, name, out_shape, in_specs, scratch, flops=0, moved=0):
    many = isinstance(out_shape, (list, tuple))
    return pl.pallas_call(
        body,
        name=name,
        out_shape=out_shape,
        in_specs=in_specs,
        out_specs=[vmem() for _ in out_shape] if many else vmem(),
        scratch_shapes=scratch,
        compiler_params=pltpu.CompilerParams(vmem_limit_bytes=VMEM_LIMIT),
        cost_estimate=pl.CostEstimate(flops=flops, transcendentals=0, bytes_accessed=moved),
    )


def fetch(sources, target, me, sems, first):
    copies = []
    for offset, source in enumerate(sources):
        copy = pltpu.make_async_copy(
            source, target.at[jnp.bitwise_xor(me, offset)], sems.at[first + offset]
        )
        copy.start()
        copies.append(copy)
    return copies


def fetch_routed(sources, target, me, parity, sems, first):
    quarter = target.shape[-2] // 4
    copies = []
    for index, source in enumerate(sources):
        slot = jnp.bitwise_xor(me, (0, 1, 2, 2, 2, 3, 3, 3)[index])
        place = target.at[slot]
        if index >= 2:
            kind = (index - 2) % 3
            rows = 2 * quarter if kind == 0 else quarter
            half = parity if kind == 0 else 1 - parity
            start = half * 2 * quarter + (quarter if kind == 2 else 0)
            start = pl.multiple_of(start, quarter)
            lead = (slice(None),) * (len(place.shape) - 2)
            place = place.at[lead + (pl.ds(start, rows), slice(None))]
        copy = pltpu.make_async_copy(source, place, sems.at[first + index])
        copy.start()
        copies.append(copy)
    return copies


def wait_all(copies):
    for copy in copies:
        copy.wait()


def fold(values):
    rows = values.shape[0]
    return jnp.sum(values.reshape(rows // 8, 8, values.shape[1]), axis=0)


def group_sum(rows8):
    lane = lax.broadcasted_iota(jnp.int32, rows8.shape, 1)
    total = jnp.broadcast_to(jnp.sum(rows8, axis=0, keepdims=True), rows8.shape)
    for step in (1, 2, 4, 8):
        up = pltpu.roll(total, step, axis=1)
        down = pltpu.roll(total, LANES - step, axis=1)
        total = total + jnp.where((lane & step) != 0, up, down)
    return total[0:1]


def column_sum(rows8):
    return jnp.sum(rows8, axis=0, keepdims=True)


def sum_strips(pixels, strip, width, function):
    zero = tuple(jnp.zeros((8, LANES), F32) for _ in range(width))

    def body(index, carry):
        start = pl.multiple_of(index * strip, strip)
        return tuple(old + fold(new) for old, new in zip(carry, function(start)))

    return lax.fori_loop(0, pixels // strip, body, zero)


def norm_rows(pixels, strip, read):
    count = pixels * (C // GROUPS)
    sums = sum_strips(pixels, strip, 4, lambda start: [read(b, start) for b in range(4)])
    means = [group_sum(s) * (1.0 / count) for s in sums]
    squares = sum_strips(
        pixels,
        strip,
        4,
        lambda start: [jnp.square(read(b, start) - means[b]) for b in range(4)],
    )
    inverses = [lax.rsqrt(group_sum(s) * (1.0 / count) + EPSILON) for s in squares]
    return means, inverses


def shifted(values):
    rows = values.shape[0]
    column = lax.broadcasted_iota(jnp.int32, values.shape, 0) & (SIDE - 1)
    left = jnp.where(column == 0, 0.0, pltpu.roll(values, 1, axis=0))
    right = jnp.where(column == SIDE - 1, 0.0, pltpu.roll(values, rows - 1, axis=0))
    return left, values, right


def store_shifted(target, block, start, values):
    rows = values.shape[0]
    for position, part in enumerate(shifted(values)):
        target[position, block, pl.ds(pl.multiple_of(PAD + start, 32), rows), :] = part.astype(BF16)


def clear_padding(target, pixels):
    zero = jnp.zeros((PAD, LANES), BF16)
    for position in range(3):
        for block in range(4):
            target[position, block, 0:PAD, :] = zero
            target[position, block, PAD + pixels : PAD + pixels + PAD, :] = zero


def conv_tiles(field, weight, pixels, tile, write):
    def body(index, carry):
        start = pl.multiple_of(index * tile, tile)
        left = jnp.concatenate(
            [
                field[b, block, pl.ds(pl.multiple_of(start + a * SIDE, 32), tile), :]
                for a in range(3)
                for b in range(3)
                for block in range(4)
            ],
            axis=1,
        )
        right = jnp.concatenate([weight[s].reshape(9 * C, LANES) for s in range(4)], axis=1)
        write(start, jnp.dot(left, right, preferred_element_type=F32))
        return carry

    lax.fori_loop(0, pixels // tile, body, 0)


def conv_back_tiles(field, weight, pixels, tile, write):
    def body(index, carry):
        start = pl.multiple_of((index // 2) * tile, tile)
        half = index % 2
        left = jnp.concatenate(
            [
                field[2 - b, block, pl.ds(pl.multiple_of(start + (2 - a) * SIDE, 32), tile), :]
                for a in range(3)
                for b in range(3)
                for block in range(4)
            ],
            axis=1,
        )
        right = jnp.concatenate(
            [
                weight[block, 3 * a + b, pl.ds(pl.multiple_of(half * 256, 256), 256), :]
                for a in range(3)
                for b in range(3)
                for block in range(4)
            ],
            axis=1,
        )
        write(
            start,
            half,
            lax.dot_general(left, right, (((1,), (1,)), ((), ())), preferred_element_type=F32),
        )
        return carry

    lax.fori_loop(0, 2 * (pixels // tile), body, 0)


def silu_slope(before, grad_out):
    gate = jax.nn.sigmoid(before)
    return grad_out * gate * (1.0 + before * (1.0 - gate))


def kernel_first(
    meta, i0, i1, i2, i3, e0, e1, e2, e3, w0, w1, w2, w3, w4, w5, w6, w7,
    image, pack, first_t, inner, field, weight, sems,
):
    pixels = image.shape[1]
    me = meta[0]
    image_copies = fetch((i0, i1, i2, i3), image, me, sems, 0)
    pack_copies = fetch((e0, e1, e2, e3), pack, me, sems, 4)
    weight_copies = fetch_routed((w0, w1, w2, w3, w4, w5, w6, w7), weight, me, meta[2], sems, 8)
    clear_padding(field, pixels)
    wait_all(image_copies)
    wait_all(pack_copies)
    strip = 128

    def read(block, start):
        return image[block, pl.ds(start, strip), :].astype(F32)

    means, inverses = norm_rows(pixels, strip, read)

    def normalise(index, carry):
        start = pl.multiple_of(index * strip, strip)
        for b in range(4):
            gain = pack[b, E_G1 : E_G1 + 1, :]
            bias = pack[b, E_B1 : E_B1 + 1, :]
            before = (read(b, start) - means[b]) * inverses[b] * gain + bias
            after = before * jax.nn.sigmoid(before)
            store_shifted(field, b, start, after)
            first_t[b, :, pl.ds(start, strip)] = after.T.astype(BF16)
        return carry

    lax.fori_loop(0, pixels // strip, normalise, 0)
    wait_all(weight_copies)

    def write(start, tile):
        for b in range(4):
            inner[b, pl.ds(start, tile.shape[0]), :] = tile[:, b * LANES : (b + 1) * LANES]

    conv_tiles(field, weight, pixels, 512, write)


def kernel_second(
    meta, inner, image, pack, p0, p1, p2, p3, w0, w1, w2, w3, w4, w5, w6, w7,
    middle, second_t, attn_t, qkv, field, weight, qkv_weight, attn, sems,
):
    pixels = image.shape[1]
    me = meta[0]
    qkv_copies = fetch((p0, p1, p2, p3), qkv_weight, me, sems, 0)
    weight_copies = fetch_routed((w0, w1, w2, w3, w4, w5, w6, w7), weight, me, meta[2], sems, 4)
    clear_padding(field, pixels)
    strip = 128
    means2, inverses2 = norm_rows(pixels, strip, lambda b, start: inner[b, pl.ds(start, strip), :])

    def modulate(index, carry):
        start = pl.multiple_of(index * strip, strip)
        for b in range(4):
            gain = pack[b, E_G2 : E_G2 + 1, :]
            bias = pack[b, E_B2 : E_B2 + 1, :]
            scale = pack[b, E_SCALE : E_SCALE + 1, :]
            shift = pack[b, E_SHIFT : E_SHIFT + 1, :]
            normed = (inner[b, pl.ds(start, strip), :] - means2[b]) * inverses2[b]
            modulated = (normed * gain + bias) * (1.0 + scale) + shift
            after = modulated * jax.nn.sigmoid(modulated)
            store_shifted(field, b, start, after)
            second_t[b, :, pl.ds(start, strip)] = after.T.astype(BF16)
        return carry

    lax.fori_loop(0, pixels // strip, modulate, 0)
    wait_all(weight_copies)

    def write(start, tile):
        rows = tile.shape[0]
        for b in range(4):
            branch = tile[:, b * LANES : (b + 1) * LANES] + pack[b, E_CB2 : E_CB2 + 1, :]
            middle[b, pl.ds(start, rows), :] = image[b, pl.ds(start, rows), :].astype(F32) + branch

    conv_tiles(field, weight, pixels, 512, write)
    means, inverses = norm_rows(pixels, strip, lambda b, start: middle[b, pl.ds(start, strip), :])

    def normalise(index, carry):
        start = pl.multiple_of(index * strip, strip)
        for b in range(4):
            normed = (middle[b, pl.ds(start, strip), :] - means[b]) * inverses[b]
            value = normed * pack[b, E_G3 : E_G3 + 1, :] + pack[b, E_B3 : E_B3 + 1, :]
            attn[b, pl.ds(start, strip), :] = value.astype(BF16)
            attn_t[b, :, pl.ds(start, strip)] = value.T.astype(BF16)
        return carry

    lax.fori_loop(0, pixels // strip, normalise, 0)
    wait_all(qkv_copies)

    def project(index, carry):
        s = index // 2
        start = pl.multiple_of((index % 2) * 512, 512)
        left = jnp.concatenate([attn[b, pl.ds(start, 512), :] for b in range(4)], axis=1)
        right = jnp.concatenate([qkv_weight[s, kind] for kind in range(3)], axis=1)
        qkv[s, pl.ds(start, 512), :] = jnp.dot(left, right, preferred_element_type=F32).astype(BF16)
        return carry

    lax.fori_loop(0, 4 * (pixels // 512), project, 0)


def kernel_attention(
    meta, qkv, pack, middle, c0, c1, c2, c3, w0, w1, w2, w3,
    o0, o1, o2, o3, cot, mixed, dqkv, dctx,
    weight, grad_mixed, score_ctx, grad_ctx_prob, prob_ctx, dscore_ctx, out_pix, dquery, dkey_t, dvalue_t, sems,
):
    pixels = qkv.shape[1]
    me = meta[0]
    alive = meta[1].astype(F32)
    cot_copies = fetch((c0, c1, c2, c3), cot, me, sems, 0)
    weight_copies = fetch((w0, w1, w2, w3), weight, me, sems, 4)
    scale = 1.0 / math.sqrt(HEAD)
    block = 256

    row32 = lax.broadcasted_iota(jnp.int32, (32, LANES), 0)
    lane32 = lax.broadcasted_iota(jnp.int32, (32, LANES), 1)

    def diagonal(kind):
        found = []
        for s in range(4):
            rows8 = pack[s, kind : kind + 8, :]
            tiled = jnp.concatenate([rows8] * 4, axis=0)
            own = (row32 // 4) == (2 * s + lane32 // HEAD)
            kept = jnp.where(own, tiled, 0.0)
            found.append(jnp.concatenate([kept, jnp.zeros((96, LANES), F32)], axis=0).astype(BF16))
        return jnp.concatenate(found, axis=1)

    keys_ctx = diagonal(E_KEY)
    values_ctx = diagonal(E_VALUE)
    wait_all(cot_copies)
    wait_all(weight_copies)

    def prepare(index, carry):
        start = pl.multiple_of(index * block, block)
        rows = pl.ds(start, block)
        for s in range(4):
            cot[s, rows, :] = (cot[s, rows, :].astype(F32) * alive).astype(BF16)
        all_cot = jnp.concatenate([cot[s, rows, :] for s in range(4)], axis=1)
        all_weight = weight[...].reshape(C, C)
        grad = lax.dot_general(
            all_cot, all_weight, (((1,), (1,)), ((), ())), preferred_element_type=F32
        ).astype(BF16)
        for s in range(4):
            grad_mixed[s, rows, :] = grad[:, s * LANES : (s + 1) * LANES]
        query = jnp.concatenate([qkv[s, rows, 0:LANES] for s in range(4)], axis=1)
        score_ctx[rows, :] = lax.dot_general(
            query, keys_ctx, (((1,), (1,)), ((), ())), preferred_element_type=F32
        )
        grad_ctx_prob[rows, :] = lax.dot_general(
            grad, values_ctx, (((1,), (1,)), ((), ())), preferred_element_type=F32
        )
        prob_ctx[rows, :] = jnp.zeros((block, LANES), F32)
        dscore_ctx[rows, :] = jnp.zeros((block, LANES), F32)
        return carry

    lax.fori_loop(0, pixels // block, prepare, 0)
    lane = lax.broadcasted_iota(jnp.int32, (block, LANES), 1)
    low = lane < HEAD
    ones = jnp.ones((pixels, LANES), BF16)
    blocks = pixels // block

    def attend(index, carry):
        s = index // blocks
        part = index % blocks
        rows = pl.ds(pl.multiple_of(part * block, block), block)

        @pl.when(part == 0)
        def _():
            dkey_t[...] = jnp.zeros((LANES, pixels), F32)
            dvalue_t[...] = jnp.zeros((LANES, pixels), F32)

        query = qkv[s, rows, 0:LANES]
        key = qkv[s, :, LANES : 2 * LANES]
        value = qkv[s, :, 2 * LANES : 3 * LANES]
        value_ones = jnp.concatenate([value, ones], axis=1)
        grad = grad_mixed[s, rows, :]
        ctx_scores = score_ctx[rows, :]
        ctx_grads = grad_ctx_prob[rows, :]
        exps, outs, inverses, ctx_exps, owns = [], [], [], [], []
        for h in range(2):
            mine = low if h == 0 else jnp.logical_not(low)
            own = lane // CTX == 2 * s + h
            score = lax.dot_general(
                jnp.where(mine, query, jnp.zeros_like(query)),
                key,
                (((1,), (1,)), ((), ())),
                preferred_element_type=F32,
            )
            top = jnp.maximum(
                jnp.max(score, axis=1, keepdims=True),
                jnp.max(jnp.where(own, ctx_scores, NEG), axis=1, keepdims=True),
            )
            exp = jnp.exp((score - top) * scale).astype(BF16)
            ctx_exp = jnp.where(own, jnp.exp((ctx_scores - top) * scale), 0.0)
            out = jnp.dot(exp, value_ones, preferred_element_type=F32)
            total = out[:, LANES:] + jnp.sum(ctx_exp, axis=1, keepdims=True)
            inverse = 1.0 / total
            exps.append(exp)
            outs.append(out[:, :LANES] * inverse)
            inverses.append(inverse)
            ctx_exps.append(ctx_exp)
            owns.append(own)
        out_pair = jnp.where(low, outs[0], outs[1])
        out_pix[s, rows, :] = out_pair
        inverse_pair = jnp.where(low, inverses[0], inverses[1])
        scaled = (grad.astype(F32) * (inverse_pair * scale)).astype(BF16)
        product = out_pair * scaled.astype(F32)
        query_t = query.astype(F32).T.astype(BF16)
        scaled_t = scaled.astype(F32).T.astype(BF16)
        prob_keep = prob_ctx[rows, :]
        dscore_keep = dscore_ctx[rows, :]
        dqs = []
        for h in range(2):
            mine = low if h == 0 else jnp.logical_not(low)
            own = owns[h]
            ctx_prob = ctx_exps[h] * inverses[h]
            ctx_grad = ctx_grads * (inverses[h] * scale)
            dot = jnp.sum(
                jnp.where(mine, product, 0.0) + ctx_prob * jnp.where(own, ctx_grad, 0.0),
                axis=1,
                keepdims=True,
            )
            weight_grad = lax.dot_general(
                jnp.where(mine, scaled, jnp.zeros_like(scaled)),
                value,
                (((1,), (1,)), ((), ())),
                preferred_element_type=F32,
            )
            dscore = (exps[h].astype(F32) * (weight_grad - dot)).astype(BF16)
            prob_keep = jnp.where(own, ctx_prob, prob_keep)
            dscore_keep = jnp.where(own, ctx_exps[h] * (ctx_grad - dot), dscore_keep)
            dqs.append(jnp.dot(dscore, key, preferred_element_type=F32))
            half = slice(h * HEAD, (h + 1) * HEAD)
            dkey_t[half, :] += jnp.dot(query_t[half], dscore, preferred_element_type=F32)
            dvalue_t[half, :] += jnp.dot(scaled_t[half], exps[h], preferred_element_type=F32)
        prob_ctx[rows, :] = prob_keep
        dscore_ctx[rows, :] = dscore_keep
        dquery[s, rows, :] = jnp.where(low, dqs[0], dqs[1])

        @pl.when(part == blocks - 1)
        def _():
            for piece in range(pixels // LANES):
                cut = slice(piece * LANES, (piece + 1) * LANES)
                dqkv[s, cut, LANES : 2 * LANES] = dkey_t[:, cut].T.astype(BF16)
                dqkv[s, cut, 2 * LANES : 3 * LANES] = (dvalue_t[:, cut] * (1.0 / scale)).T.astype(BF16)

        return carry

    lax.fori_loop(0, 4 * blocks, attend, 0)

    def finish(index, carry):
        dkeys, dvalues = carry
        start = pl.multiple_of(index * block, block)
        rows = pl.ds(start, block)
        prob = prob_ctx[rows, :].astype(BF16)
        dscore = dscore_ctx[rows, :].astype(BF16)
        out_ctx = jnp.dot(prob, values_ctx, preferred_element_type=F32)
        dquery_ctx = jnp.dot(dscore, keys_ctx, preferred_element_type=F32)
        parts = []
        for s in range(4):
            cut = slice(s * LANES, (s + 1) * LANES)
            both = (out_pix[s, rows, :] + out_ctx[:, cut]).astype(BF16)
            mixed[s, rows, :] = both
            parts.append(both)
            dqkv[s, rows, 0:LANES] = (dquery[s, rows, :] + dquery_ctx[:, cut]).astype(BF16)
        result = jnp.dot(
            jnp.concatenate(parts, axis=1), weight[...].reshape(C, C), preferred_element_type=F32
        )
        for offset, target in enumerate((o0, o1, o2, o3)):
            other = jnp.bitwise_xor(me, offset)
            value = jnp.zeros((block, LANES), F32)
            for s in range(4):
                value = jnp.where(other == s, result[:, s * LANES : (s + 1) * LANES], value)
            target[rows, :] = ((middle[other, rows, :] + value) * alive).astype(BF16)
        query = jnp.concatenate([qkv[s, rows, 0:LANES] for s in range(4)], axis=1)
        grad = jnp.concatenate([grad_mixed[s, rows, :] for s in range(4)], axis=1)
        dkeys = dkeys + jnp.dot(dscore_ctx[rows, :].T[0:32].astype(BF16), query, preferred_element_type=F32)
        dvalues = dvalues + jnp.dot(prob_ctx[rows, :].T[0:32].astype(BF16), grad, preferred_element_type=F32)
        return dkeys, dvalues

    zero = jnp.zeros((32, C), F32)
    dkeys, dvalues = lax.fori_loop(0, pixels // block, finish, (zero, zero))
    for s in range(4):
        own = (row32 // 4) == (2 * s + lane32 // HEAD)
        for position, source in enumerate((dkeys, dvalues)):
            kept = jnp.where(own, source[:, s * LANES : (s + 1) * LANES], 0.0)
            eight = jnp.sum(kept.reshape(4, 8, LANES), axis=0)
            folded = eight + pltpu.roll(eight, 4, axis=0)
            dctx[s, position * CTX : (position + 1) * CTX, :] = folded[0:CTX]


def norm_back_strips(pixels, strip, read_normed, read_grad, gains, inverses, write):
    count = pixels * (C // GROUPS)

    def terms(start):
        found = []
        for b in range(4):
            grad = read_grad(b, start)
            found += [grad, grad * read_normed(b, start)]
        return found

    sums = sum_strips(pixels, strip, 8, terms)
    bias_sums = [column_sum(sums[2 * b]) for b in range(4)]
    gain_sums = [column_sum(sums[2 * b + 1]) for b in range(4)]
    firsts = [
        group_sum(jnp.broadcast_to(bias_sums[b] * gains[b], (8, LANES)) * (1.0 / 8)) * (1.0 / count)
        for b in range(4)
    ]
    seconds = [
        group_sum(jnp.broadcast_to(gain_sums[b] * gains[b], (8, LANES)) * (1.0 / 8)) * (1.0 / count)
        for b in range(4)
    ]

    def body(index, carry):
        start = pl.multiple_of(index * strip, strip)
        for b in range(4):
            normed = read_normed(b, start)
            grad = read_grad(b, start) * gains[b]
            write(b, start, inverses[b] * (grad - firsts[b] - normed * seconds[b]))
        return carry

    lax.fori_loop(0, pixels // strip, body, 0)
    return gain_sums, bias_sums


def kernel_back_attention(
    meta, dqkv, cot, middle, pack, dctx, p0, p1, p2, p3,
    dmiddle, field, sums, d0, d1, d2, d3, qkv_weight, dattn, sems,
):
    pixels = cot.shape[1]
    me = meta[0]
    alive = meta[1].astype(F32)
    qkv_copies = fetch((p0, p1, p2, p3), qkv_weight, me, sems, 0)
    strip = 128
    clear_padding(field, pixels)
    means, inverses = norm_rows(pixels, strip, lambda b, start: middle[b, pl.ds(start, strip), :])
    wait_all(qkv_copies)

    def back(index, carry):
        start = pl.multiple_of(index * 512, 512)
        left = jnp.concatenate([dqkv[s, pl.ds(start, 512), :] for s in range(4)], axis=1)
        right = jnp.concatenate([qkv_weight[s, kind] for s in range(4) for kind in range(3)], axis=1)
        tile = lax.dot_general(left, right, (((1,), (1,)), ((), ())), preferred_element_type=F32)
        for b in range(4):
            dattn[b, pl.ds(start, 512), :] = tile[:, b * LANES : (b + 1) * LANES]
        return carry

    lax.fori_loop(0, pixels // 512, back, 0)
    gains = [pack[b, E_G3 : E_G3 + 1, :] for b in range(4)]

    def read_normed(b, start):
        return (middle[b, pl.ds(start, strip), :] - means[b]) * inverses[b]

    def write(b, start, value):
        total = cot[b, pl.ds(start, strip), :].astype(F32) + value
        dmiddle[b, pl.ds(start, strip), :] = total
        store_shifted(field, b, start, total.astype(BF16).astype(F32))

    gain_sums, bias_sums = norm_back_strips(
        pixels, strip, read_normed, lambda b, start: dattn[b, pl.ds(start, strip), :], gains, inverses, write
    )
    branch = sum_strips(
        pixels,
        strip,
        4,
        lambda start: [
            field[1, b, pl.ds(pl.multiple_of(PAD + start, 32), strip), :].astype(F32) for b in range(4)
        ],
    )
    for b in range(4):
        sums[b] = jnp.zeros((S_ROWS, LANES), F32)
        sums[b, S_G3 : S_G3 + 1, :] = gain_sums[b]
        sums[b, S_B3 : S_B3 + 1, :] = bias_sums[b]
        sums[b, S_CB2 : S_CB2 + 1, :] = column_sum(branch[b])
        sums[b, S_LIVE : S_LIVE + 1, :] = jnp.full((1, LANES), 1.0, F32) * alive
        sums[b, S_KEY : S_KEY + 8, :] = dctx[b]
    for offset, target in enumerate((d0, d1, d2, d3)):
        target[...] = field[1, jnp.bitwise_xor(me, offset), PAD : PAD + pixels, :]


def kernel_attention_grad(meta, dqkv, mixed, attn_t, cot, keep, send, cot_t):
    pixels = cot.shape[1]
    me = meta[0]
    strip = 128

    def turn(index, carry):
        start = pl.multiple_of(index * strip, strip)
        for b in range(4):
            cot_t[b, :, pl.ds(start, strip)] = cot[b, pl.ds(start, strip), :].astype(F32).T.astype(BF16)
        return carry

    lax.fori_loop(0, pixels // strip, turn, 0)

    def weights(offset, carry):
        s = jnp.bitwise_xor(me, offset)
        place = offset // 2
        attn_all = attn_t[...].reshape(C, pixels)
        cot_all = cot_t[...].reshape(C, pixels)
        grad = jnp.dot(attn_all, dqkv[s], preferred_element_type=F32).astype(BF16)
        other = jnp.dot(cot_all, mixed[s], preferred_element_type=F32).astype(BF16)

        def put(target):
            for kind in range(3):
                target[place, kind] = grad[:, kind * LANES : (kind + 1) * LANES]
            target[place, 3] = other

        @pl.when(offset % 2 == 0)
        def _():
            put(keep)

        @pl.when(offset % 2 == 1)
        def _():
            put(send)

        return carry

    lax.fori_loop(0, 4, weights, 0)


def weight_taps(half, sources, field, target):
    pixels = sources[0].shape[2]

    def body(index, carry):
        left = jnp.concatenate(
            [source[pl.ds(2 * half, 2)].reshape(2 * LANES, pixels) for source in sources], axis=1
        )
        columns = []
        for tap in (2 * index, jnp.minimum(2 * index + 1, 8)):
            start = pl.multiple_of((2 - tap // 3) * SIDE, 32)
            side = 2 - lax.rem(tap, 3)
            columns.append(
                jnp.concatenate([field[side, k, pl.ds(start, pixels), :] for k in range(4)], axis=0)
            )
        grad = jnp.dot(left, jnp.concatenate(columns, axis=1), preferred_element_type=F32)
        target[2 * index] = grad[:, :LANES].astype(target.dtype)

        @pl.when(index < 4)
        def _():
            target[2 * index + 1] = grad[:, LANES:].astype(target.dtype)

        return carry

    lax.fori_loop(0, 5, body, 0)


def kernel_weight_send(digit, u0, u1, u2, u3, d0, d1, d2, d3, send, field):
    pixels = u0.shape[2]
    clear_padding(field, pixels)
    strip = 128

    def spread(index, carry):
        start = pl.multiple_of(index * strip, strip)
        for k, source in enumerate((d0, d1, d2, d3)):
            store_shifted(field, k, start, source[pl.ds(start, strip), :].astype(F32))
        return carry

    lax.fori_loop(0, pixels // strip, spread, 0)
    weight_taps(1 - digit[0], (u0, u1, u2, u3), field, send)


def kernel_weight_own(digit, u0, u1, u2, u3, field, own):
    weight_taps(digit[0], (u0, u1, u2, u3), field, own)


def kernel_back_second(
    meta, grad_field, inner, pack, sums_in, w0, w1, w2, w3, w4, w5, w6, w7,
    field, sums, d0, d1, d2, d3, weight, grad, sems,
):
    pixels = inner.shape[1]
    me = meta[0]
    strip = 128
    weight_copies = fetch_routed((w0, w1, w2, w3, w4, w5, w6, w7), weight, me, meta[2], sems, 0)
    clear_padding(field, pixels)
    means, inverses = norm_rows(pixels, strip, lambda b, start: inner[b, pl.ds(start, strip), :])
    wait_all(weight_copies)

    def write_grad(start, half, tile):
        for b in range(2):
            grad[2 * half + b, pl.ds(start, tile.shape[0]), :] = tile[:, b * LANES : (b + 1) * LANES]

    conv_back_tiles(grad_field, weight, pixels, 512, write_grad)
    gains = [pack[b, E_G2 : E_G2 + 1, :] for b in range(4)]

    def read_normed(b, start):
        return (inner[b, pl.ds(start, strip), :] - means[b]) * inverses[b]

    def slope(index, carry):
        start = pl.multiple_of(index * strip, strip)
        found = []
        for b in range(4):
            bias = pack[b, E_B2 : E_B2 + 1, :]
            scale = pack[b, E_SCALE : E_SCALE + 1, :]
            shift = pack[b, E_SHIFT : E_SHIFT + 1, :]
            shaped = read_normed(b, start) * gains[b] + bias
            modulated = shaped * (1.0 + scale) + shift
            dmod = silu_slope(modulated, grad[b, pl.ds(start, strip), :])
            grad[b, pl.ds(start, strip), :] = dmod * (1.0 + scale)
            found += [dmod * shaped, dmod]
        return tuple(old + fold(new) for old, new in zip(carry, found))

    zero = tuple(jnp.zeros((8, LANES), F32) for _ in range(8))
    modulation = lax.fori_loop(0, pixels // strip, slope, zero)

    def write(b, start, value):
        store_shifted(field, b, start, value)

    gain_sums, bias_sums = norm_back_strips(
        pixels, strip, read_normed, lambda b, start: grad[b, pl.ds(start, strip), :], gains, inverses, write
    )
    for b in range(4):
        sums[b] = sums_in[b]
        sums[b, S_G2 : S_G2 + 1, :] = gain_sums[b]
        sums[b, S_B2 : S_B2 + 1, :] = bias_sums[b]
        sums[b, S_SCALE : S_SCALE + 1, :] = column_sum(modulation[2 * b])
        sums[b, S_SHIFT : S_SHIFT + 1, :] = column_sum(modulation[2 * b + 1])
    for offset, target in enumerate((d0, d1, d2, d3)):
        target[...] = field[1, jnp.bitwise_xor(me, offset), PAD : PAD + pixels, :]


def kernel_back_conv(meta, grad_field, w0, w1, w2, w3, w4, w5, w6, w7, grad, weight, sems):
    pixels = grad.shape[1]
    wait_all(fetch_routed((w0, w1, w2, w3, w4, w5, w6, w7), weight, meta[0], meta[2], sems, 0))

    def write_grad(start, half, tile):
        for b in range(2):
            grad[2 * half + b, pl.ds(start, tile.shape[0]), :] = tile[:, b * LANES : (b + 1) * LANES]

    conv_back_tiles(grad_field, weight, pixels, 512, write_grad)


def kernel_back_first(
    meta, grad_in, image, pack, dmiddle, sums_in, g0, g1, g2, g3, s0, s1, s2, s3, grad,
):
    pixels = image.shape[1]
    me = meta[0]
    strip = 128

    def read(b, start):
        return image[b, pl.ds(start, strip), :].astype(F32)

    means, inverses = norm_rows(pixels, strip, read)
    gains = [pack[b, E_G1 : E_G1 + 1, :] for b in range(4)]

    def read_normed(b, start):
        return (read(b, start) - means[b]) * inverses[b]

    def slope(index, carry):
        start = pl.multiple_of(index * strip, strip)
        for b in range(4):
            before = read_normed(b, start) * gains[b] + pack[b, E_B1 : E_B1 + 1, :]
            grad[b, pl.ds(start, strip), :] = silu_slope(before, grad_in[b, pl.ds(start, strip), :])
        return carry

    lax.fori_loop(0, pixels // strip, slope, 0)

    def write(b, start, value):
        grad[b, pl.ds(start, strip), :] = dmiddle[b, pl.ds(start, strip), :] + value

    gain_sums, bias_sums = norm_back_strips(
        pixels, strip, read_normed, lambda b, start: grad[b, pl.ds(start, strip), :], gains, inverses, write
    )
    for offset, (target, small) in enumerate(zip((g0, g1, g2, g3), (s0, s1, s2, s3))):
        other = jnp.bitwise_xor(me, offset)
        target[...] = grad[other].astype(BF16)
        small[...] = sums_in[other]
        for b in range(4):

            @pl.when(other == b)
            def _():
                small[S_G1 : S_G1 + 1, :] = gain_sums[b]
                small[S_B1 : S_B1 + 1, :] = bias_sums[b]


def kernel_factor_grads(
    meta, factors, small0, small1, small2, small3, embed, context, vectors, scale
):
    me = meta[0]
    groups = factors.shape[0]
    smalls = (small0, small1, small2, small3)
    total = jnp.zeros((S_ROWS, LANES), F32)
    for g in range(groups):
        for small in smalls:
            total = total + small[g]
    inverse = 1.0 / total[S_LIVE : S_LIVE + 1, :]
    vectors[...] = total * inverse
    scale[...] = jnp.broadcast_to(inverse, (8, LANES))
    over_rows = (((0,), (0,)), ((), ()))
    conditions, tokens, scales, shifts, keys, values = [], [], [], [], [], []
    for g in range(groups):
        for k, small in enumerate(smalls):
            slot = jnp.bitwise_xor(me, k)
            rows = factors[g, slot].astype(F32)
            conditions.append(rows[0:1])
            tokens.append(rows[CTX : 2 * CTX])
            scales.append(small[g, S_SCALE : S_SCALE + 1, :])
            shifts.append(small[g, S_SHIFT : S_SHIFT + 1, :])
            keys.append(small[g, S_KEY : S_KEY + CTX, :])
            values.append(small[g, S_VALUE : S_VALUE + CTX, :])
    left = jnp.concatenate(conditions, axis=0)
    for place, parts in enumerate((scales, shifts)):
        right = jnp.concatenate(parts, axis=0) * inverse
        embed[:, place, :] = lax.dot_general(
            left, right, over_rows, precision=lax.Precision.HIGHEST, preferred_element_type=F32
        )
    left = jnp.concatenate(tokens, axis=0).astype(BF16)
    for place, parts in enumerate((keys, values)):
        right = jnp.concatenate(parts, axis=0).astype(BF16)
        context[:, place, :] = (
            lax.dot_general(left, right, over_rows, preferred_element_type=F32) * inverse
        )


def kernel_slots(meta, p0, p1, p2, p3, whole, sems):
    wait_all(fetch((p0, p1, p2, p3), whole, meta[0], sems, 0))


def kernel_split(counts, width, digit, *refs):
    parts = refs[sum(counts) :]
    rows = parts[0].shape[1]
    for offset, part in enumerate(parts):
        start = pl.multiple_of(jnp.bitwise_xor(digit[0], offset) * rows, rows)
        position, base = 0, 0
        for count in counts:
            terms = refs[position : position + count]
            total = terms[0][:, pl.ds(start, rows), :].astype(F32)
            for term in terms[1:]:
                total = total + term[:, pl.ds(start, rows), :].astype(F32)
            part[base : base + total.shape[0]] = total.astype(part.dtype)
            position += count
            base += total.shape[0]


def split_sum(groups, width, digit):
    blocks = sum(terms[0].shape[0] for terms in groups)
    rows = groups[0][0].shape[1]
    flat = [term for terms in groups for term in terms]
    shape = (blocks, rows // width, LANES)
    return call(
        functools.partial(kernel_split, tuple(len(terms) for terms in groups), width),
        "split_sum",
        [struct(shape, F32)] + [struct(shape, BF16)] * (width - 1),
        [smem()] + [vmem()] * len(flat),
        [],
    )(digit, *flat)


def kernel_total(*refs):
    total = refs[0][...].astype(F32)
    for term in refs[1:-1]:
        total = total + term[...].astype(F32)
    refs[-1][...] = total.astype(BF16)


def total_sum(terms):
    return call(
        kernel_total, "total_sum", struct(terms[0].shape, BF16), [vmem()] * len(terms), []
    )(*terms)


def kernel_join(digit, *refs):
    parts, whole = refs[:-1], refs[-1]
    rows = parts[0].shape[1]
    for offset, part in enumerate(parts):
        start = pl.multiple_of(jnp.bitwise_xor(digit[0], offset) * rows, rows)
        whole[:, pl.ds(start, rows), :] = part[...]


def join(parts, digit):
    blocks, rows, _ = parts[0].shape
    return call(
        kernel_join,
        "join",
        struct((blocks, rows * len(parts), LANES), BF16),
        [smem()] + [vmem()] * len(parts),
        [],
    )(digit, *parts)


def kernel_last(digit, scale, mine, other, whole):
    rows = mine.shape[1]
    for offset, part in enumerate((mine, other)):
        start = pl.multiple_of(jnp.bitwise_xor(digit[0], offset) * rows, rows)
        whole[:, pl.ds(start, rows), :] = part[...].astype(F32) * scale[0:1, :]


def last_join(pair, digit, scale):
    blocks, rows, _ = pair[0].shape
    return call(
        kernel_last,
        "last_join",
        struct((blocks, 2 * rows, LANES), F32),
        [smem()] + [vmem()] * 3,
        [],
    )(digit, scale, *pair)


def swap(value, axis, offset):
    size = lax.axis_size(axis)
    return lax.ppermute(value, axis, [(i, i ^ offset) for i in range(size)])


def tie(*values):
    return lax.optimization_barrier(values)


def share(shard):
    near = swap(shard, "mp", 1)
    far = swap(shard, "mp", 2)
    return shard, near, far, swap(far, "mp", 1)


def exchange(pieces):
    return (pieces[0],) + tuple(swap(pieces[k], "mp", k) for k in range(1, 4))


def pick(stack, me):
    return [lax.dynamic_index_in_dim(stack, me ^ k, 0, keepdims=False) for k in range(4)]


def dp_levels(size):
    levels = []
    low = 1
    while low < size:
        width = 2 if low == 1 or size // low < 4 else 4
        levels.append((low, width))
        low *= width
    return levels


def gather_step(stacked, low):
    return jnp.concatenate([stacked, swap(stacked, "dp", low)], axis=0)


def bits(size):
    return [1 << k for k in range(size.bit_length() - 1)]


def local(
    image_in,
    out_cotangent,
    timesteps,
    clip_embed,
    context_tokens,
    image_count,
    norm1_gain,
    norm1_bias,
    conv1_weight,
    embed_weight,
    norm2_gain,
    norm2_bias,
    conv2_weight,
    conv2_bias,
    norm3_gain,
    norm3_bias,
    qkv_weight,
    context_weight,
    proj_weight,
):
    slots, pixels, width = image_in.shape
    me = lax.axis_index("mp")
    group = lax.axis_index("dp")
    parity = (group ^ (group >> 1)) & 1
    meta = jnp.stack([me, (me < image_count[0]).astype(jnp.int32), parity]).astype(jnp.int32)
    levels = dp_levels(lax.axis_size("dp"))
    digits = [((group // low) % wide).astype(jnp.int32)[None] for low, wide in levels]
    steps = bits(lax.axis_size("dp"))

    conv1_shard = conv1_weight.reshape(9, C, LANES)
    conv2_shard = conv2_weight.reshape(9, C, LANES)
    qkv_shard = jnp.transpose(qkv_weight, (1, 0, 2))

    def half_of(shard):
        rows = shard.shape[-2] // 2
        return lax.dynamic_slice_in_dim(shard, parity * rows, rows, axis=shard.ndim - 2)

    half1 = swap(half_of(conv1_shard), "mp", 2)
    images = exchange(pick(image_in, me))
    near1 = swap(conv1_shard, "mp", 1)

    half_width = EMB // 2
    frequency = jnp.exp(-math.log(10000.0) * jnp.arange(half_width, dtype=F32) / half_width)
    angles = timesteps.astype(F32)[:, None] * frequency[None, :]
    condition = jax.nn.silu(
        jnp.concatenate([jnp.cos(angles), jnp.sin(angles)], axis=1) + clip_embed.astype(F32)
    ).astype(BF16)
    scale_shift = jnp.dot(
        condition, embed_weight.reshape(EMB, 2 * LANES), preferred_element_type=F32
    ).reshape(slots, 2, LANES)
    doubled = jnp.concatenate([context_tokens, context_tokens], axis=1)
    context = jnp.dot(
        doubled.reshape(slots * 2 * CTX, EMB),
        context_weight.reshape(EMB, 2 * LANES),
        preferred_element_type=F32,
    ).astype(BF16).astype(F32).reshape(slots, 2 * CTX, 2, LANES)
    vectors = jnp.stack(
        [norm1_gain, norm1_bias, norm2_gain, norm2_bias, conv2_bias, norm3_gain, norm3_bias]
    )
    early = jnp.concatenate(
        [
            scale_shift,
            jnp.broadcast_to(vectors[None], (slots, 7, LANES)),
            jnp.zeros((slots, 7, LANES), F32),
            context[:, :, 0],
            context[:, :, 1],
        ],
        axis=1,
    )
    early, near1 = tie(early, near1)
    packs = exchange(pick(early, me))
    factors = jnp.concatenate(
        [jnp.broadcast_to(condition[:, None], (slots, CTX, EMB)), context_tokens], axis=1
    )[None]

    def relayed(shard, near, half):
        quarter = half.shape[-2] // 2
        by_x = swap(half[:, :quarter], "dp", 1)
        by_z = swap(half[:, quarter:], "dp", 2)
        return (shard, near, half, by_x, by_z) + tuple(
            swap(part, "mp", 1) for part in (half, by_x, by_z)
        )

    conv1 = relayed(conv1_shard, near1, half1)
    half2 = half_of(conv2_shard)
    half2, *tied = tie(half2, *images, *packs)
    images, packs = tied[:4], tied[4:]
    half2 = swap(half2, "mp", 2)
    near2 = swap(conv2_shard, "mp", 1)
    qkv_far = swap(qkv_shard, "mp", 2)
    proj_far = swap(proj_weight, "mp", 2)
    factors = gather_step(factors, steps[0])

    block = struct((4, pixels, LANES), BF16)
    block32 = struct((4, pixels, LANES), F32)
    turned = struct((4, LANES, pixels), BF16)
    fields = struct((3, 4, pixels + 2 * PAD, LANES), BF16)
    piece = struct((pixels, LANES), BF16)
    field_scratch = pltpu.VMEM((3, 4, pixels + 2 * PAD, LANES), BF16)
    conv_scratch = pltpu.VMEM((4, 9, C, LANES), BF16)
    qkv_scratch = pltpu.VMEM((4, 3, C, LANES), BF16)
    grad_scratch = pltpu.VMEM((4, pixels, LANES), F32)
    conv_flops = 2 * pixels * 9 * C * C

    image, pack, first_t, inner = call(
        kernel_first,
        "first",
        [block, struct((4, E_ROWS, LANES), F32), turned, block32],
        [smem()] + [anywhere()] * 16,
        [field_scratch, conv_scratch, pltpu.SemaphoreType.DMA((16,))],
        conv_flops,
    )(meta, *images, *packs, *conv1)

    inner, half2, near2, qkv_far, proj_far, factors = tie(
        inner, half2, near2, qkv_far, proj_far, factors
    )
    qkv_near = swap(qkv_shard, "mp", 1)
    conv2 = relayed(conv2_shard, near2, half2)
    qkv_w = (qkv_shard, qkv_near, qkv_far, swap(qkv_far, "mp", 1))
    proj_w = (proj_weight, swap(proj_weight, "mp", 1), proj_far, swap(proj_far, "mp", 1))
    inner, *conv2 = tie(inner, *conv2)
    cots = exchange(pick(out_cotangent, me))
    factors = gather_step(factors, steps[1])
    middle, second_t, attn_t, qkv = call(
        kernel_second,
        "second",
        [block32, turned, turned, struct((4, pixels, 3 * LANES), BF16)],
        [smem()] + [vmem()] * 3 + [anywhere()] * 12,
        [
            field_scratch,
            conv_scratch,
            qkv_scratch,
            pltpu.VMEM((4, pixels, LANES), BF16),
            pltpu.SemaphoreType.DMA((12,)),
        ],
        conv_flops + 6 * pixels * C * C,
    )(meta, inner, image, pack, *qkv_w, *conv2)
    ctx_scratch = pltpu.VMEM((pixels, LANES), F32)
    turned_scratch = pltpu.VMEM((LANES, pixels), F32)
    qkv, first_t, factors, *cots = tie(qkv, first_t, factors, *cots)
    second_y = swap(second_t, "mp", 2)
    first_y = swap(first_t, "mp", 2)
    second_c = swap(second_t, "mp", 1)
    first_c = swap(first_t, "mp", 1)
    for low in steps[2:]:
        factors = gather_step(factors, low)
    *outs, cot, mixed, dqkv, dctx = call(
        kernel_attention,
        "attention",
        [piece] * 4
        + [block, block, struct((4, pixels, 3 * LANES), BF16), struct((4, 2 * CTX, LANES), F32)],
        [smem()] + [vmem()] * 3 + [anywhere()] * 8,
        [
            pltpu.VMEM((4, LANES, C), BF16),
            pltpu.VMEM((4, pixels, LANES), BF16),
            ctx_scratch,
            ctx_scratch,
            ctx_scratch,
            ctx_scratch,
            grad_scratch,
            grad_scratch,
            turned_scratch,
            turned_scratch,
            pltpu.SemaphoreType.DMA((8,)),
        ],
        4 * 12 * pixels * pixels * C,
    )(meta, qkv, pack, middle, *cots, *proj_w)
    dqkv, second_y, first_y, second_c, first_c, factors = tie(
        dqkv, second_y, first_y, second_c, first_c, factors
    )
    second_d = swap(second_y, "mp", 1)
    first_d = swap(first_y, "mp", 1)
    dmiddle, field2, sums, *gradients2 = call(
        kernel_back_attention,
        "back_attention",
        [block32, fields, struct((4, S_ROWS, LANES), F32)] + [piece] * 4,
        [smem()] + [vmem()] * 5 + [anywhere()] * 4,
        [qkv_scratch, grad_scratch, pltpu.SemaphoreType.DMA((4,))],
        8 * pixels * C * C,
    )(meta, dqkv, cot, middle, pack, dctx, *qkv_w)
    gradients2, second_d, first_d = tie(gradients2, second_d, first_d)
    gradients2 = exchange(gradients2)
    field1, sums, *gradients1 = call(
        kernel_back_second,
        "back_second",
        [fields, struct((4, S_ROWS, LANES), F32)] + [piece] * 4,
        [smem()] + [vmem()] * 4 + [anywhere()] * 8,
        [conv_scratch, grad_scratch, pltpu.SemaphoreType.DMA((8,))],
        conv_flops,
    )(meta, field2, inner, pack, sums, *conv2)

    def weight_send(sources, gradients):
        return call(
            kernel_weight_send,
            "weight_send",
            [struct((9, C // 2, LANES), BF16), fields],
            [smem()] + [vmem()] * 8,
            [],
            conv_flops // 2,
        )(digits[0], *sources, *gradients)

    def weight_own(sources, field):
        return call(
            kernel_weight_own,
            "weight_own",
            struct((9, C // 2, LANES), F32),
            [smem()] + [vmem()] * 5,
            [],
            conv_flops // 2,
        )(digits[0], *sources, field)

    seconds = (second_t, second_c, second_y, second_d)
    firsts = (first_t, first_c, first_y, first_d)
    gradients1, gradients2 = tie(gradients1, gradients2)
    gradients1 = exchange(gradients1)
    send2, wide2 = weight_send(seconds, gradients2)
    got2 = swap(send2, "dp", 1)
    own2 = weight_own(seconds, wide2)
    own2, gradients1, outs = tie(own2, gradients1, outs)
    out_parts = exchange(outs)
    send1, wide1 = weight_send(firsts, gradients1)
    got1 = swap(send1, "dp", 1)
    own1 = weight_own(firsts, wide1)
    att_keep, att_send = call(
        kernel_attention_grad,
        "attention_grad",
        [struct((2, 4, C, LANES), BF16)] * 2,
        [smem()] + [vmem()] * 4,
        [pltpu.VMEM((4, LANES, pixels), BF16)],
        8 * pixels * C * C,
    )(meta, dqkv, mixed, attn_t, cot)
    own1, got2, out_parts = tie(own1, got2, out_parts)

    def down(groups, level):
        low, wide = levels[level]
        parts = split_sum(groups, wide, digits[level])
        return [parts[0]] + [swap(parts[k], "dp", low * k) for k in range(1, wide)]

    def spread(value, level):
        low, wide = levels[level]
        return [value] + [swap(value, "dp", low * k) for k in range(1, wide)]

    terms2 = down([[own2, got2]], 1)
    att_got = swap(att_send, "mp", 1)
    grad_first = call(
        kernel_back_conv,
        "back_conv",
        block32,
        [smem()] + [vmem()] + [anywhere()] * 8,
        [conv_scratch, pltpu.SemaphoreType.DMA((8,))],
        conv_flops,
    )(meta, field1, *conv1)
    grad_first, att_got, *terms2 = tie(grad_first, att_got, *terms2)
    att_far = swap(total_sum([att_keep[1], att_got[1]]), "mp", 2)

    def inner_levels(terms):
        for level in range(2, len(levels)):
            terms = down([terms], level)
        value = total_sum(terms)
        for level in range(len(levels) - 1, 1, -1):
            value = join(spread(value, level), digits[level])
        return value

    value2 = inner_levels(terms2)
    parts2 = spread(value2, 1)
    terms1 = down([[own1, got1]], 1)
    back = call(
        kernel_back_first,
        "back_first",
        [piece] * 4 + [struct((S_ROWS, LANES), F32)] * 4,
        [smem()] + [vmem()] * 5,
        [grad_scratch],
        conv_flops // 4,
    )(meta, grad_first, image, pack, dmiddle, sums)
    image_grads, smalls = back[:4], back[4:]
    half2_sum = join(parts2, digits[1])
    pair2 = spread(half2_sum, 0)
    value1 = inner_levels(terms1)
    parts1 = spread(value1, 1)
    half1_sum = join(parts1, digits[1])
    pair1 = spread(half1_sum, 0)
    att_terms = down([[att_keep[0], att_got[0], att_far]], 0)
    att_terms = down([att_terms], 1)
    att_value = inner_levels(att_terms)
    att_pair = spread(join(spread(att_value, 1), digits[1]), 0)

    image_parts = exchange(image_grads)
    smalls = [small[None] for small in exchange(smalls)]
    smalls = jnp.stack(smalls)
    for low in steps:
        smalls = jnp.concatenate([smalls, swap(smalls, "dp", low)], axis=1)
    embed_grad, context_grad, vector_sums, scale = call(
        kernel_factor_grads,
        "factor_grads",
        [
            struct((EMB, 2, LANES), F32),
            struct((EMB, 2, LANES), F32),
            struct((S_ROWS, LANES), F32),
            struct((8, LANES), F32),
        ],
        [smem()] + [vmem()] * 5,
        [],
    )(meta, factors, smalls[0], smalls[1], smalls[2], smalls[3])

    def in_slots(parts):
        return pl.pallas_call(
            kernel_slots,
            name="slots",
            out_shape=struct((4, pixels, LANES), BF16),
            in_specs=[smem()] + [anywhere()] * 4,
            out_specs=vmem(),
            scratch_shapes=[pltpu.SemaphoreType.DMA((4,))],
        )(meta, *parts)

    block_out = in_slots(out_parts)
    image_grad = in_slots(image_parts)
    conv2_grad = last_join(pair2, digits[0], scale)
    conv1_grad = last_join(pair1, digits[0], scale)
    att_grad = last_join(att_pair, digits[0], scale)
    return (
        block_out,
        image_grad,
        vector_sums[S_G1],
        vector_sums[S_B1],
        conv1_grad.reshape(3, 3, C, LANES),
        embed_grad,
        vector_sums[S_G2],
        vector_sums[S_B2],
        conv2_grad.reshape(3, 3, C, LANES),
        vector_sums[S_CB2],
        vector_sums[S_G3],
        vector_sums[S_B3],
        jnp.transpose(att_grad[:3], (1, 0, 2)),
        context_grad,
        att_grad[3].T,
    )


def solution(mesh):
    return jax.shard_map(
        local,
        mesh=mesh,
        in_specs=(
            P("dp", None, "mp"),
            P("dp", None, "mp"),
            P("dp"),
            P("dp", None),
            P("dp", None, None),
            P("dp"),
            P("mp"),
            P("mp"),
            P(None, None, None, "mp"),
            P(None, None, "mp"),
            P("mp"),
            P("mp"),
            P(None, None, None, "mp"),
            P("mp"),
            P("mp"),
            P("mp"),
            P(None, None, "mp"),
            P(None, None, "mp"),
            P("mp", None),
        ),
        out_specs=(
            P("dp", None, "mp"),
            P("dp", None, "mp"),
            P("mp"),
            P("mp"),
            P(None, None, None, "mp"),
            P(None, None, "mp"),
            P("mp"),
            P("mp"),
            P(None, None, None, "mp"),
            P("mp"),
            P("mp"),
            P("mp"),
            P(None, None, "mp"),
            P(None, None, "mp"),
            P("mp", None),
        ),
        check_vma=False,
    )
```

```python
import functools
import math

import jax
import jax.numpy as jnp
from jax import lax
from jax.experimental import pallas as pl
from jax.experimental.pallas import tpu as pltpu
from jax.sharding import PartitionSpec as P

C = 512
GROUPS = 32
HEAD = 64
EMB = 2048
CTX = 4
SIDE = 32
LANES = 128
PAD = SIDE
EPSILON = 1e-05
F32 = jnp.float32
BF16 = jnp.bfloat16
NEG = -1e30

E_G1, E_B1, E_G2, E_B2, E_CB2, E_G3, E_B3 = range(7)
E_ROWS = 8
M_SCALE, M_SHIFT = range(2)
M_KEY, M_VALUE, M_ROWS = 8, 16, 24
S_G3, S_B3, S_CB2, S_G2, S_B2, S_SCALE, S_SHIFT = range(7)
S_KEY, S_VALUE, S_G1, S_B1, S_ROWS = 8, 12, 16, 17, 32
MIB = 1 << 20


def vmem():
    return pl.BlockSpec(memory_space=pltpu.VMEM)


def anywhere():
    return pl.BlockSpec(memory_space=pltpu.HBM)


def smem():
    return pl.BlockSpec(memory_space=pltpu.SMEM)


def struct(shape, dtype):
    return jax.ShapeDtypeStruct(shape, dtype)


def call(body, name, out_shape, in_specs, scratch, flops=0, limit=14):
    many = isinstance(out_shape, (list, tuple))
    return pl.pallas_call(
        body,
        name=name,
        out_shape=out_shape,
        in_specs=in_specs,
        out_specs=[vmem() for _ in out_shape] if many else vmem(),
        scratch_shapes=scratch,
        compiler_params=pltpu.CompilerParams(vmem_limit_bytes=limit * MIB),
        cost_estimate=pl.CostEstimate(flops=0, transcendentals=0, bytes_accessed=0),
    )


def fetch(sources, target, me, sems, first):
    copies = []
    for offset, source in enumerate(sources):
        copy = pltpu.make_async_copy(
            source, target.at[jnp.bitwise_xor(me, offset)], sems.at[first + offset]
        )
        copy.start()
        copies.append(copy)
    return copies


def fetch_routed(sources, target, me, parity, sems, first):
    quarter = target.shape[1] // 4
    copies = []
    for index, source in enumerate(sources):
        place = target.at[jnp.bitwise_xor(me, (0, 1, 2, 2, 2, 3, 3, 3)[index])]
        if index >= 2:
            kind = (index - 2) % 3
            rows = 2 * quarter if kind == 0 else quarter
            half = parity if kind == 0 else 1 - parity
            start = half * 2 * quarter + (quarter if kind == 2 else 0)
            place = place.at[pl.ds(pl.multiple_of(start, quarter), rows), :]
        copy = pltpu.make_async_copy(source, place, sems.at[first + index])
        copy.start()
        copies.append(copy)
    return copies


def wait_all(copies):
    for copy in copies:
        copy.wait()


def fold(values):
    rows = values.shape[0]
    return jnp.sum(values.reshape(rows // 8, 8, values.shape[1]), axis=0)


def group_sum(rows8):
    lane = lax.broadcasted_iota(jnp.int32, rows8.shape, 1)
    total = jnp.broadcast_to(jnp.sum(rows8, axis=0, keepdims=True), rows8.shape)
    for step in (1, 2, 4, 8):
        up = pltpu.roll(total, step, axis=1)
        down = pltpu.roll(total, LANES - step, axis=1)
        total = total + jnp.where((lane & step) != 0, up, down)
    return total[0:1]


def column_sum(rows8):
    return jnp.sum(rows8, axis=0, keepdims=True)


def sum_strips(pixels, strip, width, function):
    zero = tuple(jnp.zeros((8, LANES), F32) for _ in range(width))

    def body(index, carry):
        start = pl.multiple_of(index * strip, strip)
        return tuple(old + fold(new) for old, new in zip(carry, function(start)))

    return lax.fori_loop(0, pixels // strip, body, zero)


def norm_rows(pixels, strip, read):
    count = pixels * (C // GROUPS)
    sums = sum_strips(pixels, strip, 4, lambda start: [read(b, start) for b in range(4)])
    means = [group_sum(s) * (1.0 / count) for s in sums]
    squares = sum_strips(
        pixels,
        strip,
        4,
        lambda start: [jnp.square(read(b, start) - means[b]) for b in range(4)],
    )
    inverses = [lax.rsqrt(group_sum(s) * (1.0 / count) + EPSILON) for s in squares]
    return means, inverses


def shifted(values):
    rows = values.shape[0]
    column = lax.broadcasted_iota(jnp.int32, values.shape, 0) & (SIDE - 1)
    left = jnp.where(column == 0, 0.0, pltpu.roll(values, 1, axis=0))
    right = jnp.where(column == SIDE - 1, 0.0, pltpu.roll(values, rows - 1, axis=0))
    return left, values, right


def store_shifted(target, block, start, values):
    rows = values.shape[0]
    for position, part in enumerate(shifted(values)):
        target[position, block, pl.ds(pl.multiple_of(PAD + start, 32), rows), :] = part.astype(BF16)


def clear_padding(target, pixels):
    zero = jnp.zeros((PAD, LANES), BF16)
    for position in range(3):
        for block in range(4):
            target[position, block, 0:PAD, :] = zero
            target[position, block, PAD + pixels : PAD + pixels + PAD, :] = zero


def conv_tiles(field, weight, pixels, tile, write):
    def body(index, carry):
        start = pl.multiple_of(index * tile, tile)
        left = jnp.concatenate(
            [
                field[b, block, pl.ds(pl.multiple_of(start + a * SIDE, 32), tile), :]
                for a in range(3)
                for b in range(3)
                for block in range(4)
            ],
            axis=1,
        )
        right = jnp.concatenate([weight[s] for s in range(4)], axis=1)
        write(start, jnp.dot(left, right, preferred_element_type=F32))
        return carry

    lax.fori_loop(0, pixels // tile, body, 0)


def conv_back_tiles(field, weight, pixels, tile, write):
    def body(index, carry):
        start = pl.multiple_of((index // 2) * tile, tile)
        half = index % 2
        left = jnp.concatenate(
            [
                field[2 - b, block, pl.ds(pl.multiple_of(start + (2 - a) * SIDE, 32), tile), :]
                for a in range(3)
                for b in range(3)
                for block in range(4)
            ],
            axis=1,
        )
        right = jnp.concatenate(
            [
                weight[block, pl.ds(pl.multiple_of((3 * a + b) * C + half * 256, 256), 256), :]
                for a in range(3)
                for b in range(3)
                for block in range(4)
            ],
            axis=1,
        )
        write(
            start,
            half,
            lax.dot_general(left, right, (((1,), (1,)), ((), ())), preferred_element_type=F32),
        )
        return carry

    lax.fori_loop(0, 2 * (pixels // tile), body, 0)


def silu_slope(before, grad_out):
    gate = jax.nn.sigmoid(before)
    return grad_out * gate * (1.0 + before * (1.0 - gate))


def kernel_first(
    meta, i0, i1, i2, i3, e0, e1, e2, e3, w0, w1, w2, w3, w4, w5, w6, w7,
    image, pack, first_t, inner, field, weight, sems,
):
    pixels = image.shape[1]
    me = meta[0]
    image_copies = fetch((i0, i1, i2, i3), image, me, sems, 0)
    pack_copies = fetch((e0, e1, e2, e3), pack, me, sems, 4)
    weight_copies = fetch_routed((w0, w1, w2, w3, w4, w5, w6, w7), weight, me, meta[2], sems, 8)
    clear_padding(field, pixels)
    wait_all(image_copies)
    wait_all(pack_copies)
    strip = 128

    def read(block, start):
        return image[block, pl.ds(start, strip), :].astype(F32)

    means, inverses = norm_rows(pixels, strip, read)

    def normalise(index, carry):
        start = pl.multiple_of(index * strip, strip)
        for b in range(4):
            gain = pack[b, E_G1 : E_G1 + 1, :]
            bias = pack[b, E_B1 : E_B1 + 1, :]
            before = (read(b, start) - means[b]) * inverses[b] * gain + bias
            after = before * jax.nn.sigmoid(before)
            store_shifted(field, b, start, after)
            first_t[b, :, pl.ds(start, strip)] = after.T.astype(BF16)
        return carry

    lax.fori_loop(0, pixels // strip, normalise, 0)
    wait_all(weight_copies)

    def write(start, tile):
        for b in range(4):
            inner[b, pl.ds(start, tile.shape[0]), :] = tile[:, b * LANES : (b + 1) * LANES]

    conv_tiles(field, weight, pixels, 512, write)


def kernel_second(
    meta, inner, image, pack, m0, m1, m2, m3, p0, p1, p2, p3, w0, w1, w2, w3, w4, w5, w6, w7,
    middle, second_t, attn_t, qkv, mod, field, weight, qkv_weight, attn, sems,
):
    pixels = image.shape[1]
    me = meta[0]
    qkv_copies = fetch((p0, p1, p2, p3), qkv_weight, me, sems, 0)
    weight_copies = fetch_routed((w0, w1, w2, w3, w4, w5, w6, w7), weight, me, meta[2], sems, 4)
    mod_copies = fetch((m0, m1, m2, m3), mod, me, sems, 12)
    clear_padding(field, pixels)
    strip = 128
    means2, inverses2 = norm_rows(pixels, strip, lambda b, start: inner[b, pl.ds(start, strip), :])

    wait_all(mod_copies)

    def modulate(index, carry):
        start = pl.multiple_of(index * strip, strip)
        for b in range(4):
            gain = pack[b, E_G2 : E_G2 + 1, :]
            bias = pack[b, E_B2 : E_B2 + 1, :]
            scale = mod[b, M_SCALE : M_SCALE + 1, :]
            shift = mod[b, M_SHIFT : M_SHIFT + 1, :]
            normed = (inner[b, pl.ds(start, strip), :] - means2[b]) * inverses2[b]
            modulated = (normed * gain + bias) * (1.0 + scale) + shift
            after = modulated * jax.nn.sigmoid(modulated)
            store_shifted(field, b, start, after)
            second_t[b, :, pl.ds(start, strip)] = after.T.astype(BF16)
        return carry

    lax.fori_loop(0, pixels // strip, modulate, 0)
    wait_all(weight_copies)

    def write(start, tile):
        rows = tile.shape[0]
        for b in range(4):
            branch = tile[:, b * LANES : (b + 1) * LANES] + pack[b, E_CB2 : E_CB2 + 1, :]
            middle[b, pl.ds(start, rows), :] = image[b, pl.ds(start, rows), :].astype(F32) + branch

    conv_tiles(field, weight, pixels, 512, write)
    means, inverses = norm_rows(pixels, strip, lambda b, start: middle[b, pl.ds(start, strip), :])

    def normalise(index, carry):
        start = pl.multiple_of(index * strip, strip)
        for b in range(4):
            normed = (middle[b, pl.ds(start, strip), :] - means[b]) * inverses[b]
            value = normed * pack[b, E_G3 : E_G3 + 1, :] + pack[b, E_B3 : E_B3 + 1, :]
            attn[b, pl.ds(start, strip), :] = value.astype(BF16)
            attn_t[b, :, pl.ds(start, strip)] = value.T.astype(BF16)
        return carry

    lax.fori_loop(0, pixels // strip, normalise, 0)
    wait_all(qkv_copies)

    def project(index, carry):
        s = index // 2
        start = pl.multiple_of((index % 2) * 512, 512)
        left = jnp.concatenate([attn[b, pl.ds(start, 512), :] for b in range(4)], axis=1)
        right = jnp.concatenate([qkv_weight[s, kind] for kind in range(3)], axis=1)
        qkv[s, pl.ds(start, 512), :] = jnp.dot(left, right, preferred_element_type=F32).astype(BF16)
        return carry

    lax.fori_loop(0, 4 * (pixels // 512), project, 0)


def kernel_attention(
    meta, qkv, mod, middle, c0, c1, c2, c3, w0, w1, w2, w3,
    o0, o1, o2, cot, mixed, dqkv, dctx,
    weight, grad_mixed, score_ctx, grad_ctx_prob, prob_ctx, dscore_ctx, out_pix, dquery, dkey_t, dvalue_t, sems,
):
    pixels = qkv.shape[1]
    me = meta[0]
    alive = meta[1].astype(F32)
    cot_copies = fetch((c0, c1, c2, c3), cot, me, sems, 0)
    weight_copies = fetch((w0, w1, w2, w3), weight, me, sems, 4)
    scale = 1.0 / math.sqrt(HEAD)
    block = 256

    row32 = lax.broadcasted_iota(jnp.int32, (32, LANES), 0)
    lane32 = lax.broadcasted_iota(jnp.int32, (32, LANES), 1)

    def diagonal(kind):
        found = []
        for s in range(4):
            rows8 = mod[s, kind : kind + 8, :]
            tiled = jnp.concatenate([rows8] * 4, axis=0)
            own = (row32 // 4) == (2 * s + lane32 // HEAD)
            kept = jnp.where(own, tiled, 0.0)
            found.append(jnp.concatenate([kept, jnp.zeros((96, LANES), F32)], axis=0).astype(BF16))
        return jnp.concatenate(found, axis=1)

    keys_ctx = diagonal(M_KEY)
    values_ctx = diagonal(M_VALUE)
    wait_all(cot_copies)
    wait_all(weight_copies)

    def prepare(index, carry):
        start = pl.multiple_of(index * block, block)
        rows = pl.ds(start, block)
        for s in range(4):
            cot[s, rows, :] = (cot[s, rows, :].astype(F32) * alive).astype(BF16)
        all_cot = jnp.concatenate([cot[s, rows, :] for s in range(4)], axis=1)
        all_weight = weight[...].reshape(C, C)
        grad = lax.dot_general(
            all_cot, all_weight, (((1,), (1,)), ((), ())), preferred_element_type=F32
        ).astype(BF16)
        for s in range(4):
            grad_mixed[s, rows, :] = grad[:, s * LANES : (s + 1) * LANES]
        query = jnp.concatenate([qkv[s, rows, 0:LANES] for s in range(4)], axis=1)
        score_ctx[rows, :] = lax.dot_general(
            query, keys_ctx, (((1,), (1,)), ((), ())), preferred_element_type=F32
        )
        grad_ctx_prob[rows, :] = lax.dot_general(
            grad, values_ctx, (((1,), (1,)), ((), ())), preferred_element_type=F32
        )
        prob_ctx[rows, :] = jnp.zeros((block, LANES), F32)
        dscore_ctx[rows, :] = jnp.zeros((block, LANES), F32)
        return carry

    lax.fori_loop(0, pixels // block, prepare, 0)
    lane = lax.broadcasted_iota(jnp.int32, (block, LANES), 1)
    low = lane < HEAD
    ones = jnp.ones((pixels, LANES), BF16)
    blocks = pixels // block

    def attend(index, carry):
        s = index // blocks
        part = index % blocks
        rows = pl.ds(pl.multiple_of(part * block, block), block)

        @pl.when(part == 0)
        def _():
            dkey_t[...] = jnp.zeros((LANES, pixels), F32)
            dvalue_t[...] = jnp.zeros((LANES, pixels), F32)

        query = qkv[s, rows, 0:LANES]
        key = qkv[s, :, LANES : 2 * LANES]
        value = qkv[s, :, 2 * LANES : 3 * LANES]
        value_ones = jnp.concatenate([value, ones], axis=1)
        grad = grad_mixed[s, rows, :]
        ctx_scores = score_ctx[rows, :]
        ctx_grads = grad_ctx_prob[rows, :]
        exps, outs, inverses, ctx_exps, owns = [], [], [], [], []
        for h in range(2):
            mine = low if h == 0 else jnp.logical_not(low)
            own = lane // CTX == 2 * s + h
            score = lax.dot_general(
                jnp.where(mine, query, jnp.zeros_like(query)),
                key,
                (((1,), (1,)), ((), ())),
                preferred_element_type=F32,
            )
            top = jnp.maximum(
                jnp.max(score, axis=1, keepdims=True),
                jnp.max(jnp.where(own, ctx_scores, NEG), axis=1, keepdims=True),
            )
            exp = jnp.exp((score - top) * scale).astype(BF16)
            ctx_exp = jnp.where(own, jnp.exp((ctx_scores - top) * scale), 0.0)
            out = jnp.dot(exp, value_ones, preferred_element_type=F32)
            total = out[:, LANES:] + jnp.sum(ctx_exp, axis=1, keepdims=True)
            inverse = 1.0 / total
            exps.append(exp)
            outs.append(out[:, :LANES] * inverse)
            inverses.append(inverse)
            ctx_exps.append(ctx_exp)
            owns.append(own)
        out_pair = jnp.where(low, outs[0], outs[1])
        out_pix[s, rows, :] = out_pair
        inverse_pair = jnp.where(low, inverses[0], inverses[1])
        scaled = (grad.astype(F32) * (inverse_pair * scale)).astype(BF16)
        product = out_pair * scaled.astype(F32)
        query_t = query.astype(F32).T.astype(BF16)
        scaled_t = scaled.astype(F32).T.astype(BF16)
        prob_keep = prob_ctx[rows, :]
        dscore_keep = dscore_ctx[rows, :]
        dqs = []
        for h in range(2):
            mine = low if h == 0 else jnp.logical_not(low)
            own = owns[h]
            ctx_prob = ctx_exps[h] * inverses[h]
            ctx_grad = ctx_grads * (inverses[h] * scale)
            dot = jnp.sum(
                jnp.where(mine, product, 0.0) + ctx_prob * jnp.where(own, ctx_grad, 0.0),
                axis=1,
                keepdims=True,
            )
            weight_grad = lax.dot_general(
                jnp.where(mine, scaled, jnp.zeros_like(scaled)),
                value,
                (((1,), (1,)), ((), ())),
                preferred_element_type=F32,
            )
            dscore = (exps[h].astype(F32) * (weight_grad - dot)).astype(BF16)
            prob_keep = jnp.where(own, ctx_prob, prob_keep)
            dscore_keep = jnp.where(own, ctx_exps[h] * (ctx_grad - dot), dscore_keep)
            dqs.append(jnp.dot(dscore, key, preferred_element_type=F32))
            half = slice(h * HEAD, (h + 1) * HEAD)
            dkey_t[half, :] += jnp.dot(query_t[half], dscore, preferred_element_type=F32)
            dvalue_t[half, :] += jnp.dot(scaled_t[half], exps[h], preferred_element_type=F32)
        prob_ctx[rows, :] = prob_keep
        dscore_ctx[rows, :] = dscore_keep
        dquery[s, rows, :] = jnp.where(low, dqs[0], dqs[1])

        @pl.when(part == blocks - 1)
        def _():
            for piece in range(pixels // LANES):
                cut = slice(piece * LANES, (piece + 1) * LANES)
                dqkv[s, cut, LANES : 2 * LANES] = dkey_t[:, cut].T.astype(BF16)
                dqkv[s, cut, 2 * LANES : 3 * LANES] = (dvalue_t[:, cut] * (1.0 / scale)).T.astype(BF16)

        return carry

    lax.fori_loop(0, 4 * blocks, attend, 0)

    def finish(index, carry):
        dkeys, dvalues = carry
        start = pl.multiple_of(index * block, block)
        rows = pl.ds(start, block)
        prob = prob_ctx[rows, :].astype(BF16)
        dscore = dscore_ctx[rows, :].astype(BF16)
        out_ctx = jnp.dot(prob, values_ctx, preferred_element_type=F32)
        dquery_ctx = jnp.dot(dscore, keys_ctx, preferred_element_type=F32)
        parts = []
        for s in range(4):
            cut = slice(s * LANES, (s + 1) * LANES)
            both = (out_pix[s, rows, :] + out_ctx[:, cut]).astype(BF16)
            mixed[s, rows, :] = both
            parts.append(both)
            dqkv[s, rows, 0:LANES] = (dquery[s, rows, :] + dquery_ctx[:, cut]).astype(BF16)
        result = jnp.dot(
            jnp.concatenate(parts, axis=1), weight[...].reshape(C, C), preferred_element_type=F32
        )
        for offset, target in enumerate((o0, o1, o2.at[0], o2.at[1])):
            other = jnp.bitwise_xor(me, offset)
            value = jnp.zeros((block, LANES), F32)
            for s in range(4):
                value = jnp.where(other == s, result[:, s * LANES : (s + 1) * LANES], value)
            target[rows, :] = ((middle[other, rows, :] + value) * alive).astype(BF16)
        query = jnp.concatenate([qkv[s, rows, 0:LANES] for s in range(4)], axis=1)
        grad = jnp.concatenate([grad_mixed[s, rows, :] for s in range(4)], axis=1)
        dkeys = dkeys + jnp.dot(dscore_ctx[rows, :].T[0:32].astype(BF16), query, preferred_element_type=F32)
        dvalues = dvalues + jnp.dot(prob_ctx[rows, :].T[0:32].astype(BF16), grad, preferred_element_type=F32)
        return dkeys, dvalues

    zero = jnp.zeros((32, C), F32)
    dkeys, dvalues = lax.fori_loop(0, pixels // block, finish, (zero, zero))
    for s in range(4):
        own = (row32 // 4) == (2 * s + lane32 // HEAD)
        for position, source in enumerate((dkeys, dvalues)):
            kept = jnp.where(own, source[:, s * LANES : (s + 1) * LANES], 0.0)
            eight = jnp.sum(kept.reshape(4, 8, LANES), axis=0)
            folded = eight + pltpu.roll(eight, 4, axis=0)
            dctx[s, position * CTX : (position + 1) * CTX, :] = folded[0:CTX]


def norm_back_strips(pixels, strip, read_normed, read_grad, gains, inverses, write):
    count = pixels * (C // GROUPS)

    def terms(start):
        found = []
        for b in range(4):
            grad = read_grad(b, start)
            found += [grad, grad * read_normed(b, start)]
        return found

    sums = sum_strips(pixels, strip, 8, terms)
    bias_sums = [column_sum(sums[2 * b]) for b in range(4)]
    gain_sums = [column_sum(sums[2 * b + 1]) for b in range(4)]
    firsts = [
        group_sum(jnp.broadcast_to(bias_sums[b] * gains[b], (8, LANES)) * (1.0 / 8)) * (1.0 / count)
        for b in range(4)
    ]
    seconds = [
        group_sum(jnp.broadcast_to(gain_sums[b] * gains[b], (8, LANES)) * (1.0 / 8)) * (1.0 / count)
        for b in range(4)
    ]

    def body(index, carry):
        start = pl.multiple_of(index * strip, strip)
        for b in range(4):
            normed = read_normed(b, start)
            grad = read_grad(b, start) * gains[b]
            write(b, start, inverses[b] * (grad - firsts[b] - normed * seconds[b]))
        return carry

    lax.fori_loop(0, pixels // strip, body, 0)
    return gain_sums, bias_sums


def kernel_back_attention(
    meta, dqkv, cot, middle, pack, dctx, p0, p1, p2, p3,
    dmiddle, field, sums, d0, d1, d2, d3, qkv_weight, dattn, sems,
):
    pixels = cot.shape[1]
    me = meta[0]
    qkv_copies = fetch((p0, p1, p2, p3), qkv_weight, me, sems, 0)
    strip = 128
    clear_padding(field, pixels)
    means, inverses = norm_rows(pixels, strip, lambda b, start: middle[b, pl.ds(start, strip), :])
    wait_all(qkv_copies)

    def back(index, carry):
        start = pl.multiple_of(index * 512, 512)
        left = jnp.concatenate([dqkv[s, pl.ds(start, 512), :] for s in range(4)], axis=1)
        right = jnp.concatenate([qkv_weight[s, kind] for s in range(4) for kind in range(3)], axis=1)
        tile = lax.dot_general(left, right, (((1,), (1,)), ((), ())), preferred_element_type=F32)
        for b in range(4):
            dattn[b, pl.ds(start, 512), :] = tile[:, b * LANES : (b + 1) * LANES]
        return carry

    lax.fori_loop(0, pixels // 512, back, 0)
    gains = [pack[b, E_G3 : E_G3 + 1, :] for b in range(4)]

    def read_normed(b, start):
        return (middle[b, pl.ds(start, strip), :] - means[b]) * inverses[b]

    def write(b, start, value):
        total = cot[b, pl.ds(start, strip), :].astype(F32) + value
        dmiddle[b, pl.ds(start, strip), :] = total
        store_shifted(field, b, start, total.astype(BF16).astype(F32))

    gain_sums, bias_sums = norm_back_strips(
        pixels, strip, read_normed, lambda b, start: dattn[b, pl.ds(start, strip), :], gains, inverses, write
    )
    branch = sum_strips(
        pixels,
        strip,
        4,
        lambda start: [
            field[1, b, pl.ds(pl.multiple_of(PAD + start, 32), strip), :].astype(F32) for b in range(4)
        ],
    )
    for b in range(4):
        sums[b] = jnp.zeros((S_ROWS, LANES), F32)
        sums[b, S_G3 : S_G3 + 1, :] = gain_sums[b]
        sums[b, S_B3 : S_B3 + 1, :] = bias_sums[b]
        sums[b, S_CB2 : S_CB2 + 1, :] = column_sum(branch[b])
        sums[b, S_KEY : S_KEY + 8, :] = dctx[b]
    for offset, target in enumerate((d0, d1, d2, d3)):
        target[...] = field[1, jnp.bitwise_xor(me, offset), PAD : PAD + pixels, :]


def kernel_attention_grad(meta, dqkv, mixed, attn_t, cot, keep, send, cot_t):
    pixels = cot.shape[1]
    me = meta[0]
    strip = 128

    def turn(index, carry):
        start = pl.multiple_of(index * strip, strip)
        for b in range(4):
            cot_t[b, :, pl.ds(start, strip)] = cot[b, pl.ds(start, strip), :].astype(F32).T.astype(BF16)
        return carry

    lax.fori_loop(0, pixels // strip, turn, 0)

    def weights(offset, carry):
        s = jnp.bitwise_xor(me, offset)
        place = offset // 2
        attn_all = attn_t[...].reshape(C, pixels)
        cot_all = cot_t[...].reshape(C, pixels)
        grad = jnp.dot(attn_all, dqkv[s], preferred_element_type=F32).astype(BF16)
        other = jnp.dot(cot_all, mixed[s], preferred_element_type=F32).astype(BF16)

        def put(target):
            for kind in range(3):
                target[place, kind] = grad[:, kind * LANES : (kind + 1) * LANES]
            target[place, 3] = other

        @pl.when(offset % 2 == 0)
        def _():
            put(keep)

        @pl.when(offset % 2 == 1)
        def _():
            put(send)

        return carry

    lax.fori_loop(0, 4, weights, 0)


def weight_taps(half, sources, field, target):
    pixels = sources[0].shape[2]

    def body(index, carry):
        left = jnp.concatenate(
            [source[pl.ds(2 * half, 2)].reshape(2 * LANES, pixels) for source in sources], axis=1
        )
        columns = []
        for tap in (2 * index, jnp.minimum(2 * index + 1, 8)):
            start = pl.multiple_of((2 - tap // 3) * SIDE, 32)
            side = 2 - lax.rem(tap, 3)
            columns.append(
                jnp.concatenate([field[side, k, pl.ds(start, pixels), :] for k in range(4)], axis=0)
            )
        grad = jnp.dot(left, jnp.concatenate(columns, axis=1), preferred_element_type=F32)
        target[2 * index] = grad[:, :LANES].astype(target.dtype)

        @pl.when(index < 4)
        def _():
            target[2 * index + 1] = grad[:, LANES:].astype(target.dtype)

        return carry

    lax.fori_loop(0, 5, body, 0)


def kernel_weight_send(meta, u0, u1, u2, u3, d0, d1, d2, d3, send, field):
    pixels = u0.shape[2]
    clear_padding(field, pixels)
    strip = 128

    def spread(index, carry):
        start = pl.multiple_of(index * strip, strip)
        for k, source in enumerate((d0, d1, d2, d3)):
            store_shifted(field, k, start, source[pl.ds(start, strip), :].astype(F32))
        return carry

    lax.fori_loop(0, pixels // strip, spread, 0)
    weight_taps(1 - meta[3], (u0, u1, u2, u3), field, send)


def kernel_weight_own(meta, u0, u1, u2, u3, field, own):
    weight_taps(meta[3], (u0, u1, u2, u3), field, own)


def kernel_back_second(
    meta, grad_field, inner, pack, mod, sums_in, w0, w1, w2, w3, w4, w5, w6, w7,
    field, sums, d0, d1, d2, d3, weight, grad, sems,
):
    pixels = inner.shape[1]
    me = meta[0]
    strip = 128
    weight_copies = fetch_routed((w0, w1, w2, w3, w4, w5, w6, w7), weight, me, meta[2], sems, 0)
    clear_padding(field, pixels)
    means, inverses = norm_rows(pixels, strip, lambda b, start: inner[b, pl.ds(start, strip), :])
    wait_all(weight_copies)

    def write_grad(start, half, tile):
        for b in range(2):
            grad[2 * half + b, pl.ds(start, tile.shape[0]), :] = tile[:, b * LANES : (b + 1) * LANES]

    conv_back_tiles(grad_field, weight, pixels, 512, write_grad)
    gains = [pack[b, E_G2 : E_G2 + 1, :] for b in range(4)]

    def read_normed(b, start):
        return (inner[b, pl.ds(start, strip), :] - means[b]) * inverses[b]

    def slope(index, carry):
        start = pl.multiple_of(index * strip, strip)
        found = []
        for b in range(4):
            bias = pack[b, E_B2 : E_B2 + 1, :]
            scale = mod[b, M_SCALE : M_SCALE + 1, :]
            shift = mod[b, M_SHIFT : M_SHIFT + 1, :]
            shaped = read_normed(b, start) * gains[b] + bias
            modulated = shaped * (1.0 + scale) + shift
            dmod = silu_slope(modulated, grad[b, pl.ds(start, strip), :])
            grad[b, pl.ds(start, strip), :] = dmod * (1.0 + scale)
            found += [dmod * shaped, dmod]
        return tuple(old + fold(new) for old, new in zip(carry, found))

    zero = tuple(jnp.zeros((8, LANES), F32) for _ in range(8))
    modulation = lax.fori_loop(0, pixels // strip, slope, zero)

    def write(b, start, value):
        store_shifted(field, b, start, value)

    gain_sums, bias_sums = norm_back_strips(
        pixels, strip, read_normed, lambda b, start: grad[b, pl.ds(start, strip), :], gains, inverses, write
    )
    for b in range(4):
        sums[b] = sums_in[b]
        sums[b, S_G2 : S_G2 + 1, :] = gain_sums[b]
        sums[b, S_B2 : S_B2 + 1, :] = bias_sums[b]
        sums[b, S_SCALE : S_SCALE + 1, :] = column_sum(modulation[2 * b])
        sums[b, S_SHIFT : S_SHIFT + 1, :] = column_sum(modulation[2 * b + 1])
    for offset, target in enumerate((d0, d1, d2, d3)):
        target[...] = field[1, jnp.bitwise_xor(me, offset), PAD : PAD + pixels, :]


def kernel_back_conv(meta, grad_field, w0, w1, w2, w3, w4, w5, w6, w7, grad, weight, sems):
    pixels = grad.shape[1]
    wait_all(fetch_routed((w0, w1, w2, w3, w4, w5, w6, w7), weight, meta[0], meta[2], sems, 0))

    def write_grad(start, half, tile):
        for b in range(2):
            grad[2 * half + b, pl.ds(start, tile.shape[0]), :] = tile[:, b * LANES : (b + 1) * LANES]

    conv_back_tiles(grad_field, weight, pixels, 512, write_grad)


def kernel_back_first(
    meta, grad_in, image, pack, dmiddle, sums_in, g0, g1, g2, grad, sums,
):
    pixels = image.shape[1]
    me = meta[0]
    strip = 128

    def read(b, start):
        return image[b, pl.ds(start, strip), :].astype(F32)

    means, inverses = norm_rows(pixels, strip, read)
    gains = [pack[b, E_G1 : E_G1 + 1, :] for b in range(4)]

    def read_normed(b, start):
        return (read(b, start) - means[b]) * inverses[b]

    def slope(index, carry):
        start = pl.multiple_of(index * strip, strip)
        for b in range(4):
            before = read_normed(b, start) * gains[b] + pack[b, E_B1 : E_B1 + 1, :]
            grad[b, pl.ds(start, strip), :] = silu_slope(before, grad_in[b, pl.ds(start, strip), :])
        return carry

    lax.fori_loop(0, pixels // strip, slope, 0)

    def write(b, start, value):
        grad[b, pl.ds(start, strip), :] = dmiddle[b, pl.ds(start, strip), :] + value

    gain_sums, bias_sums = norm_back_strips(
        pixels, strip, read_normed, lambda b, start: grad[b, pl.ds(start, strip), :], gains, inverses, write
    )
    for b in range(4):
        sums[b] = sums_in[b]
        sums[b, S_G1 : S_G1 + 1, :] = gain_sums[b]
        sums[b, S_B1 : S_B1 + 1, :] = bias_sums[b]
    for offset, target in enumerate((g0, g1, g2.at[0], g2.at[1])):
        other = jnp.bitwise_xor(me, offset)
        target[0:pixels, :] = grad[other].astype(BF16)
        target[pixels : pixels + S_ROWS, :] = sums[other].astype(BF16)


def kernel_scale(factors0, factors1, scale):
    total = jnp.zeros((1, LANES), F32)
    for factors in (factors0, factors1):
        for g in range(factors.shape[0]):
            total = total + factors[g, 0].astype(F32)[1:2, 0:LANES]
    scale[...] = jnp.broadcast_to(1.0 / total, (8, LANES))


def kernel_factor_grads(meta, scale, factors0, factors1, small0, small1, embed, context, vectors):
    me = meta[0]
    groups = factors0.shape[0]
    inverse = scale[0:1, :]
    total = jnp.zeros((S_ROWS, LANES), F32)
    for small in (small0, small1):
        for g in range(4 * groups):
            total = total + small[g].astype(F32)
    vectors[...] = total * inverse
    over_rows = (((0,), (0,)), ((), ()))
    conditions, tokens, scales, shifts, keys, values = [], [], [], [], [], []
    for factors, small in ((factors0, small0), (factors1, small1)):
        for g in range(groups):
            for k in range(4):
                rows = factors[g, jnp.bitwise_xor(me, k)].astype(F32)
                term = small[4 * g + k].astype(F32)
                conditions.append(rows[0:1])
                tokens.append(rows[CTX : 2 * CTX])
                scales.append(term[S_SCALE : S_SCALE + 1])
                shifts.append(term[S_SHIFT : S_SHIFT + 1])
                keys.append(term[S_KEY : S_KEY + CTX])
                values.append(term[S_VALUE : S_VALUE + CTX])
    for lefts, pairs, target in (
        (conditions, (scales, shifts), embed),
        (tokens, (keys, values), context),
    ):
        left = jnp.concatenate(lefts, axis=0).astype(BF16)
        right = jnp.concatenate(
            [jnp.concatenate(parts, axis=0).astype(BF16) for parts in pairs], axis=1
        )
        grad = lax.dot_general(left, right, over_rows, preferred_element_type=F32)
        for place in range(2):
            target[:, place, :] = grad[:, place * LANES : (place + 1) * LANES] * inverse


def kernel_stack(*refs):
    whole = refs[-1]
    base = 0
    for ref in refs[:-1]:
        count = ref.shape[0]
        whole[base : base + count] = ref[...]
        base += count


def stack(parts):
    shape = (sum(part.shape[0] for part in parts),) + parts[0].shape[1:]
    return call(
        kernel_stack, "stack", struct(shape, parts[0].dtype), [vmem()] * len(parts), [], limit=12
    )(*parts)


def kernel_slots(meta, own, near, far, across, whole, sems):
    rows = pl.ds(0, whole.shape[1])
    sources = (own.at[rows], near.at[rows], far.at[0, rows], across.at[1, rows])
    wait_all(fetch(sources, whole, meta[0], sems, 0))


def kernel_cut(source, first, second):
    rows = first.shape[0]
    first[...] = source[0:rows]
    second[...] = source[rows : 2 * rows]


def cut(source):
    rows, lanes = source.shape
    return call(
        kernel_cut, "cut", [struct((rows // 2, lanes), BF16)] * 2, [vmem()], [], limit=8
    )(source)


def kernel_small_stack(own, near, far, across, whole):
    rows = pl.ds(own.shape[0] - S_ROWS, S_ROWS)
    whole[0] = own[rows, :]
    whole[1] = near[rows, :]
    whole[2] = far[0, rows, :]
    whole[3] = across[1, rows, :]


def kernel_split(counts, width, digit, meta, *refs):
    parts = refs[sum(counts) :]
    rows = parts[0].shape[1]
    for offset, part in enumerate(parts):
        start = pl.multiple_of(jnp.bitwise_xor(meta[digit], offset) * rows, rows)
        position, base = 0, 0
        for count in counts:
            terms = refs[position : position + count]
            terms = [term.at[0] if len(term.shape) == 4 else term for term in terms]
            total = terms[0][:, pl.ds(start, rows), :].astype(F32)
            for term in terms[1:]:
                total = total + term[:, pl.ds(start, rows), :].astype(F32)
            part[base : base + total.shape[0]] = total.astype(part.dtype)
            position += count
            base += total.shape[0]


def split_sum(groups, width, digit, meta):
    blocks = sum(terms[-1].shape[0] for terms in groups)
    rows = groups[0][-1].shape[1]
    flat = [term for terms in groups for term in terms]
    shape = (blocks, rows // width, LANES)
    return call(
        functools.partial(kernel_split, tuple(len(terms) for terms in groups), width, digit),
        "split_sum",
        [struct(shape, F32)] + [struct(shape, BF16)] * (width - 1),
        [smem()] + [vmem()] * len(flat),
        [],
        limit=12,
    )(meta, *flat)


def kernel_far(mine, got, own, far):
    blocks = own.shape[0]
    own[...] = mine[0:blocks] + got[0:blocks].astype(F32)
    far[...] = (mine[blocks : 2 * blocks] + got[blocks : 2 * blocks].astype(F32)).astype(BF16)


def kernel_total(*refs):
    total = refs[0][...].astype(F32)
    for term in refs[1:-1]:
        total = total + term[...].astype(F32)
    refs[-1][...] = total.astype(BF16)


def total_sum(terms):
    return call(
        kernel_total, "total_sum", struct(terms[0].shape, BF16), [vmem()] * len(terms), [], limit=12
    )(*terms)


def kernel_join(digit, meta, *refs):
    parts, whole = refs[:-1], refs[-1]
    rows = parts[0].shape[1]
    for offset, part in enumerate(parts):
        start = pl.multiple_of(jnp.bitwise_xor(meta[digit], offset) * rows, rows)
        whole[:, pl.ds(start, rows), :] = part[...]


def join(parts, digit, meta):
    blocks, rows, _ = parts[0].shape
    return call(
        functools.partial(kernel_join, digit),
        "join",
        struct((blocks, rows * len(parts), LANES), BF16),
        [smem()] + [vmem()] * len(parts),
        [],
        limit=12,
    )(meta, *parts)


def kernel_last(digit, meta, scale, mine, other, conv, *more):
    rows = mine.shape[1]
    for offset, part in enumerate((mine, other)):
        start = pl.multiple_of(jnp.bitwise_xor(meta[digit], offset) * rows, rows)
        count = conv.shape[0]
        conv[:, pl.ds(start, rows), :] = part[0:count].astype(F32) * scale[0:1, :]
        for proj in more:
            proj[:, pl.ds(start, rows)] = (part[count].astype(F32) * scale[0:1, :]).T


def last_join(pair, digit, meta, scale, more=False):
    blocks, rows, _ = pair[0].shape
    shapes = [struct((3 if more else blocks, 2 * rows, LANES), F32)]
    if more:
        shapes.append(struct((LANES, 2 * rows), F32))
    return call(
        functools.partial(kernel_last, digit),
        "last_join",
        shapes,
        [smem()] + [vmem()] * 3,
        [],
        limit=12,
    )(meta, scale, *pair)


def swap(value, axis, offset):
    size = lax.axis_size(axis)
    return lax.ppermute(value, axis, [(i, i ^ offset) for i in range(size)])


def tie(*values):
    return lax.optimization_barrier(values)


def share(shard):
    near = swap(shard, "mp", 1)
    far = swap(shard, "mp", 2)
    return shard, near, far, swap(far, "mp", 1)


def exchange(pieces):
    return (pieces[0],) + tuple(swap(pieces[k], "mp", k) for k in range(1, 4))


def pick(stack, me):
    return [lax.dynamic_index_in_dim(stack, me ^ k, 0, keepdims=False) for k in range(4)]


def dp_levels(size):
    return [(1 << k, 2) for k in range(size.bit_length() - 1)]


def bits(size):
    return [1 << k for k in range(size.bit_length() - 1)]


def local(
    image_in,
    out_cotangent,
    timesteps,
    clip_embed,
    context_tokens,
    image_count,
    norm1_gain,
    norm1_bias,
    conv1_weight,
    embed_weight,
    norm2_gain,
    norm2_bias,
    conv2_weight,
    conv2_bias,
    norm3_gain,
    norm3_bias,
    qkv_weight,
    context_weight,
    proj_weight,
):
    slots, pixels, width = image_in.shape
    me = lax.axis_index("mp")
    group = lax.axis_index("dp")
    parity = (group ^ (group >> 1)) & 1
    levels = dp_levels(lax.axis_size("dp"))
    own_digits = [(group >> (low.bit_length() - 1)) & (wide - 1) for low, wide in levels]
    meta = jnp.stack(
        [me, (me < image_count[0]).astype(jnp.int32), parity] + own_digits
    ).astype(jnp.int32)
    digits = range(3, 3 + len(levels))
    steps = bits(lax.axis_size("dp"))

    conv1_weight, conv2_weight, image_in, out_cotangent, meta = tie(
        conv1_weight, conv2_weight, image_in, out_cotangent, meta
    )

    vectors = jnp.stack(
        [norm1_gain, norm1_bias, norm2_gain, norm2_bias, conv2_bias, norm3_gain, norm3_bias, norm3_bias]
    )
    conv1_shard = conv1_weight.reshape(9 * C, LANES)
    conv2_shard = conv2_weight.reshape(9 * C, LANES)
    qkv_shard = jnp.transpose(qkv_weight, (1, 0, 2))

    def half_of(shard):
        rows = shard.shape[0] // 2
        return lax.dynamic_slice_in_dim(shard, parity * rows, rows, axis=0)

    packs = share(vectors)
    half1 = swap(half_of(conv1_shard), "mp", 2)
    near1 = swap(conv1_shard, "mp", 1)
    slices, *packs = tie(image_in, *packs)
    images = exchange(pick(slices, me))

    half_width = EMB // 2
    frequency = jnp.exp(-math.log(10000.0) * jnp.arange(half_width, dtype=F32) / half_width)
    angles = timesteps.astype(F32)[:, None] * frequency[None, :]
    condition = jax.nn.silu(
        jnp.concatenate([jnp.cos(angles), jnp.sin(angles)], axis=1) + clip_embed.astype(F32)
    ).astype(BF16)
    scale_shift = jnp.dot(
        condition, embed_weight.reshape(EMB, 2 * LANES), preferred_element_type=F32
    ).reshape(slots, 2, LANES)
    doubled = jnp.concatenate([context_tokens, context_tokens], axis=1)
    context = jnp.dot(
        doubled.reshape(slots * 2 * CTX, EMB),
        context_weight.reshape(EMB, 2 * LANES),
        preferred_element_type=F32,
    ).astype(BF16).astype(F32).reshape(slots, 2 * CTX, 2, LANES)
    early = jnp.concatenate(
        [scale_shift, jnp.zeros((slots, 6, LANES), F32), context[:, :, 0], context[:, :, 1]], axis=1
    )
    count_rows = jnp.broadcast_to(image_count.astype(BF16)[:, None, None], (slots, CTX - 1, EMB))
    factors = jnp.concatenate([condition[:, None], count_rows, context_tokens], axis=1)[None]
    mods = pick(early, me)
    half2 = half_of(conv2_shard)

    def relayed(shard, near, half):
        by_x, by_z = cut(half)
        by_x = swap(by_x, "dp", 1)
        by_z = swap(by_z, "dp", 2)
        return (shard, near, half, by_x, by_z) + tuple(
            swap(part, "mp", 1) for part in (half, by_x, by_z)
        )

    cots = pick(out_cotangent, me)
    half1, near1, image_near, mods, half2, factors, cots = tie(
        half1, near1, images[1], mods, half2, factors, cots
    )
    conv1 = relayed(conv1_shard, near1, half1)
    far_images = images[2:]
    mods, *conv1 = tie(mods, *conv1)
    mods = exchange(mods)
    conv1, far_images, mods, half2 = tie(conv1, far_images, mods, half2)
    images = (images[0], image_near) + tuple(far_images)
    half2 = swap(half2, "mp", 2)
    qkv_far = swap(qkv_shard, "mp", 2)
    proj_far = swap(proj_weight, "mp", 2)
    near2 = swap(conv2_shard, "mp", 1)
    factors = [factors, swap(factors, "dp", 1)]

    block = struct((4, pixels, LANES), BF16)
    block32 = struct((4, pixels, LANES), F32)
    turned = struct((4, LANES, pixels), BF16)
    fields = struct((3, 4, pixels + 2 * PAD, LANES), BF16)
    piece = struct((pixels, LANES), BF16)
    pair_piece = struct((2, pixels, LANES), BF16)
    field_scratch = pltpu.VMEM((3, 4, pixels + 2 * PAD, LANES), BF16)
    conv_scratch = pltpu.VMEM((4, 9 * C, LANES), BF16)
    qkv_scratch = pltpu.VMEM((4, 3, C, LANES), BF16)
    grad_scratch = pltpu.VMEM((4, pixels, LANES), F32)
    conv_flops = 2 * pixels * 9 * C * C

    image, pack, first_t, inner = call(
        kernel_first,
        "first",
        [block, struct((4, E_ROWS, LANES), F32), turned, block32],
        [smem()] + [anywhere()] * 16,
        [field_scratch, conv_scratch, pltpu.SemaphoreType.DMA((16,))],
        conv_flops,
    )(meta, *images, *packs, *conv1)

    inner, half2, near2, factors = tie(inner, half2, near2, factors)
    factors = stack(factors)
    conv2 = relayed(conv2_shard, near2, half2)
    inner, qkv_far, *conv2 = tie(inner, qkv_far, *conv2)
    qkv_w = (qkv_shard, swap(qkv_shard, "mp", 1), qkv_far, swap(qkv_far, "mp", 1))
    inner, *qkv_w = tie(inner, *qkv_w)
    cots = exchange(cots)
    factors = [factors, swap(factors, "dp", 2)]
    middle, second_t, attn_t, qkv, mod = call(
        kernel_second,
        "second",
        [block32, turned, turned, struct((4, pixels, 3 * LANES), BF16), struct((4, M_ROWS, LANES), F32)],
        [smem()] + [vmem()] * 3 + [anywhere()] * 16,
        [
            field_scratch,
            conv_scratch,
            qkv_scratch,
            pltpu.VMEM((4, pixels, LANES), BF16),
            pltpu.SemaphoreType.DMA((16,)),
        ],
        conv_flops + 6 * pixels * C * C,
    )(meta, inner, image, pack, *mods, *qkv_w, *conv2)
    ctx_scratch = pltpu.VMEM((pixels, LANES), F32)
    turned_scratch = pltpu.VMEM((LANES, pixels), F32)
    proj_w = (proj_weight, swap(proj_weight, "mp", 1), proj_far, swap(proj_far, "mp", 1))
    qkv, first_t, factors, cots, proj_w = tie(qkv, first_t, factors, cots, proj_w)
    factors = stack(factors)
    second_y = swap(second_t, "mp", 2)
    first_y = swap(first_t, "mp", 2)
    second_c = swap(second_t, "mp", 1)
    first_c = swap(first_t, "mp", 1)
    for low in steps[2:-1]:
        factors = stack([factors, swap(factors, "dp", low)])
    factors = (factors, swap(factors, "dp", steps[-1]))
    out_own, out_near, out_far, cot, mixed, dqkv, dctx = call(
        kernel_attention,
        "attention",
        [piece, piece, pair_piece]
        + [block, block, struct((4, pixels, 3 * LANES), BF16), struct((4, 2 * CTX, LANES), F32)],
        [smem()] + [vmem()] * 3 + [anywhere()] * 8,
        [
            pltpu.VMEM((4, LANES, C), BF16),
            pltpu.VMEM((4, pixels, LANES), BF16),
            ctx_scratch,
            ctx_scratch,
            ctx_scratch,
            ctx_scratch,
            grad_scratch,
            grad_scratch,
            turned_scratch,
            turned_scratch,
            pltpu.SemaphoreType.DMA((8,)),
        ],
        4 * 12 * pixels * pixels * C,
    )(meta, qkv, mod, middle, *cots, *proj_w)
    def weight_send(sources, gradients):
        return call(
            kernel_weight_send,
            "weight_send",
            [struct((9, C // 2, LANES), BF16), fields],
            [smem()] + [vmem()] * 8,
            [],
            limit=16,
        )(meta, *sources, *gradients)

    def weight_own(sources, field):
        return call(
            kernel_weight_own,
            "weight_own",
            struct((9, C // 2, LANES), F32),
            [smem()] + [vmem()] * 5,
            [],
            limit=16,
        )(meta, *sources, field)

    def down(terms, level):
        own, send = split_sum([terms], 2, digits[level], meta)
        return [own, swap(send, "dp", levels[level][0])]

    def across(value, level):
        return [value, swap(value, "dp", levels[level][0])]

    def inner_levels(terms):
        for level in range(3, len(levels)):
            terms = down(terms, level)
        value = total_sum(terms)
        for level in range(len(levels) - 1, 2, -1):
            value = join(across(value, level), digits[level], meta)
        return value

    att_keep, att_send = call(
        kernel_attention_grad,
        "attention_grad",
        [struct((2, 4, C, LANES), BF16)] * 2,
        [smem()] + [vmem()] * 4,
        [pltpu.VMEM((4, LANES, pixels), BF16)],
    )(meta, dqkv, mixed, attn_t, cot)
    dqkv, att_send, second_y, first_y, second_c, first_c, factors = tie(
        dqkv, att_send, second_y, first_y, second_c, first_c, factors
    )
    second_d = swap(second_y, "mp", 1)
    first_d = swap(first_y, "mp", 1)
    att = [att_keep.reshape(8, C, LANES), swap(att_send, "mp", 1).reshape(8, C, LANES)]
    dmiddle, field2, sums, *gradients2 = call(
        kernel_back_attention,
        "back_attention",
        [block32, fields, struct((4, S_ROWS, LANES), F32)] + [piece] * 4,
        [smem()] + [vmem()] * 5 + [anywhere()] * 4,
        [qkv_scratch, grad_scratch, pltpu.SemaphoreType.DMA((4,))],
    )(meta, dqkv, cot, middle, pack, dctx, *qkv_w)
    gradients2, second_d, first_d, att, field2 = tie(gradients2, second_d, first_d, att, field2)
    seconds = (second_t, second_c, second_y, second_d)
    firsts = (first_t, first_c, first_y, first_d)
    gradients2 = exchange(gradients2)
    att = down(att, 0)
    field2, att[0] = tie(field2, att[0])
    field1, sums, *gradients1 = call(
        kernel_back_second,
        "back_second",
        [fields, struct((4, S_ROWS, LANES), F32)] + [piece] * 4,
        [smem()] + [vmem()] * 5 + [anywhere()] * 8,
        [conv_scratch, grad_scratch, pltpu.SemaphoreType.DMA((8,))],
        limit=17,
    )(meta, field2, inner, pack, mod, sums, *conv2)
    gradients1, gradients2, att = tie(gradients1, gradients2, att)
    gradients1 = exchange(gradients1)
    att = down(att, 1)
    gradients2, att[0] = tie(gradients2, att[0])
    send2, wide2 = weight_send(seconds, gradients2)
    got2 = swap(send2, "dp", 1)
    wide2, att = tie(wide2, att)
    att = down(att, 2)
    wide2, att[0] = tie(wide2, att[0])
    own2 = weight_own(seconds, wide2)
    own2, att, field1 = tie(own2, att, field1)
    for level in range(3, len(levels)):
        att = down(att, level)
    att_own, att_far = call(
        kernel_far,
        "att_far",
        [struct((4,) + att[0].shape[1:], F32), struct((4,) + att[0].shape[1:], BF16)],
        [vmem()] * 2,
        [],
        limit=12,
    )(*att)
    field1, att_own = tie(field1, att_own)
    att = [att_own, swap(att_far, "mp", 2)]
    grad_first = call(
        kernel_back_conv,
        "back_conv",
        block32,
        [smem()] + [vmem()] + [anywhere()] * 8,
        [conv_scratch, pltpu.SemaphoreType.DMA((8,))],
    )(meta, field1, *conv1)
    grad_first, gradients1, att = tie(grad_first, gradients1, att)
    att = total_sum(att)
    for level in range(len(levels) - 1, 2, -1):
        att = join(across(att, level), digits[level], meta)
    gradients1, att, out_far = tie(gradients1, att, out_far)
    att = across(att, 2)
    send1, wide1 = weight_send(firsts, gradients1)
    got1 = swap(send1, "dp", 1)
    out_far = swap(out_far, "mp", 2)
    wide1, got2, own2 = tie(wide1, got2, own2)
    terms2 = down([own2, got2], 1)
    wide1, terms2[0] = tie(wide1, terms2[0])
    own1 = weight_own(firsts, wide1)
    grad_first, own1, terms2, att = tie(grad_first, own1, terms2, att)
    terms2 = down(terms2, 2)
    att = across(join(att, digits[2], meta), 1)
    grad_first, terms2[0], att[0] = tie(grad_first, terms2[0], att[0])
    grad_own, grad_near, grad_far = call(
        kernel_back_first,
        "back_first",
        [
            struct((pixels + S_ROWS, LANES), BF16),
            struct((pixels + S_ROWS, LANES), BF16),
            struct((2, pixels + S_ROWS, LANES), BF16),
        ],
        [smem()] + [vmem()] * 5,
        [grad_scratch, pltpu.VMEM((4, S_ROWS, LANES), F32)],
    )(meta, grad_first, image, pack, dmiddle, sums)
    grad_far, terms2, got1, own1 = tie(grad_far, terms2, got1, own1)
    terms1 = down([own1, got1], 1)
    ends2 = across(inner_levels(terms2), 2)
    grad_far, ends2[0], terms1[0], att = tie(grad_far, ends2[0], terms1[0], att)
    att = across(join(att, digits[1], meta), 0)
    grad_far = swap(grad_far, "mp", 2)
    ends2, terms1, grad_near, out_far = tie(ends2, terms1, grad_near, out_far)
    terms1 = down(terms1, 2)
    ends2 = across(join(ends2, digits[2], meta), 1)
    scale = call(kernel_scale, "scale", struct((8, LANES), F32), [vmem()] * 2, [], limit=8)(*factors)
    ends2, terms1, scale, att = tie(ends2, terms1, scale, att)
    ends1 = across(inner_levels(terms1), 2)
    ends2 = across(join(ends2, digits[1], meta), 0)
    qkv_grad, proj_grad = last_join(att, digits[0], meta, scale, True)
    ends1, qkv_grad, grad_near = tie(ends1, qkv_grad, grad_near)
    ends1 = across(join(ends1, digits[2], meta), 1)
    ends1[0], grad_near, grad_far = tie(ends1[0], grad_near, grad_far)
    grad_near = swap(grad_near, "mp", 1)
    grad_across = swap(grad_far, "mp", 1)
    image_parts = (grad_own, grad_near, grad_far, grad_across)
    ends1 = across(join(ends1, digits[1], meta), 0)
    ends1[0], grad_across, grad_near, ends2 = tie(ends1[0], grad_across, grad_near, ends2)
    smalls = call(
        kernel_small_stack,
        "stack",
        struct((4, S_ROWS, LANES), BF16),
        [vmem()] * 4,
        [],
        limit=8,
    )(grad_own, grad_near, grad_far, grad_across)
    small_got = swap(smalls, "dp", 1)
    (conv2_grad,) = last_join(ends2, digits[0], meta, scale)
    small_got, conv2_grad = tie(small_got, conv2_grad)
    smalls = stack([smalls, small_got])
    for low in steps[1:-1]:
        smalls = stack([smalls, swap(smalls, "dp", low)])
    small_got = swap(smalls, "dp", steps[-1])
    smalls, out_far, out_near = tie(smalls, out_far, out_near)
    out_parts = (out_own, swap(out_near, "mp", 1), out_far, swap(out_far, "mp", 1))
    embed_grad, context_grad, vector_sums = call(
        kernel_factor_grads,
        "factor_grads",
        [
            struct((EMB, 2, LANES), F32),
            struct((EMB, 2, LANES), F32),
            struct((S_ROWS, LANES), F32),
        ],
        [smem()] + [vmem()] * 5,
        [],
        limit=12 if len(steps) < 4 else 56,
    )(meta, scale, *factors, smalls, small_got)

    def in_slots(parts):
        return pl.pallas_call(
            kernel_slots,
            name="slots",
            out_shape=struct((4, pixels, LANES), BF16),
            in_specs=[smem()] + [anywhere()] * 4,
            out_specs=vmem(),
            scratch_shapes=[pltpu.SemaphoreType.DMA((4,))],
            compiler_params=pltpu.CompilerParams(vmem_limit_bytes=8 * MIB),
        )(meta, *parts)

    block_out = in_slots(out_parts)
    image_grad = in_slots(image_parts)
    (conv1_grad,) = last_join(ends1, digits[0], meta, scale)
    return (
        block_out,
        image_grad,
        vector_sums[S_G1],
        vector_sums[S_B1],
        conv1_grad.reshape(3, 3, C, LANES),
        embed_grad,
        vector_sums[S_G2],
        vector_sums[S_B2],
        conv2_grad.reshape(3, 3, C, LANES),
        vector_sums[S_CB2],
        vector_sums[S_G3],
        vector_sums[S_B3],
        jnp.transpose(qkv_grad, (1, 0, 2)),
        context_grad,
        proj_grad,
    )


def solution(mesh):
    return jax.shard_map(
        local,
        mesh=mesh,
        in_specs=(
            P("dp", None, "mp"),
            P("dp", None, "mp"),
            P("dp"),
            P("dp", None),
            P("dp", None, None),
            P("dp"),
            P("mp"),
            P("mp"),
            P(None, None, None, "mp"),
            P(None, None, "mp"),
            P("mp"),
            P("mp"),
            P(None, None, None, "mp"),
            P("mp"),
            P("mp"),
            P("mp"),
            P(None, None, "mp"),
            P(None, None, "mp"),
            P("mp", None),
        ),
        out_specs=(
            P("dp", None, "mp"),
            P("dp", None, "mp"),
            P("mp"),
            P("mp"),
            P(None, None, None, "mp"),
            P(None, None, "mp"),
            P("mp"),
            P("mp"),
            P(None, None, None, "mp"),
            P("mp"),
            P("mp"),
            P("mp"),
            P(None, None, "mp"),
            P(None, None, "mp"),
            P("mp", None),
        ),
        check_vma=False,
    )
```

```python
import functools
import math

import jax
import jax.numpy as jnp
from jax import lax
from jax.experimental import pallas as pl
from jax.experimental.pallas import tpu as pltpu
from jax.sharding import PartitionSpec as P

C = 512
GROUPS = 32
HEAD = 64
EMB = 2048
CTX = 4
SIDE = 32
LANES = 128
PAD = SIDE
EPSILON = 1e-05
F32 = jnp.float32
BF16 = jnp.bfloat16
NEG = -1e30
QKV_ROW = 9 * C
PROJ_ROW = QKV_ROW + 3 * C

E_G1, E_B1, E_G2, E_B2, E_CB2, E_G3, E_B3, M_SCALE, M_SHIFT = range(9)
M_KEY, M_VALUE, E_ROWS = 16, 24, 32
S_G3, S_B3, S_CB2, S_G2, S_B2, S_SCALE, S_SHIFT = range(7)
S_KEY, S_VALUE, S_G1, S_B1, S_ROWS = 8, 12, 16, 17, 32
MIB = 1 << 20


def vmem():
    return pl.BlockSpec(memory_space=pltpu.VMEM)


def anywhere():
    return pl.BlockSpec(memory_space=pltpu.HBM)


def smem():
    return pl.BlockSpec(memory_space=pltpu.SMEM)


def struct(shape, dtype):
    return jax.ShapeDtypeStruct(shape, dtype)


def call(body, name, out_shape, in_specs, scratch, flops=0, limit=14):
    many = isinstance(out_shape, (list, tuple))
    return pl.pallas_call(
        body,
        name=name,
        out_shape=out_shape,
        in_specs=in_specs,
        out_specs=[vmem() for _ in out_shape] if many else vmem(),
        scratch_shapes=scratch,
        compiler_params=pltpu.CompilerParams(vmem_limit_bytes=limit * MIB),
        cost_estimate=pl.CostEstimate(flops=0, transcendentals=0, bytes_accessed=0),
    )


def fetch(sources, target, me, sems, first):
    copies = []
    for offset, source in enumerate(sources):
        copy = pltpu.make_async_copy(
            source, target.at[jnp.bitwise_xor(me, offset)], sems.at[first + offset]
        )
        copy.start()
        copies.append(copy)
    return copies


def fetch_routed(sources, target, me, parity, sems, first):
    quarter = target.shape[1] // 4
    copies = []
    for index, source in enumerate(sources):
        place = target.at[jnp.bitwise_xor(me, (0, 1, 2, 2, 2, 3, 3, 3)[index])]
        if index >= 2:
            kind = (index - 2) % 3
            rows = 2 * quarter if kind == 0 else quarter
            half = parity if kind == 0 else 1 - parity
            start = half * 2 * quarter + (quarter if kind == 2 else 0)
            place = place.at[pl.ds(pl.multiple_of(start, quarter), rows), :]
        copy = pltpu.make_async_copy(source, place, sems.at[first + index])
        copy.start()
        copies.append(copy)
    return copies


def wait_all(copies):
    for copy in copies:
        copy.wait()


def fold(values):
    rows = values.shape[0]
    return jnp.sum(values.reshape(rows // 8, 8, values.shape[1]), axis=0)


def group_sum(rows8):
    lane = lax.broadcasted_iota(jnp.int32, rows8.shape, 1)
    total = jnp.broadcast_to(jnp.sum(rows8, axis=0, keepdims=True), rows8.shape)
    for step in (1, 2, 4, 8):
        up = pltpu.roll(total, step, axis=1)
        down = pltpu.roll(total, LANES - step, axis=1)
        total = total + jnp.where((lane & step) != 0, up, down)
    return total[0:1]


def column_sum(rows8):
    return jnp.sum(rows8, axis=0, keepdims=True)


def sum_strips(pixels, strip, width, function):
    zero = tuple(jnp.zeros((8, LANES), F32) for _ in range(width))

    def body(index, carry):
        start = pl.multiple_of(index * strip, strip)
        return tuple(old + fold(new) for old, new in zip(carry, function(start)))

    return lax.fori_loop(0, pixels // strip, body, zero)


def norm_rows(pixels, strip, read):
    count = pixels * (C // GROUPS)
    sums = sum_strips(pixels, strip, 4, lambda start: [read(b, start) for b in range(4)])
    means = [group_sum(s) * (1.0 / count) for s in sums]
    squares = sum_strips(
        pixels,
        strip,
        4,
        lambda start: [jnp.square(read(b, start) - means[b]) for b in range(4)],
    )
    inverses = [lax.rsqrt(group_sum(s) * (1.0 / count) + EPSILON) for s in squares]
    return means, inverses


def shifted(values):
    rows = values.shape[0]
    column = lax.broadcasted_iota(jnp.int32, values.shape, 0) & (SIDE - 1)
    left = jnp.where(column == 0, 0.0, pltpu.roll(values, 1, axis=0))
    right = jnp.where(column == SIDE - 1, 0.0, pltpu.roll(values, rows - 1, axis=0))
    return left, values, right


def store_shifted(target, block, start, values):
    rows = values.shape[0]
    for position, part in enumerate(shifted(values)):
        target[position, block, pl.ds(pl.multiple_of(PAD + start, 32), rows), :] = part.astype(BF16)


def clear_padding(target, pixels):
    zero = jnp.zeros((PAD, LANES), BF16)
    for position in range(3):
        for block in range(4):
            target[position, block, 0:PAD, :] = zero
            target[position, block, PAD + pixels : PAD + pixels + PAD, :] = zero


def conv_tiles(field, weight, pixels, tile, write):
    def body(index, carry):
        start = pl.multiple_of(index * tile, tile)
        left = jnp.concatenate(
            [
                field[b, block, pl.ds(pl.multiple_of(start + a * SIDE, 32), tile), :]
                for a in range(3)
                for b in range(3)
                for block in range(4)
            ],
            axis=1,
        )
        right = jnp.concatenate([weight[s, 0 : 9 * C, :] for s in range(4)], axis=1)
        write(start, jnp.dot(left, right, preferred_element_type=F32))
        return carry

    lax.fori_loop(0, pixels // tile, body, 0)


def conv_back_tiles(field, weight, pixels, tile, write):
    def body(index, carry):
        start = pl.multiple_of((index // 2) * tile, tile)
        half = index % 2
        left = jnp.concatenate(
            [
                field[2 - b, block, pl.ds(pl.multiple_of(start + (2 - a) * SIDE, 32), tile), :]
                for a in range(3)
                for b in range(3)
                for block in range(4)
            ],
            axis=1,
        )
        right = jnp.concatenate(
            [
                weight[block, pl.ds(pl.multiple_of((3 * a + b) * C + half * 256, 256), 256), :]
                for a in range(3)
                for b in range(3)
                for block in range(4)
            ],
            axis=1,
        )
        write(
            start,
            half,
            lax.dot_general(left, right, (((1,), (1,)), ((), ())), preferred_element_type=F32),
        )
        return carry

    lax.fori_loop(0, 2 * (pixels // tile), body, 0)


def silu_slope(before, grad_out):
    gate = jax.nn.sigmoid(before)
    return grad_out * gate * (1.0 + before * (1.0 - gate))


def kernel_early(meta, scale_shift, context, v0, v1, v2, v3, v4, v5, v6, own, near, far):
    for offset, target in enumerate((own, near, far.at[0], far.at[1])):
        slot = jnp.bitwise_xor(meta[0], offset)
        target[...] = jnp.zeros((E_ROWS, LANES), F32)
        for row, vector in enumerate((v0, v1, v2, v3, v4, v5, v6)):
            target[row : row + 1, :] = vector[...]
        scales = scale_shift[slot]
        target[M_SCALE : M_SCALE + 1, :] = scales[:, :LANES]
        target[M_SHIFT : M_SHIFT + 1, :] = scales[:, LANES:]
        tokens = context[slot]
        target[M_KEY : M_KEY + 8, :] = tokens[:, :LANES]
        target[M_VALUE : M_VALUE + 8, :] = tokens[:, LANES:]


def kernel_first(
    meta, i0, i1, i2, i3, e0, e1, e2, e3, w0, w1, w2, w3, w4, w5, w6, w7,
    image, pack, first_t, inner, second_t, second, field, weight, sems,
):
    pixels = image.shape[1]
    me = meta[0]
    image_copies = fetch((i0, i1, i2.at[0], i3.at[1]), image, me, sems, 0)
    pack_copies = fetch((e0, e1, e2.at[0], e3.at[1]), pack, me, sems, 4)
    weight_copies = fetch_routed((w0, w1, w2, w3, w4, w5, w6, w7), weight, me, meta[2], sems, 8)
    clear_padding(field, pixels)
    clear_padding(second, pixels)
    wait_all(image_copies)
    wait_all(pack_copies)
    strip = 128

    def read(block, start):
        return image[block, pl.ds(start, strip), :].astype(F32)

    means, inverses = norm_rows(pixels, strip, read)

    def normalise(index, carry):
        start = pl.multiple_of(index * strip, strip)
        for b in range(4):
            gain = pack[b, E_G1 : E_G1 + 1, :]
            bias = pack[b, E_B1 : E_B1 + 1, :]
            before = (read(b, start) - means[b]) * inverses[b] * gain + bias
            after = before * jax.nn.sigmoid(before)
            store_shifted(field, b, start, after)
            first_t[b, :, pl.ds(start, strip)] = after.T.astype(BF16)
        return carry

    lax.fori_loop(0, pixels // strip, normalise, 0)
    wait_all(weight_copies)

    def write(start, tile):
        for b in range(4):
            inner[b, pl.ds(start, tile.shape[0]), :] = tile[:, b * LANES : (b + 1) * LANES]

    conv_tiles(field, weight, pixels, 512, write)
    means2, inverses2 = norm_rows(pixels, strip, lambda b, start: inner[b, pl.ds(start, strip), :])

    def modulate(index, carry):
        start = pl.multiple_of(index * strip, strip)
        for b in range(4):
            gain = pack[b, E_G2 : E_G2 + 1, :]
            bias = pack[b, E_B2 : E_B2 + 1, :]
            scale = pack[b, M_SCALE : M_SCALE + 1, :]
            shift = pack[b, M_SHIFT : M_SHIFT + 1, :]
            normed = (inner[b, pl.ds(start, strip), :] - means2[b]) * inverses2[b]
            modulated = (normed * gain + bias) * (1.0 + scale) + shift
            after = modulated * jax.nn.sigmoid(modulated)
            store_shifted(second, b, start, after)
            second_t[b, :, pl.ds(start, strip)] = after.T.astype(BF16)
        return carry

    lax.fori_loop(0, pixels // strip, modulate, 0)


def kernel_second(
    meta, second, image, pack, w0, w1, w2, w3, w4, w5, w6, w7,
    middle, attn_t, qkv, qkv_weight, proj_weight, weight, attn, sems,
):
    pixels = image.shape[1]
    me = meta[0]
    wait_all(fetch_routed((w0, w1, w2, w3, w4, w5, w6, w7), weight, me, meta[2], sems, 0))
    strip = 128

    def write(start, tile):
        rows = tile.shape[0]
        for b in range(4):
            branch = tile[:, b * LANES : (b + 1) * LANES] + pack[b, E_CB2 : E_CB2 + 1, :]
            middle[b, pl.ds(start, rows), :] = image[b, pl.ds(start, rows), :].astype(F32) + branch

    conv_tiles(second, weight, pixels, 512, write)
    means, inverses = norm_rows(pixels, strip, lambda b, start: middle[b, pl.ds(start, strip), :])

    def normalise(index, carry):
        start = pl.multiple_of(index * strip, strip)
        for b in range(4):
            normed = (middle[b, pl.ds(start, strip), :] - means[b]) * inverses[b]
            value = normed * pack[b, E_G3 : E_G3 + 1, :] + pack[b, E_B3 : E_B3 + 1, :]
            attn[b, pl.ds(start, strip), :] = value.astype(BF16)
            attn_t[b, :, pl.ds(start, strip)] = value.T.astype(BF16)
        return carry

    lax.fori_loop(0, pixels // strip, normalise, 0)
    for s in range(4):
        qkv_weight[s] = weight[s, QKV_ROW:PROJ_ROW, :]
        proj_weight[s] = weight[s, PROJ_ROW : PROJ_ROW + C, :]

    def project(index, carry):
        s = index // 2
        start = pl.multiple_of((index % 2) * 512, 512)
        left = jnp.concatenate([attn[b, pl.ds(start, 512), :] for b in range(4)], axis=1)
        right = jnp.concatenate(
            [weight[s, QKV_ROW + kind * C : QKV_ROW + (kind + 1) * C, :] for kind in range(3)], axis=1
        )
        qkv[s, pl.ds(start, 512), :] = jnp.dot(left, right, preferred_element_type=F32).astype(BF16)
        return carry

    lax.fori_loop(0, 4 * (pixels // 512), project, 0)


def kernel_attention(
    meta, qkv, pack, middle, weight, c0, c1, c2, c3,
    o0, o1, o2, cot, mixed, dqkv, dctx,
    grad_mixed, score_ctx, grad_ctx_prob, prob_ctx, dscore_ctx, out_pix, dquery, dkey_t, dvalue_t, sems,
):
    pixels = qkv.shape[1]
    me = meta[0]
    alive = meta[1].astype(F32)
    cot_copies = fetch((c0, c1, c2, c3), cot, me, sems, 0)
    scale = 1.0 / math.sqrt(HEAD)
    block = 256

    row32 = lax.broadcasted_iota(jnp.int32, (32, LANES), 0)
    lane32 = lax.broadcasted_iota(jnp.int32, (32, LANES), 1)

    def diagonal(kind):
        found = []
        for s in range(4):
            rows8 = pack[s, kind : kind + 8, :]
            tiled = jnp.concatenate([rows8] * 4, axis=0)
            own = (row32 // 4) == (2 * s + lane32 // HEAD)
            kept = jnp.where(own, tiled, 0.0)
            found.append(jnp.concatenate([kept, jnp.zeros((96, LANES), F32)], axis=0).astype(BF16))
        return jnp.concatenate(found, axis=1)

    keys_ctx = diagonal(M_KEY)
    values_ctx = diagonal(M_VALUE)
    wait_all(cot_copies)

    def projection():
        return jnp.concatenate(
            [
                jnp.concatenate([weight[s, o * LANES : (o + 1) * LANES, :] for o in range(4)], axis=1)
                for s in range(4)
            ],
            axis=0,
        )

    def prepare(index, carry):
        start = pl.multiple_of(index * block, block)
        rows = pl.ds(start, block)
        for s in range(4):
            cot[s, rows, :] = (cot[s, rows, :].astype(F32) * alive).astype(BF16)
        all_cot = jnp.concatenate([cot[s, rows, :] for s in range(4)], axis=1)
        all_weight = projection()
        grad = lax.dot_general(
            all_cot, all_weight, (((1,), (1,)), ((), ())), preferred_element_type=F32
        ).astype(BF16)
        for s in range(4):
            grad_mixed[s, rows, :] = grad[:, s * LANES : (s + 1) * LANES]
        query = jnp.concatenate([qkv[s, rows, 0:LANES] for s in range(4)], axis=1)
        score_ctx[rows, :] = lax.dot_general(
            query, keys_ctx, (((1,), (1,)), ((), ())), preferred_element_type=F32
        )
        grad_ctx_prob[rows, :] = lax.dot_general(
            grad, values_ctx, (((1,), (1,)), ((), ())), preferred_element_type=F32
        )
        prob_ctx[rows, :] = jnp.zeros((block, LANES), F32)
        dscore_ctx[rows, :] = jnp.zeros((block, LANES), F32)
        return carry

    lax.fori_loop(0, pixels // block, prepare, 0)
    lane = lax.broadcasted_iota(jnp.int32, (block, LANES), 1)
    low = lane < HEAD
    ones = jnp.ones((pixels, LANES), BF16)
    blocks = pixels // block

    def attend(index, carry):
        s = index // blocks
        part = index % blocks
        rows = pl.ds(pl.multiple_of(part * block, block), block)

        @pl.when(part == 0)
        def _():
            dkey_t[...] = jnp.zeros((LANES, pixels), F32)
            dvalue_t[...] = jnp.zeros((LANES, pixels), F32)

        query = qkv[s, rows, 0:LANES]
        key = qkv[s, :, LANES : 2 * LANES]
        value = qkv[s, :, 2 * LANES : 3 * LANES]
        value_ones = jnp.concatenate([value, ones], axis=1)
        grad = grad_mixed[s, rows, :]
        ctx_scores = score_ctx[rows, :]
        ctx_grads = grad_ctx_prob[rows, :]
        exps, outs, inverses, ctx_exps, owns = [], [], [], [], []
        for h in range(2):
            mine = low if h == 0 else jnp.logical_not(low)
            own = lane // CTX == 2 * s + h
            score = lax.dot_general(
                jnp.where(mine, query, jnp.zeros_like(query)),
                key,
                (((1,), (1,)), ((), ())),
                preferred_element_type=F32,
            )
            top = jnp.maximum(
                jnp.max(score, axis=1, keepdims=True),
                jnp.max(jnp.where(own, ctx_scores, NEG), axis=1, keepdims=True),
            )
            exp = jnp.exp((score - top) * scale).astype(BF16)
            ctx_exp = jnp.where(own, jnp.exp((ctx_scores - top) * scale), 0.0)
            out = jnp.dot(exp, value_ones, preferred_element_type=F32)
            total = out[:, LANES:] + jnp.sum(ctx_exp, axis=1, keepdims=True)
            inverse = 1.0 / total
            exps.append(exp)
            outs.append(out[:, :LANES] * inverse)
            inverses.append(inverse)
            ctx_exps.append(ctx_exp)
            owns.append(own)
        out_pair = jnp.where(low, outs[0], outs[1])
        out_pix[s, rows, :] = out_pair
        inverse_pair = jnp.where(low, inverses[0], inverses[1])
        scaled = (grad.astype(F32) * (inverse_pair * scale)).astype(BF16)
        product = out_pair * scaled.astype(F32)
        query_t = query.astype(F32).T.astype(BF16)
        scaled_t = scaled.astype(F32).T.astype(BF16)
        prob_keep = prob_ctx[rows, :]
        dscore_keep = dscore_ctx[rows, :]
        dqs = []
        for h in range(2):
            mine = low if h == 0 else jnp.logical_not(low)
            own = owns[h]
            ctx_prob = ctx_exps[h] * inverses[h]
            ctx_grad = ctx_grads * (inverses[h] * scale)
            dot = jnp.sum(
                jnp.where(mine, product, 0.0) + ctx_prob * jnp.where(own, ctx_grad, 0.0),
                axis=1,
                keepdims=True,
            )
            weight_grad = lax.dot_general(
                jnp.where(mine, scaled, jnp.zeros_like(scaled)),
                value,
                (((1,), (1,)), ((), ())),
                preferred_element_type=F32,
            )
            dscore = (exps[h].astype(F32) * (weight_grad - dot)).astype(BF16)
            prob_keep = jnp.where(own, ctx_prob, prob_keep)
            dscore_keep = jnp.where(own, ctx_exps[h] * (ctx_grad - dot), dscore_keep)
            dqs.append(jnp.dot(dscore, key, preferred_element_type=F32))
            half = slice(h * HEAD, (h + 1) * HEAD)
            dkey_t[half, :] += jnp.dot(query_t[half], dscore, preferred_element_type=F32)
            dvalue_t[half, :] += jnp.dot(scaled_t[half], exps[h], preferred_element_type=F32)
        prob_ctx[rows, :] = prob_keep
        dscore_ctx[rows, :] = dscore_keep
        dquery[s, rows, :] = jnp.where(low, dqs[0], dqs[1])

        @pl.when(part == blocks - 1)
        def _():
            for piece in range(pixels // LANES):
                cut = slice(piece * LANES, (piece + 1) * LANES)
                dqkv[s, cut, LANES : 2 * LANES] = dkey_t[:, cut].T.astype(BF16)
                dqkv[s, cut, 2 * LANES : 3 * LANES] = (dvalue_t[:, cut] * (1.0 / scale)).T.astype(BF16)

        return carry

    lax.fori_loop(0, 4 * blocks, attend, 0)

    def finish(index, carry):
        dkeys, dvalues = carry
        start = pl.multiple_of(index * block, block)
        rows = pl.ds(start, block)
        prob = prob_ctx[rows, :].astype(BF16)
        dscore = dscore_ctx[rows, :].astype(BF16)
        out_ctx = jnp.dot(prob, values_ctx, preferred_element_type=F32)
        dquery_ctx = jnp.dot(dscore, keys_ctx, preferred_element_type=F32)
        parts = []
        for s in range(4):
            cut = slice(s * LANES, (s + 1) * LANES)
            both = (out_pix[s, rows, :] + out_ctx[:, cut]).astype(BF16)
            mixed[s, rows, :] = both
            parts.append(both)
            dqkv[s, rows, 0:LANES] = (dquery[s, rows, :] + dquery_ctx[:, cut]).astype(BF16)
        result = jnp.dot(
            jnp.concatenate(parts, axis=1), projection(), preferred_element_type=F32
        )
        for offset, target in enumerate((o0, o1, o2.at[0], o2.at[1])):
            other = jnp.bitwise_xor(me, offset)
            value = jnp.zeros((block, LANES), F32)
            for s in range(4):
                value = jnp.where(other == s, result[:, s * LANES : (s + 1) * LANES], value)
            target[rows, :] = ((middle[other, rows, :] + value) * alive).astype(BF16)
        query = jnp.concatenate([qkv[s, rows, 0:LANES] for s in range(4)], axis=1)
        grad = jnp.concatenate([grad_mixed[s, rows, :] for s in range(4)], axis=1)
        dkeys = dkeys + jnp.dot(dscore_ctx[rows, :].T[0:32].astype(BF16), query, preferred_element_type=F32)
        dvalues = dvalues + jnp.dot(prob_ctx[rows, :].T[0:32].astype(BF16), grad, preferred_element_type=F32)
        return dkeys, dvalues

    zero = jnp.zeros((32, C), F32)
    dkeys, dvalues = lax.fori_loop(0, pixels // block, finish, (zero, zero))
    for s in range(4):
        own = (row32 // 4) == (2 * s + lane32 // HEAD)
        for position, source in enumerate((dkeys, dvalues)):
            kept = jnp.where(own, source[:, s * LANES : (s + 1) * LANES], 0.0)
            eight = jnp.sum(kept.reshape(4, 8, LANES), axis=0)
            folded = eight + pltpu.roll(eight, 4, axis=0)
            dctx[s, position * CTX : (position + 1) * CTX, :] = folded[0:CTX]


def norm_back_strips(pixels, strip, read_normed, read_grad, gains, inverses, write):
    count = pixels * (C // GROUPS)

    def terms(start):
        found = []
        for b in range(4):
            grad = read_grad(b, start)
            found += [grad, grad * read_normed(b, start)]
        return found

    sums = sum_strips(pixels, strip, 8, terms)
    bias_sums = [column_sum(sums[2 * b]) for b in range(4)]
    gain_sums = [column_sum(sums[2 * b + 1]) for b in range(4)]
    firsts = [
        group_sum(jnp.broadcast_to(bias_sums[b] * gains[b], (8, LANES)) * (1.0 / 8)) * (1.0 / count)
        for b in range(4)
    ]
    seconds = [
        group_sum(jnp.broadcast_to(gain_sums[b] * gains[b], (8, LANES)) * (1.0 / 8)) * (1.0 / count)
        for b in range(4)
    ]

    def body(index, carry):
        start = pl.multiple_of(index * strip, strip)
        for b in range(4):
            normed = read_normed(b, start)
            grad = read_grad(b, start) * gains[b]
            write(b, start, inverses[b] * (grad - firsts[b] - normed * seconds[b]))
        return carry

    lax.fori_loop(0, pixels // strip, body, 0)
    return gain_sums, bias_sums


def kernel_back_attention(
    meta, dqkv, cot, middle, pack, dctx, qkv_weight,
    dmiddle, field, sums, d0, d1, d2, d3, dattn,
):
    pixels = cot.shape[1]
    me = meta[0]
    strip = 128
    clear_padding(field, pixels)
    means, inverses = norm_rows(pixels, strip, lambda b, start: middle[b, pl.ds(start, strip), :])

    def back(index, carry):
        start = pl.multiple_of(index * 512, 512)
        left = jnp.concatenate([dqkv[s, pl.ds(start, 512), :] for s in range(4)], axis=1)
        right = jnp.concatenate(
            [qkv_weight[s, kind * C : (kind + 1) * C, :] for s in range(4) for kind in range(3)], axis=1
        )
        tile = lax.dot_general(left, right, (((1,), (1,)), ((), ())), preferred_element_type=F32)
        for b in range(4):
            dattn[b, pl.ds(start, 512), :] = tile[:, b * LANES : (b + 1) * LANES]
        return carry

    lax.fori_loop(0, pixels // 512, back, 0)
    gains = [pack[b, E_G3 : E_G3 + 1, :] for b in range(4)]

    def read_normed(b, start):
        return (middle[b, pl.ds(start, strip), :] - means[b]) * inverses[b]

    def write(b, start, value):
        total = cot[b, pl.ds(start, strip), :].astype(F32) + value
        dmiddle[b, pl.ds(start, strip), :] = total
        store_shifted(field, b, start, total.astype(BF16).astype(F32))

    gain_sums, bias_sums = norm_back_strips(
        pixels, strip, read_normed, lambda b, start: dattn[b, pl.ds(start, strip), :], gains, inverses, write
    )
    branch = sum_strips(
        pixels,
        strip,
        4,
        lambda start: [
            field[1, b, pl.ds(pl.multiple_of(PAD + start, 32), strip), :].astype(F32) for b in range(4)
        ],
    )
    for b in range(4):
        sums[b] = jnp.zeros((S_ROWS, LANES), F32)
        sums[b, S_G3 : S_G3 + 1, :] = gain_sums[b]
        sums[b, S_B3 : S_B3 + 1, :] = bias_sums[b]
        sums[b, S_CB2 : S_CB2 + 1, :] = column_sum(branch[b])
        sums[b, S_KEY : S_KEY + 8, :] = dctx[b]
    for offset, target in enumerate((d0, d1, d2, d3)):
        target[...] = field[1, jnp.bitwise_xor(me, offset), PAD : PAD + pixels, :]


def kernel_attention_grad(meta, dqkv, mixed, attn_t, cot, keep, send, cot_t):
    pixels = cot.shape[1]
    me = meta[0]
    strip = 128

    def turn(index, carry):
        start = pl.multiple_of(index * strip, strip)
        for b in range(4):
            cot_t[b, :, pl.ds(start, strip)] = cot[b, pl.ds(start, strip), :].astype(F32).T.astype(BF16)
        return carry

    lax.fori_loop(0, pixels // strip, turn, 0)

    def weights(offset, carry):
        s = jnp.bitwise_xor(me, offset)
        place = offset // 2
        attn_all = attn_t[...].reshape(C, pixels)
        cot_all = cot_t[...].reshape(C, pixels)
        grad = jnp.dot(attn_all, dqkv[s], preferred_element_type=F32).astype(BF16)
        other = jnp.dot(cot_all, mixed[s], preferred_element_type=F32).astype(BF16)

        def put(target):
            for kind in range(3):
                target[place, kind] = grad[:, kind * LANES : (kind + 1) * LANES]
            target[place, 3] = other

        @pl.when(offset % 2 == 0)
        def _():
            put(keep)

        @pl.when(offset % 2 == 1)
        def _():
            put(send)

        return carry

    lax.fori_loop(0, 4, weights, 0)


def weight_taps(half, sources, field, target):
    pixels = sources[0].shape[2]

    def body(index, carry):
        left = jnp.concatenate(
            [source[pl.ds(2 * half, 2)].reshape(2 * LANES, pixels) for source in sources], axis=1
        )
        columns = []
        for tap in (2 * index, jnp.minimum(2 * index + 1, 8)):
            start = pl.multiple_of((2 - tap // 3) * SIDE, 32)
            side = 2 - lax.rem(tap, 3)
            columns.append(
                jnp.concatenate([field[side, k, pl.ds(start, pixels), :] for k in range(4)], axis=0)
            )
        grad = jnp.dot(left, jnp.concatenate(columns, axis=1), preferred_element_type=F32)
        target[2 * index] = grad[:, :LANES].astype(target.dtype)

        @pl.when(index < 4)
        def _():
            target[2 * index + 1] = grad[:, LANES:].astype(target.dtype)

        return carry

    lax.fori_loop(0, 5, body, 0)


def kernel_weight_send(meta, u0, u1, u2, u3, d0, d1, d2, d3, send, field):
    pixels = u0.shape[2]
    clear_padding(field, pixels)
    strip = 128

    def spread(index, carry):
        start = pl.multiple_of(index * strip, strip)
        for k, source in enumerate((d0, d1, d2, d3)):
            store_shifted(field, k, start, source[pl.ds(start, strip), :].astype(F32))
        return carry

    lax.fori_loop(0, pixels // strip, spread, 0)
    weight_taps(1 - meta[3], (u0, u1, u2, u3), field, send)


def kernel_weight_own(meta, u0, u1, u2, u3, field, own):
    weight_taps(meta[3], (u0, u1, u2, u3), field, own)


def kernel_back_second(
    meta, grad_field, inner, pack, sums_in, w0, w1, w2, w3, w4, w5, w6, w7,
    field, sums, d0, d1, d2, d3, weight, grad, sems,
):
    pixels = inner.shape[1]
    me = meta[0]
    strip = 128
    weight_copies = fetch_routed((w0, w1, w2, w3, w4, w5, w6, w7), weight, me, meta[2], sems, 0)
    clear_padding(field, pixels)
    means, inverses = norm_rows(pixels, strip, lambda b, start: inner[b, pl.ds(start, strip), :])
    wait_all(weight_copies)

    def write_grad(start, half, tile):
        for b in range(2):
            grad[2 * half + b, pl.ds(start, tile.shape[0]), :] = tile[:, b * LANES : (b + 1) * LANES]

    conv_back_tiles(grad_field, weight, pixels, 512, write_grad)
    gains = [pack[b, E_G2 : E_G2 + 1, :] for b in range(4)]

    def read_normed(b, start):
        return (inner[b, pl.ds(start, strip), :] - means[b]) * inverses[b]

    def slope(index, carry):
        start = pl.multiple_of(index * strip, strip)
        found = []
        for b in range(4):
            bias = pack[b, E_B2 : E_B2 + 1, :]
            scale = pack[b, M_SCALE : M_SCALE + 1, :]
            shift = pack[b, M_SHIFT : M_SHIFT + 1, :]
            shaped = read_normed(b, start) * gains[b] + bias
            modulated = shaped * (1.0 + scale) + shift
            dmod = silu_slope(modulated, grad[b, pl.ds(start, strip), :])
            grad[b, pl.ds(start, strip), :] = dmod * (1.0 + scale)
            found += [dmod * shaped, dmod]
        return tuple(old + fold(new) for old, new in zip(carry, found))

    zero = tuple(jnp.zeros((8, LANES), F32) for _ in range(8))
    modulation = lax.fori_loop(0, pixels // strip, slope, zero)

    def write(b, start, value):
        store_shifted(field, b, start, value)

    gain_sums, bias_sums = norm_back_strips(
        pixels, strip, read_normed, lambda b, start: grad[b, pl.ds(start, strip), :], gains, inverses, write
    )
    for b in range(4):
        sums[b] = sums_in[b]
        sums[b, S_G2 : S_G2 + 1, :] = gain_sums[b]
        sums[b, S_B2 : S_B2 + 1, :] = bias_sums[b]
        sums[b, S_SCALE : S_SCALE + 1, :] = column_sum(modulation[2 * b])
        sums[b, S_SHIFT : S_SHIFT + 1, :] = column_sum(modulation[2 * b + 1])
    for offset, target in enumerate((d0, d1, d2, d3)):
        target[...] = field[1, jnp.bitwise_xor(me, offset), PAD : PAD + pixels, :]


def kernel_back_conv(meta, grad_field, w0, w1, w2, w3, w4, w5, w6, w7, grad, weight, sems):
    pixels = grad.shape[1]
    wait_all(fetch_routed((w0, w1, w2, w3, w4, w5, w6, w7), weight, meta[0], meta[2], sems, 0))

    def write_grad(start, half, tile):
        for b in range(2):
            grad[2 * half + b, pl.ds(start, tile.shape[0]), :] = tile[:, b * LANES : (b + 1) * LANES]

    conv_back_tiles(grad_field, weight, pixels, 512, write_grad)


def kernel_back_first(
    meta, grad_in, image, pack, dmiddle, sums_in, g0, g1, g2, grad, sums,
):
    pixels = image.shape[1]
    me = meta[0]
    strip = 128

    def read(b, start):
        return image[b, pl.ds(start, strip), :].astype(F32)

    means, inverses = norm_rows(pixels, strip, read)
    gains = [pack[b, E_G1 : E_G1 + 1, :] for b in range(4)]

    def read_normed(b, start):
        return (read(b, start) - means[b]) * inverses[b]

    def slope(index, carry):
        start = pl.multiple_of(index * strip, strip)
        for b in range(4):
            before = read_normed(b, start) * gains[b] + pack[b, E_B1 : E_B1 + 1, :]
            grad[b, pl.ds(start, strip), :] = silu_slope(before, grad_in[b, pl.ds(start, strip), :])
        return carry

    lax.fori_loop(0, pixels // strip, slope, 0)

    def write(b, start, value):
        grad[b, pl.ds(start, strip), :] = dmiddle[b, pl.ds(start, strip), :] + value

    gain_sums, bias_sums = norm_back_strips(
        pixels, strip, read_normed, lambda b, start: grad[b, pl.ds(start, strip), :], gains, inverses, write
    )
    for b in range(4):
        sums[b] = sums_in[b]
        sums[b, S_G1 : S_G1 + 1, :] = gain_sums[b]
        sums[b, S_B1 : S_B1 + 1, :] = bias_sums[b]
    for offset, target in enumerate((g0, g1, g2.at[0], g2.at[1])):
        other = jnp.bitwise_xor(me, offset)
        target[0:pixels, :] = grad[other].astype(BF16)
        target[pixels : pixels + S_ROWS, :] = sums[other].astype(BF16)


def kernel_scale(factors0, factors1, scale):
    total = jnp.zeros((1, LANES), F32)
    for factors in (factors0, factors1):
        for g in range(factors.shape[0]):
            total = total + factors[g, 0].astype(F32)[1:2, 0:LANES]
    scale[...] = jnp.broadcast_to(1.0 / total, (8, LANES))


def kernel_factor_grads(meta, scale, factors0, factors1, small0, small1, embed, context, vectors):
    me = meta[0]
    groups = factors0.shape[0]
    inverse = scale[0:1, :]
    total = jnp.zeros((S_ROWS, LANES), F32)
    for small in (small0, small1):
        for g in range(4 * groups):
            total = total + small[g].astype(F32)
    vectors[...] = total * inverse
    over_rows = (((0,), (0,)), ((), ()))
    conditions, tokens, scales, shifts, keys, values = [], [], [], [], [], []
    for factors, small in ((factors0, small0), (factors1, small1)):
        for g in range(groups):
            for k in range(4):
                rows = factors[g, jnp.bitwise_xor(me, k)].astype(F32)
                term = small[4 * g + k].astype(F32)
                conditions.append(rows[0:1])
                tokens.append(rows[CTX : 2 * CTX])
                scales.append(term[S_SCALE : S_SCALE + 1])
                shifts.append(term[S_SHIFT : S_SHIFT + 1])
                keys.append(term[S_KEY : S_KEY + CTX])
                values.append(term[S_VALUE : S_VALUE + CTX])
    for lefts, pairs, target in (
        (conditions, (scales, shifts), embed),
        (tokens, (keys, values), context),
    ):
        left = jnp.concatenate(lefts, axis=0).astype(BF16)
        right = jnp.concatenate(
            [jnp.concatenate(parts, axis=0).astype(BF16) for parts in pairs], axis=1
        )
        grad = lax.dot_general(left, right, over_rows, preferred_element_type=F32)
        for place in range(2):
            target[:, place, :] = grad[:, place * LANES : (place + 1) * LANES] * inverse


def kernel_stack(*refs):
    whole = refs[-1]
    base = 0
    for ref in refs[:-1]:
        count = ref.shape[0]
        whole[base : base + count] = ref[...]
        base += count


def stack(parts):
    shape = (sum(part.shape[0] for part in parts),) + parts[0].shape[1:]
    return call(
        kernel_stack, "stack", struct(shape, parts[0].dtype), [vmem()] * len(parts), [], limit=12
    )(*parts)


def kernel_slots(meta, own, near, far, across, whole, sems):
    rows = pl.ds(0, whole.shape[1])
    sources = (own.at[rows], near.at[rows], far.at[0, rows], across.at[1, rows])
    wait_all(fetch(sources, whole, meta[0], sems, 0))


def kernel_cut(source, first, second):
    rows = first.shape[0]
    first[...] = source[0:rows]
    second[...] = source[rows : 2 * rows]


def cut(source):
    rows, lanes = source.shape
    return call(
        kernel_cut, "cut", [struct((rows // 2, lanes), BF16)] * 2, [vmem()], [], limit=8
    )(source)


def kernel_small_stack(own, near, far, across, whole):
    rows = pl.ds(own.shape[0] - S_ROWS, S_ROWS)
    whole[0] = own[rows, :]
    whole[1] = near[rows, :]
    whole[2] = far[0, rows, :]
    whole[3] = across[1, rows, :]


def kernel_split(counts, width, digit, meta, *refs):
    parts = refs[sum(counts) :]
    rows = parts[0].shape[1]
    for offset, part in enumerate(parts):
        start = pl.multiple_of(jnp.bitwise_xor(meta[digit], offset) * rows, rows)
        position, base = 0, 0
        for count in counts:
            terms = refs[position : position + count]
            terms = [term.at[0] if len(term.shape) == 4 else term for term in terms]
            total = terms[0][:, pl.ds(start, rows), :].astype(F32)
            for term in terms[1:]:
                total = total + term[:, pl.ds(start, rows), :].astype(F32)
            part[base : base + total.shape[0]] = total.astype(part.dtype)
            position += count
            base += total.shape[0]


def split_sum(groups, width, digit, meta):
    blocks = sum(terms[-1].shape[0] for terms in groups)
    rows = groups[0][-1].shape[1]
    flat = [term for terms in groups for term in terms]
    shape = (blocks, rows // width, LANES)
    return call(
        functools.partial(kernel_split, tuple(len(terms) for terms in groups), width, digit),
        "split_sum",
        [struct(shape, F32)] + [struct(shape, BF16)] * (width - 1),
        [smem()] + [vmem()] * len(flat),
        [],
        limit=12,
    )(meta, *flat)


def kernel_far(mine, got, own, far):
    blocks = own.shape[0]
    own[...] = mine[0:blocks] + got[0:blocks].astype(F32)
    far[...] = (mine[blocks : 2 * blocks] + got[blocks : 2 * blocks].astype(F32)).astype(BF16)


def kernel_total(*refs):
    total = refs[0][...].astype(F32)
    for term in refs[1:-1]:
        total = total + term[...].astype(F32)
    refs[-1][...] = total.astype(BF16)


def total_sum(terms):
    return call(
        kernel_total, "total_sum", struct(terms[0].shape, BF16), [vmem()] * len(terms), [], limit=12
    )(*terms)


def kernel_join(digit, meta, *refs):
    parts, whole = refs[:-1], refs[-1]
    rows = parts[0].shape[1]
    for offset, part in enumerate(parts):
        start = pl.multiple_of(jnp.bitwise_xor(meta[digit], offset) * rows, rows)
        whole[:, pl.ds(start, rows), :] = part[...]


def join(parts, digit, meta):
    blocks, rows, _ = parts[0].shape
    return call(
        functools.partial(kernel_join, digit),
        "join",
        struct((blocks, rows * len(parts), LANES), BF16),
        [smem()] + [vmem()] * len(parts),
        [],
        limit=12,
    )(meta, *parts)


def kernel_last(digit, meta, scale, mine, other, conv, *more):
    rows = mine.shape[1]
    for offset, part in enumerate((mine, other)):
        start = pl.multiple_of(jnp.bitwise_xor(meta[digit], offset) * rows, rows)
        count = conv.shape[0]
        conv[:, pl.ds(start, rows), :] = part[0:count].astype(F32) * scale[0:1, :]
        for proj in more:
            proj[:, pl.ds(start, rows)] = (part[count].astype(F32) * scale[0:1, :]).T


def last_join(pair, digit, meta, scale, more=False):
    blocks, rows, _ = pair[0].shape
    shapes = [struct((3 if more else blocks, 2 * rows, LANES), F32)]
    if more:
        shapes.append(struct((LANES, 2 * rows), F32))
    return call(
        functools.partial(kernel_last, digit),
        "last_join",
        shapes,
        [smem()] + [vmem()] * 3,
        [],
        limit=12,
    )(meta, scale, *pair)


def swap(value, axis, offset):
    size = lax.axis_size(axis)
    return lax.ppermute(value, axis, [(i, i ^ offset) for i in range(size)])


def tie(*values):
    return lax.optimization_barrier(values)


def share(shard):
    near = swap(shard, "mp", 1)
    far = swap(shard, "mp", 2)
    return shard, near, far, swap(far, "mp", 1)


def exchange(pieces):
    return (pieces[0],) + tuple(swap(pieces[k], "mp", k) for k in range(1, 4))


def pick(stack, me):
    return [lax.dynamic_index_in_dim(stack, me ^ k, 0, keepdims=False) for k in range(4)]


def pick_pair(stack, me):
    own = lax.dynamic_index_in_dim(stack, me, 0, keepdims=False)
    near = lax.dynamic_index_in_dim(stack, me ^ 1, 0, keepdims=False)
    far = [lax.dynamic_index_in_dim(stack, me ^ k, 0, keepdims=True) for k in (2, 3)]
    return own, near, jnp.concatenate(far, axis=0)


def dp_levels(size):
    return [(1 << k, 2) for k in range(size.bit_length() - 1)]


def bits(size):
    return [1 << k for k in range(size.bit_length() - 1)]


def local(
    image_in,
    out_cotangent,
    timesteps,
    clip_embed,
    context_tokens,
    image_count,
    norm1_gain,
    norm1_bias,
    conv1_weight,
    embed_weight,
    norm2_gain,
    norm2_bias,
    conv2_weight,
    conv2_bias,
    norm3_gain,
    norm3_bias,
    qkv_weight,
    context_weight,
    proj_weight,
):
    slots, pixels, width = image_in.shape
    me = lax.axis_index("mp")
    group = lax.axis_index("dp")
    parity = (group ^ (group >> 1)) & 1
    levels = dp_levels(lax.axis_size("dp"))
    own_digits = [(group >> (low.bit_length() - 1)) & (wide - 1) for low, wide in levels]
    meta = jnp.stack(
        [me, (me < image_count[0]).astype(jnp.int32), parity] + own_digits
    ).astype(jnp.int32)
    digits = range(3, 3 + len(levels))
    steps = bits(lax.axis_size("dp"))

    conv1_weight, conv2_weight, image_in, out_cotangent, meta = tie(
        conv1_weight, conv2_weight, image_in, out_cotangent, meta
    )

    conv1_shard = conv1_weight.reshape(9 * C, LANES)

    def half_of(shard):
        rows = shard.shape[0] // 2
        return lax.dynamic_slice_in_dim(shard, parity * rows, rows, axis=0)

    half1, image_in = tie(half_of(conv1_shard), image_in)
    half1 = swap(half1, "mp", 2)
    near1 = swap(conv1_shard, "mp", 1)
    images = pick_pair(image_in, me)
    image_near = swap(images[1], "mp", 1)
    image_far = swap(images[2], "mp", 2)

    half_width = EMB // 2
    frequency = jnp.exp(-math.log(10000.0) * jnp.arange(half_width, dtype=F32) / half_width)
    angles = timesteps.astype(F32)[:, None] * frequency[None, :]
    condition = jax.nn.silu(
        jnp.concatenate([jnp.cos(angles), jnp.sin(angles)], axis=1) + clip_embed.astype(F32)
    ).astype(BF16)
    scale_shift = jnp.dot(
        condition, embed_weight.reshape(EMB, 2 * LANES), preferred_element_type=F32
    ).reshape(slots, 1, 2 * LANES)
    doubled = jnp.concatenate([context_tokens, context_tokens], axis=1)
    context = jnp.dot(
        doubled.reshape(slots * 2 * CTX, EMB),
        context_weight.reshape(EMB, 2 * LANES),
        preferred_element_type=F32,
    ).astype(BF16).astype(F32).reshape(slots, 2 * CTX, 2 * LANES)
    vectors = [norm1_gain, norm1_bias, norm2_gain, norm2_bias, conv2_bias, norm3_gain, norm3_bias]
    early = struct((E_ROWS, LANES), F32)
    packs = call(
        kernel_early,
        "early",
        [early, early, struct((2, E_ROWS, LANES), F32)],
        [smem()] + [vmem()] * 9,
        [],
        limit=8,
    )(meta, scale_shift, context, *[vector[None] for vector in vectors])
    count_rows = jnp.broadcast_to(image_count.astype(BF16)[:, None, None], (slots, CTX - 1, EMB))
    factors = jnp.concatenate([condition[:, None], count_rows, context_tokens], axis=1)[None]
    cots = pick(out_cotangent, me)
    rest_shard = jnp.concatenate(
        [
            conv2_weight.reshape(9 * C, LANES),
            jnp.transpose(qkv_weight, (1, 0, 2)).reshape(3 * C, LANES),
            jnp.transpose(proj_weight.reshape(LANES, 4, LANES), (1, 0, 2)).reshape(C, LANES),
        ],
        axis=0,
    )
    rest_half = half_of(rest_shard)

    def relayed(shard, near, half):
        by_x, by_z = cut(half)
        by_x = swap(by_x, "dp", 1)
        by_z = swap(by_z, "dp", 2)
        return (shard, near, half, by_x, by_z) + tuple(
            swap(part, "mp", 1) for part in (half, by_x, by_z)
        )

    near1, image_near, packs, half1 = tie(near1, image_near, packs, half1)
    pack_near = swap(packs[1], "mp", 1)
    pack_far = swap(packs[2], "mp", 2)
    conv1 = relayed(conv1_shard, near1, half1)
    image_far, pack_near, pack_far, rest_shard, rest_half, factors, cots, *conv1 = tie(
        image_far, pack_near, pack_far, rest_shard, rest_half, factors, cots, *conv1
    )
    images = (images[0], image_near, image_far, swap(image_far, "mp", 1))
    packs = (packs[0], pack_near, pack_far, swap(pack_far, "mp", 1))
    rest_half = swap(rest_half, "mp", 2)
    rest_near = swap(rest_shard, "mp", 1)
    factors = [factors, swap(factors, "dp", 1)]

    block = struct((4, pixels, LANES), BF16)
    block32 = struct((4, pixels, LANES), F32)
    turned = struct((4, LANES, pixels), BF16)
    fields = struct((3, 4, pixels + 2 * PAD, LANES), BF16)
    piece = struct((pixels, LANES), BF16)
    pair_piece = struct((2, pixels, LANES), BF16)
    field_scratch = pltpu.VMEM((3, 4, pixels + 2 * PAD, LANES), BF16)
    conv_scratch = pltpu.VMEM((4, 9 * C, LANES), BF16)
    rest_scratch = pltpu.VMEM((4, PROJ_ROW + C, LANES), BF16)
    grad_scratch = pltpu.VMEM((4, pixels, LANES), F32)

    image, pack, first_t, inner, second_t, second = call(
        kernel_first,
        "first",
        [block, struct((4, E_ROWS, LANES), F32), turned, block32, turned, fields],
        [smem()] + [anywhere()] * 16,
        [field_scratch, conv_scratch, pltpu.SemaphoreType.DMA((16,))],
        limit=17,
    )(meta, *images, *packs, *conv1)

    second, rest_half, rest_near, factors = tie(second, rest_half, rest_near, factors)
    rest = relayed(rest_shard, rest_near, rest_half)
    cots = exchange(cots)
    second, *rest = tie(second, *rest)
    factors = stack(factors)
    factors = [factors, swap(factors, "dp", 2)]
    middle, attn_t, qkv, qkv_w, proj_w = call(
        kernel_second,
        "second",
        [
            block32,
            turned,
            struct((4, pixels, 3 * LANES), BF16),
            struct((4, 3 * C, LANES), BF16),
            struct((4, C, LANES), BF16),
        ],
        [smem()] + [vmem()] * 3 + [anywhere()] * 8,
        [rest_scratch, pltpu.VMEM((4, pixels, LANES), BF16), pltpu.SemaphoreType.DMA((8,))],
        limit=17,
    )(meta, second, image, pack, *rest)
    ctx_scratch = pltpu.VMEM((pixels, LANES), F32)
    turned_scratch = pltpu.VMEM((LANES, pixels), F32)
    qkv, first_t, second_t, factors, cots = tie(qkv, first_t, second_t, factors, cots)
    factors = stack(factors)
    second_y = swap(second_t, "mp", 2)
    first_y = swap(first_t, "mp", 2)
    second_c = swap(second_t, "mp", 1)
    first_c = swap(first_t, "mp", 1)
    for low in steps[2:-1]:
        factors = stack([factors, swap(factors, "dp", low)])
    factors = (factors, swap(factors, "dp", steps[-1]))
    out_own, out_near, out_far, cot, mixed, dqkv, dctx = call(
        kernel_attention,
        "attention",
        [piece, piece, pair_piece]
        + [block, block, struct((4, pixels, 3 * LANES), BF16), struct((4, 2 * CTX, LANES), F32)],
        [smem()] + [vmem()] * 4 + [anywhere()] * 4,
        [
            pltpu.VMEM((4, pixels, LANES), BF16),
            ctx_scratch,
            ctx_scratch,
            ctx_scratch,
            ctx_scratch,
            grad_scratch,
            grad_scratch,
            turned_scratch,
            turned_scratch,
            pltpu.SemaphoreType.DMA((4,)),
        ],
    )(meta, qkv, pack, middle, proj_w, *cots)

    def weight_send(sources, gradients):
        return call(
            kernel_weight_send,
            "weight_send",
            [struct((9, C // 2, LANES), BF16), fields],
            [smem()] + [vmem()] * 8,
            [],
            limit=16,
        )(meta, *sources, *gradients)

    def weight_own(sources, field):
        return call(
            kernel_weight_own,
            "weight_own",
            struct((9, C // 2, LANES), F32),
            [smem()] + [vmem()] * 5,
            [],
            limit=16,
        )(meta, *sources, field)

    def down(terms, level):
        own, send = split_sum([terms], 2, digits[level], meta)
        return [own, swap(send, "dp", levels[level][0])]

    def across(value, level):
        return [value, swap(value, "dp", levels[level][0])]

    def inner_levels(terms):
        for level in range(3, len(levels)):
            terms = down(terms, level)
        value = total_sum(terms)
        for level in range(len(levels) - 1, 2, -1):
            value = join(across(value, level), digits[level], meta)
        return value

    att_keep, att_send = call(
        kernel_attention_grad,
        "attention_grad",
        [struct((2, 4, C, LANES), BF16)] * 2,
        [smem()] + [vmem()] * 4,
        [pltpu.VMEM((4, LANES, pixels), BF16)],
    )(meta, dqkv, mixed, attn_t, cot)
    dqkv, att_send, second_y, first_y, second_c, first_c, factors = tie(
        dqkv, att_send, second_y, first_y, second_c, first_c, factors
    )
    second_d = swap(second_y, "mp", 1)
    first_d = swap(first_y, "mp", 1)
    att = [att_keep.reshape(8, C, LANES), swap(att_send, "mp", 1).reshape(8, C, LANES)]
    dmiddle, field2, sums, *gradients2 = call(
        kernel_back_attention,
        "back_attention",
        [block32, fields, struct((4, S_ROWS, LANES), F32)] + [piece] * 4,
        [smem()] + [vmem()] * 6,
        [grad_scratch],
    )(meta, dqkv, cot, middle, pack, dctx, qkv_w)
    gradients2, second_d, first_d, att, field2 = tie(gradients2, second_d, first_d, att, field2)
    seconds = (second_t, second_c, second_y, second_d)
    firsts = (first_t, first_c, first_y, first_d)
    gradients2 = exchange(gradients2)
    att = down(att, 0)
    field2, att[0] = tie(field2, att[0])
    field1, sums, *gradients1 = call(
        kernel_back_second,
        "back_second",
        [fields, struct((4, S_ROWS, LANES), F32)] + [piece] * 4,
        [smem()] + [vmem()] * 4 + [anywhere()] * 8,
        [rest_scratch, grad_scratch, pltpu.SemaphoreType.DMA((8,))],
        limit=20,
    )(meta, field2, inner, pack, sums, *rest)
    gradients1, gradients2, att = tie(gradients1, gradients2, att)
    gradients1 = exchange(gradients1)
    att = down(att, 1)
    gradients2, att[0] = tie(gradients2, att[0])
    send2, wide2 = weight_send(seconds, gradients2)
    got2 = swap(send2, "dp", 1)
    wide2, att = tie(wide2, att)
    att = down(att, 2)
    wide2, att[0] = tie(wide2, att[0])
    own2 = weight_own(seconds, wide2)
    own2, att, field1 = tie(own2, att, field1)
    for level in range(3, len(levels)):
        att = down(att, level)
    att_own, att_far = call(
        kernel_far,
        "att_far",
        [struct((4,) + att[0].shape[1:], F32), struct((4,) + att[0].shape[1:], BF16)],
        [vmem()] * 2,
        [],
        limit=12,
    )(*att)
    field1, att_own = tie(field1, att_own)
    att = [att_own, swap(att_far, "mp", 2)]
    grad_first = call(
        kernel_back_conv,
        "back_conv",
        block32,
        [smem()] + [vmem()] + [anywhere()] * 8,
        [conv_scratch, pltpu.SemaphoreType.DMA((8,))],
    )(meta, field1, *conv1)
    grad_first, gradients1, att = tie(grad_first, gradients1, att)
    att = total_sum(att)
    for level in range(len(levels) - 1, 2, -1):
        att = join(across(att, level), digits[level], meta)
    gradients1, att, out_far = tie(gradients1, att, out_far)
    att = across(att, 2)
    send1, wide1 = weight_send(firsts, gradients1)
    got1 = swap(send1, "dp", 1)
    out_far = swap(out_far, "mp", 2)
    wide1, got2, own2 = tie(wide1, got2, own2)
    terms2 = down([own2, got2], 1)
    wide1, terms2[0] = tie(wide1, terms2[0])
    own1 = weight_own(firsts, wide1)
    grad_first, own1, terms2, att = tie(grad_first, own1, terms2, att)
    terms2 = down(terms2, 2)
    att = across(join(att, digits[2], meta), 1)
    grad_first, terms2[0], att[0] = tie(grad_first, terms2[0], att[0])
    grad_own, grad_near, grad_far = call(
        kernel_back_first,
        "back_first",
        [
            struct((pixels + S_ROWS, LANES), BF16),
            struct((pixels + S_ROWS, LANES), BF16),
            struct((2, pixels + S_ROWS, LANES), BF16),
        ],
        [smem()] + [vmem()] * 5,
        [grad_scratch, pltpu.VMEM((4, S_ROWS, LANES), F32)],
    )(meta, grad_first, image, pack, dmiddle, sums)
    grad_far, terms2, got1, own1 = tie(grad_far, terms2, got1, own1)
    terms1 = down([own1, got1], 1)
    ends2 = across(inner_levels(terms2), 2)
    grad_far, ends2[0], terms1[0], att = tie(grad_far, ends2[0], terms1[0], att)
    att = across(join(att, digits[1], meta), 0)
    grad_far = swap(grad_far, "mp", 2)
    ends2, terms1, grad_near, out_far = tie(ends2, terms1, grad_near, out_far)
    terms1 = down(terms1, 2)
    ends2 = across(join(ends2, digits[2], meta), 1)
    scale = call(kernel_scale, "scale", struct((8, LANES), F32), [vmem()] * 2, [], limit=8)(*factors)
    ends2, terms1, scale, att = tie(ends2, terms1, scale, att)
    ends1 = across(inner_levels(terms1), 2)
    ends2 = across(join(ends2, digits[1], meta), 0)
    qkv_grad, proj_grad = last_join(att, digits[0], meta, scale, True)
    ends1, qkv_grad, grad_near = tie(ends1, qkv_grad, grad_near)
    ends1 = across(join(ends1, digits[2], meta), 1)
    ends1[0], grad_near, grad_far = tie(ends1[0], grad_near, grad_far)
    grad_near = swap(grad_near, "mp", 1)
    grad_across = swap(grad_far, "mp", 1)
    image_parts = (grad_own, grad_near, grad_far, grad_across)
    ends1 = across(join(ends1, digits[1], meta), 0)
    ends1[0], grad_across, grad_near, ends2 = tie(ends1[0], grad_across, grad_near, ends2)
    smalls = call(
        kernel_small_stack,
        "stack",
        struct((4, S_ROWS, LANES), BF16),
        [vmem()] * 4,
        [],
        limit=8,
    )(grad_own, grad_near, grad_far, grad_across)
    small_got = swap(smalls, "dp", 1)
    (conv2_grad,) = last_join(ends2, digits[0], meta, scale)
    small_got, conv2_grad = tie(small_got, conv2_grad)
    smalls = stack([smalls, small_got])
    for low in steps[1:-1]:
        smalls = stack([smalls, swap(smalls, "dp", low)])
    small_got = swap(smalls, "dp", steps[-1])
    smalls, out_far, out_near = tie(smalls, out_far, out_near)
    out_parts = (out_own, swap(out_near, "mp", 1), out_far, swap(out_far, "mp", 1))
    embed_grad, context_grad, vector_sums = call(
        kernel_factor_grads,
        "factor_grads",
        [
            struct((EMB, 2, LANES), F32),
            struct((EMB, 2, LANES), F32),
            struct((S_ROWS, LANES), F32),
        ],
        [smem()] + [vmem()] * 5,
        [],
        limit=12 if len(steps) < 4 else 56,
    )(meta, scale, *factors, smalls, small_got)

    def in_slots(parts):
        return pl.pallas_call(
            kernel_slots,
            name="slots",
            out_shape=struct((4, pixels, LANES), BF16),
            in_specs=[smem()] + [anywhere()] * 4,
            out_specs=vmem(),
            scratch_shapes=[pltpu.SemaphoreType.DMA((4,))],
            compiler_params=pltpu.CompilerParams(vmem_limit_bytes=8 * MIB),
        )(meta, *parts)

    block_out = in_slots(out_parts)
    image_grad = in_slots(image_parts)
    (conv1_grad,) = last_join(ends1, digits[0], meta, scale)
    return (
        block_out,
        image_grad,
        vector_sums[S_G1],
        vector_sums[S_B1],
        conv1_grad.reshape(3, 3, C, LANES),
        embed_grad,
        vector_sums[S_G2],
        vector_sums[S_B2],
        conv2_grad.reshape(3, 3, C, LANES),
        vector_sums[S_CB2],
        vector_sums[S_G3],
        vector_sums[S_B3],
        jnp.transpose(qkv_grad, (1, 0, 2)),
        context_grad,
        proj_grad,
    )


def solution(mesh):
    return jax.shard_map(
        local,
        mesh=mesh,
        in_specs=(
            P("dp", None, "mp"),
            P("dp", None, "mp"),
            P("dp"),
            P("dp", None),
            P("dp", None, None),
            P("dp"),
            P("mp"),
            P("mp"),
            P(None, None, None, "mp"),
            P(None, None, "mp"),
            P("mp"),
            P("mp"),
            P(None, None, None, "mp"),
            P("mp"),
            P("mp"),
            P("mp"),
            P(None, None, "mp"),
            P(None, None, "mp"),
            P("mp", None),
        ),
        out_specs=(
            P("dp", None, "mp"),
            P("dp", None, "mp"),
            P("mp"),
            P("mp"),
            P(None, None, None, "mp"),
            P(None, None, "mp"),
            P("mp"),
            P("mp"),
            P(None, None, None, "mp"),
            P("mp"),
            P("mp"),
            P("mp"),
            P(None, None, "mp"),
            P(None, None, "mp"),
            P("mp", None),
        ),
        check_vma=False,
    )
```

```python
import functools
import math

import jax
import jax.numpy as jnp
from jax import lax
from jax.experimental import pallas as pl
from jax.experimental.pallas import tpu as pltpu
from jax.sharding import PartitionSpec as P

C = 512
GROUPS = 32
HEAD = 64
EMB = 2048
CTX = 4
SIDE = 32
LANES = 128
PAD = SIDE
EPSILON = 1e-05
F32 = jnp.float32
BF16 = jnp.bfloat16
NEG = -1e30
QKV_ROW = 9 * C
PROJ_ROW = QKV_ROW + 3 * C

E_G1, E_B1, E_G2, E_B2, E_CB2, E_G3, E_B3, M_SCALE, M_SHIFT = range(9)
M_KEY, M_VALUE, E_ROWS = 16, 24, 32
S_G3, S_B3, S_CB2, S_G2, S_B2, S_SCALE, S_SHIFT = range(7)
S_KEY, S_VALUE, S_G1, S_B1, S_ROWS = 8, 12, 16, 17, 32
MIB = 1 << 20


def vmem():
    return pl.BlockSpec(memory_space=pltpu.VMEM)


def anywhere():
    return pl.BlockSpec(memory_space=pltpu.HBM)


def smem():
    return pl.BlockSpec(memory_space=pltpu.SMEM)


def struct(shape, dtype):
    return jax.ShapeDtypeStruct(shape, dtype)


def call(body, name, out_shape, in_specs, scratch, flops=0, limit=14):
    many = isinstance(out_shape, (list, tuple))
    return pl.pallas_call(
        body,
        name=name,
        out_shape=out_shape,
        in_specs=in_specs,
        out_specs=[vmem() for _ in out_shape] if many else vmem(),
        scratch_shapes=scratch,
        compiler_params=pltpu.CompilerParams(vmem_limit_bytes=limit * MIB),
        cost_estimate=pl.CostEstimate(flops=0, transcendentals=0, bytes_accessed=0),
    )


def fetch(sources, target, me, sems, first):
    copies = []
    for offset, source in enumerate(sources):
        copy = pltpu.make_async_copy(
            source, target.at[jnp.bitwise_xor(me, offset)], sems.at[first + offset]
        )
        copy.start()
        copies.append(copy)
    return copies


def fetch_routed(sources, target, me, parity, sems, first):
    quarter = target.shape[1] // 4
    copies = []
    for index, source in enumerate(sources):
        place = target.at[jnp.bitwise_xor(me, (0, 1, 2, 2, 2, 3, 3, 3)[index])]
        if index >= 2:
            kind = (index - 2) % 3
            rows = 2 * quarter if kind == 0 else quarter
            half = parity if kind == 0 else 1 - parity
            start = half * 2 * quarter + (quarter if kind == 2 else 0)
            place = place.at[pl.ds(pl.multiple_of(start, quarter), rows), :]
        copy = pltpu.make_async_copy(source, place, sems.at[first + index])
        copy.start()
        copies.append(copy)
    return copies


def wait_all(copies):
    for copy in copies:
        copy.wait()


def fold(values):
    rows = values.shape[0]
    return jnp.sum(values.reshape(rows // 8, 8, values.shape[1]), axis=0)


def group_sum(rows8):
    lane = lax.broadcasted_iota(jnp.int32, rows8.shape, 1)
    total = jnp.broadcast_to(jnp.sum(rows8, axis=0, keepdims=True), rows8.shape)
    for step in (1, 2, 4, 8):
        up = pltpu.roll(total, step, axis=1)
        down = pltpu.roll(total, LANES - step, axis=1)
        total = total + jnp.where((lane & step) != 0, up, down)
    return total[0:1]


def column_sum(rows8):
    return jnp.sum(rows8, axis=0, keepdims=True)


def sum_strips(pixels, strip, width, function):
    zero = tuple(jnp.zeros((8, LANES), F32) for _ in range(width))

    def body(index, carry):
        start = pl.multiple_of(index * strip, strip)
        return tuple(old + fold(new) for old, new in zip(carry, function(start)))

    return lax.fori_loop(0, pixels // strip, body, zero)


def norm_rows(pixels, strip, read):
    count = pixels * (C // GROUPS)
    sums = sum_strips(pixels, strip, 4, lambda start: [read(b, start) for b in range(4)])
    means = [group_sum(s) * (1.0 / count) for s in sums]
    squares = sum_strips(
        pixels,
        strip,
        4,
        lambda start: [jnp.square(read(b, start) - means[b]) for b in range(4)],
    )
    inverses = [lax.rsqrt(group_sum(s) * (1.0 / count) + EPSILON) for s in squares]
    return means, inverses


def shifted(values):
    rows = values.shape[0]
    column = lax.broadcasted_iota(jnp.int32, values.shape, 0) & (SIDE - 1)
    left = jnp.where(column == 0, 0.0, pltpu.roll(values, 1, axis=0))
    right = jnp.where(column == SIDE - 1, 0.0, pltpu.roll(values, rows - 1, axis=0))
    return left, values, right


def store_shifted(target, block, start, values):
    rows = values.shape[0]
    for position, part in enumerate(shifted(values)):
        target[position, block, pl.ds(pl.multiple_of(PAD + start, 32), rows), :] = part.astype(BF16)


def clear_padding(target, pixels):
    zero = jnp.zeros((PAD, LANES), BF16)
    for position in range(3):
        for block in range(4):
            target[position, block, 0:PAD, :] = zero
            target[position, block, PAD + pixels : PAD + pixels + PAD, :] = zero


def conv_tiles(field, weight, pixels, tile, write):
    def body(index, carry):
        start = pl.multiple_of(index * tile, tile)
        left = jnp.concatenate(
            [
                field[b, block, pl.ds(pl.multiple_of(start + a * SIDE, 32), tile), :]
                for a in range(3)
                for b in range(3)
                for block in range(4)
            ],
            axis=1,
        )
        right = jnp.concatenate([weight[s, 0 : 9 * C, :] for s in range(4)], axis=1)
        write(start, jnp.dot(left, right, preferred_element_type=F32))
        return carry

    lax.fori_loop(0, pixels // tile, body, 0)


def conv_back_tiles(field, weight, pixels, tile, write):
    def body(index, carry):
        start = pl.multiple_of((index // 2) * tile, tile)
        half = index % 2
        left = jnp.concatenate(
            [
                field[2 - b, block, pl.ds(pl.multiple_of(start + (2 - a) * SIDE, 32), tile), :]
                for a in range(3)
                for b in range(3)
                for block in range(4)
            ],
            axis=1,
        )
        right = jnp.concatenate(
            [
                weight[block, pl.ds(pl.multiple_of((3 * a + b) * C + half * 256, 256), 256), :]
                for a in range(3)
                for b in range(3)
                for block in range(4)
            ],
            axis=1,
        )
        write(
            start,
            half,
            lax.dot_general(left, right, (((1,), (1,)), ((), ())), preferred_element_type=F32),
        )
        return carry

    lax.fori_loop(0, 2 * (pixels // tile), body, 0)


def silu_slope(before, grad_out):
    gate = jax.nn.sigmoid(before)
    return grad_out * gate * (1.0 + before * (1.0 - gate))


def kernel_early(meta, scale_shift, context, v0, v1, v2, v3, v4, v5, v6, own, near, far):
    for offset, target in enumerate((own, near, far.at[0], far.at[1])):
        slot = jnp.bitwise_xor(meta[0], offset)
        target[...] = jnp.zeros((E_ROWS, LANES), F32)
        for row, vector in enumerate((v0, v1, v2, v3, v4, v5, v6)):
            target[row : row + 1, :] = vector[...]
        scales = scale_shift[slot]
        target[M_SCALE : M_SCALE + 1, :] = scales[:, :LANES]
        target[M_SHIFT : M_SHIFT + 1, :] = scales[:, LANES:]
        tokens = context[slot]
        target[M_KEY : M_KEY + 8, :] = tokens[:, :LANES]
        target[M_VALUE : M_VALUE + 8, :] = tokens[:, LANES:]


def kernel_first(
    meta, i0, i1, i2, i3, e0, e1, e2, e3, w0, w1, w2, w3, w4, w5, w6, w7,
    image, pack, first_t, inner, second_t, second, field, weight, sems,
):
    pixels = image.shape[1]
    me = meta[0]
    image_copies = fetch((i0, i1, i2.at[0], i3.at[1]), image, me, sems, 0)
    pack_copies = fetch((e0, e1, e2.at[0], e3.at[1]), pack, me, sems, 4)
    weight_copies = fetch_routed((w0, w1, w2, w3, w4, w5, w6, w7), weight, me, meta[2], sems, 8)
    clear_padding(field, pixels)
    clear_padding(second, pixels)
    wait_all(image_copies)
    wait_all(pack_copies)
    strip = 128

    def read(block, start):
        return image[block, pl.ds(start, strip), :].astype(F32)

    means, inverses = norm_rows(pixels, strip, read)

    def normalise(index, carry):
        start = pl.multiple_of(index * strip, strip)
        for b in range(4):
            gain = pack[b, E_G1 : E_G1 + 1, :]
            bias = pack[b, E_B1 : E_B1 + 1, :]
            before = (read(b, start) - means[b]) * inverses[b] * gain + bias
            after = before * jax.nn.sigmoid(before)
            store_shifted(field, b, start, after)
            first_t[b, :, pl.ds(start, strip)] = after.T.astype(BF16)
        return carry

    lax.fori_loop(0, pixels // strip, normalise, 0)
    wait_all(weight_copies)

    def write(start, tile):
        for b in range(4):
            inner[b, pl.ds(start, tile.shape[0]), :] = tile[:, b * LANES : (b + 1) * LANES]

    conv_tiles(field, weight, pixels, 512, write)
    means2, inverses2 = norm_rows(pixels, strip, lambda b, start: inner[b, pl.ds(start, strip), :])

    def modulate(index, carry):
        start = pl.multiple_of(index * strip, strip)
        for b in range(4):
            gain = pack[b, E_G2 : E_G2 + 1, :]
            bias = pack[b, E_B2 : E_B2 + 1, :]
            scale = pack[b, M_SCALE : M_SCALE + 1, :]
            shift = pack[b, M_SHIFT : M_SHIFT + 1, :]
            normed = (inner[b, pl.ds(start, strip), :] - means2[b]) * inverses2[b]
            modulated = (normed * gain + bias) * (1.0 + scale) + shift
            after = modulated * jax.nn.sigmoid(modulated)
            store_shifted(second, b, start, after)
            second_t[b, :, pl.ds(start, strip)] = after.T.astype(BF16)
        return carry

    lax.fori_loop(0, pixels // strip, modulate, 0)


def kernel_second(
    meta, second, image, pack, w0, w1, w2, w3, w4, w5, w6, w7,
    middle, attn_t, qkv, qkv_weight, proj_weight, weight, attn, sems,
):
    pixels = image.shape[1]
    me = meta[0]
    wait_all(fetch_routed((w0, w1, w2, w3, w4, w5, w6, w7), weight, me, meta[2], sems, 0))
    strip = 128

    def write(start, tile):
        rows = tile.shape[0]
        for b in range(4):
            branch = tile[:, b * LANES : (b + 1) * LANES] + pack[b, E_CB2 : E_CB2 + 1, :]
            middle[b, pl.ds(start, rows), :] = image[b, pl.ds(start, rows), :].astype(F32) + branch

    conv_tiles(second, weight, pixels, 512, write)
    means, inverses = norm_rows(pixels, strip, lambda b, start: middle[b, pl.ds(start, strip), :])

    def normalise(index, carry):
        start = pl.multiple_of(index * strip, strip)
        for b in range(4):
            normed = (middle[b, pl.ds(start, strip), :] - means[b]) * inverses[b]
            value = normed * pack[b, E_G3 : E_G3 + 1, :] + pack[b, E_B3 : E_B3 + 1, :]
            attn[b, pl.ds(start, strip), :] = value.astype(BF16)
            attn_t[b, :, pl.ds(start, strip)] = value.T.astype(BF16)
        return carry

    lax.fori_loop(0, pixels // strip, normalise, 0)
    for s in range(4):
        qkv_weight[s] = weight[s, QKV_ROW:PROJ_ROW, :]
        proj_weight[s] = weight[s, PROJ_ROW : PROJ_ROW + C, :]

    def project(index, carry):
        s = index // 2
        start = pl.multiple_of((index % 2) * 512, 512)
        left = jnp.concatenate([attn[b, pl.ds(start, 512), :] for b in range(4)], axis=1)
        right = jnp.concatenate(
            [weight[s, QKV_ROW + kind * C : QKV_ROW + (kind + 1) * C, :] for kind in range(3)], axis=1
        )
        qkv[s, pl.ds(start, 512), :] = jnp.dot(left, right, preferred_element_type=F32).astype(BF16)
        return carry

    lax.fori_loop(0, 4 * (pixels // 512), project, 0)


def kernel_attention(
    meta, qkv, pack, middle, weight, c0, c1, c2, c3,
    o0, o1, o2, cot, mixed, dqkv, dctx,
    grad_mixed, score_ctx, grad_ctx_prob, prob_ctx, dscore_ctx, out_pix, dquery, dkey_t, dvalue_t, sems,
):
    pixels = qkv.shape[1]
    me = meta[0]
    alive = meta[1].astype(F32)
    cot_copies = fetch((c0, c1, c2, c3), cot, me, sems, 0)
    scale = 1.0 / math.sqrt(HEAD)
    block = 1024

    row32 = lax.broadcasted_iota(jnp.int32, (32, LANES), 0)
    lane32 = lax.broadcasted_iota(jnp.int32, (32, LANES), 1)

    def diagonal(kind):
        found = []
        for s in range(4):
            rows8 = pack[s, kind : kind + 8, :]
            tiled = jnp.concatenate([rows8] * 4, axis=0)
            own = (row32 // 4) == (2 * s + lane32 // HEAD)
            kept = jnp.where(own, tiled, 0.0)
            found.append(jnp.concatenate([kept, jnp.zeros((96, LANES), F32)], axis=0).astype(BF16))
        return jnp.concatenate(found, axis=1)

    keys_ctx = diagonal(M_KEY)
    values_ctx = diagonal(M_VALUE)
    wait_all(cot_copies)

    def projection():
        return jnp.concatenate(
            [
                jnp.concatenate([weight[s, o * LANES : (o + 1) * LANES, :] for o in range(4)], axis=1)
                for s in range(4)
            ],
            axis=0,
        )

    def prepare(index, carry):
        start = pl.multiple_of(index * block, block)
        rows = pl.ds(start, block)
        for s in range(4):
            cot[s, rows, :] = (cot[s, rows, :].astype(F32) * alive).astype(BF16)
        all_cot = jnp.concatenate([cot[s, rows, :] for s in range(4)], axis=1)
        all_weight = projection()
        grad = lax.dot_general(
            all_cot, all_weight, (((1,), (1,)), ((), ())), preferred_element_type=F32
        ).astype(BF16)
        for s in range(4):
            grad_mixed[s, rows, :] = grad[:, s * LANES : (s + 1) * LANES]
        query = jnp.concatenate([qkv[s, rows, 0:LANES] for s in range(4)], axis=1)
        score_ctx[rows, :] = lax.dot_general(
            query, keys_ctx, (((1,), (1,)), ((), ())), preferred_element_type=F32
        )
        grad_ctx_prob[rows, :] = lax.dot_general(
            grad, values_ctx, (((1,), (1,)), ((), ())), preferred_element_type=F32
        )
        prob_ctx[rows, :] = jnp.zeros((block, LANES), F32)
        dscore_ctx[rows, :] = jnp.zeros((block, LANES), F32)
        return carry

    lax.fori_loop(0, pixels // block, prepare, 0)
    lane = lax.broadcasted_iota(jnp.int32, (block, LANES), 1)
    low = lane < HEAD
    ones = jnp.ones((pixels, LANES), BF16)
    blocks = pixels // block

    def attend(index, carry):
        s = index // blocks
        part = index % blocks
        rows = pl.ds(pl.multiple_of(part * block, block), block)

        @pl.when(part == 0)
        def _():
            dkey_t[...] = jnp.zeros((LANES, pixels), F32)
            dvalue_t[...] = jnp.zeros((LANES, pixels), F32)

        query = qkv[s, rows, 0:LANES]
        key = qkv[s, :, LANES : 2 * LANES]
        value = qkv[s, :, 2 * LANES : 3 * LANES]
        value_ones = jnp.concatenate([value, ones], axis=1)
        grad = grad_mixed[s, rows, :]
        ctx_scores = score_ctx[rows, :]
        ctx_grads = grad_ctx_prob[rows, :]
        exps, outs, inverses, ctx_exps, owns = [], [], [], [], []
        for h in range(2):
            mine = low if h == 0 else jnp.logical_not(low)
            own = lane // CTX == 2 * s + h
            score = lax.dot_general(
                jnp.where(mine, query, jnp.zeros_like(query)),
                key,
                (((1,), (1,)), ((), ())),
                preferred_element_type=F32,
            )
            top = jnp.maximum(
                jnp.max(score, axis=1, keepdims=True),
                jnp.max(jnp.where(own, ctx_scores, NEG), axis=1, keepdims=True),
            )
            exp = jnp.exp((score - top) * scale).astype(BF16)
            ctx_exp = jnp.where(own, jnp.exp((ctx_scores - top) * scale), 0.0)
            out = jnp.dot(exp, value_ones, preferred_element_type=F32)
            total = out[:, LANES:] + jnp.sum(ctx_exp, axis=1, keepdims=True)
            inverse = 1.0 / total
            exps.append(exp)
            outs.append(out[:, :LANES] * inverse)
            inverses.append(inverse)
            ctx_exps.append(ctx_exp)
            owns.append(own)
        out_pair = jnp.where(low, outs[0], outs[1])
        out_pix[s, rows, :] = out_pair
        inverse_pair = jnp.where(low, inverses[0], inverses[1])
        scaled = (grad.astype(F32) * (inverse_pair * scale)).astype(BF16)
        product = out_pair * scaled.astype(F32)
        query_t = query.astype(F32).T.astype(BF16)
        scaled_t = scaled.astype(F32).T.astype(BF16)
        prob_keep = prob_ctx[rows, :]
        dscore_keep = dscore_ctx[rows, :]
        dqs = []
        for h in range(2):
            mine = low if h == 0 else jnp.logical_not(low)
            own = owns[h]
            ctx_prob = ctx_exps[h] * inverses[h]
            ctx_grad = ctx_grads * (inverses[h] * scale)
            dot = jnp.sum(
                jnp.where(mine, product, 0.0) + ctx_prob * jnp.where(own, ctx_grad, 0.0),
                axis=1,
                keepdims=True,
            )
            weight_grad = lax.dot_general(
                jnp.where(mine, scaled, jnp.zeros_like(scaled)),
                value,
                (((1,), (1,)), ((), ())),
                preferred_element_type=F32,
            )
            dscore = (exps[h].astype(F32) * (weight_grad - dot)).astype(BF16)
            prob_keep = jnp.where(own, ctx_prob, prob_keep)
            dscore_keep = jnp.where(own, ctx_exps[h] * (ctx_grad - dot), dscore_keep)
            dqs.append(jnp.dot(dscore, key, preferred_element_type=F32))
            half = slice(h * HEAD, (h + 1) * HEAD)
            dkey_t[half, :] += jnp.dot(query_t[half], dscore, preferred_element_type=F32)
            dvalue_t[half, :] += jnp.dot(scaled_t[half], exps[h], preferred_element_type=F32)
        prob_ctx[rows, :] = prob_keep
        dscore_ctx[rows, :] = dscore_keep
        dquery[s, rows, :] = jnp.where(low, dqs[0], dqs[1])

        @pl.when(part == blocks - 1)
        def _():
            for piece in range(pixels // LANES):
                cut = slice(piece * LANES, (piece + 1) * LANES)
                dqkv[s, cut, LANES : 2 * LANES] = dkey_t[:, cut].T.astype(BF16)
                dqkv[s, cut, 2 * LANES : 3 * LANES] = (dvalue_t[:, cut] * (1.0 / scale)).T.astype(BF16)

        return carry

    lax.fori_loop(0, 4 * blocks, attend, 0)

    def finish(index, carry):
        dkeys, dvalues = carry
        start = pl.multiple_of(index * block, block)
        rows = pl.ds(start, block)
        prob = prob_ctx[rows, :].astype(BF16)
        dscore = dscore_ctx[rows, :].astype(BF16)
        out_ctx = jnp.dot(prob, values_ctx, preferred_element_type=F32)
        dquery_ctx = jnp.dot(dscore, keys_ctx, preferred_element_type=F32)
        parts = []
        for s in range(4):
            cut = slice(s * LANES, (s + 1) * LANES)
            both = (out_pix[s, rows, :] + out_ctx[:, cut]).astype(BF16)
            mixed[s, rows, :] = both
            parts.append(both)
            dqkv[s, rows, 0:LANES] = (dquery[s, rows, :] + dquery_ctx[:, cut]).astype(BF16)
        result = jnp.dot(
            jnp.concatenate(parts, axis=1), projection(), preferred_element_type=F32
        )
        for offset, target in enumerate((o0, o1, o2.at[0], o2.at[1])):
            other = jnp.bitwise_xor(me, offset)
            value = jnp.zeros((block, LANES), F32)
            for s in range(4):
                value = jnp.where(other == s, result[:, s * LANES : (s + 1) * LANES], value)
            target[rows, :] = ((middle[other, rows, :] + value) * alive).astype(BF16)
        query = jnp.concatenate([qkv[s, rows, 0:LANES] for s in range(4)], axis=1)
        grad = jnp.concatenate([grad_mixed[s, rows, :] for s in range(4)], axis=1)
        dkeys = dkeys + jnp.dot(dscore_ctx[rows, :].T[0:32].astype(BF16), query, preferred_element_type=F32)
        dvalues = dvalues + jnp.dot(prob_ctx[rows, :].T[0:32].astype(BF16), grad, preferred_element_type=F32)
        return dkeys, dvalues

    zero = jnp.zeros((32, C), F32)
    dkeys, dvalues = lax.fori_loop(0, pixels // block, finish, (zero, zero))
    for s in range(4):
        own = (row32 // 4) == (2 * s + lane32 // HEAD)
        for position, source in enumerate((dkeys, dvalues)):
            kept = jnp.where(own, source[:, s * LANES : (s + 1) * LANES], 0.0)
            eight = jnp.sum(kept.reshape(4, 8, LANES), axis=0)
            folded = eight + pltpu.roll(eight, 4, axis=0)
            dctx[s, position * CTX : (position + 1) * CTX, :] = folded[0:CTX]


def norm_back_strips(pixels, strip, read_normed, read_grad, gains, inverses, write):
    count = pixels * (C // GROUPS)

    def terms(start):
        found = []
        for b in range(4):
            grad = read_grad(b, start)
            found += [grad, grad * read_normed(b, start)]
        return found

    sums = sum_strips(pixels, strip, 8, terms)
    bias_sums = [column_sum(sums[2 * b]) for b in range(4)]
    gain_sums = [column_sum(sums[2 * b + 1]) for b in range(4)]
    firsts = [
        group_sum(jnp.broadcast_to(bias_sums[b] * gains[b], (8, LANES)) * (1.0 / 8)) * (1.0 / count)
        for b in range(4)
    ]
    seconds = [
        group_sum(jnp.broadcast_to(gain_sums[b] * gains[b], (8, LANES)) * (1.0 / 8)) * (1.0 / count)
        for b in range(4)
    ]

    def body(index, carry):
        start = pl.multiple_of(index * strip, strip)
        for b in range(4):
            normed = read_normed(b, start)
            grad = read_grad(b, start) * gains[b]
            write(b, start, inverses[b] * (grad - firsts[b] - normed * seconds[b]))
        return carry

    lax.fori_loop(0, pixels // strip, body, 0)
    return gain_sums, bias_sums


def kernel_back_attention(
    meta, dqkv, cot, middle, pack, dctx, qkv_weight,
    dmiddle, field, sums, d0, d1, d2, d3, dattn,
):
    pixels = cot.shape[1]
    me = meta[0]
    strip = 128
    clear_padding(field, pixels)
    means, inverses = norm_rows(pixels, strip, lambda b, start: middle[b, pl.ds(start, strip), :])

    def back(index, carry):
        start = pl.multiple_of(index * 512, 512)
        left = jnp.concatenate([dqkv[s, pl.ds(start, 512), :] for s in range(4)], axis=1)
        right = jnp.concatenate(
            [qkv_weight[s, kind * C : (kind + 1) * C, :] for s in range(4) for kind in range(3)], axis=1
        )
        tile = lax.dot_general(left, right, (((1,), (1,)), ((), ())), preferred_element_type=F32)
        for b in range(4):
            dattn[b, pl.ds(start, 512), :] = tile[:, b * LANES : (b + 1) * LANES]
        return carry

    lax.fori_loop(0, pixels // 512, back, 0)
    gains = [pack[b, E_G3 : E_G3 + 1, :] for b in range(4)]

    def read_normed(b, start):
        return (middle[b, pl.ds(start, strip), :] - means[b]) * inverses[b]

    def write(b, start, value):
        total = cot[b, pl.ds(start, strip), :].astype(F32) + value
        dmiddle[b, pl.ds(start, strip), :] = total
        store_shifted(field, b, start, total.astype(BF16).astype(F32))

    gain_sums, bias_sums = norm_back_strips(
        pixels, strip, read_normed, lambda b, start: dattn[b, pl.ds(start, strip), :], gains, inverses, write
    )
    branch = sum_strips(
        pixels,
        strip,
        4,
        lambda start: [
            field[1, b, pl.ds(pl.multiple_of(PAD + start, 32), strip), :].astype(F32) for b in range(4)
        ],
    )
    for b in range(4):
        sums[b] = jnp.zeros((S_ROWS, LANES), F32)
        sums[b, S_G3 : S_G3 + 1, :] = gain_sums[b]
        sums[b, S_B3 : S_B3 + 1, :] = bias_sums[b]
        sums[b, S_CB2 : S_CB2 + 1, :] = column_sum(branch[b])
        sums[b, S_KEY : S_KEY + 8, :] = dctx[b]
    for offset, target in enumerate((d0, d1, d2, d3)):
        target[...] = field[1, jnp.bitwise_xor(me, offset), PAD : PAD + pixels, :]


def kernel_attention_grad(meta, dqkv, mixed, attn_t, cot, keep, send, cot_t):
    pixels = cot.shape[1]
    me = meta[0]
    strip = 128

    def turn(index, carry):
        start = pl.multiple_of(index * strip, strip)
        for b in range(4):
            cot_t[b, :, pl.ds(start, strip)] = cot[b, pl.ds(start, strip), :].astype(F32).T.astype(BF16)
        return carry

    lax.fori_loop(0, pixels // strip, turn, 0)

    def weights(offset, carry):
        s = jnp.bitwise_xor(me, offset)
        place = offset // 2
        attn_all = attn_t[...].reshape(C, pixels)
        cot_all = cot_t[...].reshape(C, pixels)
        grad = jnp.dot(attn_all, dqkv[s], preferred_element_type=F32).astype(BF16)
        other = jnp.dot(cot_all, mixed[s], preferred_element_type=F32).astype(BF16)

        def put(target):
            for kind in range(3):
                target[place, kind] = grad[:, kind * LANES : (kind + 1) * LANES]
            target[place, 3] = other

        @pl.when(offset % 2 == 0)
        def _():
            put(keep)

        @pl.when(offset % 2 == 1)
        def _():
            put(send)

        return carry

    lax.fori_loop(0, 4, weights, 0)


def weight_taps(half, sources, field, target):
    pixels = sources[0].shape[2]

    def body(index, carry):
        left = jnp.concatenate(
            [source[pl.ds(2 * half, 2)].reshape(2 * LANES, pixels) for source in sources], axis=1
        )
        columns = []
        for tap in (2 * index, jnp.minimum(2 * index + 1, 8)):
            start = pl.multiple_of((2 - tap // 3) * SIDE, 32)
            side = 2 - lax.rem(tap, 3)
            columns.append(
                jnp.concatenate([field[side, k, pl.ds(start, pixels), :] for k in range(4)], axis=0)
            )
        grad = jnp.dot(left, jnp.concatenate(columns, axis=1), preferred_element_type=F32)
        target[2 * index] = grad[:, :LANES].astype(target.dtype)

        @pl.when(index < 4)
        def _():
            target[2 * index + 1] = grad[:, LANES:].astype(target.dtype)

        return carry

    lax.fori_loop(0, 5, body, 0)


def kernel_weight_send(meta, u0, u1, u2, u3, d0, d1, d2, d3, send, field):
    pixels = u0.shape[2]
    clear_padding(field, pixels)
    strip = 128

    def spread(index, carry):
        start = pl.multiple_of(index * strip, strip)
        for k, source in enumerate((d0, d1, d2, d3)):
            store_shifted(field, k, start, source[pl.ds(start, strip), :].astype(F32))
        return carry

    lax.fori_loop(0, pixels // strip, spread, 0)
    weight_taps(1 - meta[3], (u0, u1, u2, u3), field, send)


def kernel_weight_own(meta, u0, u1, u2, u3, field, own):
    weight_taps(meta[3], (u0, u1, u2, u3), field, own)


def kernel_back_second(
    meta, grad_field, inner, pack, sums_in, w0, w1, w2, w3, w4, w5, w6, w7,
    field, sums, d0, d1, d2, d3, weight, grad, sems,
):
    pixels = inner.shape[1]
    me = meta[0]
    strip = 128
    weight_copies = fetch_routed((w0, w1, w2, w3, w4, w5, w6, w7), weight, me, meta[2], sems, 0)
    clear_padding(field, pixels)
    means, inverses = norm_rows(pixels, strip, lambda b, start: inner[b, pl.ds(start, strip), :])
    wait_all(weight_copies)

    def write_grad(start, half, tile):
        for b in range(2):
            grad[2 * half + b, pl.ds(start, tile.shape[0]), :] = tile[:, b * LANES : (b + 1) * LANES]

    conv_back_tiles(grad_field, weight, pixels, 512, write_grad)
    gains = [pack[b, E_G2 : E_G2 + 1, :] for b in range(4)]

    def read_normed(b, start):
        return (inner[b, pl.ds(start, strip), :] - means[b]) * inverses[b]

    def slope(index, carry):
        start = pl.multiple_of(index * strip, strip)
        found = []
        for b in range(4):
            bias = pack[b, E_B2 : E_B2 + 1, :]
            scale = pack[b, M_SCALE : M_SCALE + 1, :]
            shift = pack[b, M_SHIFT : M_SHIFT + 1, :]
            shaped = read_normed(b, start) * gains[b] + bias
            modulated = shaped * (1.0 + scale) + shift
            dmod = silu_slope(modulated, grad[b, pl.ds(start, strip), :])
            grad[b, pl.ds(start, strip), :] = dmod * (1.0 + scale)
            found += [dmod * shaped, dmod]
        return tuple(old + fold(new) for old, new in zip(carry, found))

    zero = tuple(jnp.zeros((8, LANES), F32) for _ in range(8))
    modulation = lax.fori_loop(0, pixels // strip, slope, zero)

    def write(b, start, value):
        store_shifted(field, b, start, value)

    gain_sums, bias_sums = norm_back_strips(
        pixels, strip, read_normed, lambda b, start: grad[b, pl.ds(start, strip), :], gains, inverses, write
    )
    for b in range(4):
        sums[b] = sums_in[b]
        sums[b, S_G2 : S_G2 + 1, :] = gain_sums[b]
        sums[b, S_B2 : S_B2 + 1, :] = bias_sums[b]
        sums[b, S_SCALE : S_SCALE + 1, :] = column_sum(modulation[2 * b])
        sums[b, S_SHIFT : S_SHIFT + 1, :] = column_sum(modulation[2 * b + 1])
    for offset, target in enumerate((d0, d1, d2, d3)):
        target[...] = field[1, jnp.bitwise_xor(me, offset), PAD : PAD + pixels, :]


def kernel_back_conv(meta, grad_field, w0, w1, w2, w3, w4, w5, w6, w7, grad, weight, sems):
    pixels = grad.shape[1]
    wait_all(fetch_routed((w0, w1, w2, w3, w4, w5, w6, w7), weight, meta[0], meta[2], sems, 0))

    def write_grad(start, half, tile):
        for b in range(2):
            grad[2 * half + b, pl.ds(start, tile.shape[0]), :] = tile[:, b * LANES : (b + 1) * LANES]

    conv_back_tiles(grad_field, weight, pixels, 512, write_grad)


def kernel_back_first(
    meta, grad_in, image, pack, dmiddle, sums_in, g0, g1, g2, grad, sums,
):
    pixels = image.shape[1]
    me = meta[0]
    strip = 128

    def read(b, start):
        return image[b, pl.ds(start, strip), :].astype(F32)

    means, inverses = norm_rows(pixels, strip, read)
    gains = [pack[b, E_G1 : E_G1 + 1, :] for b in range(4)]

    def read_normed(b, start):
        return (read(b, start) - means[b]) * inverses[b]

    def slope(index, carry):
        start = pl.multiple_of(index * strip, strip)
        for b in range(4):
            before = read_normed(b, start) * gains[b] + pack[b, E_B1 : E_B1 + 1, :]
            grad[b, pl.ds(start, strip), :] = silu_slope(before, grad_in[b, pl.ds(start, strip), :])
        return carry

    lax.fori_loop(0, pixels // strip, slope, 0)

    def write(b, start, value):
        grad[b, pl.ds(start, strip), :] = dmiddle[b, pl.ds(start, strip), :] + value

    gain_sums, bias_sums = norm_back_strips(
        pixels, strip, read_normed, lambda b, start: grad[b, pl.ds(start, strip), :], gains, inverses, write
    )
    for b in range(4):
        sums[b] = sums_in[b]
        sums[b, S_G1 : S_G1 + 1, :] = gain_sums[b]
        sums[b, S_B1 : S_B1 + 1, :] = bias_sums[b]
    for offset, target in enumerate((g0, g1, g2.at[0], g2.at[1])):
        other = jnp.bitwise_xor(me, offset)
        target[0:pixels, :] = grad[other].astype(BF16)
        target[pixels : pixels + S_ROWS, :] = sums[other].astype(BF16)


def kernel_scale(factors0, factors1, scale):
    total = jnp.zeros((1, LANES), F32)
    for factors in (factors0, factors1):
        for g in range(factors.shape[0]):
            total = total + factors[g, 0].astype(F32)[1:2, 0:LANES]
    scale[...] = jnp.broadcast_to(1.0 / total, (8, LANES))


def kernel_factors(meta, factors0, factors1, left):
    conditions, tokens = [], []
    for factors in (factors0, factors1):
        for g in range(factors.shape[0]):
            for k in range(4):
                rows = factors[g, jnp.bitwise_xor(meta[0], k)].astype(F32)
                conditions.append(rows[0:1])
                tokens.append(rows[CTX : 2 * CTX])
    rest = left.shape[1] - 5 * len(conditions)
    rows = tokens + conditions
    if rest:
        rows.append(jnp.zeros((rest, EMB), F32))
    left[...] = jnp.concatenate(rows, axis=0).T.astype(BF16)


def kernel_factor_grads(scale, left, small0, small1, embed, context, vectors):
    inverse = scale[0:1, :]
    total = jnp.zeros((S_ROWS, LANES), F32)
    scales, shifts, keys, values = [], [], [], []
    for small in (small0, small1):
        for k in range(small.shape[0]):
            term = small[k].astype(F32)
            total = total + term
            scales.append(term[S_SCALE : S_SCALE + 1])
            shifts.append(term[S_SHIFT : S_SHIFT + 1])
            keys.append(term[S_KEY : S_KEY + CTX])
            values.append(term[S_VALUE : S_VALUE + CTX])
    vectors[...] = total * inverse
    images = len(scales)
    rest = left.shape[1] - 5 * images
    none = jnp.zeros((4 * images, LANES), F32)
    columns = []
    for parts in (keys, values):
        whole = [jnp.concatenate(parts, axis=0), jnp.zeros((images + rest, LANES), F32)]
        columns.append(jnp.concatenate(whole, axis=0))
    for parts in (scales, shifts):
        whole = [none] + parts
        if rest:
            whole.append(jnp.zeros((rest, LANES), F32))
        columns.append(jnp.concatenate(whole, axis=0))
    right = jnp.concatenate(columns, axis=1).astype(BF16)
    grad = jnp.dot(left[...], right, preferred_element_type=F32)
    for place in range(2):
        context[:, place, :] = grad[:, place * LANES : (place + 1) * LANES] * inverse
        embed[:, place, :] = grad[:, (place + 2) * LANES : (place + 3) * LANES] * inverse


def kernel_stack(*refs):
    whole = refs[-1]
    base = 0
    for ref in refs[:-1]:
        count = ref.shape[0]
        whole[base : base + count] = ref[...]
        base += count


def stack(parts):
    shape = (sum(part.shape[0] for part in parts),) + parts[0].shape[1:]
    return call(
        kernel_stack, "stack", struct(shape, parts[0].dtype), [vmem()] * len(parts), [], limit=12
    )(*parts)


def kernel_slots(meta, own, near, far, across, whole, sems):
    rows = pl.ds(0, whole.shape[1])
    sources = (own.at[rows], near.at[rows], far.at[0, rows], across.at[1, rows])
    wait_all(fetch(sources, whole, meta[0], sems, 0))


def kernel_cut(source, first, second):
    rows = first.shape[0]
    first[...] = source[0:rows]
    second[...] = source[rows : 2 * rows]


def cut(source):
    rows, lanes = source.shape
    return call(
        kernel_cut, "cut", [struct((rows // 2, lanes), BF16)] * 2, [vmem()], [], limit=8
    )(source)


def kernel_small_stack(own, near, far, across, whole):
    rows = pl.ds(own.shape[0] - S_ROWS, S_ROWS)
    whole[0] = own[rows, :]
    whole[1] = near[rows, :]
    whole[2] = far[0, rows, :]
    whole[3] = across[1, rows, :]


def kernel_split(counts, width, digit, meta, *refs):
    parts = refs[sum(counts) :]
    rows = parts[0].shape[1]
    for offset, part in enumerate(parts):
        start = pl.multiple_of(jnp.bitwise_xor(meta[digit], offset) * rows, rows)
        position, base = 0, 0
        for count in counts:
            terms = refs[position : position + count]
            terms = [term.at[0] if len(term.shape) == 4 else term for term in terms]
            total = terms[0][:, pl.ds(start, rows), :].astype(F32)
            for term in terms[1:]:
                total = total + term[:, pl.ds(start, rows), :].astype(F32)
            part[base : base + total.shape[0]] = total.astype(part.dtype)
            position += count
            base += total.shape[0]


def split_sum(groups, width, digit, meta):
    blocks = sum(terms[-1].shape[0] for terms in groups)
    rows = groups[0][-1].shape[1]
    flat = [term for terms in groups for term in terms]
    shape = (blocks, rows // width, LANES)
    return call(
        functools.partial(kernel_split, tuple(len(terms) for terms in groups), width, digit),
        "split_sum",
        [struct(shape, F32)] + [struct(shape, BF16)] * (width - 1),
        [smem()] + [vmem()] * len(flat),
        [],
        limit=12,
    )(meta, *flat)


def kernel_far(mine, got, own, far):
    blocks = own.shape[0]
    own[...] = mine[0:blocks] + got[0:blocks].astype(F32)
    far[...] = (mine[blocks : 2 * blocks] + got[blocks : 2 * blocks].astype(F32)).astype(BF16)


def kernel_total(*refs):
    total = refs[0][...].astype(F32)
    for term in refs[1:-1]:
        total = total + term[...].astype(F32)
    refs[-1][...] = total.astype(BF16)


def total_sum(terms):
    return call(
        kernel_total, "total_sum", struct(terms[0].shape, BF16), [vmem()] * len(terms), [], limit=12
    )(*terms)


def kernel_join(digit, meta, *refs):
    parts, whole = refs[:-1], refs[-1]
    rows = parts[0].shape[1]
    for offset, part in enumerate(parts):
        start = pl.multiple_of(jnp.bitwise_xor(meta[digit], offset) * rows, rows)
        whole[:, pl.ds(start, rows), :] = part[...]


def join(parts, digit, meta):
    blocks, rows, _ = parts[0].shape
    return call(
        functools.partial(kernel_join, digit),
        "join",
        struct((blocks, rows * len(parts), LANES), BF16),
        [smem()] + [vmem()] * len(parts),
        [],
        limit=12,
    )(meta, *parts)


def kernel_last(digit, meta, scale, mine, other, conv, *more):
    rows = mine.shape[1]
    for offset, part in enumerate((mine, other)):
        start = pl.multiple_of(jnp.bitwise_xor(meta[digit], offset) * rows, rows)
        count = conv.shape[0]
        conv[:, pl.ds(start, rows), :] = part[0:count].astype(F32) * scale[0:1, :]
        for proj in more:
            proj[:, pl.ds(start, rows)] = (part[count].astype(F32) * scale[0:1, :]).T


def last_join(pair, digit, meta, scale, more=False):
    blocks, rows, _ = pair[0].shape
    shapes = [struct((3 if more else blocks, 2 * rows, LANES), F32)]
    if more:
        shapes.append(struct((LANES, 2 * rows), F32))
    return call(
        functools.partial(kernel_last, digit),
        "last_join",
        shapes,
        [smem()] + [vmem()] * 3,
        [],
        limit=12,
    )(meta, scale, *pair)


def swap(value, axis, offset):
    size = lax.axis_size(axis)
    return lax.ppermute(value, axis, [(i, i ^ offset) for i in range(size)])


def tie(*values):
    return lax.optimization_barrier(values)


def share(shard):
    near = swap(shard, "mp", 1)
    far = swap(shard, "mp", 2)
    return shard, near, far, swap(far, "mp", 1)


def exchange(pieces):
    return (pieces[0],) + tuple(swap(pieces[k], "mp", k) for k in range(1, 4))


def pick(stack, me):
    return [lax.dynamic_index_in_dim(stack, me ^ k, 0, keepdims=False) for k in range(4)]


def pick_pair(stack, me):
    own = lax.dynamic_index_in_dim(stack, me, 0, keepdims=False)
    near = lax.dynamic_index_in_dim(stack, me ^ 1, 0, keepdims=False)
    far = [lax.dynamic_index_in_dim(stack, me ^ k, 0, keepdims=True) for k in (2, 3)]
    return own, near, jnp.concatenate(far, axis=0)


def dp_levels(size):
    return [(1 << k, 2) for k in range(size.bit_length() - 1)]


def bits(size):
    return [1 << k for k in range(size.bit_length() - 1)]


def local(
    image_in,
    out_cotangent,
    timesteps,
    clip_embed,
    context_tokens,
    image_count,
    norm1_gain,
    norm1_bias,
    conv1_weight,
    embed_weight,
    norm2_gain,
    norm2_bias,
    conv2_weight,
    conv2_bias,
    norm3_gain,
    norm3_bias,
    qkv_weight,
    context_weight,
    proj_weight,
):
    slots, pixels, width = image_in.shape
    me = lax.axis_index("mp")
    group = lax.axis_index("dp")
    parity = (group ^ (group >> 1)) & 1
    levels = dp_levels(lax.axis_size("dp"))
    own_digits = [(group >> (low.bit_length() - 1)) & (wide - 1) for low, wide in levels]
    meta = jnp.stack(
        [me, (me < image_count[0]).astype(jnp.int32), parity] + own_digits
    ).astype(jnp.int32)
    digits = range(3, 3 + len(levels))
    steps = bits(lax.axis_size("dp"))

    conv1_weight, conv2_weight, image_in, out_cotangent, meta = tie(
        conv1_weight, conv2_weight, image_in, out_cotangent, meta
    )

    conv1_shard = conv1_weight.reshape(9 * C, LANES)

    def half_of(shard):
        rows = shard.shape[0] // 2
        return lax.dynamic_slice_in_dim(shard, parity * rows, rows, axis=0)

    half1, image_in = tie(half_of(conv1_shard), image_in)
    half1 = swap(half1, "mp", 2)
    near1 = swap(conv1_shard, "mp", 1)
    images = pick_pair(image_in, me)
    image_near = swap(images[1], "mp", 1)
    image_far = swap(images[2], "mp", 2)

    half_width = EMB // 2
    frequency = jnp.exp(-math.log(10000.0) * jnp.arange(half_width, dtype=F32) / half_width)
    angles = timesteps.astype(F32)[:, None] * frequency[None, :]
    condition = jax.nn.silu(
        jnp.concatenate([jnp.cos(angles), jnp.sin(angles)], axis=1) + clip_embed.astype(F32)
    ).astype(BF16)
    scale_shift = jnp.dot(
        condition, embed_weight.reshape(EMB, 2 * LANES), preferred_element_type=F32
    ).reshape(slots, 1, 2 * LANES)
    doubled = jnp.concatenate([context_tokens, context_tokens], axis=1)
    context = jnp.dot(
        doubled.reshape(slots * 2 * CTX, EMB),
        context_weight.reshape(EMB, 2 * LANES),
        preferred_element_type=F32,
    ).astype(BF16).astype(F32).reshape(slots, 2 * CTX, 2 * LANES)
    vectors = [norm1_gain, norm1_bias, norm2_gain, norm2_bias, conv2_bias, norm3_gain, norm3_bias]
    early = struct((E_ROWS, LANES), F32)
    packs = call(
        kernel_early,
        "early",
        [early, early, struct((2, E_ROWS, LANES), F32)],
        [smem()] + [vmem()] * 9,
        [],
        limit=8,
    )(meta, scale_shift, context, *[vector[None] for vector in vectors])
    count_rows = jnp.broadcast_to(image_count.astype(BF16)[:, None, None], (slots, CTX - 1, EMB))
    factors = jnp.concatenate([condition[:, None], count_rows, context_tokens], axis=1)[None]
    cots = pick(out_cotangent, me)
    rest_shard = jnp.concatenate(
        [
            conv2_weight.reshape(9 * C, LANES),
            jnp.transpose(qkv_weight, (1, 0, 2)).reshape(3 * C, LANES),
            jnp.transpose(proj_weight.reshape(LANES, 4, LANES), (1, 0, 2)).reshape(C, LANES),
        ],
        axis=0,
    )
    rest_half = half_of(rest_shard)

    def relayed(shard, near, half):
        by_x, by_z = cut(half)
        by_x = swap(by_x, "dp", 1)
        by_z = swap(by_z, "dp", 2)
        return (shard, near, half, by_x, by_z) + tuple(
            swap(part, "mp", 1) for part in (half, by_x, by_z)
        )

    near1, image_near, packs, half1 = tie(near1, image_near, packs, half1)
    pack_near = swap(packs[1], "mp", 1)
    pack_far = swap(packs[2], "mp", 2)
    conv1 = relayed(conv1_shard, near1, half1)
    image_far, pack_near, pack_far, rest_shard, rest_half, factors, cots, *conv1 = tie(
        image_far, pack_near, pack_far, rest_shard, rest_half, factors, cots, *conv1
    )
    images = (images[0], image_near, image_far, swap(image_far, "mp", 1))
    packs = (packs[0], pack_near, pack_far, swap(pack_far, "mp", 1))
    rest_half = swap(rest_half, "mp", 2)
    rest_near = swap(rest_shard, "mp", 1)
    factors = [factors, swap(factors, "dp", 1)]

    block = struct((4, pixels, LANES), BF16)
    block32 = struct((4, pixels, LANES), F32)
    turned = struct((4, LANES, pixels), BF16)
    fields = struct((3, 4, pixels + 2 * PAD, LANES), BF16)
    piece = struct((pixels, LANES), BF16)
    pair_piece = struct((2, pixels, LANES), BF16)
    field_scratch = pltpu.VMEM((3, 4, pixels + 2 * PAD, LANES), BF16)
    conv_scratch = pltpu.VMEM((4, 9 * C, LANES), BF16)
    rest_scratch = pltpu.VMEM((4, PROJ_ROW + C, LANES), BF16)
    grad_scratch = pltpu.VMEM((4, pixels, LANES), F32)

    image, pack, first_t, inner, second_t, second = call(
        kernel_first,
        "first",
        [block, struct((4, E_ROWS, LANES), F32), turned, block32, turned, fields],
        [smem()] + [anywhere()] * 16,
        [field_scratch, conv_scratch, pltpu.SemaphoreType.DMA((16,))],
        limit=17,
    )(meta, *images, *packs, *conv1)

    second, rest_half, rest_near, factors = tie(second, rest_half, rest_near, factors)
    rest = relayed(rest_shard, rest_near, rest_half)
    cots = exchange(cots)
    second, *rest = tie(second, *rest)
    factors = stack(factors)
    factors = [factors, swap(factors, "dp", 2)]
    middle, attn_t, qkv, qkv_w, proj_w = call(
        kernel_second,
        "second",
        [
            block32,
            turned,
            struct((4, pixels, 3 * LANES), BF16),
            struct((4, 3 * C, LANES), BF16),
            struct((4, C, LANES), BF16),
        ],
        [smem()] + [vmem()] * 3 + [anywhere()] * 8,
        [rest_scratch, pltpu.VMEM((4, pixels, LANES), BF16), pltpu.SemaphoreType.DMA((8,))],
        limit=17,
    )(meta, second, image, pack, *rest)
    ctx_scratch = pltpu.VMEM((pixels, LANES), F32)
    turned_scratch = pltpu.VMEM((LANES, pixels), F32)
    qkv, first_t, second_t, factors, cots = tie(qkv, first_t, second_t, factors, cots)
    factors = stack(factors)
    second_y = swap(second_t, "mp", 2)
    first_y = swap(first_t, "mp", 2)
    second_c = swap(second_t, "mp", 1)
    first_c = swap(first_t, "mp", 1)
    for low in steps[2:-1]:
        factors = stack([factors, swap(factors, "dp", low)])
    factors = (factors, swap(factors, "dp", steps[-1]))
    out_own, out_near, out_far, cot, mixed, dqkv, dctx = call(
        kernel_attention,
        "attention",
        [piece, piece, pair_piece]
        + [block, block, struct((4, pixels, 3 * LANES), BF16), struct((4, 2 * CTX, LANES), F32)],
        [smem()] + [vmem()] * 4 + [anywhere()] * 4,
        [
            pltpu.VMEM((4, pixels, LANES), BF16),
            ctx_scratch,
            ctx_scratch,
            ctx_scratch,
            ctx_scratch,
            grad_scratch,
            grad_scratch,
            turned_scratch,
            turned_scratch,
            pltpu.SemaphoreType.DMA((4,)),
        ],
        limit=30,
    )(meta, qkv, pack, middle, proj_w, *cots)

    def weight_send(sources, gradients):
        return call(
            kernel_weight_send,
            "weight_send",
            [struct((9, C // 2, LANES), BF16), fields],
            [smem()] + [vmem()] * 8,
            [],
            limit=16,
        )(meta, *sources, *gradients)

    def weight_own(sources, field):
        return call(
            kernel_weight_own,
            "weight_own",
            struct((9, C // 2, LANES), F32),
            [smem()] + [vmem()] * 5,
            [],
            limit=16,
        )(meta, *sources, field)

    def down(terms, level):
        own, send = split_sum([terms], 2, digits[level], meta)
        return [own, swap(send, "dp", levels[level][0])]

    def across(value, level):
        return [value, swap(value, "dp", levels[level][0])]

    def inner_levels(terms):
        for level in range(3, len(levels)):
            terms = down(terms, level)
        value = total_sum(terms)
        for level in range(len(levels) - 1, 2, -1):
            value = join(across(value, level), digits[level], meta)
        return value

    att_keep, att_send = call(
        kernel_attention_grad,
        "attention_grad",
        [struct((2, 4, C, LANES), BF16)] * 2,
        [smem()] + [vmem()] * 4,
        [pltpu.VMEM((4, LANES, pixels), BF16)],
    )(meta, dqkv, mixed, attn_t, cot)
    dqkv, att_send, second_y, second_c, factors = tie(dqkv, att_send, second_y, second_c, factors)
    second_d = swap(second_y, "mp", 1)
    att = [att_keep.reshape(8, C, LANES), swap(att_send, "mp", 1).reshape(8, C, LANES)]
    dmiddle, field2, sums, *gradients2 = call(
        kernel_back_attention,
        "back_attention",
        [block32, fields, struct((4, S_ROWS, LANES), F32)] + [piece] * 4,
        [smem()] + [vmem()] * 6,
        [grad_scratch],
    )(meta, dqkv, cot, middle, pack, dctx, qkv_w)
    gradients2, second_d, first_y, first_c, att, field2 = tie(
        gradients2, second_d, first_y, first_c, att, field2
    )
    first_d = swap(first_y, "mp", 1)
    seconds = (second_t, second_c, second_y, second_d)
    gradients2 = exchange(gradients2)
    att = down(att, 0)
    field2, att[0] = tie(field2, att[0])
    field1, sums, *gradients1 = call(
        kernel_back_second,
        "back_second",
        [fields, struct((4, S_ROWS, LANES), F32)] + [piece] * 4,
        [smem()] + [vmem()] * 4 + [anywhere()] * 8,
        [rest_scratch, grad_scratch, pltpu.SemaphoreType.DMA((8,))],
        limit=20,
    )(meta, field2, inner, pack, sums, *rest)
    gradients1, gradients2, att, first_d = tie(gradients1, gradients2, att, first_d)
    firsts = (first_t, first_c, first_y, first_d)
    gradients1 = exchange(gradients1)
    att = down(att, 1)
    gradients2, att[0] = tie(gradients2, att[0])
    send2, wide2 = weight_send(seconds, gradients2)
    got2 = swap(send2, "dp", 1)
    wide2, att = tie(wide2, att)
    att = down(att, 2)
    wide2, att[0] = tie(wide2, att[0])
    own2 = weight_own(seconds, wide2)
    own2, att, field1 = tie(own2, att, field1)
    for level in range(3, len(levels)):
        att = down(att, level)
    att_own, att_far = call(
        kernel_far,
        "att_far",
        [struct((4,) + att[0].shape[1:], F32), struct((4,) + att[0].shape[1:], BF16)],
        [vmem()] * 2,
        [],
        limit=12,
    )(*att)
    field1, att_own = tie(field1, att_own)
    att = [att_own, swap(att_far, "mp", 2)]
    grad_first = call(
        kernel_back_conv,
        "back_conv",
        block32,
        [smem()] + [vmem()] + [anywhere()] * 8,
        [conv_scratch, pltpu.SemaphoreType.DMA((8,))],
    )(meta, field1, *conv1)
    grad_first, gradients1, att = tie(grad_first, gradients1, att)
    att = total_sum(att)
    for level in range(len(levels) - 1, 2, -1):
        att = join(across(att, level), digits[level], meta)
    gradients1, att, out_far = tie(gradients1, att, out_far)
    att = across(att, 2)
    send1, wide1 = weight_send(firsts, gradients1)
    got1 = swap(send1, "dp", 1)
    out_far = swap(out_far, "mp", 2)
    wide1, got2, own2 = tie(wide1, got2, own2)
    terms2 = down([own2, got2], 1)
    wide1, terms2[0] = tie(wide1, terms2[0])
    own1 = weight_own(firsts, wide1)
    grad_first, own1, terms2, att = tie(grad_first, own1, terms2, att)
    terms2 = down(terms2, 2)
    att = across(join(att, digits[2], meta), 1)
    grad_first, terms2[0], att[0] = tie(grad_first, terms2[0], att[0])
    grad_own, grad_near, grad_far = call(
        kernel_back_first,
        "back_first",
        [
            struct((pixels + S_ROWS, LANES), BF16),
            struct((pixels + S_ROWS, LANES), BF16),
            struct((2, pixels + S_ROWS, LANES), BF16),
        ],
        [smem()] + [vmem()] * 5,
        [grad_scratch, pltpu.VMEM((4, S_ROWS, LANES), F32)],
    )(meta, grad_first, image, pack, dmiddle, sums)
    grad_far, terms2, got1, own1 = tie(grad_far, terms2, got1, own1)
    terms1 = down([own1, got1], 1)
    ends2 = across(inner_levels(terms2), 2)
    factors, ends2[0], terms1[0] = tie(factors, ends2[0], terms1[0])
    columns = -(-5 * slots * lax.axis_size("dp") // LANES) * LANES
    left = call(
        kernel_factors,
        "factors",
        struct((EMB, columns), BF16),
        [smem()] + [vmem()] * 2,
        [],
        limit=12 if len(steps) < 4 else 56,
    )(meta, *factors)
    grad_far, ends2[0], terms1[0], att, left = tie(grad_far, ends2[0], terms1[0], att, left)
    att = across(join(att, digits[1], meta), 0)
    grad_far = swap(grad_far, "mp", 2)
    ends2, terms1, grad_near, out_far = tie(ends2, terms1, grad_near, out_far)
    terms1 = down(terms1, 2)
    ends2 = across(join(ends2, digits[2], meta), 1)
    scale = call(kernel_scale, "scale", struct((8, LANES), F32), [vmem()] * 2, [], limit=8)(*factors)
    ends2, terms1, scale, att = tie(ends2, terms1, scale, att)
    ends1 = across(inner_levels(terms1), 2)
    ends2 = across(join(ends2, digits[1], meta), 0)
    qkv_grad, proj_grad = last_join(att, digits[0], meta, scale, True)
    ends1, qkv_grad, grad_near = tie(ends1, qkv_grad, grad_near)
    ends1 = across(join(ends1, digits[2], meta), 1)
    ends1[0], grad_near, grad_far = tie(ends1[0], grad_near, grad_far)
    grad_near = swap(grad_near, "mp", 1)
    grad_across = swap(grad_far, "mp", 1)
    image_parts = (grad_own, grad_near, grad_far, grad_across)
    smalls = call(
        kernel_small_stack,
        "stack",
        struct((4, S_ROWS, LANES), BF16),
        [vmem()] * 4,
        [],
        limit=8,
    )(grad_own, grad_near, grad_far, grad_across)
    small_got = swap(smalls, "dp", 1)
    ends1 = across(join(ends1, digits[1], meta), 0)
    ends1[0], small_got, ends2 = tie(ends1[0], small_got, ends2)
    smalls = stack([smalls, small_got])
    for low in steps[1:-1]:
        smalls = stack([smalls, swap(smalls, "dp", low)])
    small_got = swap(smalls, "dp", steps[-1])
    (conv2_grad,) = last_join(ends2, digits[0], meta, scale)
    smalls, out_far, out_near, conv2_grad = tie(smalls, out_far, out_near, conv2_grad)
    out_parts = (out_own, swap(out_near, "mp", 1), out_far, swap(out_far, "mp", 1))
    def in_slots(parts):
        return pl.pallas_call(
            kernel_slots,
            name="slots",
            out_shape=struct((4, pixels, LANES), BF16),
            in_specs=[smem()] + [anywhere()] * 4,
            out_specs=vmem(),
            scratch_shapes=[pltpu.SemaphoreType.DMA((4,))],
            compiler_params=pltpu.CompilerParams(vmem_limit_bytes=8 * MIB),
        )(meta, *parts)

    block_out = in_slots(out_parts)
    image_grad = in_slots(image_parts)
    small_got, block_out, image_grad = tie(small_got, block_out, image_grad)
    embed_grad, context_grad, vector_sums = call(
        kernel_factor_grads,
        "factor_grads",
        [
            struct((EMB, 2, LANES), F32),
            struct((EMB, 2, LANES), F32),
            struct((S_ROWS, LANES), F32),
        ],
        [vmem()] * 4,
        [],
        limit=14 if len(steps) < 4 else 56,
    )(scale, left, smalls, small_got)

    ends1, embed_grad = tie(ends1, embed_grad)
    (conv1_grad,) = last_join(ends1, digits[0], meta, scale)
    return (
        block_out,
        image_grad,
        vector_sums[S_G1],
        vector_sums[S_B1],
        conv1_grad.reshape(3, 3, C, LANES),
        embed_grad,
        vector_sums[S_G2],
        vector_sums[S_B2],
        conv2_grad.reshape(3, 3, C, LANES),
        vector_sums[S_CB2],
        vector_sums[S_G3],
        vector_sums[S_B3],
        jnp.transpose(qkv_grad, (1, 0, 2)),
        context_grad,
        proj_grad,
    )


def solution(mesh):
    return jax.shard_map(
        local,
        mesh=mesh,
        in_specs=(
            P("dp", None, "mp"),
            P("dp", None, "mp"),
            P("dp"),
            P("dp", None),
            P("dp", None, None),
            P("dp"),
            P("mp"),
            P("mp"),
            P(None, None, None, "mp"),
            P(None, None, "mp"),
            P("mp"),
            P("mp"),
            P(None, None, None, "mp"),
            P("mp"),
            P("mp"),
            P("mp"),
            P(None, None, "mp"),
            P(None, None, "mp"),
            P("mp", None),
        ),
        out_specs=(
            P("dp", None, "mp"),
            P("dp", None, "mp"),
            P("mp"),
            P("mp"),
            P(None, None, None, "mp"),
            P(None, None, "mp"),
            P("mp"),
            P("mp"),
            P(None, None, None, "mp"),
            P("mp"),
            P("mp"),
            P("mp"),
            P(None, None, "mp"),
            P(None, None, "mp"),
            P("mp", None),
        ),
        check_vma=False,
    )
```

```python
import functools
import math

import jax
import jax.numpy as jnp
from jax import lax
from jax.experimental import pallas as pl
from jax.experimental.pallas import tpu as pltpu
from jax.sharding import PartitionSpec as P

C = 512
GROUPS = 32
HEAD = 64
EMB = 2048
CTX = 4
SIDE = 32
LANES = 128
PAD = SIDE
EPSILON = 1e-05
F32 = jnp.float32
BF16 = jnp.bfloat16
NEG = -1e30
QKV_ROW = 9 * C
PROJ_ROW = QKV_ROW + 3 * C

E_G1, E_B1, E_G2, E_B2, E_CB2, E_G3, E_B3, M_SCALE, M_SHIFT = range(9)
M_KEY, M_VALUE, E_ROWS = 16, 24, 32
S_G3, S_B3, S_CB2, S_G2, S_B2, S_SCALE, S_SHIFT = range(7)
S_KEY, S_VALUE, S_G1, S_B1, S_ROWS = 8, 12, 16, 17, 32
MIB = 1 << 20


def vmem():
    return pl.BlockSpec(memory_space=pltpu.VMEM)


def anywhere():
    return pl.BlockSpec(memory_space=pltpu.HBM)


def smem():
    return pl.BlockSpec(memory_space=pltpu.SMEM)


def struct(shape, dtype):
    return jax.ShapeDtypeStruct(shape, dtype)


def call(body, name, out_shape, in_specs, scratch, flops=0, limit=14):
    many = isinstance(out_shape, (list, tuple))
    return pl.pallas_call(
        body,
        name=name,
        out_shape=out_shape,
        in_specs=in_specs,
        out_specs=[vmem() for _ in out_shape] if many else vmem(),
        scratch_shapes=scratch,
        compiler_params=pltpu.CompilerParams(vmem_limit_bytes=limit * MIB),
        cost_estimate=pl.CostEstimate(flops=0, transcendentals=0, bytes_accessed=0),
    )


def fetch(sources, target, me, sems, first):
    copies = []
    for offset, source in enumerate(sources):
        copy = pltpu.make_async_copy(
            source, target.at[jnp.bitwise_xor(me, offset)], sems.at[first + offset]
        )
        copy.start()
        copies.append(copy)
    return copies


def fetch_routed(sources, target, me, parity, sems, first):
    quarter = target.shape[1] // 4
    copies = []
    for index, source in enumerate(sources):
        place = target.at[jnp.bitwise_xor(me, (0, 1, 2, 2, 2, 3, 3, 3)[index])]
        if index >= 2:
            kind = (index - 2) % 3
            rows = 2 * quarter if kind == 0 else quarter
            half = parity if kind == 0 else 1 - parity
            start = half * 2 * quarter + (quarter if kind == 2 else 0)
            place = place.at[pl.ds(pl.multiple_of(start, quarter), rows), :]
        copy = pltpu.make_async_copy(source, place, sems.at[first + index])
        copy.start()
        copies.append(copy)
    return copies


def wait_all(copies):
    for copy in copies:
        copy.wait()


def fold(values):
    rows = values.shape[0]
    return jnp.sum(values.reshape(rows // 8, 8, values.shape[1]), axis=0)


def group_sum(rows8):
    lane = lax.broadcasted_iota(jnp.int32, rows8.shape, 1)
    total = jnp.broadcast_to(jnp.sum(rows8, axis=0, keepdims=True), rows8.shape)
    for step in (1, 2, 4, 8):
        up = pltpu.roll(total, step, axis=1)
        down = pltpu.roll(total, LANES - step, axis=1)
        total = total + jnp.where((lane & step) != 0, up, down)
    return total[0:1]


def column_sum(rows8):
    return jnp.sum(rows8, axis=0, keepdims=True)


def sum_strips(pixels, strip, width, function):
    zero = tuple(jnp.zeros((8, LANES), F32) for _ in range(width))

    def body(index, carry):
        start = pl.multiple_of(index * strip, strip)
        return tuple(old + fold(new) for old, new in zip(carry, function(start)))

    return lax.fori_loop(0, pixels // strip, body, zero)


def norm_rows(pixels, strip, read):
    count = pixels * (C // GROUPS)
    sums = sum_strips(pixels, strip, 4, lambda start: [read(b, start) for b in range(4)])
    means = [group_sum(s) * (1.0 / count) for s in sums]
    squares = sum_strips(
        pixels,
        strip,
        4,
        lambda start: [jnp.square(read(b, start) - means[b]) for b in range(4)],
    )
    inverses = [lax.rsqrt(group_sum(s) * (1.0 / count) + EPSILON) for s in squares]
    return means, inverses


def shifted(values):
    rows = values.shape[0]
    column = lax.broadcasted_iota(jnp.int32, values.shape, 0) & (SIDE - 1)
    left = jnp.where(column == 0, 0.0, pltpu.roll(values, 1, axis=0))
    right = jnp.where(column == SIDE - 1, 0.0, pltpu.roll(values, rows - 1, axis=0))
    return left, values, right


def store_shifted(target, block, start, values):
    rows = values.shape[0]
    for position, part in enumerate(shifted(values)):
        target[position, block, pl.ds(pl.multiple_of(PAD + start, 32), rows), :] = part.astype(BF16)


def clear_padding(target, pixels):
    zero = jnp.zeros((PAD, LANES), BF16)
    for position in range(3):
        for block in range(4):
            target[position, block, 0:PAD, :] = zero
            target[position, block, PAD + pixels : PAD + pixels + PAD, :] = zero


def conv_tiles(field, weight, pixels, tile, write):
    def body(index, carry):
        start = pl.multiple_of(index * tile, tile)
        left = jnp.concatenate(
            [
                field[b, block, pl.ds(pl.multiple_of(start + a * SIDE, 32), tile), :]
                for a in range(3)
                for b in range(3)
                for block in range(4)
            ],
            axis=1,
        )
        right = jnp.concatenate([weight[s, 0 : 9 * C, :] for s in range(4)], axis=1)
        write(start, jnp.dot(left, right, preferred_element_type=F32))
        return carry

    lax.fori_loop(0, pixels // tile, body, 0)


def conv_back_tiles(field, weight, pixels, tile, write):
    def body(index, carry):
        start = pl.multiple_of((index // 2) * tile, tile)
        half = index % 2
        left = jnp.concatenate(
            [
                field[2 - b, block, pl.ds(pl.multiple_of(start + (2 - a) * SIDE, 32), tile), :]
                for a in range(3)
                for b in range(3)
                for block in range(4)
            ],
            axis=1,
        )
        right = jnp.concatenate(
            [
                weight[block, pl.ds(pl.multiple_of((3 * a + b) * C + half * 256, 256), 256), :]
                for a in range(3)
                for b in range(3)
                for block in range(4)
            ],
            axis=1,
        )
        write(
            start,
            half,
            lax.dot_general(left, right, (((1,), (1,)), ((), ())), preferred_element_type=F32),
        )
        return carry

    lax.fori_loop(0, 2 * (pixels // tile), body, 0)


def silu_slope(before, grad_out):
    gate = jax.nn.sigmoid(before)
    return grad_out * gate * (1.0 + before * (1.0 - gate))


def kernel_early(meta, scale_shift, context, v0, v1, v2, v3, v4, v5, v6, own, near, far):
    for offset, target in enumerate((own, near, far.at[0], far.at[1])):
        slot = jnp.bitwise_xor(meta[0], offset)
        target[...] = jnp.zeros((E_ROWS, LANES), F32)
        for row, vector in enumerate((v0, v1, v2, v3, v4, v5, v6)):
            target[row : row + 1, :] = vector[...]
        scales = scale_shift[slot]
        target[M_SCALE : M_SCALE + 1, :] = scales[:, :LANES]
        target[M_SHIFT : M_SHIFT + 1, :] = scales[:, LANES:]
        tokens = context[slot]
        target[M_KEY : M_KEY + 8, :] = tokens[:, :LANES]
        target[M_VALUE : M_VALUE + 8, :] = tokens[:, LANES:]


def kernel_first(
    meta, i0, i1, i2, i3, e0, e1, e2, e3, w0, w1, w2, w3, w4, w5, w6, w7,
    image, pack, first_t, inner, second_t, second, weight, stats, field, sems,
):
    pixels = image.shape[1]
    me = meta[0]
    image_copies = fetch((i0, i1, i2.at[0], i3.at[1]), image, me, sems, 0)
    pack_copies = fetch((e0, e1, e2.at[0], e3.at[1]), pack, me, sems, 4)
    weight_copies = fetch_routed((w0, w1, w2, w3, w4, w5, w6, w7), weight, me, meta[2], sems, 8)
    clear_padding(field, pixels)
    clear_padding(second, pixels)
    wait_all(image_copies)
    wait_all(pack_copies)
    strip = 128

    def read(block, start):
        return image[block, pl.ds(start, strip), :].astype(F32)

    means, inverses = norm_rows(pixels, strip, read)

    def normalise(index, carry):
        start = pl.multiple_of(index * strip, strip)
        for b in range(4):
            gain = pack[b, E_G1 : E_G1 + 1, :]
            bias = pack[b, E_B1 : E_B1 + 1, :]
            before = (read(b, start) - means[b]) * inverses[b] * gain + bias
            after = before * jax.nn.sigmoid(before)
            store_shifted(field, b, start, after)
            first_t[b, :, pl.ds(start, strip)] = after.T.astype(BF16)
        return carry

    lax.fori_loop(0, pixels // strip, normalise, 0)
    wait_all(weight_copies)

    def write(start, tile):
        for b in range(4):
            inner[b, pl.ds(start, tile.shape[0]), :] = tile[:, b * LANES : (b + 1) * LANES]

    conv_tiles(field, weight, pixels, 512, write)
    means2, inverses2 = norm_rows(pixels, strip, lambda b, start: inner[b, pl.ds(start, strip), :])

    def modulate(index, carry):
        start = pl.multiple_of(index * strip, strip)
        for b in range(4):
            gain = pack[b, E_G2 : E_G2 + 1, :]
            bias = pack[b, E_B2 : E_B2 + 1, :]
            scale = pack[b, M_SCALE : M_SCALE + 1, :]
            shift = pack[b, M_SHIFT : M_SHIFT + 1, :]
            normed = (inner[b, pl.ds(start, strip), :] - means2[b]) * inverses2[b]
            modulated = (normed * gain + bias) * (1.0 + scale) + shift
            after = modulated * jax.nn.sigmoid(modulated)
            store_shifted(second, b, start, after)
            second_t[b, :, pl.ds(start, strip)] = after.T.astype(BF16)
        return carry

    lax.fori_loop(0, pixels // strip, modulate, 0)
    for b in range(4):
        for row, value in enumerate((means[b], inverses[b], means2[b], inverses2[b])):
            stats[b, row : row + 1, :] = value


def kernel_second(
    meta, second, image, pack, w0, w1, w2, w3, w4, w5, w6, w7,
    middle, attn_t, qkv, qkv_weight, proj_weight, weight, stats, attn, sems,
):
    pixels = image.shape[1]
    me = meta[0]
    wait_all(fetch_routed((w0, w1, w2, w3, w4, w5, w6, w7), weight, me, meta[2], sems, 0))
    strip = 128

    def write(start, tile):
        rows = tile.shape[0]
        for b in range(4):
            branch = tile[:, b * LANES : (b + 1) * LANES] + pack[b, E_CB2 : E_CB2 + 1, :]
            middle[b, pl.ds(start, rows), :] = image[b, pl.ds(start, rows), :].astype(F32) + branch

    conv_tiles(second, weight, pixels, 512, write)
    means, inverses = norm_rows(pixels, strip, lambda b, start: middle[b, pl.ds(start, strip), :])

    def normalise(index, carry):
        start = pl.multiple_of(index * strip, strip)
        for b in range(4):
            normed = (middle[b, pl.ds(start, strip), :] - means[b]) * inverses[b]
            value = normed * pack[b, E_G3 : E_G3 + 1, :] + pack[b, E_B3 : E_B3 + 1, :]
            attn[b, pl.ds(start, strip), :] = value.astype(BF16)
            attn_t[b, :, pl.ds(start, strip)] = value.T.astype(BF16)
        return carry

    lax.fori_loop(0, pixels // strip, normalise, 0)
    for s in range(4):
        qkv_weight[s] = weight[s, QKV_ROW:PROJ_ROW, :]
        proj_weight[s] = weight[s, PROJ_ROW : PROJ_ROW + C, :]

    def project(index, carry):
        s = index // 2
        start = pl.multiple_of((index % 2) * 512, 512)
        left = jnp.concatenate([attn[b, pl.ds(start, 512), :] for b in range(4)], axis=1)
        right = jnp.concatenate(
            [weight[s, QKV_ROW + kind * C : QKV_ROW + (kind + 1) * C, :] for kind in range(3)], axis=1
        )
        qkv[s, pl.ds(start, 512), :] = jnp.dot(left, right, preferred_element_type=F32).astype(BF16)
        return carry

    lax.fori_loop(0, 4 * (pixels // 512), project, 0)
    for b in range(4):
        for row, value in enumerate((means[b], inverses[b])):
            stats[b, row : row + 1, :] = value


def kernel_attention(
    meta, qkv, pack, middle, weight, c0, c1, c2, c3,
    o0, o1, o2, cot, mixed, dqkv, dctx,
    grad_mixed, score_ctx, grad_ctx_prob, prob_ctx, dscore_ctx, out_pix, dquery, dkey_t, dvalue_t, sems,
):
    pixels = qkv.shape[1]
    me = meta[0]
    alive = meta[1].astype(F32)
    cot_copies = fetch((c0, c1, c2, c3), cot, me, sems, 0)
    scale = 1.0 / math.sqrt(HEAD)
    block = 1024

    row32 = lax.broadcasted_iota(jnp.int32, (32, LANES), 0)
    lane32 = lax.broadcasted_iota(jnp.int32, (32, LANES), 1)

    def diagonal(kind):
        found = []
        for s in range(4):
            rows8 = pack[s, kind : kind + 8, :]
            tiled = jnp.concatenate([rows8] * 4, axis=0)
            own = (row32 // 4) == (2 * s + lane32 // HEAD)
            kept = jnp.where(own, tiled, 0.0)
            found.append(jnp.concatenate([kept, jnp.zeros((96, LANES), F32)], axis=0).astype(BF16))
        return jnp.concatenate(found, axis=1)

    keys_ctx = diagonal(M_KEY)
    values_ctx = diagonal(M_VALUE)
    wait_all(cot_copies)

    def projection():
        return jnp.concatenate(
            [
                jnp.concatenate([weight[s, o * LANES : (o + 1) * LANES, :] for o in range(4)], axis=1)
                for s in range(4)
            ],
            axis=0,
        )

    def prepare(index, carry):
        start = pl.multiple_of(index * block, block)
        rows = pl.ds(start, block)
        for s in range(4):
            cot[s, rows, :] = (cot[s, rows, :].astype(F32) * alive).astype(BF16)
        all_cot = jnp.concatenate([cot[s, rows, :] for s in range(4)], axis=1)
        all_weight = projection()
        grad = lax.dot_general(
            all_cot, all_weight, (((1,), (1,)), ((), ())), preferred_element_type=F32
        ).astype(BF16)
        for s in range(4):
            grad_mixed[s, rows, :] = grad[:, s * LANES : (s + 1) * LANES]
        query = jnp.concatenate([qkv[s, rows, 0:LANES] for s in range(4)], axis=1)
        score_ctx[rows, :] = lax.dot_general(
            query, keys_ctx, (((1,), (1,)), ((), ())), preferred_element_type=F32
        )
        grad_ctx_prob[rows, :] = lax.dot_general(
            grad, values_ctx, (((1,), (1,)), ((), ())), preferred_element_type=F32
        )
        prob_ctx[rows, :] = jnp.zeros((block, LANES), F32)
        dscore_ctx[rows, :] = jnp.zeros((block, LANES), F32)
        return carry

    lax.fori_loop(0, pixels // block, prepare, 0)
    lane = lax.broadcasted_iota(jnp.int32, (block, LANES), 1)
    low = lane < HEAD
    ones = jnp.ones((pixels, LANES), BF16)
    blocks = pixels // block

    def attend(index, carry):
        s = index // blocks
        part = index % blocks
        rows = pl.ds(pl.multiple_of(part * block, block), block)

        @pl.when(part == 0)
        def _():
            dkey_t[...] = jnp.zeros((LANES, pixels), F32)
            dvalue_t[...] = jnp.zeros((LANES, pixels), F32)

        query = qkv[s, rows, 0:LANES]
        key = qkv[s, :, LANES : 2 * LANES]
        value = qkv[s, :, 2 * LANES : 3 * LANES]
        value_ones = jnp.concatenate([value, ones], axis=1)
        grad = grad_mixed[s, rows, :]
        ctx_scores = score_ctx[rows, :]
        ctx_grads = grad_ctx_prob[rows, :]
        exps, outs, inverses, ctx_exps, owns = [], [], [], [], []
        for h in range(2):
            mine = low if h == 0 else jnp.logical_not(low)
            own = lane // CTX == 2 * s + h
            score = lax.dot_general(
                jnp.where(mine, query, jnp.zeros_like(query)),
                key,
                (((1,), (1,)), ((), ())),
                preferred_element_type=F32,
            )
            top = jnp.maximum(
                jnp.max(score, axis=1, keepdims=True),
                jnp.max(jnp.where(own, ctx_scores, NEG), axis=1, keepdims=True),
            )
            exp = jnp.exp((score - top) * scale).astype(BF16)
            ctx_exp = jnp.where(own, jnp.exp((ctx_scores - top) * scale), 0.0)
            out = jnp.dot(exp, value_ones, preferred_element_type=F32)
            total = out[:, LANES:] + jnp.sum(ctx_exp, axis=1, keepdims=True)
            inverse = 1.0 / total
            exps.append(exp)
            outs.append(out[:, :LANES] * inverse)
            inverses.append(inverse)
            ctx_exps.append(ctx_exp)
            owns.append(own)
        out_pair = jnp.where(low, outs[0], outs[1])
        out_pix[s, rows, :] = out_pair
        inverse_pair = jnp.where(low, inverses[0], inverses[1])
        scaled = (grad.astype(F32) * (inverse_pair * scale)).astype(BF16)
        product = out_pair * scaled.astype(F32)
        query_t = query.astype(F32).T.astype(BF16)
        scaled_t = scaled.astype(F32).T.astype(BF16)
        prob_keep = prob_ctx[rows, :]
        dscore_keep = dscore_ctx[rows, :]
        dqs = []
        for h in range(2):
            mine = low if h == 0 else jnp.logical_not(low)
            own = owns[h]
            ctx_prob = ctx_exps[h] * inverses[h]
            ctx_grad = ctx_grads * (inverses[h] * scale)
            dot = jnp.sum(
                jnp.where(mine, product, 0.0) + ctx_prob * jnp.where(own, ctx_grad, 0.0),
                axis=1,
                keepdims=True,
            )
            weight_grad = lax.dot_general(
                jnp.where(mine, scaled, jnp.zeros_like(scaled)),
                value,
                (((1,), (1,)), ((), ())),
                preferred_element_type=F32,
            )
            dscore = (exps[h].astype(F32) * (weight_grad - dot)).astype(BF16)
            prob_keep = jnp.where(own, ctx_prob, prob_keep)
            dscore_keep = jnp.where(own, ctx_exps[h] * (ctx_grad - dot), dscore_keep)
            dqs.append(jnp.dot(dscore, key, preferred_element_type=F32))
            half = slice(h * HEAD, (h + 1) * HEAD)
            dkey_t[half, :] += jnp.dot(query_t[half], dscore, preferred_element_type=F32)
            dvalue_t[half, :] += jnp.dot(scaled_t[half], exps[h], preferred_element_type=F32)
        prob_ctx[rows, :] = prob_keep
        dscore_ctx[rows, :] = dscore_keep
        dquery[s, rows, :] = jnp.where(low, dqs[0], dqs[1])

        @pl.when(part == blocks - 1)
        def _():
            for piece in range(pixels // LANES):
                cut = slice(piece * LANES, (piece + 1) * LANES)
                dqkv[s, cut, LANES : 2 * LANES] = dkey_t[:, cut].T.astype(BF16)
                dqkv[s, cut, 2 * LANES : 3 * LANES] = (dvalue_t[:, cut] * (1.0 / scale)).T.astype(BF16)

        return carry

    lax.fori_loop(0, 4 * blocks, attend, 0)

    def finish(index, carry):
        dkeys, dvalues = carry
        start = pl.multiple_of(index * block, block)
        rows = pl.ds(start, block)
        prob = prob_ctx[rows, :].astype(BF16)
        dscore = dscore_ctx[rows, :].astype(BF16)
        out_ctx = jnp.dot(prob, values_ctx, preferred_element_type=F32)
        dquery_ctx = jnp.dot(dscore, keys_ctx, preferred_element_type=F32)
        parts = []
        for s in range(4):
            cut = slice(s * LANES, (s + 1) * LANES)
            both = (out_pix[s, rows, :] + out_ctx[:, cut]).astype(BF16)
            mixed[s, rows, :] = both
            parts.append(both)
            dqkv[s, rows, 0:LANES] = (dquery[s, rows, :] + dquery_ctx[:, cut]).astype(BF16)
        result = jnp.dot(
            jnp.concatenate(parts, axis=1), projection(), preferred_element_type=F32
        )
        for offset, target in enumerate((o0, o1, o2.at[0], o2.at[1])):
            other = jnp.bitwise_xor(me, offset)
            value = jnp.zeros((block, LANES), F32)
            for s in range(4):
                value = jnp.where(other == s, result[:, s * LANES : (s + 1) * LANES], value)
            target[rows, :] = ((middle[other, rows, :] + value) * alive).astype(BF16)
        query = jnp.concatenate([qkv[s, rows, 0:LANES] for s in range(4)], axis=1)
        grad = jnp.concatenate([grad_mixed[s, rows, :] for s in range(4)], axis=1)
        dkeys = dkeys + jnp.dot(dscore_ctx[rows, :].T[0:32].astype(BF16), query, preferred_element_type=F32)
        dvalues = dvalues + jnp.dot(prob_ctx[rows, :].T[0:32].astype(BF16), grad, preferred_element_type=F32)
        return dkeys, dvalues

    zero = jnp.zeros((32, C), F32)
    dkeys, dvalues = lax.fori_loop(0, pixels // block, finish, (zero, zero))
    for s in range(4):
        own = (row32 // 4) == (2 * s + lane32 // HEAD)
        for position, source in enumerate((dkeys, dvalues)):
            kept = jnp.where(own, source[:, s * LANES : (s + 1) * LANES], 0.0)
            eight = jnp.sum(kept.reshape(4, 8, LANES), axis=0)
            folded = eight + pltpu.roll(eight, 4, axis=0)
            dctx[s, position * CTX : (position + 1) * CTX, :] = folded[0:CTX]


def saved(stats, row):
    return [stats[b, row : row + 1, :] for b in range(4)]


def norm_back_strips(pixels, strip, read_normed, read_grad, gains, inverses, gain_sums, bias_sums, write):
    count = pixels * (C // GROUPS)
    firsts, seconds = (
        [
            group_sum(jnp.broadcast_to(sums[b] * gains[b], (8, LANES)) * (1.0 / 8)) * (1.0 / count)
            for b in range(4)
        ]
        for sums in (bias_sums, gain_sums)
    )

    def body(index, carry):
        start = pl.multiple_of(index * strip, strip)
        found = []
        for b in range(4):
            normed = read_normed(b, start)
            grad = read_grad(b, start) * gains[b]
            found.append(write(b, start, inverses[b] * (grad - firsts[b] - normed * seconds[b])))
        if found[0] is None:
            return carry
        return tuple(old + fold(new) for old, new in zip(carry, found))

    zero = tuple(jnp.zeros((8, LANES), F32) for _ in range(4))
    return lax.fori_loop(0, pixels // strip, body, zero)


def kernel_back_attention(
    meta, dqkv, cot, middle, pack, stats, dctx, qkv_weight,
    dmiddle, field, sums, d0, d1, d2, d3, dattn,
):
    pixels = cot.shape[1]
    me = meta[0]
    strip = 128
    clear_padding(field, pixels)
    means, inverses = saved(stats, 0), saved(stats, 1)

    def back(index, carry):
        start = pl.multiple_of(index * 512, 512)
        left = jnp.concatenate([dqkv[s, pl.ds(start, 512), :] for s in range(4)], axis=1)
        right = jnp.concatenate(
            [qkv_weight[s, kind * C : (kind + 1) * C, :] for s in range(4) for kind in range(3)], axis=1
        )
        tile = lax.dot_general(left, right, (((1,), (1,)), ((), ())), preferred_element_type=F32)
        for b in range(4):
            dattn[b, pl.ds(start, 512), :] = tile[:, b * LANES : (b + 1) * LANES]
        return carry

    lax.fori_loop(0, pixels // 512, back, 0)
    gains = [pack[b, E_G3 : E_G3 + 1, :] for b in range(4)]

    def read_normed(b, start):
        return (middle[b, pl.ds(start, strip), :] - means[b]) * inverses[b]

    def write(b, start, value):
        total = cot[b, pl.ds(start, strip), :].astype(F32) + value
        dmiddle[b, pl.ds(start, strip), :] = total
        rounded = total.astype(BF16).astype(F32)
        store_shifted(field, b, start, rounded)
        return rounded

    def terms(start):
        found = []
        for b in range(4):
            grad = dattn[b, pl.ds(start, strip), :]
            found += [grad, grad * read_normed(b, start)]
        return found

    totals = [column_sum(rows8) for rows8 in sum_strips(pixels, strip, 8, terms)]
    bias_sums, gain_sums = totals[0::2], totals[1::2]
    branch = norm_back_strips(
        pixels,
        strip,
        read_normed,
        lambda b, start: dattn[b, pl.ds(start, strip), :],
        gains,
        inverses,
        gain_sums,
        bias_sums,
        write,
    )
    for b in range(4):
        sums[b] = jnp.zeros((S_ROWS, LANES), F32)
        sums[b, S_G3 : S_G3 + 1, :] = gain_sums[b]
        sums[b, S_B3 : S_B3 + 1, :] = bias_sums[b]
        sums[b, S_CB2 : S_CB2 + 1, :] = column_sum(branch[b])
        sums[b, S_KEY : S_KEY + 8, :] = dctx[b]
    for offset, target in enumerate((d0, d1, d2, d3)):
        target[...] = field[1, jnp.bitwise_xor(me, offset), PAD : PAD + pixels, :]


def kernel_attention_grad(meta, dqkv, mixed, attn_t, cot, keep, send, cot_t):
    pixels = cot.shape[1]
    me = meta[0]
    strip = 128

    def turn(index, carry):
        start = pl.multiple_of(index * strip, strip)
        for b in range(4):
            cot_t[b, :, pl.ds(start, strip)] = cot[b, pl.ds(start, strip), :].astype(F32).T.astype(BF16)
        return carry

    lax.fori_loop(0, pixels // strip, turn, 0)

    attn_all = attn_t[...].reshape(C, pixels)
    cot_all = cot_t[...].reshape(C, pixels)
    for offset, target in enumerate((keep, send)):
        s = jnp.bitwise_xor(me, offset)
        pair = (s, jnp.bitwise_xor(s, 2))
        right = jnp.concatenate([dqkv[p] for p in pair], axis=1)
        grad = jnp.dot(attn_all, right, preferred_element_type=F32).astype(BF16)
        right = jnp.concatenate([mixed[p] for p in pair], axis=1)
        other = jnp.dot(cot_all, right, preferred_element_type=F32).astype(BF16)
        for place in range(2):
            for kind in range(3):
                column = (3 * place + kind) * LANES
                target[place, kind] = grad[:, column : column + LANES]
            target[place, 3] = other[:, place * LANES : (place + 1) * LANES]


def weight_taps(half, sources, field, target):
    pixels = sources[0].shape[2]

    def body(index, carry):
        left = jnp.concatenate(
            [source[pl.ds(2 * half, 2)].reshape(2 * LANES, pixels) for source in sources], axis=1
        )
        columns = []
        for tap in (2 * index, jnp.minimum(2 * index + 1, 8)):
            start = pl.multiple_of((2 - tap // 3) * SIDE, 32)
            side = 2 - lax.rem(tap, 3)
            columns.append(
                jnp.concatenate([field[side, k, pl.ds(start, pixels), :] for k in range(4)], axis=0)
            )
        grad = jnp.dot(left, jnp.concatenate(columns, axis=1), preferred_element_type=F32)
        target[2 * index] = grad[:, :LANES].astype(target.dtype)

        @pl.when(index < 4)
        def _():
            target[2 * index + 1] = grad[:, LANES:].astype(target.dtype)

        return carry

    lax.fori_loop(0, 5, body, 0)


def kernel_weight_send(meta, u0, u1, u2, u3, d0, d1, d2, d3, send, field):
    pixels = u0.shape[2]
    clear_padding(field, pixels)
    strip = 128

    def spread(index, carry):
        start = pl.multiple_of(index * strip, strip)
        for k, source in enumerate((d0, d1, d2, d3)):
            store_shifted(field, k, start, source[pl.ds(start, strip), :].astype(F32))
        return carry

    lax.fori_loop(0, pixels // strip, spread, 0)
    weight_taps(1 - meta[3], (u0, u1, u2, u3), field, send)


def kernel_weight_own(meta, u0, u1, u2, u3, field, own):
    weight_taps(meta[3], (u0, u1, u2, u3), field, own)


def kernel_back_second(
    meta, grad_field, inner, pack, stats, sums_in, weight,
    field, sums, d0, d1, d2, d3, grad,
):
    pixels = inner.shape[1]
    me = meta[0]
    strip = 128
    clear_padding(field, pixels)
    means, inverses = saved(stats, 2), saved(stats, 3)

    def write_grad(start, half, tile):
        for b in range(2):
            grad[2 * half + b, pl.ds(start, tile.shape[0]), :] = tile[:, b * LANES : (b + 1) * LANES]

    conv_back_tiles(grad_field, weight, pixels, 512, write_grad)
    gains = [pack[b, E_G2 : E_G2 + 1, :] for b in range(4)]

    def read_normed(b, start):
        return (inner[b, pl.ds(start, strip), :] - means[b]) * inverses[b]

    def slope(index, carry):
        start = pl.multiple_of(index * strip, strip)
        found = []
        for b in range(4):
            bias = pack[b, E_B2 : E_B2 + 1, :]
            scale = pack[b, M_SCALE : M_SCALE + 1, :]
            shift = pack[b, M_SHIFT : M_SHIFT + 1, :]
            normed = read_normed(b, start)
            modulated = (normed * gains[b] + bias) * (1.0 + scale) + shift
            dmod = silu_slope(modulated, grad[b, pl.ds(start, strip), :])
            grad[b, pl.ds(start, strip), :] = dmod * (1.0 + scale)
            found += [dmod, dmod * normed]
        return tuple(old + fold(new) for old, new in zip(carry, found))

    zero = tuple(jnp.zeros((8, LANES), F32) for _ in range(8))
    totals = [column_sum(rows8) for rows8 in lax.fori_loop(0, pixels // strip, slope, zero)]
    plain, scaled = totals[0::2], totals[1::2]
    factors = [1.0 + pack[b, M_SCALE : M_SCALE + 1, :] for b in range(4)]
    bias_sums = [plain[b] * factors[b] for b in range(4)]
    gain_sums = [scaled[b] * factors[b] for b in range(4)]

    def write(b, start, value):
        store_shifted(field, b, start, value)

    norm_back_strips(
        pixels,
        strip,
        read_normed,
        lambda b, start: grad[b, pl.ds(start, strip), :],
        gains,
        inverses,
        gain_sums,
        bias_sums,
        write,
    )
    for b in range(4):
        sums[b] = sums_in[b]
        sums[b, S_G2 : S_G2 + 1, :] = gain_sums[b]
        sums[b, S_B2 : S_B2 + 1, :] = bias_sums[b]
        sums[b, S_SCALE : S_SCALE + 1, :] = (
            scaled[b] * gains[b] + plain[b] * pack[b, E_B2 : E_B2 + 1, :]
        )
        sums[b, S_SHIFT : S_SHIFT + 1, :] = plain[b]
    for offset, target in enumerate((d0, d1, d2, d3)):
        target[...] = field[1, jnp.bitwise_xor(me, offset), PAD : PAD + pixels, :]


def kernel_back_conv(grad_field, weight, grad):
    pixels = grad.shape[1]

    def write_grad(start, half, tile):
        for b in range(2):
            grad[2 * half + b, pl.ds(start, tile.shape[0]), :] = tile[:, b * LANES : (b + 1) * LANES]

    conv_back_tiles(grad_field, weight, pixels, 512, write_grad)


def kernel_back_first(
    meta, grad_in, image, pack, stats, dmiddle, sums_in, g0, g1, g2, grad, sums,
):
    pixels = image.shape[1]
    me = meta[0]
    strip = 128

    def read(b, start):
        return image[b, pl.ds(start, strip), :].astype(F32)

    means, inverses = saved(stats, 0), saved(stats, 1)
    gains = [pack[b, E_G1 : E_G1 + 1, :] for b in range(4)]

    def read_normed(b, start):
        return (read(b, start) - means[b]) * inverses[b]

    def slope(index, carry):
        start = pl.multiple_of(index * strip, strip)
        found = []
        for b in range(4):
            normed = read_normed(b, start)
            before = normed * gains[b] + pack[b, E_B1 : E_B1 + 1, :]
            value = silu_slope(before, grad_in[b, pl.ds(start, strip), :])
            grad[b, pl.ds(start, strip), :] = value
            found += [value, value * normed]
        return tuple(old + fold(new) for old, new in zip(carry, found))

    zero = tuple(jnp.zeros((8, LANES), F32) for _ in range(8))
    totals = [column_sum(rows8) for rows8 in lax.fori_loop(0, pixels // strip, slope, zero)]
    bias_sums, gain_sums = totals[0::2], totals[1::2]

    def write(b, start, value):
        grad[b, pl.ds(start, strip), :] = dmiddle[b, pl.ds(start, strip), :] + value

    norm_back_strips(
        pixels,
        strip,
        read_normed,
        lambda b, start: grad[b, pl.ds(start, strip), :],
        gains,
        inverses,
        gain_sums,
        bias_sums,
        write,
    )
    for b in range(4):
        sums[b] = sums_in[b]
        sums[b, S_G1 : S_G1 + 1, :] = gain_sums[b]
        sums[b, S_B1 : S_B1 + 1, :] = bias_sums[b]
    for offset, target in enumerate((g0, g1, g2.at[0], g2.at[1])):
        other = jnp.bitwise_xor(me, offset)
        target[0:pixels, :] = grad[other].astype(BF16)
        target[pixels : pixels + S_ROWS, :] = sums[other].astype(BF16)


def kernel_scale(factors0, factors1, scale):
    total = jnp.zeros((1, LANES), F32)
    for factors in (factors0, factors1):
        for g in range(factors.shape[0]):
            total = total + factors[g, 0].astype(F32)[1:2, 0:LANES]
    scale[...] = jnp.broadcast_to(1.0 / total, (8, LANES))


def kernel_factors(meta, factors0, factors1, left):
    conditions, tokens = [], []
    for factors in (factors0, factors1):
        for g in range(factors.shape[0]):
            for k in range(4):
                rows = factors[g, jnp.bitwise_xor(meta[0], k)].astype(F32)
                conditions.append(rows[0:1])
                tokens.append(rows[CTX : 2 * CTX])
    rest = left.shape[1] - 5 * len(conditions)
    rows = tokens + conditions
    if rest:
        rows.append(jnp.zeros((rest, EMB), F32))
    left[...] = jnp.concatenate(rows, axis=0).T.astype(BF16)


def kernel_factor_grads(scale, left, small0, small1, embed, context, vectors):
    inverse = scale[0:1, :]
    total = jnp.zeros((S_ROWS, LANES), F32)
    scales, shifts, keys, values = [], [], [], []
    for small in (small0, small1):
        for k in range(small.shape[0]):
            term = small[k].astype(F32)
            total = total + term
            scales.append(term[S_SCALE : S_SCALE + 1])
            shifts.append(term[S_SHIFT : S_SHIFT + 1])
            keys.append(term[S_KEY : S_KEY + CTX])
            values.append(term[S_VALUE : S_VALUE + CTX])
    vectors[...] = total * inverse
    images = len(scales)
    rest = left.shape[1] - 5 * images
    none = jnp.zeros((4 * images, LANES), F32)
    columns = []
    for parts in (keys, values):
        whole = [jnp.concatenate(parts, axis=0), jnp.zeros((images + rest, LANES), F32)]
        columns.append(jnp.concatenate(whole, axis=0))
    for parts in (scales, shifts):
        whole = [none] + parts
        if rest:
            whole.append(jnp.zeros((rest, LANES), F32))
        columns.append(jnp.concatenate(whole, axis=0))
    right = jnp.concatenate(columns, axis=1).astype(BF16)
    grad = jnp.dot(left[...], right, preferred_element_type=F32)
    for place in range(2):
        context[:, place, :] = grad[:, place * LANES : (place + 1) * LANES] * inverse
        embed[:, place, :] = grad[:, (place + 2) * LANES : (place + 3) * LANES] * inverse


def kernel_stack(*refs):
    whole = refs[-1]
    base = 0
    for ref in refs[:-1]:
        count = ref.shape[0]
        whole[base : base + count] = ref[...]
        base += count


def stack(parts):
    shape = (sum(part.shape[0] for part in parts),) + parts[0].shape[1:]
    return call(
        kernel_stack, "stack", struct(shape, parts[0].dtype), [vmem()] * len(parts), [], limit=12
    )(*parts)


def kernel_slots(meta, own, near, far, across, whole, sems):
    rows = pl.ds(0, whole.shape[1])
    sources = (own.at[rows], near.at[rows], far.at[0, rows], across.at[1, rows])
    wait_all(fetch(sources, whole, meta[0], sems, 0))


def kernel_cut(source, first, second):
    rows = first.shape[0]
    first[...] = source[0:rows]
    second[...] = source[rows : 2 * rows]


def cut(source):
    rows, lanes = source.shape
    return call(
        kernel_cut, "cut", [struct((rows // 2, lanes), BF16)] * 2, [vmem()], [], limit=8
    )(source)


def kernel_small_stack(own, near, far, across, whole):
    rows = pl.ds(own.shape[0] - S_ROWS, S_ROWS)
    whole[0] = own[rows, :]
    whole[1] = near[rows, :]
    whole[2] = far[0, rows, :]
    whole[3] = across[1, rows, :]


def kernel_split(counts, width, digit, meta, *refs):
    parts = refs[sum(counts) :]
    rows = parts[0].shape[1]
    for offset, part in enumerate(parts):
        start = pl.multiple_of(jnp.bitwise_xor(meta[digit], offset) * rows, rows)
        position, base = 0, 0
        for count in counts:
            terms = refs[position : position + count]
            terms = [term.at[0] if len(term.shape) == 4 else term for term in terms]
            total = terms[0][:, pl.ds(start, rows), :].astype(F32)
            for term in terms[1:]:
                total = total + term[:, pl.ds(start, rows), :].astype(F32)
            part[base : base + total.shape[0]] = total.astype(part.dtype)
            position += count
            base += total.shape[0]


def split_sum(groups, width, digit, meta):
    blocks = sum(terms[-1].shape[0] for terms in groups)
    rows = groups[0][-1].shape[1]
    flat = [term for terms in groups for term in terms]
    shape = (blocks, rows // width, LANES)
    return call(
        functools.partial(kernel_split, tuple(len(terms) for terms in groups), width, digit),
        "split_sum",
        [struct(shape, F32)] + [struct(shape, BF16)] * (width - 1),
        [smem()] + [vmem()] * len(flat),
        [],
        limit=12,
    )(meta, *flat)


def kernel_far(mine, got, own, far):
    blocks = own.shape[0]
    own[...] = mine[0:blocks] + got[0:blocks].astype(F32)
    far[...] = (mine[blocks : 2 * blocks] + got[blocks : 2 * blocks].astype(F32)).astype(BF16)


def kernel_total(*refs):
    total = refs[0][...].astype(F32)
    for term in refs[1:-1]:
        total = total + term[...].astype(F32)
    refs[-1][...] = total.astype(BF16)


def total_sum(terms):
    return call(
        kernel_total, "total_sum", struct(terms[0].shape, BF16), [vmem()] * len(terms), [], limit=12
    )(*terms)


def kernel_join(digit, meta, *refs):
    parts, whole = refs[:-1], refs[-1]
    rows = parts[0].shape[1]
    for offset, part in enumerate(parts):
        start = pl.multiple_of(jnp.bitwise_xor(meta[digit], offset) * rows, rows)
        whole[:, pl.ds(start, rows), :] = part[...]


def join(parts, digit, meta):
    blocks, rows, _ = parts[0].shape
    return call(
        functools.partial(kernel_join, digit),
        "join",
        struct((blocks, rows * len(parts), LANES), BF16),
        [smem()] + [vmem()] * len(parts),
        [],
        limit=12,
    )(meta, *parts)


def kernel_last(digit, meta, scale, mine, other, conv, *more):
    rows = mine.shape[1]
    for offset, part in enumerate((mine, other)):
        start = pl.multiple_of(jnp.bitwise_xor(meta[digit], offset) * rows, rows)
        count = conv.shape[0]
        conv[:, pl.ds(start, rows), :] = part[0:count].astype(F32) * scale[0:1, :]
        for proj in more:
            proj[:, pl.ds(start, rows)] = (part[count].astype(F32) * scale[0:1, :]).T


def last_join(pair, digit, meta, scale, more=False):
    blocks, rows, _ = pair[0].shape
    shapes = [struct((3 if more else blocks, 2 * rows, LANES), F32)]
    if more:
        shapes.append(struct((LANES, 2 * rows), F32))
    return call(
        functools.partial(kernel_last, digit),
        "last_join",
        shapes,
        [smem()] + [vmem()] * 3,
        [],
        limit=12,
    )(meta, scale, *pair)


def swap(value, axis, offset):
    size = lax.axis_size(axis)
    return lax.ppermute(value, axis, [(i, i ^ offset) for i in range(size)])


def tie(*values):
    return lax.optimization_barrier(values)


def share(shard):
    near = swap(shard, "mp", 1)
    far = swap(shard, "mp", 2)
    return shard, near, far, swap(far, "mp", 1)


def exchange(pieces):
    return (pieces[0],) + tuple(swap(pieces[k], "mp", k) for k in range(1, 4))


def pick(stack, me):
    return [lax.dynamic_index_in_dim(stack, me ^ k, 0, keepdims=False) for k in range(4)]


def pick_pair(stack, me):
    own = lax.dynamic_index_in_dim(stack, me, 0, keepdims=False)
    near = lax.dynamic_index_in_dim(stack, me ^ 1, 0, keepdims=False)
    far = [lax.dynamic_index_in_dim(stack, me ^ k, 0, keepdims=True) for k in (2, 3)]
    return own, near, jnp.concatenate(far, axis=0)


def dp_levels(size):
    return [(1 << k, 2) for k in range(size.bit_length() - 1)]


def bits(size):
    return [1 << k for k in range(size.bit_length() - 1)]


def local(
    image_in,
    out_cotangent,
    timesteps,
    clip_embed,
    context_tokens,
    image_count,
    norm1_gain,
    norm1_bias,
    conv1_weight,
    embed_weight,
    norm2_gain,
    norm2_bias,
    conv2_weight,
    conv2_bias,
    norm3_gain,
    norm3_bias,
    qkv_weight,
    context_weight,
    proj_weight,
):
    slots, pixels, width = image_in.shape
    me = lax.axis_index("mp")
    group = lax.axis_index("dp")
    parity = (group ^ (group >> 1)) & 1
    levels = dp_levels(lax.axis_size("dp"))
    own_digits = [(group >> (low.bit_length() - 1)) & (wide - 1) for low, wide in levels]
    meta = jnp.stack(
        [me, (me < image_count[0]).astype(jnp.int32), parity] + own_digits
    ).astype(jnp.int32)
    digits = range(3, 3 + len(levels))
    steps = bits(lax.axis_size("dp"))

    conv1_weight, conv2_weight, image_in, out_cotangent, meta = tie(
        conv1_weight, conv2_weight, image_in, out_cotangent, meta
    )

    conv1_shard = conv1_weight.reshape(9 * C, LANES)

    def half_of(shard):
        rows = shard.shape[0] // 2
        return lax.dynamic_slice_in_dim(shard, parity * rows, rows, axis=0)

    half1, image_in = tie(half_of(conv1_shard), image_in)
    half1 = swap(half1, "mp", 2)
    near1 = swap(conv1_shard, "mp", 1)
    images = pick_pair(image_in, me)
    image_near = swap(images[1], "mp", 1)
    image_far = swap(images[2], "mp", 2)

    half_width = EMB // 2
    frequency = jnp.exp(-math.log(10000.0) * jnp.arange(half_width, dtype=F32) / half_width)
    angles = timesteps.astype(F32)[:, None] * frequency[None, :]
    condition = jax.nn.silu(
        jnp.concatenate([jnp.cos(angles), jnp.sin(angles)], axis=1) + clip_embed.astype(F32)
    ).astype(BF16)
    scale_shift = jnp.dot(
        condition, embed_weight.reshape(EMB, 2 * LANES), preferred_element_type=F32
    ).reshape(slots, 1, 2 * LANES)
    doubled = jnp.concatenate([context_tokens, context_tokens], axis=1)
    context = jnp.dot(
        doubled.reshape(slots * 2 * CTX, EMB),
        context_weight.reshape(EMB, 2 * LANES),
        preferred_element_type=F32,
    ).astype(BF16).astype(F32).reshape(slots, 2 * CTX, 2 * LANES)
    vectors = [norm1_gain, norm1_bias, norm2_gain, norm2_bias, conv2_bias, norm3_gain, norm3_bias]
    early = struct((E_ROWS, LANES), F32)
    packs = call(
        kernel_early,
        "early",
        [early, early, struct((2, E_ROWS, LANES), F32)],
        [smem()] + [vmem()] * 9,
        [],
        limit=8,
    )(meta, scale_shift, context, *[vector[None] for vector in vectors])
    count_rows = jnp.broadcast_to(image_count.astype(BF16)[:, None, None], (slots, CTX - 1, EMB))
    factors = jnp.concatenate([condition[:, None], count_rows, context_tokens], axis=1)[None]
    cots = pick(out_cotangent, me)
    rest_shard = jnp.concatenate(
        [
            conv2_weight.reshape(9 * C, LANES),
            jnp.transpose(qkv_weight, (1, 0, 2)).reshape(3 * C, LANES),
            jnp.transpose(proj_weight.reshape(LANES, 4, LANES), (1, 0, 2)).reshape(C, LANES),
        ],
        axis=0,
    )
    rest_half = half_of(rest_shard)

    def relayed(shard, near, half):
        by_x, by_z = cut(half)
        by_x = swap(by_x, "dp", 1)
        by_z = swap(by_z, "dp", 2)
        return (shard, near, half, by_x, by_z) + tuple(
            swap(part, "mp", 1) for part in (half, by_x, by_z)
        )

    near1, image_near, packs, half1 = tie(near1, image_near, packs, half1)
    pack_near = swap(packs[1], "mp", 1)
    pack_far = swap(packs[2], "mp", 2)
    conv1 = relayed(conv1_shard, near1, half1)
    image_far, pack_near, pack_far, rest_shard, rest_half, factors, cots, *conv1 = tie(
        image_far, pack_near, pack_far, rest_shard, rest_half, factors, cots, *conv1
    )
    images = (images[0], image_near, image_far, swap(image_far, "mp", 1))
    packs = (packs[0], pack_near, pack_far, swap(pack_far, "mp", 1))
    rest_half = swap(rest_half, "mp", 2)
    rest_near = swap(rest_shard, "mp", 1)
    factors = [factors, swap(factors, "dp", 1)]

    block = struct((4, pixels, LANES), BF16)
    block32 = struct((4, pixels, LANES), F32)
    turned = struct((4, LANES, pixels), BF16)
    fields = struct((3, 4, pixels + 2 * PAD, LANES), BF16)
    piece = struct((pixels, LANES), BF16)
    pair_piece = struct((2, pixels, LANES), BF16)
    field_scratch = pltpu.VMEM((3, 4, pixels + 2 * PAD, LANES), BF16)
    grad_scratch = pltpu.VMEM((4, pixels, LANES), F32)

    image, pack, first_t, inner, second_t, second, conv1_all, stats1 = call(
        kernel_first,
        "first",
        [
            block,
            struct((4, E_ROWS, LANES), F32),
            turned,
            block32,
            turned,
            fields,
            struct((4, 9 * C, LANES), BF16),
            struct((4, 8, LANES), F32),
        ],
        [smem()] + [anywhere()] * 16,
        [field_scratch, pltpu.SemaphoreType.DMA((16,))],
        limit=12,
    )(meta, *images, *packs, *conv1)

    second, rest_half, rest_near, factors = tie(second, rest_half, rest_near, factors)
    rest = relayed(rest_shard, rest_near, rest_half)
    cots = exchange(cots)
    second, *rest = tie(second, *rest)
    factors = stack(factors)
    factors = [factors, swap(factors, "dp", 2)]
    middle, attn_t, qkv, qkv_w, proj_w, rest_all, stats2 = call(
        kernel_second,
        "second",
        [
            block32,
            turned,
            struct((4, pixels, 3 * LANES), BF16),
            struct((4, 3 * C, LANES), BF16),
            struct((4, C, LANES), BF16),
            struct((4, PROJ_ROW + C, LANES), BF16),
            struct((4, 8, LANES), F32),
        ],
        [smem()] + [vmem()] * 3 + [anywhere()] * 8,
        [pltpu.VMEM((4, pixels, LANES), BF16), pltpu.SemaphoreType.DMA((8,))],
        limit=12,
    )(meta, second, image, pack, *rest)
    ctx_scratch = pltpu.VMEM((pixels, LANES), F32)
    turned_scratch = pltpu.VMEM((LANES, pixels), F32)
    qkv, first_t, second_t, factors, cots = tie(qkv, first_t, second_t, factors, cots)
    factors = stack(factors)
    second_y = swap(second_t, "mp", 2)
    first_y = swap(first_t, "mp", 2)
    second_c = swap(second_t, "mp", 1)
    first_c = swap(first_t, "mp", 1)
    for low in steps[2:-1]:
        factors = stack([factors, swap(factors, "dp", low)])
    factors = (factors, swap(factors, "dp", steps[-1]))
    out_own, out_near, out_far, cot, mixed, dqkv, dctx = call(
        kernel_attention,
        "attention",
        [piece, piece, pair_piece]
        + [block, block, struct((4, pixels, 3 * LANES), BF16), struct((4, 2 * CTX, LANES), F32)],
        [smem()] + [vmem()] * 4 + [anywhere()] * 4,
        [
            pltpu.VMEM((4, pixels, LANES), BF16),
            ctx_scratch,
            ctx_scratch,
            ctx_scratch,
            ctx_scratch,
            grad_scratch,
            grad_scratch,
            turned_scratch,
            turned_scratch,
            pltpu.SemaphoreType.DMA((4,)),
        ],
        limit=24,
    )(meta, qkv, pack, middle, proj_w, *cots)

    def weight_send(sources, gradients):
        return call(
            kernel_weight_send,
            "weight_send",
            [struct((9, C // 2, LANES), BF16), fields],
            [smem()] + [vmem()] * 8,
            [],
            limit=16,
        )(meta, *sources, *gradients)

    def weight_own(sources, field):
        return call(
            kernel_weight_own,
            "weight_own",
            struct((9, C // 2, LANES), F32),
            [smem()] + [vmem()] * 5,
            [],
            limit=16,
        )(meta, *sources, field)

    def down(terms, level):
        own, send = split_sum([terms], 2, digits[level], meta)
        return [own, swap(send, "dp", levels[level][0])]

    def across(value, level):
        return [value, swap(value, "dp", levels[level][0])]

    def inner_levels(terms):
        for level in range(3, len(levels)):
            terms = down(terms, level)
        value = total_sum(terms)
        for level in range(len(levels) - 1, 2, -1):
            value = join(across(value, level), digits[level], meta)
        return value

    att_keep, att_send = call(
        kernel_attention_grad,
        "attention_grad",
        [struct((2, 4, C, LANES), BF16)] * 2,
        [smem()] + [vmem()] * 4,
        [pltpu.VMEM((4, LANES, pixels), BF16)],
    )(meta, dqkv, mixed, attn_t, cot)
    dqkv, att_send, second_y, second_c, factors = tie(dqkv, att_send, second_y, second_c, factors)
    second_d = swap(second_y, "mp", 1)
    att = [att_keep.reshape(8, C, LANES), swap(att_send, "mp", 1).reshape(8, C, LANES)]
    dmiddle, field2, sums, *gradients2 = call(
        kernel_back_attention,
        "back_attention",
        [block32, fields, struct((4, S_ROWS, LANES), F32)] + [piece] * 4,
        [smem()] + [vmem()] * 7,
        [grad_scratch],
    )(meta, dqkv, cot, middle, pack, stats2, dctx, qkv_w)
    gradients2, second_d, first_y, first_c, att, field2 = tie(
        gradients2, second_d, first_y, first_c, att, field2
    )
    first_d = swap(first_y, "mp", 1)
    seconds = (second_t, second_c, second_y, second_d)
    gradients2 = exchange(gradients2)
    att = down(att, 0)
    field2, att[0] = tie(field2, att[0])
    field1, sums, *gradients1 = call(
        kernel_back_second,
        "back_second",
        [fields, struct((4, S_ROWS, LANES), F32)] + [piece] * 4,
        [smem()] + [vmem()] * 6,
        [grad_scratch],
        limit=12,
    )(meta, field2, inner, pack, stats1, sums, rest_all)
    gradients1, gradients2, att, first_d = tie(gradients1, gradients2, att, first_d)
    firsts = (first_t, first_c, first_y, first_d)
    gradients1 = exchange(gradients1)
    att = down(att, 1)
    gradients2, att[0] = tie(gradients2, att[0])
    send2, wide2 = weight_send(seconds, gradients2)
    got2 = swap(send2, "dp", 1)
    wide2, att = tie(wide2, att)
    att = down(att, 2)
    wide2, att[0] = tie(wide2, att[0])
    own2 = weight_own(seconds, wide2)
    own2, att, field1 = tie(own2, att, field1)
    for level in range(3, len(levels)):
        att = down(att, level)
    att_own, att_far = call(
        kernel_far,
        "att_far",
        [struct((4,) + att[0].shape[1:], F32), struct((4,) + att[0].shape[1:], BF16)],
        [vmem()] * 2,
        [],
        limit=12,
    )(*att)
    field1, att_own = tie(field1, att_own)
    att = [att_own, swap(att_far, "mp", 2)]
    grad_first = call(
        kernel_back_conv,
        "back_conv",
        block32,
        [vmem()] * 2,
        [],
    )(field1, conv1_all)
    grad_first, gradients1, att = tie(grad_first, gradients1, att)
    att = total_sum(att)
    for level in range(len(levels) - 1, 2, -1):
        att = join(across(att, level), digits[level], meta)
    gradients1, att, out_far = tie(gradients1, att, out_far)
    att = across(att, 2)
    send1, wide1 = weight_send(firsts, gradients1)
    got1 = swap(send1, "dp", 1)
    out_far = swap(out_far, "mp", 2)
    wide1, got2, own2 = tie(wide1, got2, own2)
    terms2 = down([own2, got2], 1)
    wide1, terms2[0] = tie(wide1, terms2[0])
    own1 = weight_own(firsts, wide1)
    grad_first, own1, terms2, att = tie(grad_first, own1, terms2, att)
    terms2 = down(terms2, 2)
    att = across(join(att, digits[2], meta), 1)
    grad_first, terms2[0], att[0] = tie(grad_first, terms2[0], att[0])
    grad_own, grad_near, grad_far = call(
        kernel_back_first,
        "back_first",
        [
            struct((pixels + S_ROWS, LANES), BF16),
            struct((pixels + S_ROWS, LANES), BF16),
            struct((2, pixels + S_ROWS, LANES), BF16),
        ],
        [smem()] + [vmem()] * 6,
        [grad_scratch, pltpu.VMEM((4, S_ROWS, LANES), F32)],
    )(meta, grad_first, image, pack, stats1, dmiddle, sums)
    grad_far, terms2, got1, own1 = tie(grad_far, terms2, got1, own1)
    terms1 = down([own1, got1], 1)
    ends2 = across(inner_levels(terms2), 2)
    factors, ends2[0], terms1[0] = tie(factors, ends2[0], terms1[0])
    columns = -(-5 * slots * lax.axis_size("dp") // LANES) * LANES
    left = call(
        kernel_factors,
        "factors",
        struct((EMB, columns), BF16),
        [smem()] + [vmem()] * 2,
        [],
        limit=12 if len(steps) < 4 else 56,
    )(meta, *factors)
    grad_far, ends2[0], terms1[0], att, left = tie(grad_far, ends2[0], terms1[0], att, left)
    att = across(join(att, digits[1], meta), 0)
    grad_far = swap(grad_far, "mp", 2)
    ends2, terms1, grad_near, out_far = tie(ends2, terms1, grad_near, out_far)
    terms1 = down(terms1, 2)
    ends2 = across(join(ends2, digits[2], meta), 1)
    scale = call(kernel_scale, "scale", struct((8, LANES), F32), [vmem()] * 2, [], limit=8)(*factors)
    ends2, terms1, scale, att = tie(ends2, terms1, scale, att)
    ends1 = across(inner_levels(terms1), 2)
    ends2 = across(join(ends2, digits[1], meta), 0)
    qkv_grad, proj_grad = last_join(att, digits[0], meta, scale, True)
    ends1, qkv_grad, grad_near = tie(ends1, qkv_grad, grad_near)
    ends1 = across(join(ends1, digits[2], meta), 1)
    ends1[0], grad_near, grad_far = tie(ends1[0], grad_near, grad_far)
    grad_near = swap(grad_near, "mp", 1)
    grad_across = swap(grad_far, "mp", 1)
    image_parts = (grad_own, grad_near, grad_far, grad_across)
    smalls = call(
        kernel_small_stack,
        "stack",
        struct((4, S_ROWS, LANES), BF16),
        [vmem()] * 4,
        [],
        limit=8,
    )(grad_own, grad_near, grad_far, grad_across)
    small_got = swap(smalls, "dp", 1)
    ends1 = across(join(ends1, digits[1], meta), 0)
    ends1[0], small_got, ends2 = tie(ends1[0], small_got, ends2)
    smalls = stack([smalls, small_got])
    for low in steps[1:-1]:
        smalls = stack([smalls, swap(smalls, "dp", low)])
    small_got = swap(smalls, "dp", steps[-1])
    (conv2_grad,) = last_join(ends2, digits[0], meta, scale)
    smalls, out_far, out_near, conv2_grad = tie(smalls, out_far, out_near, conv2_grad)
    out_parts = (out_own, swap(out_near, "mp", 1), out_far, swap(out_far, "mp", 1))
    def in_slots(parts):
        return pl.pallas_call(
            kernel_slots,
            name="slots",
            out_shape=struct((4, pixels, LANES), BF16),
            in_specs=[smem()] + [anywhere()] * 4,
            out_specs=vmem(),
            scratch_shapes=[pltpu.SemaphoreType.DMA((4,))],
            compiler_params=pltpu.CompilerParams(vmem_limit_bytes=8 * MIB),
        )(meta, *parts)

    block_out = in_slots(out_parts)
    image_grad = in_slots(image_parts)
    small_got, block_out, image_grad = tie(small_got, block_out, image_grad)
    embed_grad, context_grad, vector_sums = call(
        kernel_factor_grads,
        "factor_grads",
        [
            struct((EMB, 2, LANES), F32),
            struct((EMB, 2, LANES), F32),
            struct((S_ROWS, LANES), F32),
        ],
        [vmem()] * 4,
        [],
        limit=14 if len(steps) < 4 else 56,
    )(scale, left, smalls, small_got)

    ends1, embed_grad = tie(ends1, embed_grad)
    (conv1_grad,) = last_join(ends1, digits[0], meta, scale)
    return (
        block_out,
        image_grad,
        vector_sums[S_G1],
        vector_sums[S_B1],
        conv1_grad.reshape(3, 3, C, LANES),
        embed_grad,
        vector_sums[S_G2],
        vector_sums[S_B2],
        conv2_grad.reshape(3, 3, C, LANES),
        vector_sums[S_CB2],
        vector_sums[S_G3],
        vector_sums[S_B3],
        jnp.transpose(qkv_grad, (1, 0, 2)),
        context_grad,
        proj_grad,
    )


def solution(mesh):
    return jax.shard_map(
        local,
        mesh=mesh,
        in_specs=(
            P("dp", None, "mp"),
            P("dp", None, "mp"),
            P("dp"),
            P("dp", None),
            P("dp", None, None),
            P("dp"),
            P("mp"),
            P("mp"),
            P(None, None, None, "mp"),
            P(None, None, "mp"),
            P("mp"),
            P("mp"),
            P(None, None, None, "mp"),
            P("mp"),
            P("mp"),
            P("mp"),
            P(None, None, "mp"),
            P(None, None, "mp"),
            P("mp", None),
        ),
        out_specs=(
            P("dp", None, "mp"),
            P("dp", None, "mp"),
            P("mp"),
            P("mp"),
            P(None, None, None, "mp"),
            P(None, None, "mp"),
            P("mp"),
            P("mp"),
            P(None, None, None, "mp"),
            P("mp"),
            P("mp"),
            P("mp"),
            P(None, None, "mp"),
            P(None, None, "mp"),
            P("mp", None),
        ),
        check_vma=False,
    )
```

```python
import functools
import math

import jax
import jax.numpy as jnp
from jax import lax
from jax.experimental import pallas as pl
from jax.experimental.pallas import tpu as pltpu
from jax.sharding import PartitionSpec as P

C = 512
GROUPS = 32
HEAD = 64
EMB = 2048
CTX = 4
SIDE = 32
LANES = 128
PAD = SIDE
EPSILON = 1e-05
F32 = jnp.float32
BF16 = jnp.bfloat16
NEG = -1e30
QKV_ROW = 9 * C
PROJ_ROW = QKV_ROW + 3 * C

E_G1, E_B1, E_G2, E_B2, E_CB2, E_G3, E_B3, M_SCALE, M_SHIFT = range(9)
M_KEY, M_VALUE, E_ROWS = 16, 24, 32
S_G3, S_B3, S_CB2, S_G2, S_B2, S_SCALE, S_SHIFT = range(7)
S_KEY, S_VALUE, S_G1, S_B1, S_ROWS = 8, 12, 16, 17, 32
MIB = 1 << 20


def vmem():
    return pl.BlockSpec(memory_space=pltpu.VMEM)


def anywhere():
    return pl.BlockSpec(memory_space=pltpu.HBM)


def smem():
    return pl.BlockSpec(memory_space=pltpu.SMEM)


def struct(shape, dtype):
    return jax.ShapeDtypeStruct(shape, dtype)


def call(body, name, out_shape, in_specs, scratch, flops=0, limit=14):
    many = isinstance(out_shape, (list, tuple))
    return pl.pallas_call(
        body,
        name=name,
        out_shape=out_shape,
        in_specs=in_specs,
        out_specs=[vmem() for _ in out_shape] if many else vmem(),
        scratch_shapes=scratch,
        compiler_params=pltpu.CompilerParams(vmem_limit_bytes=limit * MIB),
        cost_estimate=pl.CostEstimate(flops=0, transcendentals=0, bytes_accessed=0),
    )


def fetch(sources, target, me, sems, first):
    copies = []
    for offset, source in enumerate(sources):
        copy = pltpu.make_async_copy(
            source, target.at[jnp.bitwise_xor(me, offset)], sems.at[first + offset]
        )
        copy.start()
        copies.append(copy)
    return copies


def fetch_routed(sources, target, me, parity, sems, first):
    quarter = target.shape[1] // 4
    copies = []
    for index, source in enumerate(sources):
        place = target.at[jnp.bitwise_xor(me, (0, 1, 2, 2, 2, 3, 3, 3)[index])]
        if index >= 2:
            kind = (index - 2) % 3
            rows = 2 * quarter if kind == 0 else quarter
            half = parity if kind == 0 else 1 - parity
            start = half * 2 * quarter + (quarter if kind == 2 else 0)
            place = place.at[pl.ds(pl.multiple_of(start, quarter), rows), :]
        copy = pltpu.make_async_copy(source, place, sems.at[first + index])
        copy.start()
        copies.append(copy)
    return copies


def wait_all(copies):
    for copy in copies:
        copy.wait()


def fold(values):
    rows = values.shape[0]
    return jnp.sum(values.reshape(rows // 8, 8, values.shape[1]), axis=0)


def group_sum(rows8):
    lane = lax.broadcasted_iota(jnp.int32, rows8.shape, 1)
    total = jnp.broadcast_to(jnp.sum(rows8, axis=0, keepdims=True), rows8.shape)
    for step in (1, 2, 4, 8):
        up = pltpu.roll(total, step, axis=1)
        down = pltpu.roll(total, LANES - step, axis=1)
        total = total + jnp.where((lane & step) != 0, up, down)
    return total[0:1]


def column_sum(rows8):
    return jnp.sum(rows8, axis=0, keepdims=True)


def sum_strips(pixels, strip, width, function):
    zero = tuple(jnp.zeros((8, LANES), F32) for _ in range(width))

    def body(index, carry):
        start = pl.multiple_of(index * strip, strip)
        return tuple(old + fold(new) for old, new in zip(carry, function(start)))

    return lax.fori_loop(0, pixels // strip, body, zero)


def norm_rows(pixels, strip, read):
    count = pixels * (C // GROUPS)
    sums = sum_strips(pixels, strip, 4, lambda start: [read(b, start) for b in range(4)])
    means = [group_sum(s) * (1.0 / count) for s in sums]
    squares = sum_strips(
        pixels,
        strip,
        4,
        lambda start: [jnp.square(read(b, start) - means[b]) for b in range(4)],
    )
    inverses = [lax.rsqrt(group_sum(s) * (1.0 / count) + EPSILON) for s in squares]
    return means, inverses


def shifted(values):
    rows = values.shape[0]
    column = lax.broadcasted_iota(jnp.int32, values.shape, 0) & (SIDE - 1)
    left = jnp.where(column == 0, 0.0, pltpu.roll(values, 1, axis=0))
    right = jnp.where(column == SIDE - 1, 0.0, pltpu.roll(values, rows - 1, axis=0))
    return left, values, right


def store_shifted(target, block, start, values):
    rows = values.shape[0]
    for position, part in enumerate(shifted(values)):
        target[position, block, pl.ds(pl.multiple_of(PAD + start, 32), rows), :] = part.astype(BF16)


def clear_padding(target, pixels):
    zero = jnp.zeros((PAD, LANES), BF16)
    for position in range(3):
        for block in range(4):
            target[position, block, 0:PAD, :] = zero
            target[position, block, PAD + pixels : PAD + pixels + PAD, :] = zero


def conv_tiles(field, weight, pixels, tile, write):
    def body(index, carry):
        start = pl.multiple_of(index * tile, tile)
        left = jnp.concatenate(
            [
                field[b, block, pl.ds(pl.multiple_of(start + a * SIDE, 32), tile), :]
                for a in range(3)
                for b in range(3)
                for block in range(4)
            ],
            axis=1,
        )
        right = jnp.concatenate([weight[s, 0 : 9 * C, :] for s in range(4)], axis=1)
        write(start, jnp.dot(left, right, preferred_element_type=F32))
        return carry

    lax.fori_loop(0, pixels // tile, body, 0)


def conv_back_tiles(field, weight, pixels, tile, write):
    def body(index, carry):
        start = pl.multiple_of((index // 2) * tile, tile)
        half = index % 2
        left = jnp.concatenate(
            [
                field[2 - b, block, pl.ds(pl.multiple_of(start + (2 - a) * SIDE, 32), tile), :]
                for a in range(3)
                for b in range(3)
                for block in range(4)
            ],
            axis=1,
        )
        right = jnp.concatenate(
            [
                weight[block, pl.ds(pl.multiple_of((3 * a + b) * C + half * 256, 256), 256), :]
                for a in range(3)
                for b in range(3)
                for block in range(4)
            ],
            axis=1,
        )
        write(
            start,
            half,
            lax.dot_general(left, right, (((1,), (1,)), ((), ())), preferred_element_type=F32),
        )
        return carry

    lax.fori_loop(0, 2 * (pixels // tile), body, 0)


def silu_slope(before, grad_out):
    gate = jax.nn.sigmoid(before)
    return grad_out * gate * (1.0 + before * (1.0 - gate))


def kernel_early(meta, scale_shift, context, v0, v1, v2, v3, v4, v5, v6, own, near, far):
    for offset, target in enumerate((own, near, far.at[0], far.at[1])):
        slot = jnp.bitwise_xor(meta[0], offset)
        target[...] = jnp.zeros((E_ROWS, LANES), F32)
        for row, vector in enumerate((v0, v1, v2, v3, v4, v5, v6)):
            target[row : row + 1, :] = vector[...]
        scales = scale_shift[slot]
        target[M_SCALE : M_SCALE + 1, :] = scales[:, :LANES]
        target[M_SHIFT : M_SHIFT + 1, :] = scales[:, LANES:]
        tokens = context[slot]
        target[M_KEY : M_KEY + 8, :] = tokens[:, :LANES]
        target[M_VALUE : M_VALUE + 8, :] = tokens[:, LANES:]


def kernel_first(
    meta, i0, i1, i2, i3, e0, e1, e2, e3, w0, w1, w2, w3, w4, w5, w6, w7,
    image, pack, first_t, inner, second_t, second, weight, stats, field, sems,
):
    pixels = image.shape[1]
    me = meta[0]
    image_copies = fetch((i0, i1, i2.at[0], i3.at[1]), image, me, sems, 0)
    pack_copies = fetch((e0, e1, e2.at[0], e3.at[1]), pack, me, sems, 4)
    weight_copies = fetch_routed((w0, w1, w2, w3, w4, w5, w6, w7), weight, me, meta[2], sems, 8)
    clear_padding(field, pixels)
    clear_padding(second, pixels)
    wait_all(image_copies)
    wait_all(pack_copies)
    strip = 128

    def read(block, start):
        return image[block, pl.ds(start, strip), :].astype(F32)

    means, inverses = norm_rows(pixels, strip, read)

    def normalise(index, carry):
        start = pl.multiple_of(index * strip, strip)
        for b in range(4):
            gain = pack[b, E_G1 : E_G1 + 1, :]
            bias = pack[b, E_B1 : E_B1 + 1, :]
            before = (read(b, start) - means[b]) * inverses[b] * gain + bias
            after = before * jax.nn.sigmoid(before)
            store_shifted(field, b, start, after)
            first_t[b, :, pl.ds(start, strip)] = after.T.astype(BF16)
        return carry

    lax.fori_loop(0, pixels // strip, normalise, 0)
    wait_all(weight_copies)

    def write(start, tile):
        for b in range(4):
            inner[b, pl.ds(start, tile.shape[0]), :] = tile[:, b * LANES : (b + 1) * LANES]

    conv_tiles(field, weight, pixels, 512, write)
    means2, inverses2 = norm_rows(pixels, strip, lambda b, start: inner[b, pl.ds(start, strip), :])

    def modulate(index, carry):
        start = pl.multiple_of(index * strip, strip)
        for b in range(4):
            gain = pack[b, E_G2 : E_G2 + 1, :]
            bias = pack[b, E_B2 : E_B2 + 1, :]
            scale = pack[b, M_SCALE : M_SCALE + 1, :]
            shift = pack[b, M_SHIFT : M_SHIFT + 1, :]
            normed = (inner[b, pl.ds(start, strip), :] - means2[b]) * inverses2[b]
            modulated = (normed * gain + bias) * (1.0 + scale) + shift
            after = modulated * jax.nn.sigmoid(modulated)
            store_shifted(second, b, start, after)
            second_t[b, :, pl.ds(start, strip)] = after.T.astype(BF16)
        return carry

    lax.fori_loop(0, pixels // strip, modulate, 0)
    for b in range(4):
        for row, value in enumerate((means[b], inverses[b], means2[b], inverses2[b])):
            stats[b, row : row + 1, :] = value


def kernel_second(
    meta, second, image, pack, w0, w1, w2, w3, w4, w5, w6, w7,
    middle, attn_t, qkv, qkv_weight, proj_weight, weight, stats, attn, sems,
):
    pixels = image.shape[1]
    me = meta[0]
    wait_all(fetch_routed((w0, w1, w2, w3, w4, w5, w6, w7), weight, me, meta[2], sems, 0))
    strip = 128

    def write(start, tile):
        rows = tile.shape[0]
        for b in range(4):
            branch = tile[:, b * LANES : (b + 1) * LANES] + pack[b, E_CB2 : E_CB2 + 1, :]
            middle[b, pl.ds(start, rows), :] = image[b, pl.ds(start, rows), :].astype(F32) + branch

    conv_tiles(second, weight, pixels, 512, write)
    means, inverses = norm_rows(pixels, strip, lambda b, start: middle[b, pl.ds(start, strip), :])

    def normalise(index, carry):
        start = pl.multiple_of(index * strip, strip)
        for b in range(4):
            normed = (middle[b, pl.ds(start, strip), :] - means[b]) * inverses[b]
            value = normed * pack[b, E_G3 : E_G3 + 1, :] + pack[b, E_B3 : E_B3 + 1, :]
            attn[b, pl.ds(start, strip), :] = value.astype(BF16)
            attn_t[b, :, pl.ds(start, strip)] = value.T.astype(BF16)
        return carry

    lax.fori_loop(0, pixels // strip, normalise, 0)
    for s in range(4):
        qkv_weight[s] = weight[s, QKV_ROW:PROJ_ROW, :]
        proj_weight[s] = weight[s, PROJ_ROW : PROJ_ROW + C, :]

    def project(index, carry):
        s = index // 2
        start = pl.multiple_of((index % 2) * 512, 512)
        left = jnp.concatenate([attn[b, pl.ds(start, 512), :] for b in range(4)], axis=1)
        right = jnp.concatenate(
            [weight[s, QKV_ROW + kind * C : QKV_ROW + (kind + 1) * C, :] for kind in range(3)], axis=1
        )
        qkv[s, pl.ds(start, 512), :] = jnp.dot(left, right, preferred_element_type=F32).astype(BF16)
        return carry

    lax.fori_loop(0, 4 * (pixels // 512), project, 0)
    for b in range(4):
        for row, value in enumerate((means[b], inverses[b])):
            stats[b, row : row + 1, :] = value


def kernel_attention(
    meta, qkv, pack, middle, weight, c0, c1, c2, c3,
    o0, o1, o2, cot, mixed, dqkv, dctx,
    grad_mixed, score_ctx, grad_ctx_prob, prob_ctx, dscore_ctx, out_pix, dquery, dkey_t, dvalue_t, sems,
):
    pixels = qkv.shape[1]
    me = meta[0]
    alive = meta[1].astype(F32)
    cot_copies = fetch((c0, c1, c2, c3), cot, me, sems, 0)
    scale = 1.0 / math.sqrt(HEAD)
    block = 1024

    row32 = lax.broadcasted_iota(jnp.int32, (32, LANES), 0)
    lane32 = lax.broadcasted_iota(jnp.int32, (32, LANES), 1)

    def diagonal(kind):
        found = []
        for s in range(4):
            rows8 = pack[s, kind : kind + 8, :]
            tiled = jnp.concatenate([rows8] * 4, axis=0)
            own = (row32 // 4) == (2 * s + lane32 // HEAD)
            kept = jnp.where(own, tiled, 0.0)
            found.append(jnp.concatenate([kept, jnp.zeros((96, LANES), F32)], axis=0).astype(BF16))
        return jnp.concatenate(found, axis=1)

    keys_ctx = diagonal(M_KEY)
    values_ctx = diagonal(M_VALUE)
    wait_all(cot_copies)

    def projection():
        return jnp.concatenate(
            [
                jnp.concatenate([weight[s, o * LANES : (o + 1) * LANES, :] for o in range(4)], axis=1)
                for s in range(4)
            ],
            axis=0,
        )

    def prepare(index, carry):
        start = pl.multiple_of(index * block, block)
        rows = pl.ds(start, block)
        for s in range(4):
            cot[s, rows, :] = (cot[s, rows, :].astype(F32) * alive).astype(BF16)
        all_cot = jnp.concatenate([cot[s, rows, :] for s in range(4)], axis=1)
        all_weight = projection()
        grad = lax.dot_general(
            all_cot, all_weight, (((1,), (1,)), ((), ())), preferred_element_type=F32
        ).astype(BF16)
        for s in range(4):
            grad_mixed[s, rows, :] = grad[:, s * LANES : (s + 1) * LANES]
        query = jnp.concatenate([qkv[s, rows, 0:LANES] for s in range(4)], axis=1)
        score_ctx[rows, :] = lax.dot_general(
            query, keys_ctx, (((1,), (1,)), ((), ())), preferred_element_type=F32
        )
        grad_ctx_prob[rows, :] = lax.dot_general(
            grad, values_ctx, (((1,), (1,)), ((), ())), preferred_element_type=F32
        )
        prob_ctx[rows, :] = jnp.zeros((block, LANES), F32)
        dscore_ctx[rows, :] = jnp.zeros((block, LANES), F32)
        return carry

    lax.fori_loop(0, pixels // block, prepare, 0)
    lane = lax.broadcasted_iota(jnp.int32, (block, LANES), 1)
    low = lane < HEAD
    ones = jnp.ones((pixels, LANES), BF16)
    blocks = pixels // block

    def attend(index, carry):
        s = index // blocks
        part = index % blocks
        rows = pl.ds(pl.multiple_of(part * block, block), block)

        @pl.when(part == 0)
        def _():
            dkey_t[...] = jnp.zeros((LANES, pixels), F32)
            dvalue_t[...] = jnp.zeros((LANES, pixels), F32)

        query = qkv[s, rows, 0:LANES]
        key = qkv[s, :, LANES : 2 * LANES]
        value = qkv[s, :, 2 * LANES : 3 * LANES]
        value_ones = jnp.concatenate([value, ones], axis=1)
        grad = grad_mixed[s, rows, :]
        ctx_scores = score_ctx[rows, :]
        ctx_grads = grad_ctx_prob[rows, :]
        exps, outs, inverses, ctx_exps, owns = [], [], [], [], []
        for h in range(2):
            mine = low if h == 0 else jnp.logical_not(low)
            own = lane // CTX == 2 * s + h
            score = lax.dot_general(
                jnp.where(mine, query, jnp.zeros_like(query)),
                key,
                (((1,), (1,)), ((), ())),
                preferred_element_type=F32,
            )
            top = jnp.maximum(
                jnp.max(score, axis=1, keepdims=True),
                jnp.max(jnp.where(own, ctx_scores, NEG), axis=1, keepdims=True),
            )
            exp = jnp.exp((score - top) * scale).astype(BF16)
            ctx_exp = jnp.where(own, jnp.exp((ctx_scores - top) * scale), 0.0)
            out = jnp.dot(exp, value_ones, preferred_element_type=F32)
            total = out[:, LANES:] + jnp.sum(ctx_exp, axis=1, keepdims=True)
            inverse = 1.0 / total
            exps.append(exp)
            outs.append(out[:, :LANES] * inverse)
            inverses.append(inverse)
            ctx_exps.append(ctx_exp)
            owns.append(own)
        out_pair = jnp.where(low, outs[0], outs[1])
        out_pix[s, rows, :] = out_pair
        inverse_pair = jnp.where(low, inverses[0], inverses[1])
        scaled = (grad.astype(F32) * (inverse_pair * scale)).astype(BF16)
        product = out_pair * scaled.astype(F32)
        query_t = query.astype(F32).T.astype(BF16)
        scaled_t = scaled.astype(F32).T.astype(BF16)
        prob_keep = prob_ctx[rows, :]
        dscore_keep = dscore_ctx[rows, :]
        dqs = []
        for h in range(2):
            mine = low if h == 0 else jnp.logical_not(low)
            own = owns[h]
            ctx_prob = ctx_exps[h] * inverses[h]
            ctx_grad = ctx_grads * (inverses[h] * scale)
            dot = jnp.sum(
                jnp.where(mine, product, 0.0) + ctx_prob * jnp.where(own, ctx_grad, 0.0),
                axis=1,
                keepdims=True,
            )
            weight_grad = lax.dot_general(
                jnp.where(mine, scaled, jnp.zeros_like(scaled)),
                value,
                (((1,), (1,)), ((), ())),
                preferred_element_type=F32,
            )
            dscore = (exps[h].astype(F32) * (weight_grad - dot)).astype(BF16)
            prob_keep = jnp.where(own, ctx_prob, prob_keep)
            dscore_keep = jnp.where(own, ctx_exps[h] * (ctx_grad - dot), dscore_keep)
            dqs.append(jnp.dot(dscore, key, preferred_element_type=F32))
            half = slice(h * HEAD, (h + 1) * HEAD)
            dkey_t[half, :] += jnp.dot(query_t[half], dscore, preferred_element_type=F32)
            dvalue_t[half, :] += jnp.dot(scaled_t[half], exps[h], preferred_element_type=F32)
        prob_ctx[rows, :] = prob_keep
        dscore_ctx[rows, :] = dscore_keep
        dquery[s, rows, :] = jnp.where(low, dqs[0], dqs[1])

        @pl.when(part == blocks - 1)
        def _():
            for piece in range(pixels // LANES):
                cut = slice(piece * LANES, (piece + 1) * LANES)
                dqkv[s, cut, LANES : 2 * LANES] = dkey_t[:, cut].T.astype(BF16)
                dqkv[s, cut, 2 * LANES : 3 * LANES] = (dvalue_t[:, cut] * (1.0 / scale)).T.astype(BF16)

        return carry

    lax.fori_loop(0, 4 * blocks, attend, 0)

    def finish(index, carry):
        dkeys, dvalues = carry
        start = pl.multiple_of(index * block, block)
        rows = pl.ds(start, block)
        prob = prob_ctx[rows, :].astype(BF16)
        dscore = dscore_ctx[rows, :].astype(BF16)
        out_ctx = jnp.dot(prob, values_ctx, preferred_element_type=F32)
        dquery_ctx = jnp.dot(dscore, keys_ctx, preferred_element_type=F32)
        parts = []
        for s in range(4):
            cut = slice(s * LANES, (s + 1) * LANES)
            both = (out_pix[s, rows, :] + out_ctx[:, cut]).astype(BF16)
            mixed[s, rows, :] = both
            parts.append(both)
            dqkv[s, rows, 0:LANES] = (dquery[s, rows, :] + dquery_ctx[:, cut]).astype(BF16)
        result = jnp.dot(
            jnp.concatenate(parts, axis=1), projection(), preferred_element_type=F32
        )
        for offset, target in enumerate((o0, o1, o2.at[0], o2.at[1])):
            other = jnp.bitwise_xor(me, offset)
            value = jnp.zeros((block, LANES), F32)
            for s in range(4):
                value = jnp.where(other == s, result[:, s * LANES : (s + 1) * LANES], value)
            target[rows, :] = ((middle[other, rows, :] + value) * alive).astype(BF16)
        query = jnp.concatenate([qkv[s, rows, 0:LANES] for s in range(4)], axis=1)
        grad = jnp.concatenate([grad_mixed[s, rows, :] for s in range(4)], axis=1)
        dkeys = dkeys + jnp.dot(dscore_ctx[rows, :].T[0:32].astype(BF16), query, preferred_element_type=F32)
        dvalues = dvalues + jnp.dot(prob_ctx[rows, :].T[0:32].astype(BF16), grad, preferred_element_type=F32)
        return dkeys, dvalues

    zero = jnp.zeros((32, C), F32)
    dkeys, dvalues = lax.fori_loop(0, pixels // block, finish, (zero, zero))
    for s in range(4):
        own = (row32 // 4) == (2 * s + lane32 // HEAD)
        for position, source in enumerate((dkeys, dvalues)):
            kept = jnp.where(own, source[:, s * LANES : (s + 1) * LANES], 0.0)
            eight = jnp.sum(kept.reshape(4, 8, LANES), axis=0)
            folded = eight + pltpu.roll(eight, 4, axis=0)
            dctx[s, position * CTX : (position + 1) * CTX, :] = folded[0:CTX]


def saved(stats, row):
    return [stats[b, row : row + 1, :] for b in range(4)]


def norm_back_strips(pixels, strip, read_normed, read_grad, gains, inverses, gain_sums, bias_sums, write):
    count = pixels * (C // GROUPS)
    firsts, seconds = (
        [
            group_sum(jnp.broadcast_to(sums[b] * gains[b], (8, LANES)) * (1.0 / 8)) * (1.0 / count)
            for b in range(4)
        ]
        for sums in (bias_sums, gain_sums)
    )

    def body(index, carry):
        start = pl.multiple_of(index * strip, strip)
        found = []
        for b in range(4):
            normed = read_normed(b, start)
            grad = read_grad(b, start) * gains[b]
            found.append(write(b, start, inverses[b] * (grad - firsts[b] - normed * seconds[b])))
        if found[0] is None:
            return carry
        return tuple(old + fold(new) for old, new in zip(carry, found))

    zero = tuple(jnp.zeros((8, LANES), F32) for _ in range(4))
    return lax.fori_loop(0, pixels // strip, body, zero)


def kernel_back_attention(
    meta, dqkv, cot, middle, pack, stats, dctx, qkv_weight,
    dmiddle, field, sums, d0, d1, d2, d3, dattn,
):
    pixels = cot.shape[1]
    me = meta[0]
    strip = 128
    clear_padding(field, pixels)
    means, inverses = saved(stats, 0), saved(stats, 1)

    def back(index, carry):
        start = pl.multiple_of(index * 512, 512)
        left = jnp.concatenate([dqkv[s, pl.ds(start, 512), :] for s in range(4)], axis=1)
        right = jnp.concatenate(
            [qkv_weight[s, kind * C : (kind + 1) * C, :] for s in range(4) for kind in range(3)], axis=1
        )
        tile = lax.dot_general(left, right, (((1,), (1,)), ((), ())), preferred_element_type=F32)
        for b in range(4):
            dattn[b, pl.ds(start, 512), :] = tile[:, b * LANES : (b + 1) * LANES]
        return carry

    lax.fori_loop(0, pixels // 512, back, 0)
    gains = [pack[b, E_G3 : E_G3 + 1, :] for b in range(4)]

    def read_normed(b, start):
        return (middle[b, pl.ds(start, strip), :] - means[b]) * inverses[b]

    def write(b, start, value):
        total = cot[b, pl.ds(start, strip), :].astype(F32) + value
        dmiddle[b, pl.ds(start, strip), :] = total
        rounded = total.astype(BF16).astype(F32)
        store_shifted(field, b, start, rounded)
        return rounded

    def terms(start):
        found = []
        for b in range(4):
            grad = dattn[b, pl.ds(start, strip), :]
            found += [grad, grad * read_normed(b, start)]
        return found

    totals = [column_sum(rows8) for rows8 in sum_strips(pixels, strip, 8, terms)]
    bias_sums, gain_sums = totals[0::2], totals[1::2]
    branch = norm_back_strips(
        pixels,
        strip,
        read_normed,
        lambda b, start: dattn[b, pl.ds(start, strip), :],
        gains,
        inverses,
        gain_sums,
        bias_sums,
        write,
    )
    for b in range(4):
        sums[b] = jnp.zeros((S_ROWS, LANES), F32)
        sums[b, S_G3 : S_G3 + 1, :] = gain_sums[b]
        sums[b, S_B3 : S_B3 + 1, :] = bias_sums[b]
        sums[b, S_CB2 : S_CB2 + 1, :] = column_sum(branch[b])
        sums[b, S_KEY : S_KEY + 8, :] = dctx[b]
    for offset, target in enumerate((d0, d1, d2, d3)):
        target[...] = field[1, jnp.bitwise_xor(me, offset), PAD : PAD + pixels, :]


def kernel_attention_grad(meta, dqkv, mixed, attn_t, cot, keep, send, cot_t):
    pixels = cot.shape[1]
    me = meta[0]
    strip = 128

    def turn(index, carry):
        start = pl.multiple_of(index * strip, strip)
        for b in range(4):
            cot_t[b, :, pl.ds(start, strip)] = cot[b, pl.ds(start, strip), :].astype(F32).T.astype(BF16)
        return carry

    lax.fori_loop(0, pixels // strip, turn, 0)

    attn_all = attn_t[...].reshape(C, pixels)
    cot_all = cot_t[...].reshape(C, pixels)
    for offset, target in enumerate((keep, send)):
        s = jnp.bitwise_xor(me, offset)
        pair = (s, jnp.bitwise_xor(s, 2))
        right = jnp.concatenate([dqkv[p] for p in pair], axis=1)
        grad = jnp.dot(attn_all, right, preferred_element_type=F32).astype(BF16)
        right = jnp.concatenate([mixed[p] for p in pair], axis=1)
        other = jnp.dot(cot_all, right, preferred_element_type=F32).astype(BF16)
        for place in range(2):
            for kind in range(3):
                column = (3 * place + kind) * LANES
                target[place, kind] = grad[:, column : column + LANES]
            target[place, 3] = other[:, place * LANES : (place + 1) * LANES]


def weight_taps(half, sources, field, target):
    pixels = sources[0].shape[2]

    def body(index, carry):
        left = jnp.concatenate(
            [source[pl.ds(2 * half, 2)].reshape(2 * LANES, pixels) for source in sources], axis=1
        )
        columns = []
        for tap in (2 * index, jnp.minimum(2 * index + 1, 8)):
            start = pl.multiple_of((2 - tap // 3) * SIDE, 32)
            side = 2 - lax.rem(tap, 3)
            columns.append(
                jnp.concatenate([field[side, k, pl.ds(start, pixels), :] for k in range(4)], axis=0)
            )
        grad = jnp.dot(left, jnp.concatenate(columns, axis=1), preferred_element_type=F32)
        target[2 * index] = grad[:, :LANES].astype(target.dtype)

        @pl.when(index < 4)
        def _():
            target[2 * index + 1] = grad[:, LANES:].astype(target.dtype)

        return carry

    lax.fori_loop(0, 5, body, 0)


def kernel_weight_send(meta, u0, u1, u2, u3, d0, d1, d2, d3, send, field):
    pixels = u0.shape[2]
    clear_padding(field, pixels)
    strip = 128

    def spread(index, carry):
        start = pl.multiple_of(index * strip, strip)
        for k, source in enumerate((d0, d1, d2, d3)):
            store_shifted(field, k, start, source[pl.ds(start, strip), :].astype(F32))
        return carry

    lax.fori_loop(0, pixels // strip, spread, 0)
    weight_taps(1 - meta[3], (u0, u1, u2, u3), field, send)


def kernel_weight_own(meta, u0, u1, u2, u3, field, own):
    weight_taps(meta[3], (u0, u1, u2, u3), field, own)


def kernel_back_second(
    meta, grad_field, inner, pack, stats, sums_in, weight,
    field, sums, d0, d1, d2, d3, grad,
):
    pixels = inner.shape[1]
    me = meta[0]
    strip = 128
    clear_padding(field, pixels)
    means, inverses = saved(stats, 2), saved(stats, 3)

    def write_grad(start, half, tile):
        for b in range(2):
            grad[2 * half + b, pl.ds(start, tile.shape[0]), :] = tile[:, b * LANES : (b + 1) * LANES]

    conv_back_tiles(grad_field, weight, pixels, 512, write_grad)
    gains = [pack[b, E_G2 : E_G2 + 1, :] for b in range(4)]

    def read_normed(b, start):
        return (inner[b, pl.ds(start, strip), :] - means[b]) * inverses[b]

    def slope(index, carry):
        start = pl.multiple_of(index * strip, strip)
        found = []
        for b in range(4):
            bias = pack[b, E_B2 : E_B2 + 1, :]
            scale = pack[b, M_SCALE : M_SCALE + 1, :]
            shift = pack[b, M_SHIFT : M_SHIFT + 1, :]
            normed = read_normed(b, start)
            modulated = (normed * gains[b] + bias) * (1.0 + scale) + shift
            dmod = silu_slope(modulated, grad[b, pl.ds(start, strip), :])
            grad[b, pl.ds(start, strip), :] = dmod * (1.0 + scale)
            found += [dmod, dmod * normed]
        return tuple(old + fold(new) for old, new in zip(carry, found))

    zero = tuple(jnp.zeros((8, LANES), F32) for _ in range(8))
    totals = [column_sum(rows8) for rows8 in lax.fori_loop(0, pixels // strip, slope, zero)]
    plain, scaled = totals[0::2], totals[1::2]
    factors = [1.0 + pack[b, M_SCALE : M_SCALE + 1, :] for b in range(4)]
    bias_sums = [plain[b] * factors[b] for b in range(4)]
    gain_sums = [scaled[b] * factors[b] for b in range(4)]

    def write(b, start, value):
        store_shifted(field, b, start, value)

    norm_back_strips(
        pixels,
        strip,
        read_normed,
        lambda b, start: grad[b, pl.ds(start, strip), :],
        gains,
        inverses,
        gain_sums,
        bias_sums,
        write,
    )
    for b in range(4):
        sums[b] = sums_in[b]
        sums[b, S_G2 : S_G2 + 1, :] = gain_sums[b]
        sums[b, S_B2 : S_B2 + 1, :] = bias_sums[b]
        sums[b, S_SCALE : S_SCALE + 1, :] = (
            scaled[b] * gains[b] + plain[b] * pack[b, E_B2 : E_B2 + 1, :]
        )
        sums[b, S_SHIFT : S_SHIFT + 1, :] = plain[b]
    for offset, target in enumerate((d0, d1, d2, d3)):
        target[...] = field[1, jnp.bitwise_xor(me, offset), PAD : PAD + pixels, :]


def kernel_back_conv(grad_field, weight, grad):
    pixels = grad.shape[1]

    def write_grad(start, half, tile):
        for b in range(2):
            grad[2 * half + b, pl.ds(start, tile.shape[0]), :] = tile[:, b * LANES : (b + 1) * LANES]

    conv_back_tiles(grad_field, weight, pixels, 512, write_grad)


def kernel_back_first(
    meta, grad_in, image, pack, stats, dmiddle, sums_in, g0, g1, g2, grad, sums,
):
    pixels = image.shape[1]
    me = meta[0]
    strip = 128

    def read(b, start):
        return image[b, pl.ds(start, strip), :].astype(F32)

    means, inverses = saved(stats, 0), saved(stats, 1)
    gains = [pack[b, E_G1 : E_G1 + 1, :] for b in range(4)]

    def read_normed(b, start):
        return (read(b, start) - means[b]) * inverses[b]

    def slope(index, carry):
        start = pl.multiple_of(index * strip, strip)
        found = []
        for b in range(4):
            normed = read_normed(b, start)
            before = normed * gains[b] + pack[b, E_B1 : E_B1 + 1, :]
            value = silu_slope(before, grad_in[b, pl.ds(start, strip), :])
            grad[b, pl.ds(start, strip), :] = value
            found += [value, value * normed]
        return tuple(old + fold(new) for old, new in zip(carry, found))

    zero = tuple(jnp.zeros((8, LANES), F32) for _ in range(8))
    totals = [column_sum(rows8) for rows8 in lax.fori_loop(0, pixels // strip, slope, zero)]
    bias_sums, gain_sums = totals[0::2], totals[1::2]

    def write(b, start, value):
        grad[b, pl.ds(start, strip), :] = dmiddle[b, pl.ds(start, strip), :] + value

    norm_back_strips(
        pixels,
        strip,
        read_normed,
        lambda b, start: grad[b, pl.ds(start, strip), :],
        gains,
        inverses,
        gain_sums,
        bias_sums,
        write,
    )
    for b in range(4):
        sums[b] = sums_in[b]
        sums[b, S_G1 : S_G1 + 1, :] = gain_sums[b]
        sums[b, S_B1 : S_B1 + 1, :] = bias_sums[b]
    for offset, target in enumerate((g0, g1, g2.at[0], g2.at[1])):
        other = jnp.bitwise_xor(me, offset)
        target[0:pixels, :] = grad[other].astype(BF16)
        target[pixels : pixels + S_ROWS, :] = sums[other].astype(BF16)


def kernel_scale(factors0, factors1, scale):
    total = jnp.zeros((1, LANES), F32)
    for factors in (factors0, factors1):
        for g in range(factors.shape[0]):
            total = total + factors[g, 0].astype(F32)[1:2, 0:LANES]
    scale[...] = jnp.broadcast_to(1.0 / total, (8, LANES))


def kernel_factors(meta, factors0, factors1, left):
    conditions, tokens = [], []
    for factors in (factors0, factors1):
        for g in range(factors.shape[0]):
            for k in range(4):
                rows = factors[g, jnp.bitwise_xor(meta[0], k)].astype(F32)
                conditions.append(rows[0:1])
                tokens.append(rows[CTX : 2 * CTX])
    rest = left.shape[1] - 5 * len(conditions)
    rows = tokens + conditions
    if rest:
        rows.append(jnp.zeros((rest, EMB), F32))
    left[...] = jnp.concatenate(rows, axis=0).T.astype(BF16)


def kernel_factor_grads(scale, left, small0, small1, embed, context, vectors):
    inverse = scale[0:1, :]
    total = jnp.zeros((S_ROWS, LANES), F32)
    scales, shifts, keys, values = [], [], [], []
    for small in (small0, small1):
        for k in range(small.shape[0]):
            term = small[k].astype(F32)
            total = total + term
            scales.append(term[S_SCALE : S_SCALE + 1])
            shifts.append(term[S_SHIFT : S_SHIFT + 1])
            keys.append(term[S_KEY : S_KEY + CTX])
            values.append(term[S_VALUE : S_VALUE + CTX])
    vectors[...] = total * inverse
    images = len(scales)
    rest = left.shape[1] - 5 * images
    none = jnp.zeros((4 * images, LANES), F32)
    columns = []
    for parts in (keys, values):
        whole = [jnp.concatenate(parts, axis=0), jnp.zeros((images + rest, LANES), F32)]
        columns.append(jnp.concatenate(whole, axis=0))
    for parts in (scales, shifts):
        whole = [none] + parts
        if rest:
            whole.append(jnp.zeros((rest, LANES), F32))
        columns.append(jnp.concatenate(whole, axis=0))
    right = jnp.concatenate(columns, axis=1).astype(BF16)
    grad = jnp.dot(left[...], right, preferred_element_type=F32)
    for place in range(2):
        context[:, place, :] = grad[:, place * LANES : (place + 1) * LANES] * inverse
        embed[:, place, :] = grad[:, (place + 2) * LANES : (place + 3) * LANES] * inverse


def kernel_stack(*refs):
    whole = refs[-1]
    base = 0
    for ref in refs[:-1]:
        count = ref.shape[0]
        whole[base : base + count] = ref[...]
        base += count


def stack(parts):
    shape = (sum(part.shape[0] for part in parts),) + parts[0].shape[1:]
    return call(
        kernel_stack, "stack", struct(shape, parts[0].dtype), [vmem()] * len(parts), [], limit=12
    )(*parts)


def kernel_slots(meta, own, near, far, across, whole, sems):
    rows = pl.ds(0, whole.shape[1])
    sources = (own.at[rows], near.at[rows], far.at[0, rows], across.at[1, rows])
    wait_all(fetch(sources, whole, meta[0], sems, 0))


def kernel_cut(source, first, second):
    rows = first.shape[0]
    first[...] = source[0:rows]
    second[...] = source[rows : 2 * rows]


def cut(source):
    rows, lanes = source.shape
    return call(
        kernel_cut, "cut", [struct((rows // 2, lanes), BF16)] * 2, [vmem()], [], limit=8
    )(source)


def kernel_small_stack(own, near, far, across, whole):
    rows = pl.ds(own.shape[0] - S_ROWS, S_ROWS)
    whole[0] = own[rows, :]
    whole[1] = near[rows, :]
    whole[2] = far[0, rows, :]
    whole[3] = across[1, rows, :]


def kernel_split(counts, width, digit, meta, *refs):
    parts = refs[sum(counts) :]
    rows = parts[0].shape[1]
    for offset, part in enumerate(parts):
        start = pl.multiple_of(jnp.bitwise_xor(meta[digit], offset) * rows, rows)
        position, base = 0, 0
        for count in counts:
            terms = refs[position : position + count]
            terms = [term.at[0] if len(term.shape) == 4 else term for term in terms]
            total = terms[0][:, pl.ds(start, rows), :].astype(F32)
            for term in terms[1:]:
                total = total + term[:, pl.ds(start, rows), :].astype(F32)
            part[base : base + total.shape[0]] = total.astype(part.dtype)
            position += count
            base += total.shape[0]


def split_sum(groups, width, digit, meta):
    blocks = sum(terms[-1].shape[0] for terms in groups)
    rows = groups[0][-1].shape[1]
    flat = [term for terms in groups for term in terms]
    shape = (blocks, rows // width, LANES)
    return call(
        functools.partial(kernel_split, tuple(len(terms) for terms in groups), width, digit),
        "split_sum",
        [struct(shape, F32)] + [struct(shape, BF16)] * (width - 1),
        [smem()] + [vmem()] * len(flat),
        [],
        limit=12,
    )(meta, *flat)


def kernel_far(mine, got, own, far):
    blocks = own.shape[0]
    own[...] = mine[0:blocks] + got[0:blocks].astype(F32)
    far[...] = (mine[blocks : 2 * blocks] + got[blocks : 2 * blocks].astype(F32)).astype(BF16)


def kernel_total(*refs):
    total = refs[0][...].astype(F32)
    for term in refs[1:-1]:
        total = total + term[...].astype(F32)
    refs[-1][...] = total.astype(BF16)


def total_sum(terms):
    return call(
        kernel_total, "total_sum", struct(terms[0].shape, BF16), [vmem()] * len(terms), [], limit=12
    )(*terms)


def kernel_join(digit, meta, *refs):
    parts, whole = refs[:-1], refs[-1]
    rows = parts[0].shape[1]
    for offset, part in enumerate(parts):
        start = pl.multiple_of(jnp.bitwise_xor(meta[digit], offset) * rows, rows)
        whole[:, pl.ds(start, rows), :] = part[...]


def join(parts, digit, meta):
    blocks, rows, _ = parts[0].shape
    return call(
        functools.partial(kernel_join, digit),
        "join",
        struct((blocks, rows * len(parts), LANES), BF16),
        [smem()] + [vmem()] * len(parts),
        [],
        limit=12,
    )(meta, *parts)


def kernel_last(digit, meta, scale, mine, other, conv, *more):
    rows = mine.shape[1]
    for offset, part in enumerate((mine, other)):
        start = pl.multiple_of(jnp.bitwise_xor(meta[digit], offset) * rows, rows)
        count = conv.shape[0]
        conv[:, pl.ds(start, rows), :] = part[0:count].astype(F32) * scale[0:1, :]
        for proj in more:
            proj[:, pl.ds(start, rows)] = (part[count].astype(F32) * scale[0:1, :]).T


def last_join(pair, digit, meta, scale, more=False):
    blocks, rows, _ = pair[0].shape
    shapes = [struct((3 if more else blocks, 2 * rows, LANES), F32)]
    if more:
        shapes.append(struct((LANES, 2 * rows), F32))
    return call(
        functools.partial(kernel_last, digit),
        "last_join",
        shapes,
        [smem()] + [vmem()] * 3,
        [],
        limit=12,
    )(meta, scale, *pair)


def swap(value, axis, offset):
    size = lax.axis_size(axis)
    return lax.ppermute(value, axis, [(i, i ^ offset) for i in range(size)])


def tie(*values):
    return lax.optimization_barrier(values)


def share(shard):
    near = swap(shard, "mp", 1)
    far = swap(shard, "mp", 2)
    return shard, near, far, swap(far, "mp", 1)


def exchange(pieces):
    return (pieces[0],) + tuple(swap(pieces[k], "mp", k) for k in range(1, 4))


def pick(stack, me):
    return [lax.dynamic_index_in_dim(stack, me ^ k, 0, keepdims=False) for k in range(4)]


def pick_pair(stack, me):
    own = lax.dynamic_index_in_dim(stack, me, 0, keepdims=False)
    near = lax.dynamic_index_in_dim(stack, me ^ 1, 0, keepdims=False)
    far = [lax.dynamic_index_in_dim(stack, me ^ k, 0, keepdims=True) for k in (2, 3)]
    return own, near, jnp.concatenate(far, axis=0)


def dp_levels(size):
    return [(1 << k, 2) for k in range(size.bit_length() - 1)]


def bits(size):
    return [1 << k for k in range(size.bit_length() - 1)]


def local(
    image_in,
    out_cotangent,
    timesteps,
    clip_embed,
    context_tokens,
    image_count,
    norm1_gain,
    norm1_bias,
    conv1_weight,
    embed_weight,
    norm2_gain,
    norm2_bias,
    conv2_weight,
    conv2_bias,
    norm3_gain,
    norm3_bias,
    qkv_weight,
    context_weight,
    proj_weight,
):
    slots, pixels, width = image_in.shape
    me = lax.axis_index("mp")
    group = lax.axis_index("dp")
    parity = (group ^ (group >> 1)) & 1
    levels = dp_levels(lax.axis_size("dp"))
    own_digits = [(group >> (low.bit_length() - 1)) & (wide - 1) for low, wide in levels]
    meta = jnp.stack(
        [me, (me < image_count[0]).astype(jnp.int32), parity] + own_digits
    ).astype(jnp.int32)
    digits = range(3, 3 + len(levels))
    steps = bits(lax.axis_size("dp"))

    conv1_weight, conv2_weight, image_in, out_cotangent, meta = tie(
        conv1_weight, conv2_weight, image_in, out_cotangent, meta
    )

    conv1_shard = conv1_weight.reshape(9 * C, LANES)

    def half_of(shard):
        rows = shard.shape[0] // 2
        return lax.dynamic_slice_in_dim(shard, parity * rows, rows, axis=0)

    half1, image_in = tie(half_of(conv1_shard), image_in)
    half1 = swap(half1, "mp", 2)
    near1 = swap(conv1_shard, "mp", 1)
    images = pick_pair(image_in, me)
    image_near = swap(images[1], "mp", 1)
    image_far = swap(images[2], "mp", 2)

    half_width = EMB // 2
    frequency = jnp.exp(-math.log(10000.0) * jnp.arange(half_width, dtype=F32) / half_width)
    angles = timesteps.astype(F32)[:, None] * frequency[None, :]
    condition = jax.nn.silu(
        jnp.concatenate([jnp.cos(angles), jnp.sin(angles)], axis=1) + clip_embed.astype(F32)
    ).astype(BF16)
    scale_shift = jnp.dot(
        condition, embed_weight.reshape(EMB, 2 * LANES), preferred_element_type=F32
    ).reshape(slots, 1, 2 * LANES)
    doubled = jnp.concatenate([context_tokens, context_tokens], axis=1)
    context = jnp.dot(
        doubled.reshape(slots * 2 * CTX, EMB),
        context_weight.reshape(EMB, 2 * LANES),
        preferred_element_type=F32,
    ).astype(BF16).astype(F32).reshape(slots, 2 * CTX, 2 * LANES)
    vectors = [norm1_gain, norm1_bias, norm2_gain, norm2_bias, conv2_bias, norm3_gain, norm3_bias]
    early = struct((E_ROWS, LANES), F32)
    packs = call(
        kernel_early,
        "early",
        [early, early, struct((2, E_ROWS, LANES), F32)],
        [smem()] + [vmem()] * 9,
        [],
        limit=8,
    )(meta, scale_shift, context, *[vector[None] for vector in vectors])
    count_rows = jnp.broadcast_to(image_count.astype(BF16)[:, None, None], (slots, CTX - 1, EMB))
    factors = jnp.concatenate([condition[:, None], count_rows, context_tokens], axis=1)[None]
    cots = pick(out_cotangent, me)
    rest_shard = jnp.concatenate(
        [
            conv2_weight.reshape(9 * C, LANES),
            jnp.transpose(qkv_weight, (1, 0, 2)).reshape(3 * C, LANES),
            jnp.transpose(proj_weight.reshape(LANES, 4, LANES), (1, 0, 2)).reshape(C, LANES),
        ],
        axis=0,
    )
    rest_half = half_of(rest_shard)

    def relayed(shard, near, half):
        by_x, by_z = cut(half)
        by_x = swap(by_x, "dp", 1)
        by_z = swap(by_z, "dp", 2)
        return (shard, near, half, by_x, by_z) + tuple(
            swap(part, "mp", 1) for part in (half, by_x, by_z)
        )

    near1, image_near, packs, half1 = tie(near1, image_near, packs, half1)
    pack_near = swap(packs[1], "mp", 1)
    pack_far = swap(packs[2], "mp", 2)
    conv1 = relayed(conv1_shard, near1, half1)
    image_far, pack_near, pack_far, rest_shard, rest_half, factors, cots, *conv1 = tie(
        image_far, pack_near, pack_far, rest_shard, rest_half, factors, cots, *conv1
    )
    images = (images[0], image_near, image_far, swap(image_far, "mp", 1))
    packs = (packs[0], pack_near, pack_far, swap(pack_far, "mp", 1))
    rest_half = swap(rest_half, "mp", 2)
    rest_near = swap(rest_shard, "mp", 1)
    factors = [factors, swap(factors, "dp", 1)]

    block = struct((4, pixels, LANES), BF16)
    block32 = struct((4, pixels, LANES), F32)
    turned = struct((4, LANES, pixels), BF16)
    fields = struct((3, 4, pixels + 2 * PAD, LANES), BF16)
    piece = struct((pixels, LANES), BF16)
    pair_piece = struct((2, pixels, LANES), BF16)
    field_scratch = pltpu.VMEM((3, 4, pixels + 2 * PAD, LANES), BF16)
    grad_scratch = pltpu.VMEM((4, pixels, LANES), F32)

    image, pack, first_t, inner, second_t, second, conv1_all, stats1 = call(
        kernel_first,
        "first",
        [
            block,
            struct((4, E_ROWS, LANES), F32),
            turned,
            block32,
            turned,
            fields,
            struct((4, 9 * C, LANES), BF16),
            struct((4, 8, LANES), F32),
        ],
        [smem()] + [anywhere()] * 16,
        [field_scratch, pltpu.SemaphoreType.DMA((16,))],
        limit=12,
    )(meta, *images, *packs, *conv1)

    second, rest_half, rest_near, factors = tie(second, rest_half, rest_near, factors)
    rest = relayed(rest_shard, rest_near, rest_half)
    cots = exchange(cots)
    second, *rest = tie(second, *rest)
    factors = stack(factors)
    factors = [factors, swap(factors, "dp", 2)]
    middle, attn_t, qkv, qkv_w, proj_w, rest_all, stats2 = call(
        kernel_second,
        "second",
        [
            block32,
            turned,
            struct((4, pixels, 3 * LANES), BF16),
            struct((4, 3 * C, LANES), BF16),
            struct((4, C, LANES), BF16),
            struct((4, PROJ_ROW + C, LANES), BF16),
            struct((4, 8, LANES), F32),
        ],
        [smem()] + [vmem()] * 3 + [anywhere()] * 8,
        [pltpu.VMEM((4, pixels, LANES), BF16), pltpu.SemaphoreType.DMA((8,))],
        limit=12,
    )(meta, second, image, pack, *rest)
    ctx_scratch = pltpu.VMEM((pixels, LANES), F32)
    turned_scratch = pltpu.VMEM((LANES, pixels), F32)
    qkv, first_t, second_t, factors, cots = tie(qkv, first_t, second_t, factors, cots)
    factors = stack(factors)
    second_y = swap(second_t, "mp", 2)
    first_y = swap(first_t, "mp", 2)
    second_c = swap(second_t, "mp", 1)
    first_c = swap(first_t, "mp", 1)
    for low in steps[2:-1]:
        factors = stack([factors, swap(factors, "dp", low)])
    factors = (factors, swap(factors, "dp", steps[-1]))
    out_own, out_near, out_far, cot, mixed, dqkv, dctx = call(
        kernel_attention,
        "attention",
        [piece, piece, pair_piece]
        + [block, block, struct((4, pixels, 3 * LANES), BF16), struct((4, 2 * CTX, LANES), F32)],
        [smem()] + [vmem()] * 4 + [anywhere()] * 4,
        [
            pltpu.VMEM((4, pixels, LANES), BF16),
            ctx_scratch,
            ctx_scratch,
            ctx_scratch,
            ctx_scratch,
            grad_scratch,
            grad_scratch,
            turned_scratch,
            turned_scratch,
            pltpu.SemaphoreType.DMA((4,)),
        ],
        limit=24,
    )(meta, qkv, pack, middle, proj_w, *cots)

    def weight_send(sources, gradients):
        return call(
            kernel_weight_send,
            "weight_send",
            [struct((9, C // 2, LANES), BF16), fields],
            [smem()] + [vmem()] * 8,
            [],
            limit=16,
        )(meta, *sources, *gradients)

    def weight_own(sources, field):
        return call(
            kernel_weight_own,
            "weight_own",
            struct((9, C // 2, LANES), F32),
            [smem()] + [vmem()] * 5,
            [],
            limit=16,
        )(meta, *sources, field)

    def down(terms, level):
        own, send = split_sum([terms], 2, digits[level], meta)
        return [own, swap(send, "dp", levels[level][0])]

    def across(value, level):
        return [value, swap(value, "dp", levels[level][0])]

    def inner_levels(terms):
        for level in range(3, len(levels)):
            terms = down(terms, level)
        value = total_sum(terms)
        for level in range(len(levels) - 1, 2, -1):
            value = join(across(value, level), digits[level], meta)
        return value

    att_keep, att_send = call(
        kernel_attention_grad,
        "attention_grad",
        [struct((2, 4, C, LANES), BF16)] * 2,
        [smem()] + [vmem()] * 4,
        [pltpu.VMEM((4, LANES, pixels), BF16)],
    )(meta, dqkv, mixed, attn_t, cot)
    dqkv, att_send, second_y, second_c, factors = tie(dqkv, att_send, second_y, second_c, factors)
    second_d = swap(second_y, "mp", 1)
    att = [att_keep.reshape(8, C, LANES), swap(att_send, "mp", 1).reshape(8, C, LANES)]
    dmiddle, field2, sums, *gradients2 = call(
        kernel_back_attention,
        "back_attention",
        [block32, fields, struct((4, S_ROWS, LANES), F32)] + [piece] * 4,
        [smem()] + [vmem()] * 7,
        [grad_scratch],
    )(meta, dqkv, cot, middle, pack, stats2, dctx, qkv_w)
    gradients2, second_d, first_y, first_c, att, field2 = tie(
        gradients2, second_d, first_y, first_c, att, field2
    )
    first_d = swap(first_y, "mp", 1)
    seconds = (second_t, second_c, second_y, second_d)
    gradients2 = exchange(gradients2)
    att = down(att, 0)
    field2, att[0] = tie(field2, att[0])
    field1, sums, *gradients1 = call(
        kernel_back_second,
        "back_second",
        [fields, struct((4, S_ROWS, LANES), F32)] + [piece] * 4,
        [smem()] + [vmem()] * 6,
        [grad_scratch],
        limit=12,
    )(meta, field2, inner, pack, stats1, sums, rest_all)
    gradients1, gradients2, att, first_d = tie(gradients1, gradients2, att, first_d)
    firsts = (first_t, first_c, first_y, first_d)
    gradients1 = exchange(gradients1)
    att = down(att, 1)
    gradients2, att[0] = tie(gradients2, att[0])
    send2, wide2 = weight_send(seconds, gradients2)
    got2 = swap(send2, "dp", 1)
    wide2, att = tie(wide2, att)
    att = down(att, 2)
    wide2, att[0] = tie(wide2, att[0])
    own2 = weight_own(seconds, wide2)
    own2, att, field1 = tie(own2, att, field1)
    for level in range(3, len(levels)):
        att = down(att, level)
    att_own, att_far = call(
        kernel_far,
        "att_far",
        [struct((4,) + att[0].shape[1:], F32), struct((4,) + att[0].shape[1:], BF16)],
        [vmem()] * 2,
        [],
        limit=12,
    )(*att)
    field1, att_own = tie(field1, att_own)
    att = [att_own, swap(att_far, "mp", 2)]
    grad_first = call(
        kernel_back_conv,
        "back_conv",
        block32,
        [vmem()] * 2,
        [],
    )(field1, conv1_all)
    grad_first, gradients1, att = tie(grad_first, gradients1, att)
    att = total_sum(att)
    for level in range(len(levels) - 1, 2, -1):
        att = join(across(att, level), digits[level], meta)
    gradients1, att, out_far = tie(gradients1, att, out_far)
    att = across(att, 2)
    send1, wide1 = weight_send(firsts, gradients1)
    got1 = swap(send1, "dp", 1)
    out_far = swap(out_far, "mp", 2)
    wide1, got2, own2 = tie(wide1, got2, own2)
    terms2 = down([own2, got2], 1)
    wide1, terms2[0] = tie(wide1, terms2[0])
    own1 = weight_own(firsts, wide1)
    grad_first, own1, terms2, att = tie(grad_first, own1, terms2, att)
    terms2 = down(terms2, 2)
    att = across(join(att, digits[2], meta), 1)
    grad_first, terms2[0], att[0] = tie(grad_first, terms2[0], att[0])
    grad_own, grad_near, grad_far = call(
        kernel_back_first,
        "back_first",
        [
            struct((pixels + S_ROWS, LANES), BF16),
            struct((pixels + S_ROWS, LANES), BF16),
            struct((2, pixels + S_ROWS, LANES), BF16),
        ],
        [smem()] + [vmem()] * 6,
        [grad_scratch, pltpu.VMEM((4, S_ROWS, LANES), F32)],
    )(meta, grad_first, image, pack, stats1, dmiddle, sums)
    grad_far, got1, own1 = tie(grad_far, got1, own1)
    terms1 = down([own1, got1], 1)
    terms1[0], terms2 = tie(terms1[0], terms2)
    ends2 = across(inner_levels(terms2), 2)
    factors, ends2[0], terms1[0] = tie(factors, ends2[0], terms1[0])
    columns = -(-5 * slots * lax.axis_size("dp") // LANES) * LANES
    left = call(
        kernel_factors,
        "factors",
        struct((EMB, columns), BF16),
        [smem()] + [vmem()] * 2,
        [],
        limit=12 if len(steps) < 4 else 56,
    )(meta, *factors)
    grad_far, ends2, terms1, left, out_far = tie(grad_far, ends2, terms1, left, out_far)
    terms1 = down(terms1, 2)
    ends2 = across(join(ends2, digits[2], meta), 1)
    grad_far = swap(grad_far, "mp", 2)
    scale = call(kernel_scale, "scale", struct((8, LANES), F32), [vmem()] * 2, [], limit=8)(*factors)
    ends2, terms1, scale = tie(ends2, terms1, scale)
    ends1 = across(inner_levels(terms1), 2)
    ends2 = across(join(ends2, digits[1], meta), 0)
    ends1, grad_near, grad_far, att = tie(ends1, grad_near, grad_far, att)
    ends1 = across(join(ends1, digits[2], meta), 1)
    att = across(join(att, digits[1], meta), 0)
    grad_near = swap(grad_near, "mp", 1)
    grad_across = swap(grad_far, "mp", 1)
    image_parts = (grad_own, grad_near, grad_far, grad_across)
    smalls = call(
        kernel_small_stack,
        "stack",
        struct((4, S_ROWS, LANES), BF16),
        [vmem()] * 4,
        [],
        limit=8,
    )(grad_own, grad_near, grad_far, grad_across)
    small_got = swap(smalls, "dp", 1)
    ends1 = across(join(ends1, digits[1], meta), 0)
    ends1[0], small_got, ends2, att = tie(ends1[0], small_got, ends2, att)
    smalls = stack([smalls, small_got])
    for low in steps[1:-1]:
        smalls = stack([smalls, swap(smalls, "dp", low)])
    small_got = swap(smalls, "dp", steps[-1])
    (conv2_grad,) = last_join(ends2, digits[0], meta, scale)
    qkv_grad, proj_grad = last_join(att, digits[0], meta, scale, True)
    def in_slots(parts):
        return pl.pallas_call(
            kernel_slots,
            name="slots",
            out_shape=struct((4, pixels, LANES), BF16),
            in_specs=[smem()] + [anywhere()] * 4,
            out_specs=vmem(),
            scratch_shapes=[pltpu.SemaphoreType.DMA((4,))],
            compiler_params=pltpu.CompilerParams(vmem_limit_bytes=8 * MIB),
        )(meta, *parts)

    image_grad = in_slots(image_parts)
    small_got, image_grad, conv2_grad, qkv_grad, out_far, out_near = tie(
        small_got, image_grad, conv2_grad, qkv_grad, out_far, out_near
    )
    out_parts = (out_own, swap(out_near, "mp", 1), out_far, swap(out_far, "mp", 1))
    embed_grad, context_grad, vector_sums = call(
        kernel_factor_grads,
        "factor_grads",
        [
            struct((EMB, 2, LANES), F32),
            struct((EMB, 2, LANES), F32),
            struct((S_ROWS, LANES), F32),
        ],
        [vmem()] * 4,
        [],
        limit=14 if len(steps) < 4 else 56,
    )(scale, left, smalls, small_got)

    out_parts, embed_grad = tie(out_parts, embed_grad)
    block_out = in_slots(out_parts)
    ends1, block_out = tie(ends1, block_out)
    (conv1_grad,) = last_join(ends1, digits[0], meta, scale)
    return (
        block_out,
        image_grad,
        vector_sums[S_G1],
        vector_sums[S_B1],
        conv1_grad.reshape(3, 3, C, LANES),
        embed_grad,
        vector_sums[S_G2],
        vector_sums[S_B2],
        conv2_grad.reshape(3, 3, C, LANES),
        vector_sums[S_CB2],
        vector_sums[S_G3],
        vector_sums[S_B3],
        jnp.transpose(qkv_grad, (1, 0, 2)),
        context_grad,
        proj_grad,
    )


def solution(mesh):
    return jax.shard_map(
        local,
        mesh=mesh,
        in_specs=(
            P("dp", None, "mp"),
            P("dp", None, "mp"),
            P("dp"),
            P("dp", None),
            P("dp", None, None),
            P("dp"),
            P("mp"),
            P("mp"),
            P(None, None, None, "mp"),
            P(None, None, "mp"),
            P("mp"),
            P("mp"),
            P(None, None, None, "mp"),
            P("mp"),
            P("mp"),
            P("mp"),
            P(None, None, "mp"),
            P(None, None, "mp"),
            P("mp", None),
        ),
        out_specs=(
            P("dp", None, "mp"),
            P("dp", None, "mp"),
            P("mp"),
            P("mp"),
            P(None, None, None, "mp"),
            P(None, None, "mp"),
            P("mp"),
            P("mp"),
            P(None, None, None, "mp"),
            P("mp"),
            P("mp"),
            P("mp"),
            P(None, None, "mp"),
            P(None, None, "mp"),
            P("mp", None),
        ),
        check_vma=False,
    )
```

```python
import functools
import math

import jax
import jax.numpy as jnp
from jax import lax
from jax.experimental import pallas as pl
from jax.experimental.pallas import tpu as pltpu
from jax.sharding import PartitionSpec as P

C = 512
GROUPS = 32
HEAD = 64
EMB = 2048
CTX = 4
SIDE = 32
LANES = 128
PAD = SIDE
EPSILON = 1e-05
F32 = jnp.float32
BF16 = jnp.bfloat16
NEG = -1e30
QKV_ROW = 9 * C
PROJ_ROW = QKV_ROW + 3 * C

E_G1, E_B1, E_G2, E_B2, E_CB2, E_G3, E_B3, M_SCALE, M_SHIFT = range(9)
M_KEY, M_VALUE, E_ROWS = 16, 24, 32
S_G3, S_B3, S_CB2, S_G2, S_B2, S_SCALE, S_SHIFT = range(7)
S_KEY, S_VALUE, S_G1, S_B1, S_ROWS = 8, 12, 16, 17, 32
MIB = 1 << 20


def vmem():
    return pl.BlockSpec(memory_space=pltpu.VMEM)


def anywhere():
    return pl.BlockSpec(memory_space=pltpu.HBM)


def smem():
    return pl.BlockSpec(memory_space=pltpu.SMEM)


def struct(shape, dtype):
    return jax.ShapeDtypeStruct(shape, dtype)


def call(body, name, out_shape, in_specs, scratch, flops=0, limit=14):
    many = isinstance(out_shape, (list, tuple))
    return pl.pallas_call(
        body,
        name=name,
        out_shape=out_shape,
        in_specs=in_specs,
        out_specs=[vmem() for _ in out_shape] if many else vmem(),
        scratch_shapes=scratch,
        compiler_params=pltpu.CompilerParams(vmem_limit_bytes=limit * MIB),
        cost_estimate=pl.CostEstimate(flops=0, transcendentals=0, bytes_accessed=0),
    )


def fetch(sources, target, me, sems, first):
    copies = []
    for offset, source in enumerate(sources):
        copy = pltpu.make_async_copy(
            source, target.at[jnp.bitwise_xor(me, offset)], sems.at[first + offset]
        )
        copy.start()
        copies.append(copy)
    return copies


def fetch_routed(sources, target, me, parity, sems, first):
    quarter = target.shape[1] // 4
    copies = []
    for index, source in enumerate(sources):
        place = target.at[jnp.bitwise_xor(me, (0, 1, 2, 2, 2, 3, 3, 3)[index])]
        if index >= 2:
            kind = (index - 2) % 3
            rows = 2 * quarter if kind == 0 else quarter
            half = parity if kind == 0 else 1 - parity
            start = half * 2 * quarter + (quarter if kind == 2 else 0)
            place = place.at[pl.ds(pl.multiple_of(start, quarter), rows), :]
        copy = pltpu.make_async_copy(source, place, sems.at[first + index])
        copy.start()
        copies.append(copy)
    return copies


def wait_all(copies):
    for copy in copies:
        copy.wait()


def fold(values):
    rows = values.shape[0]
    return jnp.sum(values.reshape(rows // 8, 8, values.shape[1]), axis=0)


def group_sum(rows8):
    lane = lax.broadcasted_iota(jnp.int32, rows8.shape, 1)
    total = jnp.broadcast_to(jnp.sum(rows8, axis=0, keepdims=True), rows8.shape)
    for step in (1, 2, 4, 8):
        up = pltpu.roll(total, step, axis=1)
        down = pltpu.roll(total, LANES - step, axis=1)
        total = total + jnp.where((lane & step) != 0, up, down)
    return total[0:1]


def column_sum(rows8):
    return jnp.sum(rows8, axis=0, keepdims=True)


def sum_strips(pixels, strip, width, function):
    zero = tuple(jnp.zeros((8, LANES), F32) for _ in range(width))

    def body(index, carry):
        start = pl.multiple_of(index * strip, strip)
        return tuple(old + fold(new) for old, new in zip(carry, function(start)))

    return lax.fori_loop(0, pixels // strip, body, zero)


def norm_rows(pixels, strip, read):
    count = pixels * (C // GROUPS)
    sums = sum_strips(pixels, strip, 4, lambda start: [read(b, start) for b in range(4)])
    means = [group_sum(s) * (1.0 / count) for s in sums]
    squares = sum_strips(
        pixels,
        strip,
        4,
        lambda start: [jnp.square(read(b, start) - means[b]) for b in range(4)],
    )
    inverses = [lax.rsqrt(group_sum(s) * (1.0 / count) + EPSILON) for s in squares]
    return means, inverses


def shifted(values):
    rows = values.shape[0]
    column = lax.broadcasted_iota(jnp.int32, values.shape, 0) & (SIDE - 1)
    left = jnp.where(column == 0, 0.0, pltpu.roll(values, 1, axis=0))
    right = jnp.where(column == SIDE - 1, 0.0, pltpu.roll(values, rows - 1, axis=0))
    return left, values, right


def store_shifted(target, block, start, values):
    rows = values.shape[0]
    for position, part in enumerate(shifted(values)):
        target[position, block, pl.ds(pl.multiple_of(PAD + start, 32), rows), :] = part.astype(BF16)


def clear_padding(target, pixels):
    zero = jnp.zeros((PAD, LANES), BF16)
    for position in range(3):
        for block in range(4):
            target[position, block, 0:PAD, :] = zero
            target[position, block, PAD + pixels : PAD + pixels + PAD, :] = zero


def conv_tiles(field, weight, pixels, tile, write):
    def body(index, carry):
        start = pl.multiple_of(index * tile, tile)
        left = jnp.concatenate(
            [
                field[b, block, pl.ds(pl.multiple_of(start + a * SIDE, 32), tile), :]
                for a in range(3)
                for b in range(3)
                for block in range(4)
            ],
            axis=1,
        )
        right = jnp.concatenate([weight[s, 0 : 9 * C, :] for s in range(4)], axis=1)
        write(start, jnp.dot(left, right, preferred_element_type=F32))
        return carry

    lax.fori_loop(0, pixels // tile, body, 0)


def conv_back_tiles(field, weight, pixels, tile, write):
    def body(index, carry):
        start = pl.multiple_of((index // 2) * tile, tile)
        half = index % 2
        left = jnp.concatenate(
            [
                field[2 - b, block, pl.ds(pl.multiple_of(start + (2 - a) * SIDE, 32), tile), :]
                for a in range(3)
                for b in range(3)
                for block in range(4)
            ],
            axis=1,
        )
        right = jnp.concatenate(
            [
                weight[block, pl.ds(pl.multiple_of((3 * a + b) * C + half * 256, 256), 256), :]
                for a in range(3)
                for b in range(3)
                for block in range(4)
            ],
            axis=1,
        )
        write(
            start,
            half,
            lax.dot_general(left, right, (((1,), (1,)), ((), ())), preferred_element_type=F32),
        )
        return carry

    lax.fori_loop(0, 2 * (pixels // tile), body, 0)


def silu_slope(before, grad_out):
    gate = jax.nn.sigmoid(before)
    return grad_out * gate * (1.0 + before * (1.0 - gate))


def kernel_early(meta, scale_shift, context, v0, v1, v2, v3, v4, v5, v6, own, near, far):
    for offset, target in enumerate((own, near, far.at[0], far.at[1])):
        slot = jnp.bitwise_xor(meta[0], offset)
        target[...] = jnp.zeros((E_ROWS, LANES), F32)
        for row, vector in enumerate((v0, v1, v2, v3, v4, v5, v6)):
            target[row : row + 1, :] = vector[...]
        scales = scale_shift[slot]
        target[M_SCALE : M_SCALE + 1, :] = scales[:, :LANES]
        target[M_SHIFT : M_SHIFT + 1, :] = scales[:, LANES:]
        tokens = context[slot]
        target[M_KEY : M_KEY + 8, :] = tokens[:, :LANES]
        target[M_VALUE : M_VALUE + 8, :] = tokens[:, LANES:]


def kernel_first(
    meta, i0, i1, i2, i3, e0, e1, e2, e3, w0, w1, w2, w3, w4, w5, w6, w7,
    image, pack, first_t, inner, second_t, second, weight, stats, field, sems,
):
    pixels = image.shape[1]
    me = meta[0]
    image_copies = fetch((i0, i1, i2.at[0], i3.at[1]), image, me, sems, 0)
    pack_copies = fetch((e0, e1, e2.at[0], e3.at[1]), pack, me, sems, 4)
    weight_copies = fetch_routed((w0, w1, w2, w3, w4, w5, w6, w7), weight, me, meta[2], sems, 8)
    clear_padding(field, pixels)
    clear_padding(second, pixels)
    wait_all(image_copies)
    wait_all(pack_copies)
    strip = 128

    def read(block, start):
        return image[block, pl.ds(start, strip), :].astype(F32)

    means, inverses = norm_rows(pixels, strip, read)

    def normalise(index, carry):
        start = pl.multiple_of(index * strip, strip)
        for b in range(4):
            gain = pack[b, E_G1 : E_G1 + 1, :]
            bias = pack[b, E_B1 : E_B1 + 1, :]
            before = (read(b, start) - means[b]) * inverses[b] * gain + bias
            after = before * jax.nn.sigmoid(before)
            store_shifted(field, b, start, after)
            first_t[b, :, pl.ds(start, strip)] = after.T.astype(BF16)
        return carry

    lax.fori_loop(0, pixels // strip, normalise, 0)
    wait_all(weight_copies)

    def write(start, tile):
        for b in range(4):
            inner[b, pl.ds(start, tile.shape[0]), :] = tile[:, b * LANES : (b + 1) * LANES]

    conv_tiles(field, weight, pixels, 512, write)
    means2, inverses2 = norm_rows(pixels, strip, lambda b, start: inner[b, pl.ds(start, strip), :])

    def modulate(index, carry):
        start = pl.multiple_of(index * strip, strip)
        for b in range(4):
            gain = pack[b, E_G2 : E_G2 + 1, :]
            bias = pack[b, E_B2 : E_B2 + 1, :]
            scale = pack[b, M_SCALE : M_SCALE + 1, :]
            shift = pack[b, M_SHIFT : M_SHIFT + 1, :]
            normed = (inner[b, pl.ds(start, strip), :] - means2[b]) * inverses2[b]
            modulated = (normed * gain + bias) * (1.0 + scale) + shift
            after = modulated * jax.nn.sigmoid(modulated)
            store_shifted(second, b, start, after)
            second_t[b, :, pl.ds(start, strip)] = after.T.astype(BF16)
        return carry

    lax.fori_loop(0, pixels // strip, modulate, 0)
    for b in range(4):
        for row, value in enumerate((means[b], inverses[b], means2[b], inverses2[b])):
            stats[b, row : row + 1, :] = value


def kernel_second(
    meta, second, image, pack, w0, w1, w2, w3, w4, w5, w6, w7,
    middle, attn_t, qkv, qkv_weight, proj_weight, weight, stats, attn, sems,
):
    pixels = image.shape[1]
    me = meta[0]
    wait_all(fetch_routed((w0, w1, w2, w3, w4, w5, w6, w7), weight, me, meta[2], sems, 0))
    strip = 128

    def write(start, tile):
        rows = tile.shape[0]
        for b in range(4):
            branch = tile[:, b * LANES : (b + 1) * LANES] + pack[b, E_CB2 : E_CB2 + 1, :]
            middle[b, pl.ds(start, rows), :] = image[b, pl.ds(start, rows), :].astype(F32) + branch

    conv_tiles(second, weight, pixels, 512, write)
    means, inverses = norm_rows(pixels, strip, lambda b, start: middle[b, pl.ds(start, strip), :])

    def normalise(index, carry):
        start = pl.multiple_of(index * strip, strip)
        for b in range(4):
            normed = (middle[b, pl.ds(start, strip), :] - means[b]) * inverses[b]
            value = normed * pack[b, E_G3 : E_G3 + 1, :] + pack[b, E_B3 : E_B3 + 1, :]
            attn[b, pl.ds(start, strip), :] = value.astype(BF16)
            attn_t[b, :, pl.ds(start, strip)] = value.T.astype(BF16)
        return carry

    lax.fori_loop(0, pixels // strip, normalise, 0)
    for s in range(4):
        qkv_weight[s] = weight[s, QKV_ROW:PROJ_ROW, :]
        proj_weight[s] = weight[s, PROJ_ROW : PROJ_ROW + C, :]

    def project(index, carry):
        s = index // 2
        start = pl.multiple_of((index % 2) * 512, 512)
        left = jnp.concatenate([attn[b, pl.ds(start, 512), :] for b in range(4)], axis=1)
        right = jnp.concatenate(
            [weight[s, QKV_ROW + kind * C : QKV_ROW + (kind + 1) * C, :] for kind in range(3)], axis=1
        )
        qkv[s, pl.ds(start, 512), :] = jnp.dot(left, right, preferred_element_type=F32).astype(BF16)
        return carry

    lax.fori_loop(0, 4 * (pixels // 512), project, 0)
    for b in range(4):
        for row, value in enumerate((means[b], inverses[b])):
            stats[b, row : row + 1, :] = value


def kernel_attention(
    meta, qkv, pack, middle, weight, c0, c1, c2, c3,
    o0, o1, o2, cot, mixed, dqkv, dctx,
    grad_mixed, score_ctx, grad_ctx_prob, prob_ctx, dscore_ctx, out_pix, dquery, dkey_t, dvalue_t, sems,
):
    pixels = qkv.shape[1]
    me = meta[0]
    alive = meta[1].astype(F32)
    cot_copies = fetch((c0, c1, c2, c3), cot, me, sems, 0)
    scale = 1.0 / math.sqrt(HEAD)
    block = 1024

    row32 = lax.broadcasted_iota(jnp.int32, (32, LANES), 0)
    lane32 = lax.broadcasted_iota(jnp.int32, (32, LANES), 1)

    def diagonal(kind):
        found = []
        for s in range(4):
            rows8 = pack[s, kind : kind + 8, :]
            tiled = jnp.concatenate([rows8] * 4, axis=0)
            own = (row32 // 4) == (2 * s + lane32 // HEAD)
            kept = jnp.where(own, tiled, 0.0)
            found.append(jnp.concatenate([kept, jnp.zeros((96, LANES), F32)], axis=0).astype(BF16))
        return jnp.concatenate(found, axis=1)

    keys_ctx = diagonal(M_KEY)
    values_ctx = diagonal(M_VALUE)
    wait_all(cot_copies)

    def projection():
        return jnp.concatenate(
            [
                jnp.concatenate([weight[s, o * LANES : (o + 1) * LANES, :] for o in range(4)], axis=1)
                for s in range(4)
            ],
            axis=0,
        )

    def prepare(index, carry):
        start = pl.multiple_of(index * block, block)
        rows = pl.ds(start, block)
        for s in range(4):
            cot[s, rows, :] = (cot[s, rows, :].astype(F32) * alive).astype(BF16)
        all_cot = jnp.concatenate([cot[s, rows, :] for s in range(4)], axis=1)
        all_weight = projection()
        grad = lax.dot_general(
            all_cot, all_weight, (((1,), (1,)), ((), ())), preferred_element_type=F32
        ).astype(BF16)
        for s in range(4):
            grad_mixed[s, rows, :] = grad[:, s * LANES : (s + 1) * LANES]
        query = jnp.concatenate([qkv[s, rows, 0:LANES] for s in range(4)], axis=1)
        score_ctx[rows, :] = lax.dot_general(
            query, keys_ctx, (((1,), (1,)), ((), ())), preferred_element_type=F32
        )
        grad_ctx_prob[rows, :] = lax.dot_general(
            grad, values_ctx, (((1,), (1,)), ((), ())), preferred_element_type=F32
        )
        prob_ctx[rows, :] = jnp.zeros((block, LANES), F32)
        dscore_ctx[rows, :] = jnp.zeros((block, LANES), F32)
        return carry

    lax.fori_loop(0, pixels // block, prepare, 0)
    lane = lax.broadcasted_iota(jnp.int32, (block, LANES), 1)
    low = lane < HEAD
    ones = jnp.ones((pixels, LANES), BF16)
    blocks = pixels // block

    def attend(index, carry):
        s = index // blocks
        part = index % blocks
        rows = pl.ds(pl.multiple_of(part * block, block), block)

        @pl.when(part == 0)
        def _():
            dkey_t[...] = jnp.zeros((LANES, pixels), F32)
            dvalue_t[...] = jnp.zeros((LANES, pixels), F32)

        query = qkv[s, rows, 0:LANES]
        key = qkv[s, :, LANES : 2 * LANES]
        value = qkv[s, :, 2 * LANES : 3 * LANES]
        value_ones = jnp.concatenate([value, ones], axis=1)
        grad = grad_mixed[s, rows, :]
        ctx_scores = score_ctx[rows, :]
        ctx_grads = grad_ctx_prob[rows, :]
        exps, outs, inverses, ctx_exps, owns = [], [], [], [], []
        for h in range(2):
            mine = low if h == 0 else jnp.logical_not(low)
            own = lane // CTX == 2 * s + h
            score = lax.dot_general(
                jnp.where(mine, query, jnp.zeros_like(query)),
                key,
                (((1,), (1,)), ((), ())),
                preferred_element_type=F32,
            )
            top = jnp.maximum(
                jnp.max(score, axis=1, keepdims=True),
                jnp.max(jnp.where(own, ctx_scores, NEG), axis=1, keepdims=True),
            )
            exp = jnp.exp((score - top) * scale).astype(BF16)
            ctx_exp = jnp.where(own, jnp.exp((ctx_scores - top) * scale), 0.0)
            out = jnp.dot(exp, value_ones, preferred_element_type=F32)
            total = out[:, LANES:] + jnp.sum(ctx_exp, axis=1, keepdims=True)
            inverse = 1.0 / total
            exps.append(exp)
            outs.append(out[:, :LANES] * inverse)
            inverses.append(inverse)
            ctx_exps.append(ctx_exp)
            owns.append(own)
        out_pair = jnp.where(low, outs[0], outs[1])
        out_pix[s, rows, :] = out_pair
        inverse_pair = jnp.where(low, inverses[0], inverses[1])
        scaled = (grad.astype(F32) * (inverse_pair * scale)).astype(BF16)
        product = out_pair * scaled.astype(F32)
        query_t = query.astype(F32).T.astype(BF16)
        scaled_t = scaled.astype(F32).T.astype(BF16)
        prob_keep = prob_ctx[rows, :]
        dscore_keep = dscore_ctx[rows, :]
        dqs = []
        for h in range(2):
            mine = low if h == 0 else jnp.logical_not(low)
            own = owns[h]
            ctx_prob = ctx_exps[h] * inverses[h]
            ctx_grad = ctx_grads * (inverses[h] * scale)
            dot = jnp.sum(
                jnp.where(mine, product, 0.0) + ctx_prob * jnp.where(own, ctx_grad, 0.0),
                axis=1,
                keepdims=True,
            )
            weight_grad = lax.dot_general(
                jnp.where(mine, scaled, jnp.zeros_like(scaled)),
                value,
                (((1,), (1,)), ((), ())),
                preferred_element_type=F32,
            )
            dscore = (exps[h].astype(F32) * (weight_grad - dot)).astype(BF16)
            prob_keep = jnp.where(own, ctx_prob, prob_keep)
            dscore_keep = jnp.where(own, ctx_exps[h] * (ctx_grad - dot), dscore_keep)
            dqs.append(jnp.dot(dscore, key, preferred_element_type=F32))
            half = slice(h * HEAD, (h + 1) * HEAD)
            dkey_t[half, :] += jnp.dot(query_t[half], dscore, preferred_element_type=F32)
            dvalue_t[half, :] += jnp.dot(scaled_t[half], exps[h], preferred_element_type=F32)
        prob_ctx[rows, :] = prob_keep
        dscore_ctx[rows, :] = dscore_keep
        dquery[s, rows, :] = jnp.where(low, dqs[0], dqs[1])

        @pl.when(part == blocks - 1)
        def _():
            for piece in range(pixels // LANES):
                cut = slice(piece * LANES, (piece + 1) * LANES)
                dqkv[s, cut, LANES : 2 * LANES] = dkey_t[:, cut].T.astype(BF16)
                dqkv[s, cut, 2 * LANES : 3 * LANES] = (dvalue_t[:, cut] * (1.0 / scale)).T.astype(BF16)

        return carry

    lax.fori_loop(0, 4 * blocks, attend, 0)

    def finish(index, carry):
        dkeys, dvalues = carry
        start = pl.multiple_of(index * block, block)
        rows = pl.ds(start, block)
        prob = prob_ctx[rows, :].astype(BF16)
        dscore = dscore_ctx[rows, :].astype(BF16)
        out_ctx = jnp.dot(prob, values_ctx, preferred_element_type=F32)
        dquery_ctx = jnp.dot(dscore, keys_ctx, preferred_element_type=F32)
        parts = []
        for s in range(4):
            cut = slice(s * LANES, (s + 1) * LANES)
            both = (out_pix[s, rows, :] + out_ctx[:, cut]).astype(BF16)
            mixed[s, rows, :] = both
            parts.append(both)
            dqkv[s, rows, 0:LANES] = (dquery[s, rows, :] + dquery_ctx[:, cut]).astype(BF16)
        result = jnp.dot(
            jnp.concatenate(parts, axis=1), projection(), preferred_element_type=F32
        )
        for offset, target in enumerate((o0, o1, o2.at[0], o2.at[1])):
            other = jnp.bitwise_xor(me, offset)
            value = jnp.zeros((block, LANES), F32)
            for s in range(4):
                value = jnp.where(other == s, result[:, s * LANES : (s + 1) * LANES], value)
            target[rows, :] = ((middle[other, rows, :] + value) * alive).astype(BF16)
        query = jnp.concatenate([qkv[s, rows, 0:LANES] for s in range(4)], axis=1)
        grad = jnp.concatenate([grad_mixed[s, rows, :] for s in range(4)], axis=1)
        dkeys = dkeys + jnp.dot(dscore_ctx[rows, :].T[0:32].astype(BF16), query, preferred_element_type=F32)
        dvalues = dvalues + jnp.dot(prob_ctx[rows, :].T[0:32].astype(BF16), grad, preferred_element_type=F32)
        return dkeys, dvalues

    zero = jnp.zeros((32, C), F32)
    dkeys, dvalues = lax.fori_loop(0, pixels // block, finish, (zero, zero))
    for s in range(4):
        own = (row32 // 4) == (2 * s + lane32 // HEAD)
        for position, source in enumerate((dkeys, dvalues)):
            kept = jnp.where(own, source[:, s * LANES : (s + 1) * LANES], 0.0)
            eight = jnp.sum(kept.reshape(4, 8, LANES), axis=0)
            folded = eight + pltpu.roll(eight, 4, axis=0)
            dctx[s, position * CTX : (position + 1) * CTX, :] = folded[0:CTX]


def saved(stats, row):
    return [stats[b, row : row + 1, :] for b in range(4)]


def norm_back_strips(pixels, strip, read_normed, read_grad, gains, inverses, gain_sums, bias_sums, write):
    count = pixels * (C // GROUPS)
    firsts, seconds = (
        [
            group_sum(jnp.broadcast_to(sums[b] * gains[b], (8, LANES)) * (1.0 / 8)) * (1.0 / count)
            for b in range(4)
        ]
        for sums in (bias_sums, gain_sums)
    )

    def body(index, carry):
        start = pl.multiple_of(index * strip, strip)
        found = []
        for b in range(4):
            normed = read_normed(b, start)
            grad = read_grad(b, start) * gains[b]
            found.append(write(b, start, inverses[b] * (grad - firsts[b] - normed * seconds[b])))
        if found[0] is None:
            return carry
        return tuple(old + fold(new) for old, new in zip(carry, found))

    zero = tuple(jnp.zeros((8, LANES), F32) for _ in range(4))
    return lax.fori_loop(0, pixels // strip, body, zero)


def kernel_back_attention(
    meta, dqkv, cot, middle, pack, stats, dctx, qkv_weight,
    dmiddle, field, sums, d0, d1, d2, d3, dattn,
):
    pixels = cot.shape[1]
    me = meta[0]
    strip = 128
    clear_padding(field, pixels)
    means, inverses = saved(stats, 0), saved(stats, 1)

    def back(index, carry):
        start = pl.multiple_of(index * 512, 512)
        left = jnp.concatenate([dqkv[s, pl.ds(start, 512), :] for s in range(4)], axis=1)
        right = jnp.concatenate(
            [qkv_weight[s, kind * C : (kind + 1) * C, :] for s in range(4) for kind in range(3)], axis=1
        )
        tile = lax.dot_general(left, right, (((1,), (1,)), ((), ())), preferred_element_type=F32)
        for b in range(4):
            dattn[b, pl.ds(start, 512), :] = tile[:, b * LANES : (b + 1) * LANES]
        return carry

    lax.fori_loop(0, pixels // 512, back, 0)
    gains = [pack[b, E_G3 : E_G3 + 1, :] for b in range(4)]

    def read_normed(b, start):
        return (middle[b, pl.ds(start, strip), :] - means[b]) * inverses[b]

    def write(b, start, value):
        total = cot[b, pl.ds(start, strip), :].astype(F32) + value
        dmiddle[b, pl.ds(start, strip), :] = total
        rounded = total.astype(BF16).astype(F32)
        store_shifted(field, b, start, rounded)
        return rounded

    def terms(start):
        found = []
        for b in range(4):
            grad = dattn[b, pl.ds(start, strip), :]
            found += [grad, grad * read_normed(b, start)]
        return found

    totals = [column_sum(rows8) for rows8 in sum_strips(pixels, strip, 8, terms)]
    bias_sums, gain_sums = totals[0::2], totals[1::2]
    branch = norm_back_strips(
        pixels,
        strip,
        read_normed,
        lambda b, start: dattn[b, pl.ds(start, strip), :],
        gains,
        inverses,
        gain_sums,
        bias_sums,
        write,
    )
    for b in range(4):
        sums[b] = jnp.zeros((S_ROWS, LANES), F32)
        sums[b, S_G3 : S_G3 + 1, :] = gain_sums[b]
        sums[b, S_B3 : S_B3 + 1, :] = bias_sums[b]
        sums[b, S_CB2 : S_CB2 + 1, :] = column_sum(branch[b])
        sums[b, S_KEY : S_KEY + 8, :] = dctx[b]
    for offset, target in enumerate((d0, d1, d2, d3)):
        target[...] = field[1, jnp.bitwise_xor(me, offset), PAD : PAD + pixels, :]


def kernel_attention_grad(meta, dqkv, mixed, attn_t, cot, keep, send, cot_t):
    pixels = cot.shape[1]
    me = meta[0]
    strip = 128

    def turn(index, carry):
        start = pl.multiple_of(index * strip, strip)
        for b in range(4):
            cot_t[b, :, pl.ds(start, strip)] = cot[b, pl.ds(start, strip), :].astype(F32).T.astype(BF16)
        return carry

    lax.fori_loop(0, pixels // strip, turn, 0)

    attn_all = attn_t[...].reshape(C, pixels)
    cot_all = cot_t[...].reshape(C, pixels)
    for offset, target in enumerate((keep, send)):
        s = jnp.bitwise_xor(me, offset)
        pair = (s, jnp.bitwise_xor(s, 2))
        right = jnp.concatenate([dqkv[p] for p in pair], axis=1)
        grad = jnp.dot(attn_all, right, preferred_element_type=F32).astype(BF16)
        right = jnp.concatenate([mixed[p] for p in pair], axis=1)
        other = jnp.dot(cot_all, right, preferred_element_type=F32).astype(BF16)
        for place in range(2):
            for kind in range(3):
                column = (3 * place + kind) * LANES
                target[place, kind] = grad[:, column : column + LANES]
            target[place, 3] = other[:, place * LANES : (place + 1) * LANES]


def weight_taps(half, sources, field, target):
    pixels = sources[0].shape[2]

    def body(index, carry):
        left = jnp.concatenate(
            [source[pl.ds(2 * half, 2)].reshape(2 * LANES, pixels) for source in sources], axis=1
        )
        columns = []
        for tap in (2 * index, jnp.minimum(2 * index + 1, 8)):
            start = pl.multiple_of((2 - tap // 3) * SIDE, 32)
            side = 2 - lax.rem(tap, 3)
            columns.append(
                jnp.concatenate([field[side, k, pl.ds(start, pixels), :] for k in range(4)], axis=0)
            )
        grad = jnp.dot(left, jnp.concatenate(columns, axis=1), preferred_element_type=F32)
        target[2 * index] = grad[:, :LANES].astype(target.dtype)

        @pl.when(index < 4)
        def _():
            target[2 * index + 1] = grad[:, LANES:].astype(target.dtype)

        return carry

    lax.fori_loop(0, 5, body, 0)


def kernel_weight_send(meta, u0, u1, u2, u3, d0, d1, d2, d3, send, field):
    pixels = u0.shape[2]
    clear_padding(field, pixels)
    strip = 128

    def spread(index, carry):
        start = pl.multiple_of(index * strip, strip)
        for k, source in enumerate((d0, d1, d2, d3)):
            store_shifted(field, k, start, source[pl.ds(start, strip), :].astype(F32))
        return carry

    lax.fori_loop(0, pixels // strip, spread, 0)
    weight_taps(1 - meta[3], (u0, u1, u2, u3), field, send)


def kernel_weight_own(meta, u0, u1, u2, u3, field, own):
    weight_taps(meta[3], (u0, u1, u2, u3), field, own)


def kernel_back_second(
    meta, grad_field, inner, pack, stats, sums_in, weight,
    field, sums, d0, d1, d2, d3, grad,
):
    pixels = inner.shape[1]
    me = meta[0]
    strip = 128
    clear_padding(field, pixels)
    means, inverses = saved(stats, 2), saved(stats, 3)

    def write_grad(start, half, tile):
        for b in range(2):
            grad[2 * half + b, pl.ds(start, tile.shape[0]), :] = tile[:, b * LANES : (b + 1) * LANES]

    conv_back_tiles(grad_field, weight, pixels, 512, write_grad)
    gains = [pack[b, E_G2 : E_G2 + 1, :] for b in range(4)]

    def read_normed(b, start):
        return (inner[b, pl.ds(start, strip), :] - means[b]) * inverses[b]

    def slope(index, carry):
        start = pl.multiple_of(index * strip, strip)
        found = []
        for b in range(4):
            bias = pack[b, E_B2 : E_B2 + 1, :]
            scale = pack[b, M_SCALE : M_SCALE + 1, :]
            shift = pack[b, M_SHIFT : M_SHIFT + 1, :]
            normed = read_normed(b, start)
            modulated = (normed * gains[b] + bias) * (1.0 + scale) + shift
            dmod = silu_slope(modulated, grad[b, pl.ds(start, strip), :])
            grad[b, pl.ds(start, strip), :] = dmod * (1.0 + scale)
            found += [dmod, dmod * normed]
        return tuple(old + fold(new) for old, new in zip(carry, found))

    zero = tuple(jnp.zeros((8, LANES), F32) for _ in range(8))
    totals = [column_sum(rows8) for rows8 in lax.fori_loop(0, pixels // strip, slope, zero)]
    plain, scaled = totals[0::2], totals[1::2]
    factors = [1.0 + pack[b, M_SCALE : M_SCALE + 1, :] for b in range(4)]
    bias_sums = [plain[b] * factors[b] for b in range(4)]
    gain_sums = [scaled[b] * factors[b] for b in range(4)]

    def write(b, start, value):
        store_shifted(field, b, start, value)

    norm_back_strips(
        pixels,
        strip,
        read_normed,
        lambda b, start: grad[b, pl.ds(start, strip), :],
        gains,
        inverses,
        gain_sums,
        bias_sums,
        write,
    )
    for b in range(4):
        sums[b] = sums_in[b]
        sums[b, S_G2 : S_G2 + 1, :] = gain_sums[b]
        sums[b, S_B2 : S_B2 + 1, :] = bias_sums[b]
        sums[b, S_SCALE : S_SCALE + 1, :] = (
            scaled[b] * gains[b] + plain[b] * pack[b, E_B2 : E_B2 + 1, :]
        )
        sums[b, S_SHIFT : S_SHIFT + 1, :] = plain[b]
    for offset, target in enumerate((d0, d1, d2, d3)):
        target[...] = field[1, jnp.bitwise_xor(me, offset), PAD : PAD + pixels, :]


def kernel_back_conv(grad_field, weight, grad):
    pixels = grad.shape[1]

    def write_grad(start, half, tile):
        for b in range(2):
            grad[2 * half + b, pl.ds(start, tile.shape[0]), :] = tile[:, b * LANES : (b + 1) * LANES]

    conv_back_tiles(grad_field, weight, pixels, 512, write_grad)


def kernel_back_first(
    meta, grad_in, image, pack, stats, dmiddle, sums_in, g0, g1, g2, grad, sums,
):
    pixels = image.shape[1]
    me = meta[0]
    strip = 128

    def read(b, start):
        return image[b, pl.ds(start, strip), :].astype(F32)

    means, inverses = saved(stats, 0), saved(stats, 1)
    gains = [pack[b, E_G1 : E_G1 + 1, :] for b in range(4)]

    def read_normed(b, start):
        return (read(b, start) - means[b]) * inverses[b]

    def slope(index, carry):
        start = pl.multiple_of(index * strip, strip)
        found = []
        for b in range(4):
            normed = read_normed(b, start)
            before = normed * gains[b] + pack[b, E_B1 : E_B1 + 1, :]
            value = silu_slope(before, grad_in[b, pl.ds(start, strip), :])
            grad[b, pl.ds(start, strip), :] = value
            found += [value, value * normed]
        return tuple(old + fold(new) for old, new in zip(carry, found))

    zero = tuple(jnp.zeros((8, LANES), F32) for _ in range(8))
    totals = [column_sum(rows8) for rows8 in lax.fori_loop(0, pixels // strip, slope, zero)]
    bias_sums, gain_sums = totals[0::2], totals[1::2]

    def write(b, start, value):
        grad[b, pl.ds(start, strip), :] = dmiddle[b, pl.ds(start, strip), :] + value

    norm_back_strips(
        pixels,
        strip,
        read_normed,
        lambda b, start: grad[b, pl.ds(start, strip), :],
        gains,
        inverses,
        gain_sums,
        bias_sums,
        write,
    )
    for b in range(4):
        sums[b] = sums_in[b]
        sums[b, S_G1 : S_G1 + 1, :] = gain_sums[b]
        sums[b, S_B1 : S_B1 + 1, :] = bias_sums[b]
    for offset, target in enumerate((g0, g1, g2.at[0], g2.at[1])):
        other = jnp.bitwise_xor(me, offset)
        target[0:pixels, :] = grad[other].astype(BF16)
        target[pixels : pixels + S_ROWS, :] = sums[other].astype(BF16)


def kernel_scale(factors0, factors1, scale):
    total = jnp.zeros((1, LANES), F32)
    for factors in (factors0, factors1):
        for g in range(factors.shape[0]):
            total = total + factors[g, 0].astype(F32)[1:2, 0:LANES]
    scale[...] = jnp.broadcast_to(1.0 / total, (8, LANES))


def kernel_factors(meta, factors0, factors1, left):
    conditions, tokens = [], []
    for factors in (factors0, factors1):
        for g in range(factors.shape[0]):
            for k in range(4):
                rows = factors[g, jnp.bitwise_xor(meta[0], k)].astype(F32)
                conditions.append(rows[0:1])
                tokens.append(rows[CTX : 2 * CTX])
    rest = left.shape[1] - 5 * len(conditions)
    rows = tokens + conditions
    if rest:
        rows.append(jnp.zeros((rest, EMB), F32))
    left[...] = jnp.concatenate(rows, axis=0).T.astype(BF16)


def kernel_factor_grads(scale, left, small0, small1, embed, context, vectors):
    inverse = scale[0:1, :]
    total = jnp.zeros((S_ROWS, LANES), F32)
    scales, shifts, keys, values = [], [], [], []
    for small in (small0, small1):
        for k in range(small.shape[0]):
            term = small[k].astype(F32)
            total = total + term
            scales.append(term[S_SCALE : S_SCALE + 1])
            shifts.append(term[S_SHIFT : S_SHIFT + 1])
            keys.append(term[S_KEY : S_KEY + CTX])
            values.append(term[S_VALUE : S_VALUE + CTX])
    vectors[...] = total * inverse
    images = len(scales)
    rest = left.shape[1] - 5 * images
    none = jnp.zeros((4 * images, LANES), F32)
    columns = []
    for parts in (keys, values):
        whole = [jnp.concatenate(parts, axis=0), jnp.zeros((images + rest, LANES), F32)]
        columns.append(jnp.concatenate(whole, axis=0))
    for parts in (scales, shifts):
        whole = [none] + parts
        if rest:
            whole.append(jnp.zeros((rest, LANES), F32))
        columns.append(jnp.concatenate(whole, axis=0))
    right = jnp.concatenate(columns, axis=1).astype(BF16)
    grad = jnp.dot(left[...], right, preferred_element_type=F32)
    for place in range(2):
        context[:, place, :] = grad[:, place * LANES : (place + 1) * LANES] * inverse
        embed[:, place, :] = grad[:, (place + 2) * LANES : (place + 3) * LANES] * inverse


def kernel_stack(*refs):
    whole = refs[-1]
    base = 0
    for ref in refs[:-1]:
        count = ref.shape[0]
        whole[base : base + count] = ref[...]
        base += count


def stack(parts):
    shape = (sum(part.shape[0] for part in parts),) + parts[0].shape[1:]
    return call(
        kernel_stack, "stack", struct(shape, parts[0].dtype), [vmem()] * len(parts), [], limit=12
    )(*parts)


def kernel_slots(meta, own, near, far, across, whole, sems):
    rows = pl.ds(0, whole.shape[1])
    sources = (own.at[rows], near.at[rows], far.at[0, rows], across.at[1, rows])
    wait_all(fetch(sources, whole, meta[0], sems, 0))


def kernel_cut(source, first, second):
    rows = first.shape[0]
    first[...] = source[0:rows]
    second[...] = source[rows : 2 * rows]


def cut(source):
    rows, lanes = source.shape
    return call(
        kernel_cut, "cut", [struct((rows // 2, lanes), BF16)] * 2, [vmem()], [], limit=8
    )(source)


def kernel_small_stack(own, near, far, across, whole):
    rows = pl.ds(own.shape[0] - S_ROWS, S_ROWS)
    whole[0] = own[rows, :]
    whole[1] = near[rows, :]
    whole[2] = far[0, rows, :]
    whole[3] = across[1, rows, :]


def kernel_split(counts, width, digit, meta, *refs):
    parts = refs[sum(counts) :]
    rows = parts[0].shape[1]
    for offset, part in enumerate(parts):
        start = pl.multiple_of(jnp.bitwise_xor(meta[digit], offset) * rows, rows)
        position, base = 0, 0
        for count in counts:
            terms = refs[position : position + count]
            terms = [term.at[0] if len(term.shape) == 4 else term for term in terms]
            total = terms[0][:, pl.ds(start, rows), :].astype(F32)
            for term in terms[1:]:
                total = total + term[:, pl.ds(start, rows), :].astype(F32)
            part[base : base + total.shape[0]] = total.astype(part.dtype)
            position += count
            base += total.shape[0]


def split_sum(groups, width, digit, meta):
    blocks = sum(terms[-1].shape[0] for terms in groups)
    rows = groups[0][-1].shape[1]
    flat = [term for terms in groups for term in terms]
    shape = (blocks, rows // width, LANES)
    return call(
        functools.partial(kernel_split, tuple(len(terms) for terms in groups), width, digit),
        "split_sum",
        [struct(shape, F32)] + [struct(shape, BF16)] * (width - 1),
        [smem()] + [vmem()] * len(flat),
        [],
        limit=12,
    )(meta, *flat)


def kernel_far(mine, got, own, far):
    blocks = own.shape[0]
    own[...] = mine[0:blocks] + got[0:blocks].astype(F32)
    far[...] = (mine[blocks : 2 * blocks] + got[blocks : 2 * blocks].astype(F32)).astype(BF16)


def kernel_total(*refs):
    total = refs[0][...].astype(F32)
    for term in refs[1:-1]:
        total = total + term[...].astype(F32)
    refs[-1][...] = total.astype(BF16)


def total_sum(terms):
    return call(
        kernel_total, "total_sum", struct(terms[0].shape, BF16), [vmem()] * len(terms), [], limit=12
    )(*terms)


def kernel_join(digit, meta, *refs):
    parts, whole = refs[:-1], refs[-1]
    rows = parts[0].shape[1]
    for offset, part in enumerate(parts):
        start = pl.multiple_of(jnp.bitwise_xor(meta[digit], offset) * rows, rows)
        whole[:, pl.ds(start, rows), :] = part[...]


def join(parts, digit, meta):
    blocks, rows, _ = parts[0].shape
    return call(
        functools.partial(kernel_join, digit),
        "join",
        struct((blocks, rows * len(parts), LANES), BF16),
        [smem()] + [vmem()] * len(parts),
        [],
        limit=12,
    )(meta, *parts)


def kernel_last(digit, meta, scale, mine, other, conv, *more):
    rows = mine.shape[1]
    for offset, part in enumerate((mine, other)):
        start = pl.multiple_of(jnp.bitwise_xor(meta[digit], offset) * rows, rows)
        count = conv.shape[0]
        conv[:, pl.ds(start, rows), :] = part[0:count].astype(F32) * scale[0:1, :]
        for proj in more:
            proj[:, pl.ds(start, rows)] = (part[count].astype(F32) * scale[0:1, :]).T


def last_join(pair, digit, meta, scale, more=False):
    blocks, rows, _ = pair[0].shape
    shapes = [struct((3 if more else blocks, 2 * rows, LANES), F32)]
    if more:
        shapes.append(struct((LANES, 2 * rows), F32))
    return call(
        functools.partial(kernel_last, digit),
        "last_join",
        shapes,
        [smem()] + [vmem()] * 3,
        [],
        limit=12,
    )(meta, scale, *pair)


def swap(value, axis, offset):
    size = lax.axis_size(axis)
    return lax.ppermute(value, axis, [(i, i ^ offset) for i in range(size)])


def tie(*values):
    return lax.optimization_barrier(values)


def share(shard):
    near = swap(shard, "mp", 1)
    far = swap(shard, "mp", 2)
    return shard, near, far, swap(far, "mp", 1)


def exchange(pieces):
    return (pieces[0],) + tuple(swap(pieces[k], "mp", k) for k in range(1, 4))


def pick(stack, me):
    return [lax.dynamic_index_in_dim(stack, me ^ k, 0, keepdims=False) for k in range(4)]


def pick_pair(stack, me):
    own = lax.dynamic_index_in_dim(stack, me, 0, keepdims=False)
    near = lax.dynamic_index_in_dim(stack, me ^ 1, 0, keepdims=False)
    far = [lax.dynamic_index_in_dim(stack, me ^ k, 0, keepdims=True) for k in (2, 3)]
    return own, near, jnp.concatenate(far, axis=0)


def dp_levels(size):
    return [(1 << k, 2) for k in range(size.bit_length() - 1)]


def bits(size):
    return [1 << k for k in range(size.bit_length() - 1)]


def local(
    image_in,
    out_cotangent,
    timesteps,
    clip_embed,
    context_tokens,
    image_count,
    norm1_gain,
    norm1_bias,
    conv1_weight,
    embed_weight,
    norm2_gain,
    norm2_bias,
    conv2_weight,
    conv2_bias,
    norm3_gain,
    norm3_bias,
    qkv_weight,
    context_weight,
    proj_weight,
):
    slots, pixels, width = image_in.shape
    me = lax.axis_index("mp")
    group = lax.axis_index("dp")
    parity = (group ^ (group >> 1)) & 1
    levels = dp_levels(lax.axis_size("dp"))
    own_digits = [(group >> (low.bit_length() - 1)) & (wide - 1) for low, wide in levels]
    meta = jnp.stack(
        [me, (me < image_count[0]).astype(jnp.int32), parity] + own_digits
    ).astype(jnp.int32)
    digits = range(3, 3 + len(levels))
    steps = bits(lax.axis_size("dp"))

    conv1_weight, conv2_weight, image_in, out_cotangent, meta = tie(
        conv1_weight, conv2_weight, image_in, out_cotangent, meta
    )

    conv1_shard = conv1_weight.reshape(9 * C, LANES)

    def half_of(shard):
        rows = shard.shape[0] // 2
        return lax.dynamic_slice_in_dim(shard, parity * rows, rows, axis=0)

    half1, image_in = tie(half_of(conv1_shard), image_in)
    half1 = swap(half1, "mp", 2)
    near1 = swap(conv1_shard, "mp", 1)
    images = pick_pair(image_in, me)
    image_near = swap(images[1], "mp", 1)
    image_far = swap(images[2], "mp", 2)

    half_width = EMB // 2
    frequency = jnp.exp(-math.log(10000.0) * jnp.arange(half_width, dtype=F32) / half_width)
    angles = timesteps.astype(F32)[:, None] * frequency[None, :]
    condition = jax.nn.silu(
        jnp.concatenate([jnp.cos(angles), jnp.sin(angles)], axis=1) + clip_embed.astype(F32)
    ).astype(BF16)
    scale_shift = jnp.dot(
        condition, embed_weight.reshape(EMB, 2 * LANES), preferred_element_type=F32
    ).reshape(slots, 1, 2 * LANES)
    doubled = jnp.concatenate([context_tokens, context_tokens], axis=1)
    context = jnp.dot(
        doubled.reshape(slots * 2 * CTX, EMB),
        context_weight.reshape(EMB, 2 * LANES),
        preferred_element_type=F32,
    ).astype(BF16).astype(F32).reshape(slots, 2 * CTX, 2 * LANES)
    vectors = [norm1_gain, norm1_bias, norm2_gain, norm2_bias, conv2_bias, norm3_gain, norm3_bias]
    early = struct((E_ROWS, LANES), F32)
    packs = call(
        kernel_early,
        "early",
        [early, early, struct((2, E_ROWS, LANES), F32)],
        [smem()] + [vmem()] * 9,
        [],
        limit=8,
    )(meta, scale_shift, context, *[vector[None] for vector in vectors])
    count_rows = jnp.broadcast_to(image_count.astype(BF16)[:, None, None], (slots, CTX - 1, EMB))
    factors = jnp.concatenate([condition[:, None], count_rows, context_tokens], axis=1)[None]
    cots = pick(out_cotangent, me)
    rest_shard = jnp.concatenate(
        [
            conv2_weight.reshape(9 * C, LANES),
            jnp.transpose(qkv_weight, (1, 0, 2)).reshape(3 * C, LANES),
            jnp.transpose(proj_weight.reshape(LANES, 4, LANES), (1, 0, 2)).reshape(C, LANES),
        ],
        axis=0,
    )
    rest_half = half_of(rest_shard)

    def relayed(shard, near, half):
        by_x, by_z = cut(half)
        by_x = swap(by_x, "dp", 1)
        by_z = swap(by_z, "dp", 2)
        return (shard, near, half, by_x, by_z) + tuple(
            swap(part, "mp", 1) for part in (half, by_x, by_z)
        )

    near1, image_near, packs, half1 = tie(near1, image_near, packs, half1)
    pack_near = swap(packs[1], "mp", 1)
    pack_far = swap(packs[2], "mp", 2)
    conv1 = relayed(conv1_shard, near1, half1)
    image_far, pack_near, pack_far, rest_shard, rest_half, factors, cots, *conv1 = tie(
        image_far, pack_near, pack_far, rest_shard, rest_half, factors, cots, *conv1
    )
    images = (images[0], image_near, image_far, swap(image_far, "mp", 1))
    packs = (packs[0], pack_near, pack_far, swap(pack_far, "mp", 1))
    rest_half = swap(rest_half, "mp", 2)
    rest_near = swap(rest_shard, "mp", 1)
    factors = [factors, swap(factors, "dp", 1)]

    block = struct((4, pixels, LANES), BF16)
    block32 = struct((4, pixels, LANES), F32)
    turned = struct((4, LANES, pixels), BF16)
    fields = struct((3, 4, pixels + 2 * PAD, LANES), BF16)
    piece = struct((pixels, LANES), BF16)
    pair_piece = struct((2, pixels, LANES), BF16)
    field_scratch = pltpu.VMEM((3, 4, pixels + 2 * PAD, LANES), BF16)
    grad_scratch = pltpu.VMEM((4, pixels, LANES), F32)

    image, pack, first_t, inner, second_t, second, conv1_all, stats1 = call(
        kernel_first,
        "first",
        [
            block,
            struct((4, E_ROWS, LANES), F32),
            turned,
            block32,
            turned,
            fields,
            struct((4, 9 * C, LANES), BF16),
            struct((4, 8, LANES), F32),
        ],
        [smem()] + [anywhere()] * 16,
        [field_scratch, pltpu.SemaphoreType.DMA((16,))],
        limit=12,
    )(meta, *images, *packs, *conv1)

    second, rest_half, rest_near, factors = tie(second, rest_half, rest_near, factors)
    rest = relayed(rest_shard, rest_near, rest_half)
    cots = exchange(cots)
    second, *rest = tie(second, *rest)
    factors = stack(factors)
    factors = [factors, swap(factors, "dp", 2)]
    middle, attn_t, qkv, qkv_w, proj_w, rest_all, stats2 = call(
        kernel_second,
        "second",
        [
            block32,
            turned,
            struct((4, pixels, 3 * LANES), BF16),
            struct((4, 3 * C, LANES), BF16),
            struct((4, C, LANES), BF16),
            struct((4, PROJ_ROW + C, LANES), BF16),
            struct((4, 8, LANES), F32),
        ],
        [smem()] + [vmem()] * 3 + [anywhere()] * 8,
        [pltpu.VMEM((4, pixels, LANES), BF16), pltpu.SemaphoreType.DMA((8,))],
        limit=12,
    )(meta, second, image, pack, *rest)
    ctx_scratch = pltpu.VMEM((pixels, LANES), F32)
    turned_scratch = pltpu.VMEM((LANES, pixels), F32)
    qkv, first_t, second_t, factors, cots = tie(qkv, first_t, second_t, factors, cots)
    factors = stack(factors)
    second_y = swap(second_t, "mp", 2)
    first_y = swap(first_t, "mp", 2)
    second_c = swap(second_t, "mp", 1)
    first_c = swap(first_t, "mp", 1)
    for low in steps[2:-1]:
        factors = stack([factors, swap(factors, "dp", low)])
    factors = (factors, swap(factors, "dp", steps[-1]))
    out_own, out_near, out_far, cot, mixed, dqkv, dctx = call(
        kernel_attention,
        "attention",
        [piece, piece, pair_piece]
        + [block, block, struct((4, pixels, 3 * LANES), BF16), struct((4, 2 * CTX, LANES), F32)],
        [smem()] + [vmem()] * 4 + [anywhere()] * 4,
        [
            pltpu.VMEM((4, pixels, LANES), BF16),
            ctx_scratch,
            ctx_scratch,
            ctx_scratch,
            ctx_scratch,
            grad_scratch,
            grad_scratch,
            turned_scratch,
            turned_scratch,
            pltpu.SemaphoreType.DMA((4,)),
        ],
        limit=24,
    )(meta, qkv, pack, middle, proj_w, *cots)

    def weight_send(sources, gradients):
        return call(
            kernel_weight_send,
            "weight_send",
            [struct((9, C // 2, LANES), BF16), fields],
            [smem()] + [vmem()] * 8,
            [],
            limit=16,
        )(meta, *sources, *gradients)

    def weight_own(sources, field):
        return call(
            kernel_weight_own,
            "weight_own",
            struct((9, C // 2, LANES), F32),
            [smem()] + [vmem()] * 5,
            [],
            limit=16,
        )(meta, *sources, field)

    def down(terms, level):
        own, send = split_sum([terms], 2, digits[level], meta)
        return [own, swap(send, "dp", levels[level][0])]

    def across(value, level):
        return [value, swap(value, "dp", levels[level][0])]

    def inner_levels(terms):
        for level in range(3, len(levels)):
            terms = down(terms, level)
        value = total_sum(terms)
        for level in range(len(levels) - 1, 2, -1):
            value = join(across(value, level), digits[level], meta)
        return value

    att_keep, att_send = call(
        kernel_attention_grad,
        "attention_grad",
        [struct((2, 4, C, LANES), BF16)] * 2,
        [smem()] + [vmem()] * 4,
        [pltpu.VMEM((4, LANES, pixels), BF16)],
    )(meta, dqkv, mixed, attn_t, cot)
    dqkv, att_send, second_y, second_c, factors = tie(dqkv, att_send, second_y, second_c, factors)
    second_d = swap(second_y, "mp", 1)
    att = [att_keep.reshape(8, C, LANES), swap(att_send, "mp", 1).reshape(8, C, LANES)]
    dmiddle, field2, sums, *gradients2 = call(
        kernel_back_attention,
        "back_attention",
        [block32, fields, struct((4, S_ROWS, LANES), F32)] + [piece] * 4,
        [smem()] + [vmem()] * 7,
        [grad_scratch],
    )(meta, dqkv, cot, middle, pack, stats2, dctx, qkv_w)
    gradients2, second_d, first_y, first_c, att, field2 = tie(
        gradients2, second_d, first_y, first_c, att, field2
    )
    first_d = swap(first_y, "mp", 1)
    seconds = (second_t, second_c, second_y, second_d)
    gradients2 = exchange(gradients2)
    att = down(att, 0)
    field2, att[0] = tie(field2, att[0])
    field1, sums, *gradients1 = call(
        kernel_back_second,
        "back_second",
        [fields, struct((4, S_ROWS, LANES), F32)] + [piece] * 4,
        [smem()] + [vmem()] * 6,
        [grad_scratch],
        limit=12,
    )(meta, field2, inner, pack, stats1, sums, rest_all)
    gradients1, gradients2, att, first_d = tie(gradients1, gradients2, att, first_d)
    firsts = (first_t, first_c, first_y, first_d)
    gradients1 = exchange(gradients1)
    att = down(att, 1)
    gradients2, att[0] = tie(gradients2, att[0])
    send2, wide2 = weight_send(seconds, gradients2)
    got2 = swap(send2, "dp", 1)
    wide2, att = tie(wide2, att)
    att = down(att, 2)
    field1, wide2, att[0] = tie(field1, wide2, att[0])
    grad_first = call(
        kernel_back_conv,
        "back_conv",
        block32,
        [vmem()] * 2,
        [],
    )(field1, conv1_all)
    grad_first, att, wide2 = tie(grad_first, att, wide2)
    for level in range(3, len(levels)):
        att = down(att, level)
    att_own, att_far = call(
        kernel_far,
        "att_far",
        [struct((4,) + att[0].shape[1:], F32), struct((4,) + att[0].shape[1:], BF16)],
        [vmem()] * 2,
        [],
        limit=12,
    )(*att)
    wide2, att_own = tie(wide2, att_own)
    att = [att_own, swap(att_far, "mp", 2)]
    own2 = weight_own(seconds, wide2)
    own2, gradients1, att = tie(own2, gradients1, att)
    att = total_sum(att)
    for level in range(len(levels) - 1, 2, -1):
        att = join(across(att, level), digits[level], meta)
    gradients1, att, out_far = tie(gradients1, att, out_far)
    att = across(att, 2)
    send1, wide1 = weight_send(firsts, gradients1)
    got1 = swap(send1, "dp", 1)
    out_far = swap(out_far, "mp", 2)
    wide1, got2, own2 = tie(wide1, got2, own2)
    terms2 = down([own2, got2], 1)
    wide1, terms2[0] = tie(wide1, terms2[0])
    own1 = weight_own(firsts, wide1)
    grad_first, own1, terms2, att = tie(grad_first, own1, terms2, att)
    terms2 = down(terms2, 2)
    att = across(join(att, digits[2], meta), 1)
    grad_first, terms2[0], att[0] = tie(grad_first, terms2[0], att[0])
    grad_own, grad_near, grad_far = call(
        kernel_back_first,
        "back_first",
        [
            struct((pixels + S_ROWS, LANES), BF16),
            struct((pixels + S_ROWS, LANES), BF16),
            struct((2, pixels + S_ROWS, LANES), BF16),
        ],
        [smem()] + [vmem()] * 6,
        [grad_scratch, pltpu.VMEM((4, S_ROWS, LANES), F32)],
    )(meta, grad_first, image, pack, stats1, dmiddle, sums)
    grad_far, got1, own1 = tie(grad_far, got1, own1)
    terms1 = down([own1, got1], 1)
    terms1[0], terms2 = tie(terms1[0], terms2)
    ends2 = across(inner_levels(terms2), 2)
    factors, ends2[0], terms1[0] = tie(factors, ends2[0], terms1[0])
    columns = -(-5 * slots * lax.axis_size("dp") // LANES) * LANES
    left = call(
        kernel_factors,
        "factors",
        struct((EMB, columns), BF16),
        [smem()] + [vmem()] * 2,
        [],
        limit=12 if len(steps) < 4 else 56,
    )(meta, *factors)
    grad_far, ends2, terms1, left, out_far = tie(grad_far, ends2, terms1, left, out_far)
    terms1 = down(terms1, 2)
    ends2 = across(join(ends2, digits[2], meta), 1)
    grad_far = swap(grad_far, "mp", 2)
    scale = call(kernel_scale, "scale", struct((8, LANES), F32), [vmem()] * 2, [], limit=8)(*factors)
    ends2, terms1, scale = tie(ends2, terms1, scale)
    ends1 = across(inner_levels(terms1), 2)
    ends2 = across(join(ends2, digits[1], meta), 0)
    ends1, grad_near, grad_far, att = tie(ends1, grad_near, grad_far, att)
    ends1 = across(join(ends1, digits[2], meta), 1)
    att = across(join(att, digits[1], meta), 0)
    grad_near = swap(grad_near, "mp", 1)
    grad_across = swap(grad_far, "mp", 1)
    image_parts = (grad_own, grad_near, grad_far, grad_across)
    smalls = call(
        kernel_small_stack,
        "stack",
        struct((4, S_ROWS, LANES), BF16),
        [vmem()] * 4,
        [],
        limit=8,
    )(grad_own, grad_near, grad_far, grad_across)
    small_got = swap(smalls, "dp", 1)
    ends1 = across(join(ends1, digits[1], meta), 0)
    ends1[0], small_got, ends2, att = tie(ends1[0], small_got, ends2, att)
    smalls = stack([smalls, small_got])
    for low in steps[1:-1]:
        smalls = stack([smalls, swap(smalls, "dp", low)])
    small_got = swap(smalls, "dp", steps[-1])
    (conv2_grad,) = last_join(ends2, digits[0], meta, scale)
    qkv_grad, proj_grad = last_join(att, digits[0], meta, scale, True)
    def in_slots(parts):
        return pl.pallas_call(
            kernel_slots,
            name="slots",
            out_shape=struct((4, pixels, LANES), BF16),
            in_specs=[smem()] + [anywhere()] * 4,
            out_specs=vmem(),
            scratch_shapes=[pltpu.SemaphoreType.DMA((4,))],
            compiler_params=pltpu.CompilerParams(vmem_limit_bytes=8 * MIB),
        )(meta, *parts)

    image_grad = in_slots(image_parts)
    small_got, image_grad, conv2_grad, qkv_grad, out_far, out_near = tie(
        small_got, image_grad, conv2_grad, qkv_grad, out_far, out_near
    )
    out_parts = (out_own, swap(out_near, "mp", 1), out_far, swap(out_far, "mp", 1))
    embed_grad, context_grad, vector_sums = call(
        kernel_factor_grads,
        "factor_grads",
        [
            struct((EMB, 2, LANES), F32),
            struct((EMB, 2, LANES), F32),
            struct((S_ROWS, LANES), F32),
        ],
        [vmem()] * 4,
        [],
        limit=14 if len(steps) < 4 else 56,
    )(scale, left, smalls, small_got)

    out_parts, embed_grad = tie(out_parts, embed_grad)
    block_out = in_slots(out_parts)
    ends1, block_out = tie(ends1, block_out)
    (conv1_grad,) = last_join(ends1, digits[0], meta, scale)
    return (
        block_out,
        image_grad,
        vector_sums[S_G1],
        vector_sums[S_B1],
        conv1_grad.reshape(3, 3, C, LANES),
        embed_grad,
        vector_sums[S_G2],
        vector_sums[S_B2],
        conv2_grad.reshape(3, 3, C, LANES),
        vector_sums[S_CB2],
        vector_sums[S_G3],
        vector_sums[S_B3],
        jnp.transpose(qkv_grad, (1, 0, 2)),
        context_grad,
        proj_grad,
    )


def solution(mesh):
    return jax.shard_map(
        local,
        mesh=mesh,
        in_specs=(
            P("dp", None, "mp"),
            P("dp", None, "mp"),
            P("dp"),
            P("dp", None),
            P("dp", None, None),
            P("dp"),
            P("mp"),
            P("mp"),
            P(None, None, None, "mp"),
            P(None, None, "mp"),
            P("mp"),
            P("mp"),
            P(None, None, None, "mp"),
            P("mp"),
            P("mp"),
            P("mp"),
            P(None, None, "mp"),
            P(None, None, "mp"),
            P("mp", None),
        ),
        out_specs=(
            P("dp", None, "mp"),
            P("dp", None, "mp"),
            P("mp"),
            P("mp"),
            P(None, None, None, "mp"),
            P(None, None, "mp"),
            P("mp"),
            P("mp"),
            P(None, None, None, "mp"),
            P("mp"),
            P("mp"),
            P("mp"),
            P(None, None, "mp"),
            P(None, None, "mp"),
            P("mp", None),
        ),
        check_vma=False,
    )
```
